32 devices in a mesh: dp: 2 (over core), seq: 16 (over z, y, x).
Axes of the slice: x: 2, y: 2, z: 4, core: 2. Of those that a mesh axis runs over, the one named last changes fastest.
Arguments:
- tokens: bfloat16 [32768, 768], P(('dp', 'seq')), may hold values from -6 to 6
- doc_start: int32 [32768], P(('dp', 'seq')), may hold values from 0 to 32767, as said below
- real: int32 [32768], P(('dp', 'seq')), may hold values from 0 to 1, as said below
- w_qkv: bfloat16 [768, 2304], P('dp', 'seq'), may hold values from -0.3125 to 0.3125
- w_out: bfloat16 [768, 768], P('dp', 'seq'), may hold values from -1 to 1
- w_in: bfloat16 [768, 2304], P('dp', 'seq'), may hold values from -0.21875 to 0.21875
- w_down: bfloat16 [1152, 768], P('dp', 'seq'), may hold values from -0.375 to 0.375
- gain_attn: bfloat16 [768], P('seq'), may hold values from 0.5 to 1.5
- gain_mlp: bfloat16 [768], P('seq'), may hold values from 0.5 to 1.5
- cotangent: bfloat16 [32768, 768], P(('dp', 'seq')), may hold values from -6 to 6
Outputs:
- output: bfloat16 [32768, 768], P(('dp', 'seq'))
- grad_tokens: float32 [32768, 768], P(('dp', 'seq'))
- grad_w_qkv: float32 [768, 2304], P('dp', 'seq')
- grad_w_out: float32 [768, 768], P('dp', 'seq')
- grad_w_in: float32 [768, 2304], P('dp', 'seq')
- grad_w_down: float32 [1152, 768], P('dp', 'seq')
- grad_gain_attn: float32 [768], P('seq')
- grad_gain_mlp: float32 [768], P('seq')
The draws below stay inside these ranges and needn't reach their ends.
Inputs may be any that keep to these rules, and one draw needn't show every extreme that they name: `doc_start`: for each slot, the index in the whole stream of 32768 slots of the first slot of its document; packed rows begin at slots 8192 / 2 + k * 8192, so the first and the last row hold 4096 slots and the others 8192; documents never cross a row, and a row's padding forms a document of its own. `real`: each packed row ends in one or more padding slots and has no others.
All inputs are finite; a program needn't handle non-finite values.
Results may differ from the reference program's by a relative error of at most 0.014.
The reference program's roundings to bfloat16 on the way count: a program that leaves them out, or rounds other values in their place, can miss the bound.
Values may be sent and summed in bfloat16 or wider, within the bound.
A program may use at most 192 MiB of HBM per device.

```python
import math
import jax
import jax.numpy as jnp
from jax import lax

D = 768
HEADS = 12
HEAD = 64
FF = 1152
HALF = 64
ROW_LENGTH = 8192
TOKEN_SLOTS = 32768


def doc_layout(key):
    first_random_key, second_random_key = jax.random.split(jax.random.fold_in(key, 11))
    slot_index = jnp.arange(TOKEN_SLOTS, dtype=jnp.int32)
    shifted = slot_index + ROW_LENGTH // 2
    within_row = shifted % ROW_LENGTH
    packed_row_index = shifted // ROW_LENGTH
    packed_row_count = TOKEN_SLOTS // ROW_LENGTH + 1
    padding_count = jax.random.randint(second_random_key, (packed_row_count,), 1, ROW_LENGTH // 16 + 2, dtype=jnp.int32)
    row_end = jnp.where(packed_row_index == packed_row_count - 1, ROW_LENGTH // 2, ROW_LENGTH)
    used_slots = row_end - padding_count[packed_row_index]
    real = (within_row < used_slots).astype(jnp.int32)
    middle = TOKEN_SLOTS // 2
    far_from_middle = jnp.abs(slot_index - middle) > 2 * HALF
    document_begins = jax.random.randint(first_random_key, (TOKEN_SLOTS,), 0, max(ROW_LENGTH // 32, 2), dtype=jnp.int32) == 0
    document_begins = document_begins & (within_row < used_slots) & far_from_middle | (within_row == 0) | (within_row == used_slots) | (slot_index == 0)
    starts = lax.cummax(jnp.where(document_begins, slot_index, 0), axis=0)
    return (starts, real)


def draw_doc_start(key, part):
    return doc_layout(key)[0]


def draw_real(key, part):
    return doc_layout(key)[1]


def levels(rng, dims, cuts, smallest, largest):
    def one(position, blocks):
        draws = jax.random.uniform(jax.random.fold_in(jax.random.fold_in(rng, 6), position), (blocks,), jnp.float32, smallest / len(cuts), largest / len(cuts))
        return jnp.repeat(jnp.exp(draws), dims[position] // blocks).reshape((-1,) + (1,) * (len(dims) - position - 1))

    factor_of = one(*cuts[0])
    for cut in cuts[1:]:
        factor_of = factor_of * one(*cut)
    return factor_of


def normal_values(rng, extent, deviation, limit, pieces=(), kind=jnp.bfloat16):
    loudness = levels(rng, extent, pieces, -0.22, 0.18) if pieces else 1.0
    values = jax.random.normal(rng, extent, jnp.float32) * deviation * loudness
    return jnp.minimum(jnp.maximum(values, -limit), limit).astype(kind)


def setup_inputs(seed: int = 0) -> dict:
    key_of = jax.random.split(jax.random.key(seed), 11)
    tokens = normal_values(key_of[0], (TOKEN_SLOTS, D), 1.0, 6.0, ((0, 32),))
    doc_start = draw_doc_start(jax.random.fold_in(key_of[10], 71), 0)
    real = draw_real(jax.random.fold_in(key_of[10], 71), 0)
    w_qkv = normal_values(key_of[3], (D, 3 * D), (D // 2) ** -0.5, 0.3125, ((0, 2), (1, 16)))
    w_out = normal_values(key_of[4], (D, D), 32 ** -0.5, 1.0, ((0, 2), (1, 16)))
    w_in = normal_values(key_of[5], (D, 2 * FF), D ** -0.5, 0.21875, ((0, 2), (1, 16)))
    w_down = normal_values(key_of[6], (FF, D), (FF // 4) ** -0.5, 0.375, ((0, 2), (1, 16)))
    gain_attn = jnp.clip(1.0 + 0.1 * jax.random.normal(key_of[7], (D,), jnp.float32), 0.5, 1.5).astype(jnp.bfloat16)
    gain_mlp = jnp.clip(1.0 + 0.1 * jax.random.normal(key_of[8], (D,), jnp.float32), 0.5, 1.5).astype(jnp.bfloat16)
    cotangent = normal_values(key_of[9], (TOKEN_SLOTS, D), 1.0, 6.0, ((0, 32),))
    return dict(tokens=tokens, doc_start=doc_start, real=real, w_qkv=w_qkv, w_out=w_out, w_in=w_in, w_down=w_down, gain_attn=gain_attn, gain_mlp=gain_mlp, cotangent=cotangent)


@jax.custom_vjp
def low(v):
    return lax.optimization_barrier(v.astype(jnp.bfloat16)).astype(jnp.float32)

@jax.custom_vjp
def low_back(v):
    return v

def low_keep(v):
    return (low(v), None)

def low_pass(kept, grad):
    return (grad,)

def back_keep(v):
    return (v, None)

def back_low(kept, grad):
    return (low(grad),)
low.defvjp(low_keep, low_pass)
low_back.defvjp(back_keep, back_low)

def matmul(left, right):
    return jnp.dot(left, right, precision=lax.Precision.HIGHEST, preferred_element_type=jnp.float32)

def layer_norm(value):
    centre = value - lax.optimization_barrier(jnp.mean(value, axis=-1, keepdims=True))
    return centre * lax.rsqrt(lax.optimization_barrier(jnp.mean(centre * centre, axis=-1, keepdims=True)) + 1e-05)

def rotary_tables(place):
    freq = jnp.exp(jnp.arange(HEAD // 2, dtype=jnp.float32) * (-2.0 * math.log(10000.0) / HEAD))
    angle = place[:, None] * freq[None, :]
    cosine = jnp.tile(jnp.concatenate([jnp.cos(angle), jnp.cos(angle)], 1), (1, HEADS))
    sine = jnp.tile(jnp.concatenate([jnp.sin(angle), jnp.sin(angle)], 1), (1, HEADS))
    return (cosine, sine)

def rotate(value):
    count = value.shape[0]
    shaped = value.reshape(count, HEADS, HEAD)
    first = shaped[..., :HEAD // 2]
    second = shaped[..., HEAD // 2:]
    return jnp.concatenate([-second, first], -1).reshape(count, HEADS * HEAD)

def window_mask(own, other, count, width):
    offset = jnp.arange(width, dtype=jnp.int32)[None, :] - jnp.arange(count, dtype=jnp.int32)[:, None] - HALF
    near = jnp.abs(offset) <= HALF
    return near & ((other[None, :] == own[:, None]) | (offset == 0))

def local_attention(query, keys, values, tag_q, tag_k):
    count = query.shape[0]
    block_rows = 512 if count % 512 == 0 else count
    width = block_rows + 2 * HALF
    keys_pad = jnp.pad(keys, ((HALF, HALF), (0, 0)))
    values_pad = jnp.pad(values, ((HALF, HALF), (0, 0)))
    tag_pad = jnp.pad(tag_k, (HALF, HALF))

    def one_block(slot_index):
        start = slot_index * block_rows
        q_blk = lax.dynamic_slice_in_dim(query, start, block_rows, 0).reshape(block_rows, HEADS, HEAD)
        k_blk = lax.dynamic_slice_in_dim(keys_pad, start, width, 0).reshape(width, HEADS, HEAD)
        v_blk = lax.dynamic_slice_in_dim(values_pad, start, width, 0).reshape(width, HEADS, HEAD)
        own = lax.dynamic_slice_in_dim(tag_q, start, block_rows, 0)
        other = lax.dynamic_slice_in_dim(tag_pad, start, width, 0)
        scores = jnp.einsum('qhd,khd->hqk', q_blk, k_blk, precision=lax.Precision.HIGHEST) * 0.125
        mask = window_mask(own, other, block_rows, width)
        scores = low_back(jnp.where(mask[None], scores, -1e+30))
        probs = jax.nn.softmax(scores, axis=-1)
        mixed = jnp.einsum('hqk,khd->qhd', low(probs), v_blk, precision=lax.Precision.HIGHEST)
        return mixed.reshape(block_rows, HEADS * HEAD)
    blocks = lax.map(jax.checkpoint(one_block), jnp.arange(count // block_rows, dtype=jnp.int32))
    return blocks.reshape(count, HEADS * HEAD)

def reference(tokens, doc_start, real, w_qkv, w_out, w_in, w_down, gain_attn, gain_mlp, cotangent):
    stream = tokens.astype(jnp.float32)
    tag_q = doc_start + 1
    tag_k = jnp.where(real == 1, tag_q, 0)
    place = (jnp.arange(TOKEN_SLOTS, dtype=jnp.int32) - doc_start).astype(jnp.float32)
    cosine, sine = rotary_tables(place)

    def rope(value):
        return value * cosine + rotate(value) * sine

    def forward(inputs, qkv_weight, out_weight, in_weight, down_weight, gain_one, gain_two):
        h_attn = low(layer_norm(inputs) * gain_one)
        qkv = low_back(matmul(h_attn, qkv_weight))
        query = low(rope(qkv[:, :D]))
        keys = low(rope(qkv[:, D:2 * D]))
        values = low(qkv[:, 2 * D:])
        attended = low_back(low(local_attention(query, keys, values, tag_q, tag_k)))
        mid = inputs + low_back(matmul(attended, out_weight))
        h_mlp = low(layer_norm(mid) * gain_two)
        gate_up = low_back(matmul(h_mlp, in_weight))
        hidden = low(jax.nn.gelu(gate_up[:, :FF], approximate=False) * gate_up[:, FF:])
        return mid + low_back(matmul(hidden, down_weight))
    result, pull = jax.vjp(forward, stream, w_qkv.astype(jnp.float32), w_out.astype(jnp.float32), w_in.astype(jnp.float32), w_down.astype(jnp.float32), gain_attn.astype(jnp.float32), gain_mlp.astype(jnp.float32))
    grads = pull(cotangent.astype(jnp.float32))
    return (result.astype(jnp.bfloat16), grads[0], grads[1], grads[2], grads[3], grads[4], grads[5], grads[6])
```

```python
import math

import jax
import jax.numpy as jnp
from jax import lax
from jax.sharding import PartitionSpec as P

D = 768
HEADS = 12
HEAD = 64
FF = 1152
HALF = 64


def padded(value, sides, width):
    for axis, dim in sides:
        size, length = (lax.axis_size(axis), value.shape[dim])
        up = [(i, (i + 1) % size) for i in range(size - 1)]
        down = [(j, i) for i, j in up]
        last = lax.slice_in_dim(value, length - width, length, axis=dim)
        initial = lax.slice_in_dim(value, 0, width, axis=dim)
        before = lax.ppermute(last, axis, up)
        after = lax.ppermute(initial, axis, down)
        value = jnp.concatenate([before, value, after], axis=dim)
    return value


def shifted(value, axis, by):
    length = lax.axis_size(axis)
    pairs = [(i, i + by) for i in range(length) if 0 <= i + by < length]
    return lax.ppermute(value, axis, pairs)


def layer_norm(value):
    centre = value - jnp.mean(value, axis=-1, keepdims=True)
    factor = lax.rsqrt(jnp.mean(centre * centre, axis=-1, keepdims=True) + 1e-05)
    return (centre * factor, factor)


def norm_back(grad, normed, factor):
    return factor * (
        grad
        - jnp.mean(grad, axis=-1, keepdims=True)
        - normed * jnp.mean(grad * normed, axis=-1, keepdims=True)
    )


def rotary_tables(place):
    freq = jnp.exp(jnp.arange(HEAD // 2, dtype=jnp.float32) * (-2.0 * math.log(10000.0) / HEAD))
    angle = place[:, None] * freq[None, :]
    cosine = jnp.tile(jnp.concatenate([jnp.cos(angle), jnp.cos(angle)], 1), (1, HEADS))
    sine = jnp.tile(jnp.concatenate([jnp.sin(angle), jnp.sin(angle)], 1), (1, HEADS))
    return (cosine, sine)


def rotate(value):
    count = value.shape[0]
    shaped = value.reshape(count, HEADS, HEAD)
    first = shaped[..., : HEAD // 2]
    second = shaped[..., HEAD // 2 :]
    return jnp.concatenate([-second, first], -1).reshape(count, HEADS * HEAD)


def window_mask(own, other, count, width):
    offset = (
        jnp.arange(width, dtype=jnp.int32)[None, :]
        - jnp.arange(count, dtype=jnp.int32)[:, None]
        - HALF
    )
    near = jnp.abs(offset) <= HALF
    return near & ((other[None, :] == own[:, None]) | (offset == 0))


def left_dot(left, right):
    return lax.dot_general(
        left, right, (((0,), (0,)), ((), ())), preferred_element_type=jnp.float32
    )


def right_dot(left, right):
    return lax.dot_general(
        left, right, (((1,), (1,)), ((), ())), preferred_element_type=jnp.float32
    )


def glu_piece(gate_up):
    return jax.nn.gelu(gate_up[:, :FF], approximate=False) * gate_up[:, FF:]


def gather_blocks(parts, n_dp, n_seq):
    flat = jnp.concatenate([p.reshape(-1) for p in parts])
    every = lax.all_gather(flat, ("dp", "seq"), axis=0, tiled=False)
    out = []
    offset = 0
    for p in parts:
        size = p.size
        piece = every[:, offset : offset + size]
        offset += size
        if p.ndim == 2:
            rows, cols = p.shape
            out.append(
                piece.reshape(n_dp, n_seq, rows, cols)
                .transpose(0, 2, 1, 3)
                .reshape(n_dp * rows, n_seq * cols)
            )
        else:
            out.append(piece[:n_seq].reshape(-1))
    return out


def scatter_blocks(parts, n_dp, n_seq):
    pieces = []
    for p in parts:
        if p.ndim == 2:
            rows, cols = p.shape
            pieces.append(
                p.reshape(n_dp, rows // n_dp, n_seq, cols // n_seq)
                .transpose(0, 2, 1, 3)
                .reshape(n_dp * n_seq, -1)
            )
        else:
            block = p.reshape(1, n_seq, -1)
            pieces.append(jnp.broadcast_to(block, (n_dp, n_seq, block.shape[-1])).reshape(n_dp * n_seq, -1))
    flat = jnp.concatenate(pieces, 1)
    mine = lax.psum_scatter(flat, ("dp", "seq"), scatter_dimension=0, tiled=False)
    out = []
    offset = 0
    for p in parts:
        if p.ndim == 2:
            rows, cols = p.shape
            shape = (rows // n_dp, cols // n_seq)
        else:
            shape = (p.shape[0] // n_seq,)
        size = math.prod(shape)
        out.append(mine[offset : offset + size].reshape(shape))
        offset += size
    return out


def on_device(tokens, doc_start, real, w_qkv, w_out, w_in, w_down, gain_attn, gain_mlp, cotangent):
    count = tokens.shape[0]
    n_dp, n_seq = lax.axis_size("dp"), lax.axis_size("seq")
    full_qkv, gain_one = gather_blocks((w_qkv, gain_attn), n_dp, n_seq)
    full_out, full_in, full_down, gain_two = gather_blocks((w_out, w_in, w_down, gain_mlp), n_dp, n_seq)
    gain_one = gain_one.astype(jnp.float32)
    gain_two = gain_two.astype(jnp.float32)
    stream = tokens.astype(jnp.float32)
    normed_a, factor_a = layer_norm(stream)
    h_attn = (normed_a * gain_one).astype(jnp.bfloat16)
    qkv = jnp.dot(h_attn, full_qkv, preferred_element_type=jnp.float32)
    offset_base = lax.axis_index(("dp", "seq")) * count
    place = (offset_base + jnp.arange(count, dtype=jnp.int32) - doc_start).astype(jnp.float32)
    cosine, sine = rotary_tables(place)
    query = (qkv[:, :D] * cosine + rotate(qkv[:, :D]) * sine).astype(jnp.bfloat16)
    key_rows = (qkv[:, D : 2 * D] * cosine + rotate(qkv[:, D : 2 * D]) * sine).astype(jnp.bfloat16)
    value_rows = qkv[:, 2 * D :].astype(jnp.bfloat16)
    tag_query = doc_start + 1
    tag_key = jnp.where(real == 1, tag_query, 0)
    key_value = jnp.concatenate([key_rows, value_rows], 1)
    wide_kv, wide_tag = (
        padded(key_value, ((("dp", "seq"), 0),), HALF),
        padded(tag_key, ((("dp", "seq"), 0),), HALF),
    )
    block_rows = 512
    width = block_rows + 2 * HALF
    blocks = count // block_rows

    def block_scores(start):
        q_blk = query[start : start + block_rows].reshape(block_rows, HEADS, HEAD)
        k_blk = wide_kv[start : start + width, :D].reshape(width, HEADS, HEAD)
        v_blk = wide_kv[start : start + width, D:].reshape(width, HEADS, HEAD)
        scores = (
            jnp.einsum("qhd,khd->hqk", q_blk, k_blk, preferred_element_type=jnp.float32) * 0.125
        )
        mask = window_mask(
            tag_query[start : start + block_rows],
            wide_tag[start : start + width],
            block_rows,
            width,
        )
        return (jnp.where(mask[None], scores, -1e30), q_blk, k_blk, v_blk)

    attended = []
    log_totals = []
    for number in range(blocks):
        scores, q_blk, k_blk, v_blk = block_scores(number * block_rows)
        largest = jnp.max(scores, axis=-1, keepdims=True)
        raised = jnp.exp(scores - largest)
        total = jnp.sum(raised, axis=-1, keepdims=True)
        probs = raised / total
        log_totals.append(largest + jnp.log(total))
        mixed = jnp.einsum(
            "hqk,khd->qhd", probs.astype(jnp.bfloat16), v_blk, preferred_element_type=jnp.float32
        )
        attended.append(mixed.reshape(block_rows, D))
    attn_out = jnp.concatenate(attended, 0).astype(jnp.bfloat16)
    mid = stream + jnp.dot(attn_out, full_out, preferred_element_type=jnp.float32)
    normed_m, factor_m = layer_norm(mid)
    h_mlp = (normed_m * gain_two).astype(jnp.bfloat16)
    gate_up = jnp.dot(h_mlp, full_in, preferred_element_type=jnp.float32)
    hidden_out, glu_pull = jax.vjp(glu_piece, gate_up)
    hidden = hidden_out.astype(jnp.bfloat16)
    result = mid + jnp.dot(hidden, full_down, preferred_element_type=jnp.float32)
    output = result.astype(jnp.bfloat16)
    grad_down = left_dot(hidden, cotangent)
    grad_hidden = right_dot(cotangent, full_down)
    grad_gate_up = glu_pull(grad_hidden)[0].astype(jnp.bfloat16)
    grad_inw = left_dot(h_mlp, grad_gate_up)
    grad_hmlp = right_dot(grad_gate_up, full_in)
    grad_gain_two = jnp.sum(grad_hmlp * normed_m, axis=0)
    grad_mid = cotangent.astype(jnp.float32) + norm_back(grad_hmlp * gain_two, normed_m, factor_m)
    grad_branch = grad_mid.astype(jnp.bfloat16)
    grad_outw = left_dot(attn_out, grad_branch)
    grad_attn = right_dot(grad_branch, full_out).astype(jnp.bfloat16)
    grad_wide = jnp.zeros((count + 2 * HALF, 2 * D), jnp.float32)
    grad_queries = []
    for number in range(blocks):
        start = number * block_rows
        scores, q_blk, k_blk, v_blk = block_scores(start)
        probs = jnp.exp(scores - log_totals[number])
        probs_low = probs.astype(jnp.bfloat16)
        grad_blk = grad_attn[start : start + block_rows].reshape(block_rows, HEADS, HEAD)
        grad_probs = jnp.einsum("qhd,khd->hqk", grad_blk, v_blk, preferred_element_type=jnp.float32)
        inner = jnp.sum(probs * grad_probs, axis=-1, keepdims=True)
        grad_scores = (probs * (grad_probs - inner)).astype(jnp.bfloat16)
        grad_qblk = (
            jnp.einsum("hqk,khd->qhd", grad_scores, k_blk, preferred_element_type=jnp.float32)
            * 0.125
        )
        grad_kblk = (
            jnp.einsum("hqk,qhd->khd", grad_scores, q_blk, preferred_element_type=jnp.float32)
            * 0.125
        )
        grad_vblk = jnp.einsum(
            "hqk,qhd->khd", probs_low, grad_blk, preferred_element_type=jnp.float32
        )
        grad_queries.append(grad_qblk.reshape(block_rows, D))
        grad_wide = grad_wide.at[start : start + width].add(
            jnp.concatenate([grad_kblk.reshape(width, D), grad_vblk.reshape(width, D)], 1)
        )
    from_above = shifted(grad_wide[:HALF].astype(jnp.bfloat16), ("dp", "seq"), -1).astype(
        jnp.float32
    )
    from_below = shifted(grad_wide[count + HALF :].astype(jnp.bfloat16), ("dp", "seq"), 1).astype(
        jnp.float32
    )
    grad_kv = grad_wide[HALF : HALF + count]
    grad_kv = grad_kv.at[:HALF].add(from_below)
    grad_kv = grad_kv.at[count - HALF :].add(from_above)
    grad_query = jnp.concatenate(grad_queries, 0)
    grad_keys = grad_kv[:, :D]
    grad_qkv = jnp.concatenate(
        [
            grad_query * cosine - rotate(grad_query) * sine,
            grad_keys * cosine - rotate(grad_keys) * sine,
            grad_kv[:, D:],
        ],
        1,
    ).astype(jnp.bfloat16)
    grad_qkvw = left_dot(h_attn, grad_qkv)
    grad_hattn = right_dot(grad_qkv, full_qkv)
    grad_gain_one = jnp.sum(grad_hattn * normed_a, axis=0)
    grad_tokens = grad_mid + norm_back(grad_hattn * gain_one, normed_a, factor_a)
    final = scatter_blocks(
        (grad_qkvw, grad_outw, grad_inw, grad_down, grad_gain_one, grad_gain_two), n_dp, n_seq
    )
    return (output, grad_tokens) + tuple(final)


def solution(mesh):
    placed = (
        P(("dp", "seq"), None),
        P(("dp", "seq")),
        P(("dp", "seq")),
        P("dp", "seq"),
        P("dp", "seq"),
        P("dp", "seq"),
        P("dp", "seq"),
        P("seq"),
        P("seq"),
        P(("dp", "seq"), None),
    )
    return jax.shard_map(
        on_device,
        mesh=mesh,
        in_specs=placed,
        out_specs=(
            P(("dp", "seq"), None),
            P(("dp", "seq"), None),
            P("dp", "seq"),
            P("dp", "seq"),
            P("dp", "seq"),
            P("dp", "seq"),
            P("seq"),
            P("seq"),
        ),
        check_vma=False,
    )
```

```python
import math

import jax
import jax.numpy as jnp
from jax import lax
from jax.sharding import PartitionSpec as P

D = 768
HEADS = 12
HEAD = 64
FF = 1152
HALF = 64


def padded(value, sides, width):
    for axis, dim in sides:
        size, length = (lax.axis_size(axis), value.shape[dim])
        up = [(i, (i + 1) % size) for i in range(size - 1)]
        down = [(j, i) for i, j in up]
        last = lax.slice_in_dim(value, length - width, length, axis=dim)
        initial = lax.slice_in_dim(value, 0, width, axis=dim)
        before = lax.ppermute(last, axis, up)
        after = lax.ppermute(initial, axis, down)
        value = jnp.concatenate([before, value, after], axis=dim)
    return value


def shifted(value, axis, by):
    length = lax.axis_size(axis)
    pairs = [(i, i + by) for i in range(length) if 0 <= i + by < length]
    return lax.ppermute(value, axis, pairs)


def layer_norm(value):
    centre = value - jnp.mean(value, axis=-1, keepdims=True)
    factor = lax.rsqrt(jnp.mean(centre * centre, axis=-1, keepdims=True) + 1e-05)
    return (centre * factor, factor)


def norm_back(grad, normed, factor):
    return factor * (
        grad
        - jnp.mean(grad, axis=-1, keepdims=True)
        - normed * jnp.mean(grad * normed, axis=-1, keepdims=True)
    )


def rotary_tables(place):
    freq = jnp.exp(jnp.arange(HEAD // 2, dtype=jnp.float32) * (-2.0 * math.log(10000.0) / HEAD))
    angle = place[:, None] * freq[None, :]
    cosine = jnp.tile(jnp.concatenate([jnp.cos(angle), jnp.cos(angle)], 1), (1, HEADS))
    sine = jnp.tile(jnp.concatenate([jnp.sin(angle), jnp.sin(angle)], 1), (1, HEADS))
    return (cosine, sine)


def rotate(value):
    count = value.shape[0]
    shaped = value.reshape(count, HEADS, HEAD)
    first = shaped[..., : HEAD // 2]
    second = shaped[..., HEAD // 2 :]
    return jnp.concatenate([-second, first], -1).reshape(count, HEADS * HEAD)


def window_mask(own, other, count, width):
    offset = (
        jnp.arange(width, dtype=jnp.int32)[None, :]
        - jnp.arange(count, dtype=jnp.int32)[:, None]
        - HALF
    )
    near = jnp.abs(offset) <= HALF
    return near & ((other[None, :] == own[:, None]) | (offset == 0))


def left_dot(left, right):
    return lax.dot_general(
        left, right, (((0,), (0,)), ((), ())), preferred_element_type=jnp.float32
    )


def right_dot(left, right):
    return lax.dot_general(
        left, right, (((1,), (1,)), ((), ())), preferred_element_type=jnp.float32
    )


def glu_piece(gate_up):
    return jax.nn.gelu(gate_up[:, :FF], approximate=False) * gate_up[:, FF:]


def padded_to(flat, unit):
    extra = (-flat.shape[0]) % unit
    return jnp.pad(flat, (0, extra)) if extra else flat


def gather_blocks(parts, n_dp, n_seq):
    flat = jnp.concatenate([p.reshape(-1) for p in parts])
    size = flat.shape[0]
    flat = padded_to(flat, 8 * 128)
    every = lax.all_gather(flat.reshape(8, -1), ("dp", "seq"), axis=0, tiled=True)
    every = every.reshape(n_dp * n_seq, -1)[:, :size]
    out = []
    offset = 0
    for p in parts:
        size = p.size
        piece = every[:, offset : offset + size]
        offset += size
        if p.ndim == 2:
            rows, cols = p.shape
            out.append(
                piece.reshape(n_dp, n_seq, rows, cols)
                .transpose(0, 2, 1, 3)
                .reshape(n_dp * rows, n_seq * cols)
            )
        else:
            out.append(piece[:n_seq].reshape(-1))
    return out


def scatter_blocks(parts, n_dp, n_seq):
    pieces = []
    for p in parts:
        if p.ndim == 2:
            rows, cols = p.shape
            pieces.append(
                p.reshape(n_dp, rows // n_dp, n_seq, cols // n_seq)
                .transpose(0, 2, 1, 3)
                .reshape(n_dp * n_seq, -1)
            )
        else:
            block = p.reshape(1, n_seq, -1)
            pieces.append(jnp.broadcast_to(block, (n_dp, n_seq, block.shape[-1])).reshape(n_dp * n_seq, -1))
    flat = jnp.concatenate(pieces, 1)
    size = flat.shape[1]
    extra = (-size) % (8 * 128)
    if extra:
        flat = jnp.pad(flat, ((0, 0), (0, extra)))
    flat = flat.reshape(n_dp * n_seq * 8, -1)
    half = lax.psum_scatter(flat, "dp", scatter_dimension=0, tiled=True)
    mine = lax.psum_scatter(half, "seq", scatter_dimension=0, tiled=True).reshape(-1)
    out = []
    offset = 0
    for p in parts:
        if p.ndim == 2:
            rows, cols = p.shape
            shape = (rows // n_dp, cols // n_seq)
        else:
            shape = (p.shape[0] // n_seq,)
        size = math.prod(shape)
        out.append(mine[offset : offset + size].reshape(shape))
        offset += size
    return out


def on_device(tokens, doc_start, real, w_qkv, w_out, w_in, w_down, gain_attn, gain_mlp, cotangent):
    count = tokens.shape[0]
    n_dp, n_seq = lax.axis_size("dp"), lax.axis_size("seq")
    full_qkv, gain_one = gather_blocks((w_qkv, gain_attn), n_dp, n_seq)
    full_out, full_in, full_down, gain_two = gather_blocks((w_out, w_in, w_down, gain_mlp), n_dp, n_seq)
    gain_one = gain_one.astype(jnp.float32)
    gain_two = gain_two.astype(jnp.float32)
    stream = tokens.astype(jnp.float32)
    normed_a, factor_a = layer_norm(stream)
    h_attn = (normed_a * gain_one).astype(jnp.bfloat16)
    qkv = jnp.dot(h_attn, full_qkv, preferred_element_type=jnp.float32)
    offset_base = lax.axis_index(("dp", "seq")) * count
    place = (offset_base + jnp.arange(count, dtype=jnp.int32) - doc_start).astype(jnp.float32)
    cosine, sine = rotary_tables(place)
    query = (qkv[:, :D] * cosine + rotate(qkv[:, :D]) * sine).astype(jnp.bfloat16)
    key_rows = (qkv[:, D : 2 * D] * cosine + rotate(qkv[:, D : 2 * D]) * sine).astype(jnp.bfloat16)
    value_rows = qkv[:, 2 * D :].astype(jnp.bfloat16)
    tag_query = doc_start + 1
    tag_key = jnp.where(real == 1, tag_query, 0)
    key_value = jnp.concatenate([key_rows, value_rows], 1)
    wide_kv, wide_tag = (
        padded(key_value, ((("dp", "seq"), 0),), HALF),
        padded(tag_key, ((("dp", "seq"), 0),), HALF),
    )
    block_rows = 512
    width = block_rows + 2 * HALF
    blocks = count // block_rows

    def block_scores(start):
        q_blk = query[start : start + block_rows].reshape(block_rows, HEADS, HEAD)
        k_blk = wide_kv[start : start + width, :D].reshape(width, HEADS, HEAD)
        v_blk = wide_kv[start : start + width, D:].reshape(width, HEADS, HEAD)
        scores = (
            jnp.einsum("qhd,khd->hqk", q_blk, k_blk, preferred_element_type=jnp.float32) * 0.125
        )
        mask = window_mask(
            tag_query[start : start + block_rows],
            wide_tag[start : start + width],
            block_rows,
            width,
        )
        return (jnp.where(mask[None], scores, -1e30), q_blk, k_blk, v_blk)

    attended = []
    log_totals = []
    for number in range(blocks):
        scores, q_blk, k_blk, v_blk = block_scores(number * block_rows)
        largest = jnp.max(scores, axis=-1, keepdims=True)
        raised = jnp.exp(scores - largest)
        total = jnp.sum(raised, axis=-1, keepdims=True)
        probs = raised / total
        log_totals.append(largest + jnp.log(total))
        mixed = jnp.einsum(
            "hqk,khd->qhd", probs.astype(jnp.bfloat16), v_blk, preferred_element_type=jnp.float32
        )
        attended.append(mixed.reshape(block_rows, D))
    attn_out = jnp.concatenate(attended, 0).astype(jnp.bfloat16)
    mid = stream + jnp.dot(attn_out, full_out, preferred_element_type=jnp.float32)
    normed_m, factor_m = layer_norm(mid)
    h_mlp = (normed_m * gain_two).astype(jnp.bfloat16)
    gate_up = jnp.dot(h_mlp, full_in, preferred_element_type=jnp.float32)
    hidden_out, glu_pull = jax.vjp(glu_piece, gate_up)
    hidden = hidden_out.astype(jnp.bfloat16)
    result = mid + jnp.dot(hidden, full_down, preferred_element_type=jnp.float32)
    output = result.astype(jnp.bfloat16)
    grad_down = left_dot(hidden, cotangent)
    grad_hidden = right_dot(cotangent, full_down)
    grad_gate_up = glu_pull(grad_hidden)[0].astype(jnp.bfloat16)
    grad_inw = left_dot(h_mlp, grad_gate_up)
    grad_hmlp = right_dot(grad_gate_up, full_in)
    grad_gain_two = jnp.sum(grad_hmlp * normed_m, axis=0)
    grad_mid = cotangent.astype(jnp.float32) + norm_back(grad_hmlp * gain_two, normed_m, factor_m)
    grad_branch = grad_mid.astype(jnp.bfloat16)
    grad_outw = left_dot(attn_out, grad_branch)
    grad_attn = right_dot(grad_branch, full_out).astype(jnp.bfloat16)
    grad_wide = jnp.zeros((count + 2 * HALF, 2 * D), jnp.float32)
    grad_queries = []
    for number in range(blocks):
        start = number * block_rows
        scores, q_blk, k_blk, v_blk = block_scores(start)
        probs = jnp.exp(scores - log_totals[number])
        probs_low = probs.astype(jnp.bfloat16)
        grad_blk = grad_attn[start : start + block_rows].reshape(block_rows, HEADS, HEAD)
        grad_probs = jnp.einsum("qhd,khd->hqk", grad_blk, v_blk, preferred_element_type=jnp.float32)
        inner = jnp.sum(probs * grad_probs, axis=-1, keepdims=True)
        grad_scores = (probs * (grad_probs - inner)).astype(jnp.bfloat16)
        grad_qblk = (
            jnp.einsum("hqk,khd->qhd", grad_scores, k_blk, preferred_element_type=jnp.float32)
            * 0.125
        )
        grad_kblk = (
            jnp.einsum("hqk,qhd->khd", grad_scores, q_blk, preferred_element_type=jnp.float32)
            * 0.125
        )
        grad_vblk = jnp.einsum(
            "hqk,qhd->khd", probs_low, grad_blk, preferred_element_type=jnp.float32
        )
        grad_queries.append(grad_qblk.reshape(block_rows, D))
        grad_wide = grad_wide.at[start : start + width].add(
            jnp.concatenate([grad_kblk.reshape(width, D), grad_vblk.reshape(width, D)], 1)
        )
    from_above = shifted(grad_wide[:HALF].astype(jnp.bfloat16), ("dp", "seq"), -1).astype(
        jnp.float32
    )
    from_below = shifted(grad_wide[count + HALF :].astype(jnp.bfloat16), ("dp", "seq"), 1).astype(
        jnp.float32
    )
    grad_kv = grad_wide[HALF : HALF + count]
    grad_kv = grad_kv.at[:HALF].add(from_below)
    grad_kv = grad_kv.at[count - HALF :].add(from_above)
    grad_query = jnp.concatenate(grad_queries, 0)
    grad_keys = grad_kv[:, :D]
    grad_qkv = jnp.concatenate(
        [
            grad_query * cosine - rotate(grad_query) * sine,
            grad_keys * cosine - rotate(grad_keys) * sine,
            grad_kv[:, D:],
        ],
        1,
    ).astype(jnp.bfloat16)
    grad_qkvw = left_dot(h_attn, grad_qkv)
    grad_hattn = right_dot(grad_qkv, full_qkv)
    grad_gain_one = jnp.sum(grad_hattn * normed_a, axis=0)
    grad_tokens = grad_mid + norm_back(grad_hattn * gain_one, normed_a, factor_a)
    late_out, late_in, late_down, late_gain_two = scatter_blocks(
        (grad_outw, grad_inw, grad_down, grad_gain_two), n_dp, n_seq
    )
    late_qkv, late_gain_one = scatter_blocks((grad_qkvw, grad_gain_one), n_dp, n_seq)
    return (
        output,
        grad_tokens,
        late_qkv,
        late_out,
        late_in,
        late_down,
        late_gain_one,
        late_gain_two,
    )


def solution(mesh):
    placed = (
        P(("dp", "seq"), None),
        P(("dp", "seq")),
        P(("dp", "seq")),
        P("dp", "seq"),
        P("dp", "seq"),
        P("dp", "seq"),
        P("dp", "seq"),
        P("seq"),
        P("seq"),
        P(("dp", "seq"), None),
    )
    return jax.shard_map(
        on_device,
        mesh=mesh,
        in_specs=placed,
        out_specs=(
            P(("dp", "seq"), None),
            P(("dp", "seq"), None),
            P("dp", "seq"),
            P("dp", "seq"),
            P("dp", "seq"),
            P("dp", "seq"),
            P("seq"),
            P("seq"),
        ),
        check_vma=False,
    )
```

```python
import math

import jax
import jax.numpy as jnp
from jax import lax
from jax.sharding import PartitionSpec as P

D = 768
HEADS = 12
HEAD = 64
FF = 1152
HALF = 64


def padded(value, sides, width):
    for axis, dim in sides:
        size, length = (lax.axis_size(axis), value.shape[dim])
        up = [(i, (i + 1) % size) for i in range(size - 1)]
        down = [(j, i) for i, j in up]
        last = lax.slice_in_dim(value, length - width, length, axis=dim)
        initial = lax.slice_in_dim(value, 0, width, axis=dim)
        before = lax.ppermute(last, axis, up)
        after = lax.ppermute(initial, axis, down)
        value = jnp.concatenate([before, value, after], axis=dim)
    return value


def shifted(value, axis, by):
    length = lax.axis_size(axis)
    pairs = [(i, i + by) for i in range(length) if 0 <= i + by < length]
    return lax.ppermute(value, axis, pairs)


def layer_norm(value):
    centre = value - jnp.mean(value, axis=-1, keepdims=True)
    factor = lax.rsqrt(jnp.mean(centre * centre, axis=-1, keepdims=True) + 1e-05)
    return (centre * factor, factor)


def norm_back(grad, normed, factor):
    return factor * (
        grad
        - jnp.mean(grad, axis=-1, keepdims=True)
        - normed * jnp.mean(grad * normed, axis=-1, keepdims=True)
    )


def rotary_tables(place):
    freq = jnp.exp(jnp.arange(HEAD // 2, dtype=jnp.float32) * (-2.0 * math.log(10000.0) / HEAD))
    angle = place[:, None] * freq[None, :]
    cosine = jnp.tile(jnp.concatenate([jnp.cos(angle), jnp.cos(angle)], 1), (1, HEADS))
    sine = jnp.tile(jnp.concatenate([jnp.sin(angle), jnp.sin(angle)], 1), (1, HEADS))
    return (cosine, sine)


def rotate(value):
    count = value.shape[0]
    shaped = value.reshape(count, HEADS, HEAD)
    first = shaped[..., : HEAD // 2]
    second = shaped[..., HEAD // 2 :]
    return jnp.concatenate([-second, first], -1).reshape(count, HEADS * HEAD)


def window_mask(own, other, count, width):
    offset = (
        jnp.arange(width, dtype=jnp.int32)[None, :]
        - jnp.arange(count, dtype=jnp.int32)[:, None]
        - HALF
    )
    near = jnp.abs(offset) <= HALF
    return near & ((other[None, :] == own[:, None]) | (offset == 0))


def left_dot(left, right):
    return lax.dot_general(
        left, right, (((0,), (0,)), ((), ())), preferred_element_type=jnp.float32
    )


def right_dot(left, right):
    return lax.dot_general(
        left, right, (((1,), (1,)), ((), ())), preferred_element_type=jnp.float32
    )


def glu_piece(gate_up):
    return jax.nn.gelu(gate_up[:, :FF], approximate=False) * gate_up[:, FF:]


def gain_rows(gain, width, rows=8):
    line = jnp.pad(gain, (0, width - gain.shape[0]))
    return jnp.concatenate([line[None], jnp.zeros((rows - 1, width), gain.dtype)], 0)


def gather_rows(payload, n_dp, n_seq):
    every = lax.all_gather(payload, ("dp", "seq"), axis=0, tiled=True)
    return every.reshape(n_dp, n_seq, payload.shape[0], payload.shape[1])


def reduce_rows(blocks):
    n_dp, n_seq, rows, width = blocks.shape
    half = lax.psum_scatter(
        blocks.reshape(n_dp, n_seq * rows, width), "dp", scatter_dimension=0, tiled=True
    )
    return lax.psum_scatter(
        half.reshape(n_seq * rows, width), "seq", scatter_dimension=0, tiled=True
    )


def gain_blocks(grad_gain, n_dp, n_seq, width):
    part = jnp.pad(grad_gain.reshape(n_seq, -1), ((0, 0), (0, width - grad_gain.shape[0] // n_seq)))
    rows = jnp.concatenate([part[:, None], jnp.zeros((n_seq, 7, width), part.dtype)], 1)
    return jnp.broadcast_to(rows[None], (n_dp, n_seq, 8, width))


def front(value, n_dp):
    return value.reshape(value.shape[0], n_dp, -1)


def apply_t(left, weight_t, n_dp):
    return jnp.einsum("tdr,dnr->tn", front(left, n_dp), weight_t, preferred_element_type=jnp.float32)


def apply_back(grad, weight_t):
    out = jnp.einsum("tn,dnr->tdr", grad, weight_t, preferred_element_type=jnp.float32)
    return out.reshape(out.shape[0], -1)


def grad_t(grad, left, n_dp):
    return jnp.einsum("tn,tdr->dnr", grad, front(left, n_dp), preferred_element_type=jnp.float32)


def on_device(tokens, doc_start, real, w_qkv, w_out, w_in, w_down, gain_attn, gain_mlp, cotangent):
    count = tokens.shape[0]
    n_dp, n_seq = lax.axis_size("dp"), lax.axis_size("seq")
    rows, qkv_cols = w_qkv.shape
    out_cols, in_cols = w_out.shape[1], w_in.shape[1]
    down_rows, down_cols = w_down.shape
    down_lines = down_rows * down_cols // rows
    first = gather_rows(jnp.concatenate([w_qkv.T, gain_rows(gain_attn, rows)], 0), n_dp, n_seq)
    second = gather_rows(
        jnp.concatenate(
            [w_out.T, w_in.T, w_down.T.reshape(down_lines, rows), gain_rows(gain_mlp, rows)], 0
        ),
        n_dp,
        n_seq,
    )
    full_qkv = first[:, :, :qkv_cols].reshape(n_dp, n_seq * qkv_cols, rows)
    gain_one = first[0, :, qkv_cols, : gain_attn.shape[0]].reshape(-1).astype(jnp.float32)
    at = 0
    full_out = second[:, :, at : at + out_cols].reshape(n_dp, n_seq * out_cols, rows)
    at += out_cols
    full_in = second[:, :, at : at + in_cols].reshape(n_dp, n_seq * in_cols, rows)
    at += in_cols
    full_down = (
        second[:, :, at : at + down_lines]
        .reshape(n_dp, n_seq, down_cols, down_rows)
        .reshape(n_dp, n_seq * down_cols, down_rows)
    )
    at += down_lines
    gain_two = second[0, :, at, : gain_mlp.shape[0]].reshape(-1).astype(jnp.float32)
    stream = tokens.astype(jnp.float32)
    normed_a, factor_a = layer_norm(stream)
    h_attn = (normed_a * gain_one).astype(jnp.bfloat16)
    qkv = apply_t(h_attn, full_qkv, n_dp)
    offset_base = lax.axis_index(("dp", "seq")) * count
    place = (offset_base + jnp.arange(count, dtype=jnp.int32) - doc_start).astype(jnp.float32)
    cosine, sine = rotary_tables(place)
    query = (qkv[:, :D] * cosine + rotate(qkv[:, :D]) * sine).astype(jnp.bfloat16)
    key_rows = (qkv[:, D : 2 * D] * cosine + rotate(qkv[:, D : 2 * D]) * sine).astype(jnp.bfloat16)
    value_rows = qkv[:, 2 * D :].astype(jnp.bfloat16)
    tag_query = doc_start + 1
    tag_key = jnp.where(real == 1, tag_query, 0)
    key_value = jnp.concatenate([key_rows, value_rows], 1)
    wide_kv, wide_tag = (
        padded(key_value, ((("dp", "seq"), 0),), HALF),
        padded(tag_key, ((("dp", "seq"), 0),), HALF),
    )
    block_rows = 512
    width = block_rows + 2 * HALF
    blocks = count // block_rows

    def block_scores(start):
        q_blk = query[start : start + block_rows].reshape(block_rows, HEADS, HEAD)
        k_blk = wide_kv[start : start + width, :D].reshape(width, HEADS, HEAD)
        v_blk = wide_kv[start : start + width, D:].reshape(width, HEADS, HEAD)
        scores = (
            jnp.einsum("qhd,khd->hqk", q_blk, k_blk, preferred_element_type=jnp.float32) * 0.125
        )
        mask = window_mask(
            tag_query[start : start + block_rows],
            wide_tag[start : start + width],
            block_rows,
            width,
        )
        return (jnp.where(mask[None], scores, -1e30), q_blk, k_blk, v_blk)

    attended = []
    log_totals = []
    for number in range(blocks):
        scores, q_blk, k_blk, v_blk = block_scores(number * block_rows)
        largest = jnp.max(scores, axis=-1, keepdims=True)
        raised = jnp.exp(scores - largest)
        total = jnp.sum(raised, axis=-1, keepdims=True)
        probs = raised / total
        log_totals.append(largest + jnp.log(total))
        mixed = jnp.einsum(
            "hqk,khd->qhd", probs.astype(jnp.bfloat16), v_blk, preferred_element_type=jnp.float32
        )
        attended.append(mixed.reshape(block_rows, D))
    attn_out = jnp.concatenate(attended, 0).astype(jnp.bfloat16)
    mid = stream + apply_t(attn_out, full_out, n_dp)
    normed_m, factor_m = layer_norm(mid)
    h_mlp = (normed_m * gain_two).astype(jnp.bfloat16)
    gate_up = apply_t(h_mlp, full_in, n_dp)
    hidden_out, glu_pull = jax.vjp(glu_piece, gate_up)
    hidden = hidden_out.astype(jnp.bfloat16)
    result = mid + apply_t(hidden, full_down, n_dp)
    output = result.astype(jnp.bfloat16)
    grad_down = grad_t(cotangent, hidden, n_dp)
    grad_hidden = apply_back(cotangent, full_down)
    grad_gate_up = glu_pull(grad_hidden)[0].astype(jnp.bfloat16)
    grad_inw = grad_t(grad_gate_up, h_mlp, n_dp)
    grad_hmlp = apply_back(grad_gate_up, full_in)
    grad_gain_two = jnp.sum(grad_hmlp * normed_m, axis=0)
    grad_mid = cotangent.astype(jnp.float32) + norm_back(grad_hmlp * gain_two, normed_m, factor_m)
    grad_branch = grad_mid.astype(jnp.bfloat16)
    grad_outw = grad_t(grad_branch, attn_out, n_dp)
    grad_attn = apply_back(grad_branch, full_out).astype(jnp.bfloat16)
    grad_wide = jnp.zeros((count + 2 * HALF, 2 * D), jnp.float32)
    grad_queries = []
    for number in range(blocks):
        start = number * block_rows
        scores, q_blk, k_blk, v_blk = block_scores(start)
        probs = jnp.exp(scores - log_totals[number])
        probs_low = probs.astype(jnp.bfloat16)
        grad_blk = grad_attn[start : start + block_rows].reshape(block_rows, HEADS, HEAD)
        grad_probs = jnp.einsum("qhd,khd->hqk", grad_blk, v_blk, preferred_element_type=jnp.float32)
        inner = jnp.sum(probs * grad_probs, axis=-1, keepdims=True)
        grad_scores = (probs * (grad_probs - inner)).astype(jnp.bfloat16)
        grad_qblk = (
            jnp.einsum("hqk,khd->qhd", grad_scores, k_blk, preferred_element_type=jnp.float32)
            * 0.125
        )
        grad_kblk = (
            jnp.einsum("hqk,qhd->khd", grad_scores, q_blk, preferred_element_type=jnp.float32)
            * 0.125
        )
        grad_vblk = jnp.einsum(
            "hqk,qhd->khd", probs_low, grad_blk, preferred_element_type=jnp.float32
        )
        grad_queries.append(grad_qblk.reshape(block_rows, D))
        grad_wide = grad_wide.at[start : start + width].add(
            jnp.concatenate([grad_kblk.reshape(width, D), grad_vblk.reshape(width, D)], 1)
        )
    from_above = shifted(grad_wide[:HALF].astype(jnp.bfloat16), ("dp", "seq"), -1).astype(
        jnp.float32
    )
    from_below = shifted(grad_wide[count + HALF :].astype(jnp.bfloat16), ("dp", "seq"), 1).astype(
        jnp.float32
    )
    grad_kv = grad_wide[HALF : HALF + count]
    grad_kv = grad_kv.at[:HALF].add(from_below)
    grad_kv = grad_kv.at[count - HALF :].add(from_above)
    grad_query = jnp.concatenate(grad_queries, 0)
    grad_keys = grad_kv[:, :D]
    grad_qkv = jnp.concatenate(
        [
            grad_query * cosine - rotate(grad_query) * sine,
            grad_keys * cosine - rotate(grad_keys) * sine,
            grad_kv[:, D:],
        ],
        1,
    ).astype(jnp.bfloat16)
    grad_qkvw = grad_t(grad_qkv, h_attn, n_dp)
    grad_hattn = apply_back(grad_qkv, full_qkv)
    grad_gain_one = jnp.sum(grad_hattn * normed_a, axis=0)
    grad_tokens = grad_mid + norm_back(grad_hattn * gain_one, normed_a, factor_a)
    late = reduce_rows(
        jnp.concatenate(
            [
                grad_outw.reshape(n_dp, n_seq, out_cols, rows),
                grad_inw.reshape(n_dp, n_seq, in_cols, rows),
                grad_down.reshape(n_dp, n_seq, down_cols, down_rows).reshape(
                    n_dp, n_seq, down_lines, rows
                ),
                gain_blocks(grad_gain_two, n_dp, n_seq, rows),
            ],
            2,
        )
    )
    last = reduce_rows(
        jnp.concatenate(
            [
                grad_qkvw.reshape(n_dp, n_seq, qkv_cols, rows),
                gain_blocks(grad_gain_one, n_dp, n_seq, rows),
            ],
            2,
        )
    )
    at = 0
    late_out = late[at : at + out_cols].T
    at += out_cols
    late_in = late[at : at + in_cols].T
    at += in_cols
    late_down = late[at : at + down_lines].reshape(down_cols, down_rows).T
    at += down_lines
    late_gain_two = late[at, : gain_mlp.shape[0]]
    return (
        output,
        grad_tokens,
        last[:qkv_cols].T,
        late_out,
        late_in,
        late_down,
        last[qkv_cols, : gain_attn.shape[0]],
        late_gain_two,
    )


def solution(mesh):
    placed = (
        P(("dp", "seq"), None),
        P(("dp", "seq")),
        P(("dp", "seq")),
        P("dp", "seq"),
        P("dp", "seq"),
        P("dp", "seq"),
        P("dp", "seq"),
        P("seq"),
        P("seq"),
        P(("dp", "seq"), None),
    )
    return jax.shard_map(
        on_device,
        mesh=mesh,
        in_specs=placed,
        out_specs=(
            P(("dp", "seq"), None),
            P(("dp", "seq"), None),
            P("dp", "seq"),
            P("dp", "seq"),
            P("dp", "seq"),
            P("dp", "seq"),
            P("seq"),
            P("seq"),
        ),
        check_vma=False,
    )
```

```python
import functools
import math

import jax
import jax.numpy as jnp
from jax import lax
from jax.experimental import pallas as pl
from jax.experimental.pallas import tpu as pltpu
from jax.sharding import PartitionSpec as P

D = 768
HEADS = 12
HEAD = 64
FF = 1152
HALF = 64


def padded(value, sides, width):
    for axis, dim in sides:
        size, length = (lax.axis_size(axis), value.shape[dim])
        up = [(i, (i + 1) % size) for i in range(size - 1)]
        down = [(j, i) for i, j in up]
        last = lax.slice_in_dim(value, length - width, length, axis=dim)
        initial = lax.slice_in_dim(value, 0, width, axis=dim)
        before = lax.ppermute(last, axis, up)
        after = lax.ppermute(initial, axis, down)
        value = jnp.concatenate([before, value, after], axis=dim)
    return value


def shifted(value, axis, by):
    length = lax.axis_size(axis)
    pairs = [(i, i + by) for i in range(length) if 0 <= i + by < length]
    return lax.ppermute(value, axis, pairs)


def layer_norm(value):
    centre = value - jnp.mean(value, axis=-1, keepdims=True)
    factor = lax.rsqrt(jnp.mean(centre * centre, axis=-1, keepdims=True) + 1e-05)
    return (centre * factor, factor)


def norm_back(grad, normed, factor):
    return factor * (
        grad
        - jnp.mean(grad, axis=-1, keepdims=True)
        - normed * jnp.mean(grad * normed, axis=-1, keepdims=True)
    )


def rotary_tables(place):
    freq = jnp.exp(jnp.arange(HEAD // 2, dtype=jnp.float32) * (-2.0 * math.log(10000.0) / HEAD))
    angle = place[:, None] * freq[None, :]
    cosine = jnp.tile(jnp.concatenate([jnp.cos(angle), jnp.cos(angle)], 1), (1, HEADS))
    sine = jnp.tile(jnp.concatenate([jnp.sin(angle), jnp.sin(angle)], 1), (1, HEADS))
    return (cosine, sine)


def rotate(value):
    count = value.shape[0]
    shaped = value.reshape(count, HEADS, HEAD)
    first = shaped[..., : HEAD // 2]
    second = shaped[..., HEAD // 2 :]
    return jnp.concatenate([-second, first], -1).reshape(count, HEADS * HEAD)


def window_mask(own, other, count, width):
    offset = (
        jnp.arange(width, dtype=jnp.int32)[None, :]
        - jnp.arange(count, dtype=jnp.int32)[:, None]
        - HALF
    )
    near = jnp.abs(offset) <= HALF
    return near & ((other[None, :] == own[:, None]) | (offset == 0))


def left_dot(left, right):
    return lax.dot_general(
        left, right, (((0,), (0,)), ((), ())), preferred_element_type=jnp.float32
    )


def right_dot(left, right):
    return lax.dot_general(
        left, right, (((1,), (1,)), ((), ())), preferred_element_type=jnp.float32
    )


def glu_piece(gate_up):
    return jax.nn.gelu(gate_up[:, :FF], approximate=False) * gate_up[:, FF:]


MESH = pl.DeviceIdType.MESH


def ring_order(mesh):
    n = mesh.shape["seq"]
    try:
        coords = [tuple(mesh.devices[0, s].coords) for s in range(n)]
    except Exception:
        return list(range(n))
    near = [
        [t for t in range(n) if sum(abs(a - b) for a, b in zip(coords[s], coords[t])) == 1]
        for s in range(n)
    ]
    path, seen = [0], {0}

    def grow(budget=[200000]):
        budget[0] -= 1
        if budget[0] < 0:
            return False
        if len(path) == n:
            return 0 in near[path[-1]]
        options = sorted(
            (t for t in near[path[-1]] if t not in seen),
            key=lambda t: sum(1 for u in near[t] if u not in seen),
        )
        for t in options:
            path.append(t)
            seen.add(t)
            if grow():
                return True
            path.pop()
            seen.discard(t)
        return False

    return list(path) if n > 2 and grow() else list(range(n))


def lookup(index, table):
    n = len(table)
    square = n * n
    total = jnp.int32(0)
    for k, value in enumerate(table):
        if value:
            gap = index - k
            differs = lax.div(gap * gap + (square - 1), jnp.int32(square))
            total = total + value * (1 - differs)
    return total


def ring_kernel(order, per_way, h_ref, out_ref, recv, send, ssem, rsem, free):
    n = len(order)
    where = [0] * n
    for p, s in enumerate(order):
        where[s] = p
    d = lax.axis_index("dp")
    me = lax.axis_index("seq")
    pos = lookup(me, where)
    nxt = lookup(lax.rem(pos + 1, n), order)
    prv = lookup(lax.rem(pos + n - 1, n), order)
    piece = out_ref.shape[0] // (2 * per_way)

    barrier = pltpu.get_barrier_semaphore()
    pl.semaphore_signal(barrier, 1, device_id=(d, nxt), device_id_type=MESH)
    pl.semaphore_signal(barrier, 1, device_id=(d, prv), device_id_type=MESH)
    pl.semaphore_wait(barrier, 2)

    lanes = []
    for li in range(2 * per_way):
        forward = li % 2 == 0
        lanes.append((recv.at[li], send.at[li], ssem.at[li], rsem.at[li], free.at[li],
                      nxt if forward else prv, prv if forward else nxt,
                      slice(li * piece, (li + 1) * piece), -1 if forward else 1))
    copies = {}
    for step in range(n - 1):
        slot = step % 2
        for li, (recv, send, ssem, rsem, free, to, frm, rows, sign) in enumerate(lanes):
            q = lax.rem(pos + sign * (1 + step) + n * (step + 2), n)
            own = h_ref[q, rows, :]
            if step == 0:
                part = own
            else:
                copies[(li, step - 1)].wait_recv()
                part = recv[1 - slot].astype(jnp.float32) + own
                if step <= n - 3:
                    pl.semaphore_signal(free, 1, device_id=(d, frm), device_id_type=MESH)
            if step >= 2:
                copies[(li, step - 2)].wait_send()
                pl.semaphore_wait(free, 1)
            send[slot] = part.astype(send.dtype)
            c = pltpu.make_async_remote_copy(
                src_ref=send.at[slot], dst_ref=recv.at[slot],
                send_sem=ssem.at[slot], recv_sem=rsem.at[slot],
                device_id=(d, to), device_id_type=MESH)
            c.start()
            copies[(li, step)] = c
    last = n - 2
    for li, (recv, send, ssem, rsem, free, to, frm, rows, sign) in enumerate(lanes):
        copies[(li, last)].wait_recv()
        out_ref[rows, :] = recv[last % 2].astype(jnp.float32) + h_ref[pos, rows, :]
        if last >= 1:
            copies[(li, last - 1)].wait_send()
        copies[(li, last)].wait_send()


RING_WAYS = 2


def ring_reduce(h, order, per_way, link_dtype=jnp.bfloat16):
    n, rows, width = h.shape
    lanes = 2 * per_way
    piece = rows // lanes
    return pl.pallas_call(
        functools.partial(ring_kernel, tuple(order), per_way),
        out_shape=jax.ShapeDtypeStruct((rows, width), jnp.float32),
        in_specs=[pl.BlockSpec(memory_space=pltpu.VMEM)],
        out_specs=pl.BlockSpec(memory_space=pltpu.VMEM),
        scratch_shapes=[
            pltpu.VMEM((lanes, 2, piece, width), link_dtype),
            pltpu.VMEM((lanes, 2, piece, width), link_dtype),
            pltpu.SemaphoreType.DMA((lanes, 2)),
            pltpu.SemaphoreType.DMA((lanes, 2)),
            pltpu.SemaphoreType.REGULAR((lanes,)),
        ],
        compiler_params=pltpu.CompilerParams(collective_id=1, has_side_effects=True,
                                             vmem_limit_bytes=48 * 1024 * 1024),
    )(h)


def gain_rows(gain, width, rows=8):
    line = jnp.pad(gain, (0, width - gain.shape[0]))
    return jnp.concatenate([line[None], jnp.zeros((rows - 1, width), gain.dtype)], 0)


def gather_rows(payload, n_dp, n_seq):
    every = lax.all_gather(payload, ("dp", "seq"), axis=0, tiled=True)
    return every.reshape(n_dp, n_seq, payload.shape[0], payload.shape[1])


def gain_blocks(grad_gain, n_dp, n_seq, width):
    part = jnp.pad(grad_gain.reshape(n_seq, -1), ((0, 0), (0, width - grad_gain.shape[0] // n_seq)))
    rows = jnp.concatenate([part[:, None], jnp.zeros((n_seq, 7, width), part.dtype)], 1)
    return jnp.broadcast_to(rows[None], (n_dp, n_seq, 8, width))


def front(value, n_dp):
    return value.reshape(value.shape[0], n_dp, -1)


def apply_t(left, weight_t, n_dp):
    return jnp.einsum("tdr,dnr->tn", front(left, n_dp), weight_t, preferred_element_type=jnp.float32)


def apply_back(grad, weight_t):
    out = jnp.einsum("tn,dnr->tdr", grad, weight_t, preferred_element_type=jnp.float32)
    return out.reshape(out.shape[0], -1)


def grad_t(grad, left, n_dp):
    return jnp.einsum("tn,tdr->dnr", grad, front(left, n_dp), preferred_element_type=jnp.float32)


def on_device(order, tokens, doc_start, real, w_qkv, w_out, w_in, w_down, gain_attn, gain_mlp, cotangent):
    count = tokens.shape[0]
    n_dp, n_seq = lax.axis_size("dp"), lax.axis_size("seq")
    rows, qkv_cols = w_qkv.shape
    out_cols, in_cols = w_out.shape[1], w_in.shape[1]
    down_rows, down_cols = w_down.shape
    down_lines = down_rows * down_cols // rows
    first = gather_rows(jnp.concatenate([w_qkv.T, gain_rows(gain_attn, rows)], 0), n_dp, n_seq)
    second = gather_rows(
        jnp.concatenate(
            [w_out.T, w_in.T, w_down.T.reshape(down_lines, rows), gain_rows(gain_mlp, rows)], 0
        ),
        n_dp,
        n_seq,
    )
    full_qkv = first[:, :, :qkv_cols].reshape(n_dp, n_seq * qkv_cols, rows)
    gain_one = first[0, :, qkv_cols, : gain_attn.shape[0]].reshape(-1).astype(jnp.float32)
    at = 0
    full_out = second[:, :, at : at + out_cols].reshape(n_dp, n_seq * out_cols, rows)
    at += out_cols
    full_in = second[:, :, at : at + in_cols].reshape(n_dp, n_seq * in_cols, rows)
    at += in_cols
    full_down = (
        second[:, :, at : at + down_lines]
        .reshape(n_dp, n_seq, down_cols, down_rows)
        .reshape(n_dp, n_seq * down_cols, down_rows)
    )
    at += down_lines
    gain_two = second[0, :, at, : gain_mlp.shape[0]].reshape(-1).astype(jnp.float32)
    stream = tokens.astype(jnp.float32)
    normed_a, factor_a = layer_norm(stream)
    h_attn = (normed_a * gain_one).astype(jnp.bfloat16)
    qkv = apply_t(h_attn, full_qkv, n_dp)
    offset_base = lax.axis_index(("dp", "seq")) * count
    place = (offset_base + jnp.arange(count, dtype=jnp.int32) - doc_start).astype(jnp.float32)
    cosine, sine = rotary_tables(place)
    query = (qkv[:, :D] * cosine + rotate(qkv[:, :D]) * sine).astype(jnp.bfloat16)
    key_rows = (qkv[:, D : 2 * D] * cosine + rotate(qkv[:, D : 2 * D]) * sine).astype(jnp.bfloat16)
    value_rows = qkv[:, 2 * D :].astype(jnp.bfloat16)
    tag_query = doc_start + 1
    tag_key = jnp.where(real == 1, tag_query, 0)
    key_value = jnp.concatenate([key_rows, value_rows], 1)
    wide_kv, wide_tag = (
        padded(key_value, ((("dp", "seq"), 0),), HALF),
        padded(tag_key, ((("dp", "seq"), 0),), HALF),
    )
    block_rows = 512
    width = block_rows + 2 * HALF
    blocks = count // block_rows

    def block_scores(start):
        q_blk = query[start : start + block_rows].reshape(block_rows, HEADS, HEAD)
        k_blk = wide_kv[start : start + width, :D].reshape(width, HEADS, HEAD)
        v_blk = wide_kv[start : start + width, D:].reshape(width, HEADS, HEAD)
        scores = (
            jnp.einsum("qhd,khd->hqk", q_blk, k_blk, preferred_element_type=jnp.float32) * 0.125
        )
        mask = window_mask(
            tag_query[start : start + block_rows],
            wide_tag[start : start + width],
            block_rows,
            width,
        )
        return (jnp.where(mask[None], scores, -1e30), q_blk, k_blk, v_blk)

    attended = []
    log_totals = []
    for number in range(blocks):
        scores, q_blk, k_blk, v_blk = block_scores(number * block_rows)
        largest = jnp.max(scores, axis=-1, keepdims=True)
        raised = jnp.exp(scores - largest)
        total = jnp.sum(raised, axis=-1, keepdims=True)
        probs = raised / total
        log_totals.append(largest + jnp.log(total))
        mixed = jnp.einsum(
            "hqk,khd->qhd", probs.astype(jnp.bfloat16), v_blk, preferred_element_type=jnp.float32
        )
        attended.append(mixed.reshape(block_rows, D))
    attn_out = jnp.concatenate(attended, 0).astype(jnp.bfloat16)
    mid = stream + apply_t(attn_out, full_out, n_dp)
    normed_m, factor_m = layer_norm(mid)
    h_mlp = (normed_m * gain_two).astype(jnp.bfloat16)
    gate_up = apply_t(h_mlp, full_in, n_dp)
    hidden_out, glu_pull = jax.vjp(glu_piece, gate_up)
    hidden = hidden_out.astype(jnp.bfloat16)
    result = mid + apply_t(hidden, full_down, n_dp)
    output = result.astype(jnp.bfloat16)
    grad_down = grad_t(cotangent, hidden, n_dp)
    grad_hidden = apply_back(cotangent, full_down)
    grad_gate_up = glu_pull(grad_hidden)[0].astype(jnp.bfloat16)
    grad_inw = grad_t(grad_gate_up, h_mlp, n_dp)
    grad_hmlp = apply_back(grad_gate_up, full_in)
    grad_gain_two = jnp.sum(grad_hmlp * normed_m, axis=0)
    grad_mid = cotangent.astype(jnp.float32) + norm_back(grad_hmlp * gain_two, normed_m, factor_m)
    grad_branch = grad_mid.astype(jnp.bfloat16)
    grad_outw = grad_t(grad_branch, attn_out, n_dp)
    grad_attn = apply_back(grad_branch, full_out).astype(jnp.bfloat16)
    grad_wide = jnp.zeros((count + 2 * HALF, 2 * D), jnp.float32)
    grad_queries = []
    for number in range(blocks):
        start = number * block_rows
        scores, q_blk, k_blk, v_blk = block_scores(start)
        probs = jnp.exp(scores - log_totals[number])
        probs_low = probs.astype(jnp.bfloat16)
        grad_blk = grad_attn[start : start + block_rows].reshape(block_rows, HEADS, HEAD)
        grad_probs = jnp.einsum("qhd,khd->hqk", grad_blk, v_blk, preferred_element_type=jnp.float32)
        inner = jnp.sum(probs * grad_probs, axis=-1, keepdims=True)
        grad_scores = (probs * (grad_probs - inner)).astype(jnp.bfloat16)
        grad_qblk = (
            jnp.einsum("hqk,khd->qhd", grad_scores, k_blk, preferred_element_type=jnp.float32)
            * 0.125
        )
        grad_kblk = (
            jnp.einsum("hqk,qhd->khd", grad_scores, q_blk, preferred_element_type=jnp.float32)
            * 0.125
        )
        grad_vblk = jnp.einsum(
            "hqk,qhd->khd", probs_low, grad_blk, preferred_element_type=jnp.float32
        )
        grad_queries.append(grad_qblk.reshape(block_rows, D))
        grad_wide = grad_wide.at[start : start + width].add(
            jnp.concatenate([grad_kblk.reshape(width, D), grad_vblk.reshape(width, D)], 1)
        )
    from_above = shifted(grad_wide[:HALF].astype(jnp.bfloat16), ("dp", "seq"), -1).astype(
        jnp.float32
    )
    from_below = shifted(grad_wide[count + HALF :].astype(jnp.bfloat16), ("dp", "seq"), 1).astype(
        jnp.float32
    )
    grad_kv = grad_wide[HALF : HALF + count]
    grad_kv = grad_kv.at[:HALF].add(from_below)
    grad_kv = grad_kv.at[count - HALF :].add(from_above)
    grad_query = jnp.concatenate(grad_queries, 0)
    grad_keys = grad_kv[:, :D]
    grad_qkv = jnp.concatenate(
        [
            grad_query * cosine - rotate(grad_query) * sine,
            grad_keys * cosine - rotate(grad_keys) * sine,
            grad_kv[:, D:],
        ],
        1,
    ).astype(jnp.bfloat16)
    grad_qkvw = grad_t(grad_qkv, h_attn, n_dp)
    grad_hattn = apply_back(grad_qkv, full_qkv)
    grad_gain_one = jnp.sum(grad_hattn * normed_a, axis=0)
    grad_tokens = grad_mid + norm_back(grad_hattn * gain_one, normed_a, factor_a)
    blocks = jnp.concatenate(
        [
            grad_outw.reshape(n_dp, n_seq, out_cols, rows),
            grad_inw.reshape(n_dp, n_seq, in_cols, rows),
            grad_down.reshape(n_dp, n_seq, down_cols, down_rows).reshape(
                n_dp, n_seq, down_lines, rows
            ),
            gain_blocks(grad_gain_two, n_dp, n_seq, rows),
            grad_qkvw.reshape(n_dp, n_seq, qkv_cols, rows),
            gain_blocks(grad_gain_one, n_dp, n_seq, rows),
        ],
        2,
    )
    height = blocks.shape[2]
    lanes_rows = 2 * RING_WAYS * 16
    extra = (-height) % lanes_rows
    if extra:
        blocks = jnp.pad(blocks, ((0, 0), (0, 0), (0, extra), (0, 0)))
    blocks = jnp.stack([blocks[:, s] for s in order], 1)
    depth = blocks.shape[2]
    half = lax.psum_scatter(
        blocks.reshape(n_dp, n_seq * depth, rows), "dp", scatter_dimension=0, tiled=True
    )
    late = ring_reduce(half.reshape(n_seq, depth, rows), order, RING_WAYS)
    last = late[out_cols + in_cols + down_lines + 8 :]
    at = 0
    late_out = late[at : at + out_cols].T
    at += out_cols
    late_in = late[at : at + in_cols].T
    at += in_cols
    late_down = late[at : at + down_lines].reshape(down_cols, down_rows).T
    at += down_lines
    late_gain_two = late[at, : gain_mlp.shape[0]]
    return (
        output,
        grad_tokens,
        last[:qkv_cols].T,
        late_out,
        late_in,
        late_down,
        last[qkv_cols, : gain_attn.shape[0]],
        late_gain_two,
    )


def solution(mesh):
    placed = (
        P(("dp", "seq"), None),
        P(("dp", "seq")),
        P(("dp", "seq")),
        P("dp", "seq"),
        P("dp", "seq"),
        P("dp", "seq"),
        P("dp", "seq"),
        P("seq"),
        P("seq"),
        P(("dp", "seq"), None),
    )
    return jax.shard_map(
        functools.partial(on_device, ring_order(mesh)),
        mesh=mesh,
        in_specs=placed,
        out_specs=(
            P(("dp", "seq"), None),
            P(("dp", "seq"), None),
            P("dp", "seq"),
            P("dp", "seq"),
            P("dp", "seq"),
            P("dp", "seq"),
            P("seq"),
            P("seq"),
        ),
        check_vma=False,
    )
```

```python
import functools
import math

import jax
import jax.numpy as jnp
from jax import lax
from jax.experimental import pallas as pl
from jax.experimental.pallas import tpu as pltpu
from jax.sharding import PartitionSpec as P

D = 768
HEADS = 12
HEAD = 64
FF = 1152
HALF = 64


def padded(value, sides, width):
    for axis, dim in sides:
        size, length = (lax.axis_size(axis), value.shape[dim])
        up = [(i, (i + 1) % size) for i in range(size - 1)]
        down = [(j, i) for i, j in up]
        last = lax.slice_in_dim(value, length - width, length, axis=dim)
        initial = lax.slice_in_dim(value, 0, width, axis=dim)
        before = lax.ppermute(last, axis, up)
        after = lax.ppermute(initial, axis, down)
        value = jnp.concatenate([before, value, after], axis=dim)
    return value


def shifted(value, axis, by):
    length = lax.axis_size(axis)
    pairs = [(i, i + by) for i in range(length) if 0 <= i + by < length]
    return lax.ppermute(value, axis, pairs)


def layer_norm(value):
    centre = value - jnp.mean(value, axis=-1, keepdims=True)
    factor = lax.rsqrt(jnp.mean(centre * centre, axis=-1, keepdims=True) + 1e-05)
    return (centre * factor, factor)


def norm_back(grad, normed, factor):
    return factor * (
        grad
        - jnp.mean(grad, axis=-1, keepdims=True)
        - normed * jnp.mean(grad * normed, axis=-1, keepdims=True)
    )


def rotary_tables(place):
    freq = jnp.exp(jnp.arange(HEAD // 2, dtype=jnp.float32) * (-2.0 * math.log(10000.0) / HEAD))
    angle = place[:, None] * freq[None, :]
    cosine = jnp.tile(jnp.concatenate([jnp.cos(angle), jnp.cos(angle)], 1), (1, HEADS))
    sine = jnp.tile(jnp.concatenate([jnp.sin(angle), jnp.sin(angle)], 1), (1, HEADS))
    return (cosine, sine)


def rotate(value):
    count = value.shape[0]
    shaped = value.reshape(count, HEADS, HEAD)
    first = shaped[..., : HEAD // 2]
    second = shaped[..., HEAD // 2 :]
    return jnp.concatenate([-second, first], -1).reshape(count, HEADS * HEAD)


def left_dot(left, right):
    return lax.dot_general(
        left, right, (((0,), (0,)), ((), ())), preferred_element_type=jnp.float32
    )


def right_dot(left, right):
    return lax.dot_general(
        left, right, (((1,), (1,)), ((), ())), preferred_element_type=jnp.float32
    )


def glu_piece(gate_up):
    return jax.nn.gelu(gate_up[:, :FF], approximate=False) * gate_up[:, FF:]


MESH = pl.DeviceIdType.MESH


def ring_order(mesh):
    n = mesh.shape["seq"]
    try:
        coords = [tuple(mesh.devices[0, s].coords) for s in range(n)]
    except Exception:
        return list(range(n))
    near = [
        [t for t in range(n) if sum(abs(a - b) for a, b in zip(coords[s], coords[t])) == 1]
        for s in range(n)
    ]
    path, seen = [0], {0}

    def grow(budget=[200000]):
        budget[0] -= 1
        if budget[0] < 0:
            return False
        if len(path) == n:
            return 0 in near[path[-1]]
        options = sorted(
            (t for t in near[path[-1]] if t not in seen),
            key=lambda t: sum(1 for u in near[t] if u not in seen),
        )
        for t in options:
            path.append(t)
            seen.add(t)
            if grow():
                return True
            path.pop()
            seen.discard(t)
        return False

    return list(path) if n > 2 and grow() else list(range(n))


def lookup(index, table):
    n = len(table)
    square = n * n
    total = jnp.int32(0)
    for k, value in enumerate(table):
        if value:
            gap = index - k
            differs = lax.div(gap * gap + (square - 1), jnp.int32(square))
            total = total + value * (1 - differs)
    return total


def ring_kernel(order, per_way, h_ref, out_ref, recv, send, ssem, rsem, free):
    n = len(order)
    where = [0] * n
    for p, s in enumerate(order):
        where[s] = p
    d = lax.axis_index("dp")
    me = lax.axis_index("seq")
    pos = lookup(me, where)
    nxt = lookup(lax.rem(pos + 1, n), order)
    prv = lookup(lax.rem(pos + n - 1, n), order)
    piece = out_ref.shape[0] // (2 * per_way)

    barrier = pltpu.get_barrier_semaphore()
    pl.semaphore_signal(barrier, 1, device_id=(d, nxt), device_id_type=MESH)
    pl.semaphore_signal(barrier, 1, device_id=(d, prv), device_id_type=MESH)
    pl.semaphore_wait(barrier, 2)

    lanes = []
    for li in range(2 * per_way):
        forward = li % 2 == 0
        lanes.append((recv.at[li], send.at[li], ssem.at[li], rsem.at[li], free.at[li],
                      nxt if forward else prv, prv if forward else nxt,
                      slice(li * piece, (li + 1) * piece), -1 if forward else 1))
    copies = {}
    for step in range(n - 1):
        slot = step % 2
        for li, (recv, send, ssem, rsem, free, to, frm, rows, sign) in enumerate(lanes):
            q = lax.rem(pos + sign * (1 + step) + n * (step + 2), n)
            own = h_ref[q, rows, :]
            if step == 0:
                part = own
            else:
                copies[(li, step - 1)].wait_recv()
                part = recv[1 - slot].astype(jnp.float32) + own
                if step <= n - 3:
                    pl.semaphore_signal(free, 1, device_id=(d, frm), device_id_type=MESH)
            if step >= 2:
                copies[(li, step - 2)].wait_send()
                pl.semaphore_wait(free, 1)
            send[slot] = part.astype(send.dtype)
            c = pltpu.make_async_remote_copy(
                src_ref=send.at[slot], dst_ref=recv.at[slot],
                send_sem=ssem.at[slot], recv_sem=rsem.at[slot],
                device_id=(d, to), device_id_type=MESH)
            c.start()
            copies[(li, step)] = c
    last = n - 2
    for li, (recv, send, ssem, rsem, free, to, frm, rows, sign) in enumerate(lanes):
        copies[(li, last)].wait_recv()
        out_ref[rows, :] = recv[last % 2].astype(jnp.float32) + h_ref[pos, rows, :]
        if last >= 1:
            copies[(li, last - 1)].wait_send()
        copies[(li, last)].wait_send()


RING_WAYS = 2


def ring_reduce(h, order, per_way, link_dtype=jnp.bfloat16):
    n, rows, width = h.shape
    lanes = 2 * per_way
    piece = rows // lanes
    return pl.pallas_call(
        functools.partial(ring_kernel, tuple(order), per_way),
        out_shape=jax.ShapeDtypeStruct((rows, width), jnp.float32),
        in_specs=[pl.BlockSpec(memory_space=pltpu.VMEM)],
        out_specs=pl.BlockSpec(memory_space=pltpu.VMEM),
        scratch_shapes=[
            pltpu.VMEM((lanes, 2, piece, width), link_dtype),
            pltpu.VMEM((lanes, 2, piece, width), link_dtype),
            pltpu.SemaphoreType.DMA((lanes, 2)),
            pltpu.SemaphoreType.DMA((lanes, 2)),
            pltpu.SemaphoreType.REGULAR((lanes,)),
        ],
        compiler_params=pltpu.CompilerParams(collective_id=1, has_side_effects=True,
                                             vmem_limit_bytes=48 * 1024 * 1024),
    )(h)


QB = 128


def window_allow(tq_ref, tk_ref, a0, w0):
    rows = lax.broadcasted_iota(jnp.int32, (QB, QB + 2 * HALF), 0)
    cols = lax.broadcasted_iota(jnp.int32, (QB, QB + 2 * HALF), 1)
    offset = cols - rows - HALF
    near = jnp.abs(offset) <= HALF
    same = tk_ref[:, pl.ds(w0, QB + 2 * HALF)] == tq_ref[pl.ds(a0, QB), :]
    return near & (same | (offset == 0))


def nt(a, b):
    return lax.dot_general(a, b, (((1,), (1,)), ((), ())), preferred_element_type=jnp.float32)


def tn(a, b):
    return lax.dot_general(a, b, (((0,), (0,)), ((), ())), preferred_element_type=jnp.float32)


def probs_of(q_ref, kv_ref, allow, a0, w0, h):
    q_h = q_ref[pl.ds(a0, QB), pl.ds(h * HEAD, HEAD)]
    k_h = kv_ref[pl.ds(w0, QB + 2 * HALF), pl.ds(h * HEAD, HEAD)]
    scores = jnp.where(allow, nt(q_h, k_h) * 0.125, -1e30)
    largest = jnp.max(scores, axis=-1, keepdims=True)
    raised = jnp.exp(scores - largest)
    return raised / jnp.sum(raised, axis=-1, keepdims=True), q_h, k_h


def attn_fwd_kernel(q_ref, kv_ref, tq_ref, tk_ref, o_ref):
    width = q_ref.shape[1]

    def block(b, carry):
        a0 = pl.multiple_of(b * QB, QB)
        allow = window_allow(tq_ref, tk_ref, a0, a0)
        for h in range(HEADS):
            probs, _, _ = probs_of(q_ref, kv_ref, allow, a0, a0, h)
            v_h = kv_ref[pl.ds(a0, QB + 2 * HALF), pl.ds(width + h * HEAD, HEAD)]
            mixed = jnp.dot(probs.astype(jnp.bfloat16), v_h, preferred_element_type=jnp.float32)
            o_ref[pl.ds(a0, QB), pl.ds(h * HEAD, HEAD)] = mixed.astype(o_ref.dtype)
        return carry

    lax.fori_loop(0, q_ref.shape[0] // QB, block, 0)


def attn_bwd_kernel(q_ref, kv_ref, tq_ref, tk_ref, do_ref, dq_ref, dkv_ref):
    width = q_ref.shape[1]
    dkv_ref[...] = jnp.zeros(dkv_ref.shape, dkv_ref.dtype)

    def block(b, carry):
        a0 = pl.multiple_of(b * QB, QB)
        allow = window_allow(tq_ref, tk_ref, a0, a0)
        for h in range(HEADS):
            probs, q_h, k_h = probs_of(q_ref, kv_ref, allow, a0, a0, h)
            v_h = kv_ref[pl.ds(a0, QB + 2 * HALF), pl.ds(width + h * HEAD, HEAD)]
            do_h = do_ref[pl.ds(a0, QB), pl.ds(h * HEAD, HEAD)]
            grad_probs = nt(do_h, v_h)
            inner = jnp.sum(probs * grad_probs, axis=-1, keepdims=True)
            grad_scores = (probs * (grad_probs - inner)).astype(jnp.bfloat16)
            dq_ref[pl.ds(a0, QB), pl.ds(h * HEAD, HEAD)] = (
                jnp.dot(grad_scores, k_h, preferred_element_type=jnp.float32) * 0.125
            )
            rows = pl.ds(a0, QB + 2 * HALF)
            dkv_ref[rows, pl.ds(h * HEAD, HEAD)] += tn(grad_scores, q_h) * 0.125
            dkv_ref[rows, pl.ds(width + h * HEAD, HEAD)] += tn(probs.astype(jnp.bfloat16), do_h)
        return carry

    lax.fori_loop(0, q_ref.shape[0] // QB, block, 0)


VMEM_LIMIT = 48 * 1024 * 1024


def attn_fwd(query, wide_kv, tag_q, tag_k):
    count, width = query.shape
    vm = pl.BlockSpec(memory_space=pltpu.VMEM)
    return pl.pallas_call(
        attn_fwd_kernel,
        out_shape=jax.ShapeDtypeStruct((count, width), jnp.bfloat16),
        in_specs=[vm] * 4,
        out_specs=vm,
        compiler_params=pltpu.CompilerParams(vmem_limit_bytes=VMEM_LIMIT),
    )(query, wide_kv, tag_q.reshape(count, 1), tag_k.reshape(1, -1))


def attn_bwd(query, wide_kv, tag_q, tag_k, grad_out):
    count, width = query.shape
    vm = pl.BlockSpec(memory_space=pltpu.VMEM)
    return pl.pallas_call(
        attn_bwd_kernel,
        out_shape=(
            jax.ShapeDtypeStruct((count, width), jnp.float32),
            jax.ShapeDtypeStruct(wide_kv.shape, jnp.float32),
        ),
        in_specs=[vm] * 5,
        out_specs=(vm, vm),
        compiler_params=pltpu.CompilerParams(vmem_limit_bytes=VMEM_LIMIT),
    )(query, wide_kv, tag_q.reshape(count, 1), tag_k.reshape(1, -1), grad_out)


def gain_rows(gain, width, rows=8):
    line = jnp.pad(gain, (0, width - gain.shape[0]))
    return jnp.concatenate([line[None], jnp.zeros((rows - 1, width), gain.dtype)], 0)


def gather_rows(payload, n_dp, n_seq):
    every = lax.all_gather(payload, ("dp", "seq"), axis=0, tiled=True)
    return every.reshape(n_dp, n_seq, payload.shape[0], payload.shape[1])


def gain_blocks(grad_gain, n_dp, n_seq, width):
    part = jnp.pad(grad_gain.reshape(n_seq, -1), ((0, 0), (0, width - grad_gain.shape[0] // n_seq)))
    rows = jnp.concatenate([part[:, None], jnp.zeros((n_seq, 7, width), part.dtype)], 1)
    return jnp.broadcast_to(rows[None], (n_dp, n_seq, 8, width))


def front(value, n_dp):
    return value.reshape(value.shape[0], n_dp, -1)


def apply_t(left, weight_t, n_dp):
    return jnp.einsum("tdr,dnr->tn", front(left, n_dp), weight_t, preferred_element_type=jnp.float32)


def apply_back(grad, weight_t):
    out = jnp.einsum("tn,dnr->tdr", grad, weight_t, preferred_element_type=jnp.float32)
    return out.reshape(out.shape[0], -1)


def grad_t(grad, left, n_dp):
    return jnp.einsum("tn,tdr->dnr", grad, front(left, n_dp), preferred_element_type=jnp.float32)


def on_device(order, tokens, doc_start, real, w_qkv, w_out, w_in, w_down, gain_attn, gain_mlp, cotangent):
    count = tokens.shape[0]
    n_dp, n_seq = lax.axis_size("dp"), lax.axis_size("seq")
    rows, qkv_cols = w_qkv.shape
    out_cols, in_cols = w_out.shape[1], w_in.shape[1]
    down_rows, down_cols = w_down.shape
    down_lines = down_rows * down_cols // rows
    first = gather_rows(jnp.concatenate([w_qkv.T, gain_rows(gain_attn, rows)], 0), n_dp, n_seq)
    second = gather_rows(
        jnp.concatenate(
            [w_out.T, w_in.T, w_down.T.reshape(down_lines, rows), gain_rows(gain_mlp, rows)], 0
        ),
        n_dp,
        n_seq,
    )
    full_qkv = first[:, :, :qkv_cols].reshape(n_dp, n_seq * qkv_cols, rows)
    gain_one = first[0, :, qkv_cols, : gain_attn.shape[0]].reshape(-1).astype(jnp.float32)
    at = 0
    full_out = second[:, :, at : at + out_cols].reshape(n_dp, n_seq * out_cols, rows)
    at += out_cols
    full_in = second[:, :, at : at + in_cols].reshape(n_dp, n_seq * in_cols, rows)
    at += in_cols
    full_down = (
        second[:, :, at : at + down_lines]
        .reshape(n_dp, n_seq, down_cols, down_rows)
        .reshape(n_dp, n_seq * down_cols, down_rows)
    )
    at += down_lines
    gain_two = second[0, :, at, : gain_mlp.shape[0]].reshape(-1).astype(jnp.float32)
    stream = tokens.astype(jnp.float32)
    normed_a, factor_a = layer_norm(stream)
    h_attn = (normed_a * gain_one).astype(jnp.bfloat16)
    qkv = apply_t(h_attn, full_qkv, n_dp)
    offset_base = lax.axis_index(("dp", "seq")) * count
    place = (offset_base + jnp.arange(count, dtype=jnp.int32) - doc_start).astype(jnp.float32)
    cosine, sine = rotary_tables(place)
    query = (qkv[:, :D] * cosine + rotate(qkv[:, :D]) * sine).astype(jnp.bfloat16)
    key_rows = (qkv[:, D : 2 * D] * cosine + rotate(qkv[:, D : 2 * D]) * sine).astype(jnp.bfloat16)
    value_rows = qkv[:, 2 * D :].astype(jnp.bfloat16)
    tag_query = doc_start + 1
    tag_key = jnp.where(real == 1, tag_query, 0)
    key_value = jnp.concatenate([key_rows, value_rows], 1)
    wide_kv, wide_tag = (
        padded(key_value, ((("dp", "seq"), 0),), HALF),
        padded(tag_key, ((("dp", "seq"), 0),), HALF),
    )
    attn_out = attn_fwd(query, wide_kv, tag_query, wide_tag)
    mid = stream + apply_t(attn_out, full_out, n_dp)
    normed_m, factor_m = layer_norm(mid)
    h_mlp = (normed_m * gain_two).astype(jnp.bfloat16)
    gate_up = apply_t(h_mlp, full_in, n_dp)
    hidden_out, glu_pull = jax.vjp(glu_piece, gate_up)
    hidden = hidden_out.astype(jnp.bfloat16)
    result = mid + apply_t(hidden, full_down, n_dp)
    output = result.astype(jnp.bfloat16)
    grad_down = grad_t(cotangent, hidden, n_dp)
    grad_hidden = apply_back(cotangent, full_down)
    grad_gate_up = glu_pull(grad_hidden)[0].astype(jnp.bfloat16)
    grad_inw = grad_t(grad_gate_up, h_mlp, n_dp)
    grad_hmlp = apply_back(grad_gate_up, full_in)
    grad_gain_two = jnp.sum(grad_hmlp * normed_m, axis=0)
    grad_mid = cotangent.astype(jnp.float32) + norm_back(grad_hmlp * gain_two, normed_m, factor_m)
    grad_branch = grad_mid.astype(jnp.bfloat16)
    grad_outw = grad_t(grad_branch, attn_out, n_dp)
    grad_attn = apply_back(grad_branch, full_out).astype(jnp.bfloat16)
    grad_query, grad_wide = attn_bwd(query, wide_kv, tag_query, wide_tag, grad_attn)
    from_above = shifted(grad_wide[:HALF].astype(jnp.bfloat16), ("dp", "seq"), -1).astype(
        jnp.float32
    )
    from_below = shifted(grad_wide[count + HALF :].astype(jnp.bfloat16), ("dp", "seq"), 1).astype(
        jnp.float32
    )
    grad_kv = grad_wide[HALF : HALF + count]
    grad_kv = grad_kv.at[:HALF].add(from_below)
    grad_kv = grad_kv.at[count - HALF :].add(from_above)
    grad_keys = grad_kv[:, :D]
    grad_qkv = jnp.concatenate(
        [
            grad_query * cosine - rotate(grad_query) * sine,
            grad_keys * cosine - rotate(grad_keys) * sine,
            grad_kv[:, D:],
        ],
        1,
    ).astype(jnp.bfloat16)
    grad_qkvw = grad_t(grad_qkv, h_attn, n_dp)
    grad_hattn = apply_back(grad_qkv, full_qkv)
    grad_gain_one = jnp.sum(grad_hattn * normed_a, axis=0)
    grad_tokens = grad_mid + norm_back(grad_hattn * gain_one, normed_a, factor_a)
    blocks = jnp.concatenate(
        [
            grad_outw.reshape(n_dp, n_seq, out_cols, rows),
            grad_inw.reshape(n_dp, n_seq, in_cols, rows),
            grad_down.reshape(n_dp, n_seq, down_cols, down_rows).reshape(
                n_dp, n_seq, down_lines, rows
            ),
            gain_blocks(grad_gain_two, n_dp, n_seq, rows),
            grad_qkvw.reshape(n_dp, n_seq, qkv_cols, rows),
            gain_blocks(grad_gain_one, n_dp, n_seq, rows),
        ],
        2,
    )
    height = blocks.shape[2]
    lanes_rows = 2 * RING_WAYS * 16
    extra = (-height) % lanes_rows
    if extra:
        blocks = jnp.pad(blocks, ((0, 0), (0, 0), (0, extra), (0, 0)))
    blocks = jnp.stack([blocks[:, s] for s in order], 1)
    depth = blocks.shape[2]
    half = lax.psum_scatter(
        blocks.reshape(n_dp, n_seq * depth, rows), "dp", scatter_dimension=0, tiled=True
    )
    late = ring_reduce(half.reshape(n_seq, depth, rows), order, RING_WAYS)
    last = late[out_cols + in_cols + down_lines + 8 :]
    at = 0
    late_out = late[at : at + out_cols].T
    at += out_cols
    late_in = late[at : at + in_cols].T
    at += in_cols
    late_down = late[at : at + down_lines].reshape(down_cols, down_rows).T
    at += down_lines
    late_gain_two = late[at, : gain_mlp.shape[0]]
    return (
        output,
        grad_tokens,
        last[:qkv_cols].T,
        late_out,
        late_in,
        late_down,
        last[qkv_cols, : gain_attn.shape[0]],
        late_gain_two,
    )


def solution(mesh):
    placed = (
        P(("dp", "seq"), None),
        P(("dp", "seq")),
        P(("dp", "seq")),
        P("dp", "seq"),
        P("dp", "seq"),
        P("dp", "seq"),
        P("dp", "seq"),
        P("seq"),
        P("seq"),
        P(("dp", "seq"), None),
    )
    return jax.shard_map(
        functools.partial(on_device, ring_order(mesh)),
        mesh=mesh,
        in_specs=placed,
        out_specs=(
            P(("dp", "seq"), None),
            P(("dp", "seq"), None),
            P("dp", "seq"),
            P("dp", "seq"),
            P("dp", "seq"),
            P("dp", "seq"),
            P("seq"),
            P("seq"),
        ),
        check_vma=False,
    )
```

```python
import functools
import math

import jax
import jax.numpy as jnp
from jax import lax
from jax.experimental import pallas as pl
from jax.experimental.pallas import tpu as pltpu
from jax.sharding import PartitionSpec as P

D = 768
HEADS = 12
HEAD = 64
FF = 1152
HALF = 64


def padded(value, sides, width):
    for axis, dim in sides:
        size, length = (lax.axis_size(axis), value.shape[dim])
        up = [(i, (i + 1) % size) for i in range(size - 1)]
        down = [(j, i) for i, j in up]
        last = lax.slice_in_dim(value, length - width, length, axis=dim)
        initial = lax.slice_in_dim(value, 0, width, axis=dim)
        before = lax.ppermute(last, axis, up)
        after = lax.ppermute(initial, axis, down)
        value = jnp.concatenate([before, value, after], axis=dim)
    return value


def shifted(value, axis, by):
    length = lax.axis_size(axis)
    pairs = [(i, i + by) for i in range(length) if 0 <= i + by < length]
    return lax.ppermute(value, axis, pairs)


def layer_norm(value):
    centre = value - jnp.mean(value, axis=-1, keepdims=True)
    factor = lax.rsqrt(jnp.mean(centre * centre, axis=-1, keepdims=True) + 1e-05)
    return (centre * factor, factor)


def norm_back(grad, normed, factor):
    return factor * (
        grad
        - jnp.mean(grad, axis=-1, keepdims=True)
        - normed * jnp.mean(grad * normed, axis=-1, keepdims=True)
    )


def rotary_tables(place):
    freq = jnp.exp(jnp.arange(HEAD // 2, dtype=jnp.float32) * (-2.0 * math.log(10000.0) / HEAD))
    angle = place[:, None] * freq[None, :]
    cosine = jnp.tile(jnp.concatenate([jnp.cos(angle), jnp.cos(angle)], 1), (1, HEADS))
    sine = jnp.tile(jnp.concatenate([jnp.sin(angle), jnp.sin(angle)], 1), (1, HEADS))
    return (cosine, sine)


def rotate(value):
    count = value.shape[0]
    shaped = value.reshape(count, HEADS, HEAD)
    first = shaped[..., : HEAD // 2]
    second = shaped[..., HEAD // 2 :]
    return jnp.concatenate([-second, first], -1).reshape(count, HEADS * HEAD)


def left_dot(left, right):
    return lax.dot_general(
        left, right, (((0,), (0,)), ((), ())), preferred_element_type=jnp.float32
    )


def right_dot(left, right):
    return lax.dot_general(
        left, right, (((1,), (1,)), ((), ())), preferred_element_type=jnp.float32
    )


def glu_piece(gate_up):
    return jax.nn.gelu(gate_up[:, :FF], approximate=False) * gate_up[:, FF:]


MESH = pl.DeviceIdType.MESH


def ring_order(mesh):
    n = mesh.shape["seq"]
    try:
        coords = [tuple(mesh.devices[0, s].coords) for s in range(n)]
    except Exception:
        return list(range(n))
    near = [
        [t for t in range(n) if sum(abs(a - b) for a, b in zip(coords[s], coords[t])) == 1]
        for s in range(n)
    ]
    path, seen = [0], {0}

    def grow(budget=[200000]):
        budget[0] -= 1
        if budget[0] < 0:
            return False
        if len(path) == n:
            return 0 in near[path[-1]]
        options = sorted(
            (t for t in near[path[-1]] if t not in seen),
            key=lambda t: sum(1 for u in near[t] if u not in seen),
        )
        for t in options:
            path.append(t)
            seen.add(t)
            if grow():
                return True
            path.pop()
            seen.discard(t)
        return False

    return list(path) if n > 2 and grow() else list(range(n))


def lookup(index, table):
    n = len(table)
    square = n * n
    total = jnp.int32(0)
    for k, value in enumerate(table):
        if value:
            gap = index - k
            differs = lax.div(gap * gap + (square - 1), jnp.int32(square))
            total = total + value * (1 - differs)
    return total


def ring_kernel(order, per_way, h_ref, out_ref, recv, send, ssem, rsem, free):
    n = len(order)
    where = [0] * n
    for p, s in enumerate(order):
        where[s] = p
    d = lax.axis_index("dp")
    me = lax.axis_index("seq")
    pos = lookup(me, where)
    nxt = lookup(lax.rem(pos + 1, n), order)
    prv = lookup(lax.rem(pos + n - 1, n), order)
    piece = out_ref.shape[0] // (2 * per_way)

    barrier = pltpu.get_barrier_semaphore()
    pl.semaphore_signal(barrier, 1, device_id=(d, nxt), device_id_type=MESH)
    pl.semaphore_signal(barrier, 1, device_id=(d, prv), device_id_type=MESH)
    pl.semaphore_wait(barrier, 2)

    lanes = []
    for li in range(2 * per_way):
        forward = li % 2 == 0
        lanes.append((recv.at[li], send.at[li], ssem.at[li], rsem.at[li], free.at[li],
                      nxt if forward else prv, prv if forward else nxt,
                      slice(li * piece, (li + 1) * piece), -1 if forward else 1))
    copies = {}
    for step in range(n - 1):
        slot = step % 2
        for li, (recv, send, ssem, rsem, free, to, frm, rows, sign) in enumerate(lanes):
            q = lookup(lax.rem(pos + sign * (1 + step) + n * (step + 2), n), order)
            own = h_ref[q, rows, :]
            if step == 0:
                part = own
            else:
                copies[(li, step - 1)].wait_recv()
                part = recv[1 - slot].astype(jnp.float32) + own
                if step <= n - 3:
                    pl.semaphore_signal(free, 1, device_id=(d, frm), device_id_type=MESH)
            if step >= 2:
                copies[(li, step - 2)].wait_send()
                pl.semaphore_wait(free, 1)
            send[slot] = part.astype(send.dtype)
            c = pltpu.make_async_remote_copy(
                src_ref=send.at[slot], dst_ref=recv.at[slot],
                send_sem=ssem.at[slot], recv_sem=rsem.at[slot],
                device_id=(d, to), device_id_type=MESH)
            c.start()
            copies[(li, step)] = c
    last = n - 2
    for li, (recv, send, ssem, rsem, free, to, frm, rows, sign) in enumerate(lanes):
        copies[(li, last)].wait_recv()
        out_ref[rows, :] = recv[last % 2].astype(jnp.float32) + h_ref[me, rows, :]
        if last >= 1:
            copies[(li, last - 1)].wait_send()
        copies[(li, last)].wait_send()


RING_WAYS = 2


def ring_reduce(h, order, per_way, link_dtype=jnp.bfloat16):
    n, rows, width = h.shape
    lanes = 2 * per_way
    piece = rows // lanes
    return pl.pallas_call(
        functools.partial(ring_kernel, tuple(order), per_way),
        out_shape=jax.ShapeDtypeStruct((rows, width), jnp.float32),
        in_specs=[pl.BlockSpec(memory_space=pltpu.VMEM)],
        out_specs=pl.BlockSpec(memory_space=pltpu.VMEM),
        scratch_shapes=[
            pltpu.VMEM((lanes, 2, piece, width), link_dtype),
            pltpu.VMEM((lanes, 2, piece, width), link_dtype),
            pltpu.SemaphoreType.DMA((lanes, 2)),
            pltpu.SemaphoreType.DMA((lanes, 2)),
            pltpu.SemaphoreType.REGULAR((lanes,)),
        ],
        compiler_params=pltpu.CompilerParams(collective_id=1, has_side_effects=True,
                                             vmem_limit_bytes=48 * 1024 * 1024),
    )(h)


QB = 128


def window_allow(tq_ref, tk_ref, a0, w0):
    rows = lax.broadcasted_iota(jnp.int32, (QB, QB + 2 * HALF), 0)
    cols = lax.broadcasted_iota(jnp.int32, (QB, QB + 2 * HALF), 1)
    offset = cols - rows - HALF
    near = jnp.abs(offset) <= HALF
    same = tk_ref[:, pl.ds(w0, QB + 2 * HALF)] == tq_ref[pl.ds(a0, QB), :]
    return near & (same | (offset == 0))


def nt(a, b):
    return lax.dot_general(a, b, (((1,), (1,)), ((), ())), preferred_element_type=jnp.float32)


def tn(a, b):
    return lax.dot_general(a, b, (((0,), (0,)), ((), ())), preferred_element_type=jnp.float32)


def probs_of(q_ref, kv_ref, allow, a0, w0, h):
    q_h = q_ref[pl.ds(a0, QB), pl.ds(h * HEAD, HEAD)]
    k_h = kv_ref[pl.ds(w0, QB + 2 * HALF), pl.ds(h * HEAD, HEAD)]
    scores = jnp.where(allow, nt(q_h, k_h) * 0.125, -1e30)
    largest = jnp.max(scores, axis=-1, keepdims=True)
    raised = jnp.exp(scores - largest)
    return raised / jnp.sum(raised, axis=-1, keepdims=True), q_h, k_h


def attn_fwd_kernel(q_ref, kv_ref, tq_ref, tk_ref, o_ref):
    width = q_ref.shape[1]

    def block(b, carry):
        a0 = pl.multiple_of(b * QB, QB)
        allow = window_allow(tq_ref, tk_ref, a0, a0)
        for h in range(HEADS):
            probs, _, _ = probs_of(q_ref, kv_ref, allow, a0, a0, h)
            v_h = kv_ref[pl.ds(a0, QB + 2 * HALF), pl.ds(width + h * HEAD, HEAD)]
            mixed = jnp.dot(probs.astype(jnp.bfloat16), v_h, preferred_element_type=jnp.float32)
            o_ref[pl.ds(a0, QB), pl.ds(h * HEAD, HEAD)] = mixed.astype(o_ref.dtype)
        return carry

    lax.fori_loop(0, q_ref.shape[0] // QB, block, 0)


def attn_bwd_kernel(q_ref, kv_ref, tq_ref, tk_ref, do_ref, dq_ref, dkv_ref):
    width = q_ref.shape[1]
    dkv_ref[...] = jnp.zeros(dkv_ref.shape, dkv_ref.dtype)

    def block(b, carry):
        a0 = pl.multiple_of(b * QB, QB)
        allow = window_allow(tq_ref, tk_ref, a0, a0)
        for h in range(HEADS):
            probs, q_h, k_h = probs_of(q_ref, kv_ref, allow, a0, a0, h)
            v_h = kv_ref[pl.ds(a0, QB + 2 * HALF), pl.ds(width + h * HEAD, HEAD)]
            do_h = do_ref[pl.ds(a0, QB), pl.ds(h * HEAD, HEAD)]
            grad_probs = nt(do_h, v_h)
            inner = jnp.sum(probs * grad_probs, axis=-1, keepdims=True)
            grad_scores = (probs * (grad_probs - inner)).astype(jnp.bfloat16)
            dq_ref[pl.ds(a0, QB), pl.ds(h * HEAD, HEAD)] = (
                jnp.dot(grad_scores, k_h, preferred_element_type=jnp.float32) * 0.125
            )
            rows = pl.ds(a0, QB + 2 * HALF)
            dkv_ref[rows, pl.ds(h * HEAD, HEAD)] += tn(grad_scores, q_h) * 0.125
            dkv_ref[rows, pl.ds(width + h * HEAD, HEAD)] += tn(probs.astype(jnp.bfloat16), do_h)
        return carry

    lax.fori_loop(0, q_ref.shape[0] // QB, block, 0)


VMEM_LIMIT = 48 * 1024 * 1024


def attn_fwd(query, wide_kv, tag_q, tag_k):
    count, width = query.shape
    vm = pl.BlockSpec(memory_space=pltpu.VMEM)
    return pl.pallas_call(
        attn_fwd_kernel,
        out_shape=jax.ShapeDtypeStruct((count, width), jnp.bfloat16),
        in_specs=[vm] * 4,
        out_specs=vm,
        compiler_params=pltpu.CompilerParams(vmem_limit_bytes=VMEM_LIMIT),
    )(query, wide_kv, tag_q.reshape(count, 1), tag_k.reshape(1, -1))


def attn_bwd(query, wide_kv, tag_q, tag_k, grad_out):
    count, width = query.shape
    vm = pl.BlockSpec(memory_space=pltpu.VMEM)
    return pl.pallas_call(
        attn_bwd_kernel,
        out_shape=(
            jax.ShapeDtypeStruct((count, width), jnp.float32),
            jax.ShapeDtypeStruct(wide_kv.shape, jnp.float32),
        ),
        in_specs=[vm] * 5,
        out_specs=(vm, vm),
        compiler_params=pltpu.CompilerParams(vmem_limit_bytes=VMEM_LIMIT),
    )(query, wide_kv, tag_q.reshape(count, 1), tag_k.reshape(1, -1), grad_out)


def gain_rows(gain, width, rows=8):
    line = jnp.pad(gain, (0, width - gain.shape[0]))
    return jnp.concatenate([line[None], jnp.zeros((rows - 1, width), gain.dtype)], 0)


def gather_rows(payload, n_dp, n_seq):
    every = lax.all_gather(payload, ("dp", "seq"), axis=0, tiled=True)
    return every.reshape(n_dp, n_seq, payload.shape[0], payload.shape[1])


def gain_blocks(grad_gain, n_dp, n_seq, width):
    part = jnp.pad(grad_gain.reshape(n_seq, -1), ((0, 0), (0, width - grad_gain.shape[0] // n_seq)))
    rows = jnp.concatenate([part[:, None], jnp.zeros((n_seq, 7, width), part.dtype)], 1)
    return jnp.broadcast_to(rows[None], (n_dp, n_seq, 8, width))


def front(value, n_dp):
    return value.reshape(value.shape[0], n_dp, -1)


def apply_t(left, weight_t, n_dp):
    return jnp.einsum("tdr,dnr->tn", front(left, n_dp), weight_t, preferred_element_type=jnp.float32)


def apply_back(grad, weight_t):
    out = jnp.einsum("tn,dnr->tdr", grad, weight_t, preferred_element_type=jnp.float32)
    return out.reshape(out.shape[0], -1)


def grad_t(grad, left, n_dp):
    return jnp.einsum("tn,tdr->dnr", grad, front(left, n_dp), preferred_element_type=jnp.float32)


def on_device(order, tokens, doc_start, real, w_qkv, w_out, w_in, w_down, gain_attn, gain_mlp, cotangent):
    count = tokens.shape[0]
    n_dp, n_seq = lax.axis_size("dp"), lax.axis_size("seq")
    rows, qkv_cols = w_qkv.shape
    out_cols, in_cols = w_out.shape[1], w_in.shape[1]
    down_rows, down_cols = w_down.shape
    down_lines = down_rows * down_cols // rows
    first = gather_rows(jnp.concatenate([w_qkv.T, gain_rows(gain_attn, rows)], 0), n_dp, n_seq)
    second = gather_rows(
        jnp.concatenate(
            [w_out.T, w_in.T, w_down.T.reshape(down_lines, rows), gain_rows(gain_mlp, rows)], 0
        ),
        n_dp,
        n_seq,
    )
    full_qkv = first[:, :, :qkv_cols].reshape(n_dp, n_seq * qkv_cols, rows)
    gain_one = first[0, :, qkv_cols, : gain_attn.shape[0]].reshape(-1).astype(jnp.float32)
    at = 0
    full_out = second[:, :, at : at + out_cols].reshape(n_dp, n_seq * out_cols, rows)
    at += out_cols
    full_in = second[:, :, at : at + in_cols].reshape(n_dp, n_seq * in_cols, rows)
    at += in_cols
    full_down = (
        second[:, :, at : at + down_lines]
        .reshape(n_dp, n_seq, down_cols, down_rows)
        .reshape(n_dp, n_seq * down_cols, down_rows)
    )
    at += down_lines
    gain_two = second[0, :, at, : gain_mlp.shape[0]].reshape(-1).astype(jnp.float32)
    stream = tokens.astype(jnp.float32)
    normed_a, factor_a = layer_norm(stream)
    h_attn = (normed_a * gain_one).astype(jnp.bfloat16)
    qkv = apply_t(h_attn, full_qkv, n_dp)
    offset_base = lax.axis_index(("dp", "seq")) * count
    place = (offset_base + jnp.arange(count, dtype=jnp.int32) - doc_start).astype(jnp.float32)
    cosine, sine = rotary_tables(place)
    query = (qkv[:, :D] * cosine + rotate(qkv[:, :D]) * sine).astype(jnp.bfloat16)
    key_rows = (qkv[:, D : 2 * D] * cosine + rotate(qkv[:, D : 2 * D]) * sine).astype(jnp.bfloat16)
    value_rows = qkv[:, 2 * D :].astype(jnp.bfloat16)
    tag_query = doc_start + 1
    tag_key = jnp.where(real == 1, tag_query, 0)
    key_value = jnp.concatenate([key_rows, value_rows], 1)
    wide_kv, wide_tag = (
        padded(key_value, ((("dp", "seq"), 0),), HALF),
        padded(tag_key, ((("dp", "seq"), 0),), HALF),
    )
    attn_out = attn_fwd(query, wide_kv, tag_query, wide_tag)
    mid = stream + apply_t(attn_out, full_out, n_dp)
    normed_m, factor_m = layer_norm(mid)
    h_mlp = (normed_m * gain_two).astype(jnp.bfloat16)
    gate_up = apply_t(h_mlp, full_in, n_dp)
    hidden_out, glu_pull = jax.vjp(glu_piece, gate_up)
    hidden = hidden_out.astype(jnp.bfloat16)
    result = mid + apply_t(hidden, full_down, n_dp)
    output = result.astype(jnp.bfloat16)
    grad_down = grad_t(cotangent, hidden, n_dp)
    grad_hidden = apply_back(cotangent, full_down)
    grad_gate_up = glu_pull(grad_hidden)[0].astype(jnp.bfloat16)
    grad_inw = grad_t(grad_gate_up, h_mlp, n_dp)
    grad_hmlp = apply_back(grad_gate_up, full_in)
    grad_gain_two = jnp.sum(grad_hmlp * normed_m, axis=0)
    grad_mid = cotangent.astype(jnp.float32) + norm_back(grad_hmlp * gain_two, normed_m, factor_m)
    grad_branch = grad_mid.astype(jnp.bfloat16)
    grad_outw = grad_t(grad_branch, attn_out, n_dp)
    grad_attn = apply_back(grad_branch, full_out).astype(jnp.bfloat16)
    grad_query, grad_wide = attn_bwd(query, wide_kv, tag_query, wide_tag, grad_attn)
    from_above = shifted(grad_wide[:HALF].astype(jnp.bfloat16), ("dp", "seq"), -1).astype(
        jnp.float32
    )
    from_below = shifted(grad_wide[count + HALF :].astype(jnp.bfloat16), ("dp", "seq"), 1).astype(
        jnp.float32
    )
    grad_kv = grad_wide[HALF : HALF + count]
    grad_kv = grad_kv.at[:HALF].add(from_below)
    grad_kv = grad_kv.at[count - HALF :].add(from_above)
    grad_keys = grad_kv[:, :D]
    grad_qkv = jnp.concatenate(
        [
            grad_query * cosine - rotate(grad_query) * sine,
            grad_keys * cosine - rotate(grad_keys) * sine,
            grad_kv[:, D:],
        ],
        1,
    ).astype(jnp.bfloat16)
    grad_qkvw = grad_t(grad_qkv, h_attn, n_dp)
    grad_hattn = apply_back(grad_qkv, full_qkv)
    grad_gain_one = jnp.sum(grad_hattn * normed_a, axis=0)
    grad_tokens = grad_mid + norm_back(grad_hattn * gain_one, normed_a, factor_a)
    blocks = jnp.concatenate(
        [
            grad_outw.reshape(n_dp, n_seq, out_cols, rows),
            grad_inw.reshape(n_dp, n_seq, in_cols, rows),
            grad_down.reshape(n_dp, n_seq, down_cols, down_rows).reshape(
                n_dp, n_seq, down_lines, rows
            ),
            gain_blocks(grad_gain_two, n_dp, n_seq, rows),
            grad_qkvw.reshape(n_dp, n_seq, qkv_cols, rows),
            gain_blocks(grad_gain_one, n_dp, n_seq, rows),
        ],
        2,
    )
    height = blocks.shape[2]
    lanes_rows = 2 * RING_WAYS * 16
    extra = (-height) % lanes_rows
    if extra:
        blocks = jnp.pad(blocks, ((0, 0), (0, 0), (0, extra), (0, 0)))
    depth = blocks.shape[2]
    half = lax.psum_scatter(
        blocks.reshape(n_dp, n_seq * depth, rows), "dp", scatter_dimension=0, tiled=True
    )
    late = ring_reduce(half.reshape(n_seq, depth, rows), order, RING_WAYS)
    last = late[out_cols + in_cols + down_lines + 8 :]
    at = 0
    late_out = late[at : at + out_cols].T
    at += out_cols
    late_in = late[at : at + in_cols].T
    at += in_cols
    late_down = late[at : at + down_lines].reshape(down_cols, down_rows).T
    at += down_lines
    late_gain_two = late[at, : gain_mlp.shape[0]]
    return (
        output,
        grad_tokens,
        last[:qkv_cols].T,
        late_out,
        late_in,
        late_down,
        last[qkv_cols, : gain_attn.shape[0]],
        late_gain_two,
    )


def solution(mesh):
    placed = (
        P(("dp", "seq"), None),
        P(("dp", "seq")),
        P(("dp", "seq")),
        P("dp", "seq"),
        P("dp", "seq"),
        P("dp", "seq"),
        P("dp", "seq"),
        P("seq"),
        P("seq"),
        P(("dp", "seq"), None),
    )
    return jax.shard_map(
        functools.partial(on_device, ring_order(mesh)),
        mesh=mesh,
        in_specs=placed,
        out_specs=(
            P(("dp", "seq"), None),
            P(("dp", "seq"), None),
            P("dp", "seq"),
            P("dp", "seq"),
            P("dp", "seq"),
            P("dp", "seq"),
            P("seq"),
            P("seq"),
        ),
        check_vma=False,
    )
```

```python
import functools
import math

import jax
import jax.numpy as jnp
from jax import lax
from jax.experimental import pallas as pl
from jax.experimental.pallas import tpu as pltpu
from jax.sharding import PartitionSpec as P

D = 768
HEADS = 12
HEAD = 64
FF = 1152
HALF = 64


def padded(value, sides, width):
    for axis, dim in sides:
        size, length = (lax.axis_size(axis), value.shape[dim])
        up = [(i, (i + 1) % size) for i in range(size - 1)]
        down = [(j, i) for i, j in up]
        last = lax.slice_in_dim(value, length - width, length, axis=dim)
        initial = lax.slice_in_dim(value, 0, width, axis=dim)
        before = lax.ppermute(last, axis, up)
        after = lax.ppermute(initial, axis, down)
        value = jnp.concatenate([before, value, after], axis=dim)
    return value


def shifted(value, axis, by):
    length = lax.axis_size(axis)
    pairs = [(i, i + by) for i in range(length) if 0 <= i + by < length]
    return lax.ppermute(value, axis, pairs)


def layer_norm(value):
    centre = value - jnp.mean(value, axis=-1, keepdims=True)
    factor = lax.rsqrt(jnp.mean(centre * centre, axis=-1, keepdims=True) + 1e-05)
    return (centre * factor, factor)


def norm_back(grad, normed, factor):
    return factor * (
        grad
        - jnp.mean(grad, axis=-1, keepdims=True)
        - normed * jnp.mean(grad * normed, axis=-1, keepdims=True)
    )


def rotary_tables(place):
    freq = jnp.exp(jnp.arange(HEAD // 2, dtype=jnp.float32) * (-2.0 * math.log(10000.0) / HEAD))
    angle = place[:, None] * freq[None, :]
    cosine = jnp.tile(jnp.concatenate([jnp.cos(angle), jnp.cos(angle)], 1), (1, HEADS))
    sine = jnp.tile(jnp.concatenate([jnp.sin(angle), jnp.sin(angle)], 1), (1, HEADS))
    return (cosine, sine)


def rotate(value):
    count = value.shape[0]
    shaped = value.reshape(count, HEADS, HEAD)
    first = shaped[..., : HEAD // 2]
    second = shaped[..., HEAD // 2 :]
    return jnp.concatenate([-second, first], -1).reshape(count, HEADS * HEAD)


def left_dot(left, right):
    return lax.dot_general(
        left, right, (((0,), (0,)), ((), ())), preferred_element_type=jnp.float32
    )


def right_dot(left, right):
    return lax.dot_general(
        left, right, (((1,), (1,)), ((), ())), preferred_element_type=jnp.float32
    )


def glu_piece(gate_up):
    return jax.nn.gelu(gate_up[:, :FF], approximate=False) * gate_up[:, FF:]


MESH = pl.DeviceIdType.MESH


def ring_order(mesh):
    n = mesh.shape["seq"]
    try:
        coords = [tuple(mesh.devices[0, s].coords) for s in range(n)]
    except Exception:
        return list(range(n))
    near = [
        [t for t in range(n) if sum(abs(a - b) for a, b in zip(coords[s], coords[t])) == 1]
        for s in range(n)
    ]
    path, seen = [0], {0}

    def grow(budget=[200000]):
        budget[0] -= 1
        if budget[0] < 0:
            return False
        if len(path) == n:
            return 0 in near[path[-1]]
        options = sorted(
            (t for t in near[path[-1]] if t not in seen),
            key=lambda t: sum(1 for u in near[t] if u not in seen),
        )
        for t in options:
            path.append(t)
            seen.add(t)
            if grow():
                return True
            path.pop()
            seen.discard(t)
        return False

    return list(path) if n > 2 and grow() else list(range(n))


def lookup(index, table):
    n = len(table)
    square = n * n
    total = jnp.int32(0)
    for k, value in enumerate(table):
        if value:
            gap = index - k
            differs = lax.div(gap * gap + (square - 1), jnp.int32(square))
            total = total + value * (1 - differs)
    return total


def ring_kernel(order, per_way, h_ref, out_ref, recv, send, ssem, rsem, free):
    n = len(order)
    where = [0] * n
    for p, s in enumerate(order):
        where[s] = p
    d = lax.axis_index("dp")
    me = lax.axis_index("seq")
    pos = lookup(me, where)
    nxt = lookup(lax.rem(pos + 1, n), order)
    prv = lookup(lax.rem(pos + n - 1, n), order)
    piece = out_ref.shape[0] // (2 * per_way)

    barrier = pltpu.get_barrier_semaphore()
    pl.semaphore_signal(barrier, 1, device_id=(d, nxt), device_id_type=MESH)
    pl.semaphore_signal(barrier, 1, device_id=(d, prv), device_id_type=MESH)
    pl.semaphore_wait(barrier, 2)

    lanes = []
    for li in range(2 * per_way):
        forward = li % 2 == 0
        lanes.append((recv.at[li], send.at[li], ssem.at[li], rsem.at[li], free.at[li],
                      nxt if forward else prv, prv if forward else nxt,
                      slice(li * piece, (li + 1) * piece), -1 if forward else 1))
    copies = {}
    for step in range(n - 1):
        slot = step % 2
        for li, (recv, send, ssem, rsem, free, to, frm, rows, sign) in enumerate(lanes):
            q = lookup(lax.rem(pos + sign * (1 + step) + n * (step + 2), n), order)
            own = h_ref[q, rows, :]
            if step == 0:
                part = own
            else:
                copies[(li, step - 1)].wait_recv()
                part = recv[1 - slot].astype(jnp.float32) + own
                if step <= n - 3:
                    pl.semaphore_signal(free, 1, device_id=(d, frm), device_id_type=MESH)
            if step >= 2:
                copies[(li, step - 2)].wait_send()
                pl.semaphore_wait(free, 1)
            send[slot] = part.astype(send.dtype)
            c = pltpu.make_async_remote_copy(
                src_ref=send.at[slot], dst_ref=recv.at[slot],
                send_sem=ssem.at[slot], recv_sem=rsem.at[slot],
                device_id=(d, to), device_id_type=MESH)
            c.start()
            copies[(li, step)] = c
    last = n - 2
    for li, (recv, send, ssem, rsem, free, to, frm, rows, sign) in enumerate(lanes):
        copies[(li, last)].wait_recv()
        out_ref[rows, :] = recv[last % 2].astype(jnp.float32) + h_ref[me, rows, :]
        if last >= 1:
            copies[(li, last - 1)].wait_send()
        copies[(li, last)].wait_send()


RING_WAYS = 2


def ring_reduce(h, order, per_way, link_dtype=jnp.bfloat16):
    n, rows, width = h.shape
    lanes = 2 * per_way
    piece = rows // lanes
    return pl.pallas_call(
        functools.partial(ring_kernel, tuple(order), per_way),
        out_shape=jax.ShapeDtypeStruct((rows, width), jnp.float32),
        in_specs=[pl.BlockSpec(memory_space=pltpu.VMEM)],
        out_specs=pl.BlockSpec(memory_space=pltpu.VMEM),
        scratch_shapes=[
            pltpu.VMEM((lanes, 2, piece, width), link_dtype),
            pltpu.VMEM((lanes, 2, piece, width), link_dtype),
            pltpu.SemaphoreType.DMA((lanes, 2)),
            pltpu.SemaphoreType.DMA((lanes, 2)),
            pltpu.SemaphoreType.REGULAR((lanes,)),
        ],
        compiler_params=pltpu.CompilerParams(collective_id=1, has_side_effects=True,
                                             vmem_limit_bytes=48 * 1024 * 1024),
    )(h)


QB = 128


def window_allow(tq_ref, tk_ref, a0, w0):
    rows = lax.broadcasted_iota(jnp.int32, (QB, QB + 2 * HALF), 0)
    cols = lax.broadcasted_iota(jnp.int32, (QB, QB + 2 * HALF), 1)
    offset = cols - rows - HALF
    near = jnp.abs(offset) <= HALF
    same = tk_ref[:, pl.ds(w0, QB + 2 * HALF)] == tq_ref[pl.ds(a0, QB), :]
    return near & (same | (offset == 0))


def nt(a, b):
    return lax.dot_general(a, b, (((1,), (1,)), ((), ())), preferred_element_type=jnp.float32)


def tn(a, b):
    return lax.dot_general(a, b, (((0,), (0,)), ((), ())), preferred_element_type=jnp.float32)


def probs_of(q_ref, kv_ref, allow, a0, w0, h):
    q_h = q_ref[pl.ds(a0, QB), pl.ds(h * HEAD, HEAD)]
    k_h = kv_ref[pl.ds(w0, QB + 2 * HALF), pl.ds(h * HEAD, HEAD)]
    scores = jnp.where(allow, nt(q_h, k_h) * 0.125, -1e30)
    largest = jnp.max(scores, axis=-1, keepdims=True)
    raised = jnp.exp(scores - largest)
    return raised / jnp.sum(raised, axis=-1, keepdims=True), q_h, k_h


def attn_fwd_kernel(q_ref, kv_ref, tq_ref, tk_ref, o_ref):
    width = q_ref.shape[1]

    def block(b, carry):
        a0 = pl.multiple_of(b * QB, QB)
        allow = window_allow(tq_ref, tk_ref, a0, a0)
        for h in range(HEADS):
            probs, _, _ = probs_of(q_ref, kv_ref, allow, a0, a0, h)
            v_h = kv_ref[pl.ds(a0, QB + 2 * HALF), pl.ds(width + h * HEAD, HEAD)]
            mixed = jnp.dot(probs.astype(jnp.bfloat16), v_h, preferred_element_type=jnp.float32)
            o_ref[pl.ds(a0, QB), pl.ds(h * HEAD, HEAD)] = mixed.astype(o_ref.dtype)
        return carry

    lax.fori_loop(0, q_ref.shape[0] // QB, block, 0)


def attn_bwd_kernel(q_ref, kv_ref, tq_ref, tk_ref, do_ref, dq_ref, dkv_ref):
    width = q_ref.shape[1]
    dkv_ref[...] = jnp.zeros(dkv_ref.shape, dkv_ref.dtype)

    def block(b, carry):
        a0 = pl.multiple_of(b * QB, QB)
        allow = window_allow(tq_ref, tk_ref, a0, a0)
        for h in range(HEADS):
            probs, q_h, k_h = probs_of(q_ref, kv_ref, allow, a0, a0, h)
            v_h = kv_ref[pl.ds(a0, QB + 2 * HALF), pl.ds(width + h * HEAD, HEAD)]
            do_h = do_ref[pl.ds(a0, QB), pl.ds(h * HEAD, HEAD)]
            grad_probs = nt(do_h, v_h)
            inner = jnp.sum(probs * grad_probs, axis=-1, keepdims=True)
            grad_scores = (probs * (grad_probs - inner)).astype(jnp.bfloat16)
            dq_ref[pl.ds(a0, QB), pl.ds(h * HEAD, HEAD)] = (
                jnp.dot(grad_scores, k_h, preferred_element_type=jnp.float32) * 0.125
            )
            rows = pl.ds(a0, QB + 2 * HALF)
            dkv_ref[rows, pl.ds(h * HEAD, HEAD)] += tn(grad_scores, q_h) * 0.125
            dkv_ref[rows, pl.ds(width + h * HEAD, HEAD)] += tn(probs.astype(jnp.bfloat16), do_h)
        return carry

    lax.fori_loop(0, q_ref.shape[0] // QB, block, 0)


VMEM_LIMIT = 48 * 1024 * 1024


def attn_fwd(query, wide_kv, tag_q, tag_k):
    count, width = query.shape
    vm = pl.BlockSpec(memory_space=pltpu.VMEM)
    return pl.pallas_call(
        attn_fwd_kernel,
        out_shape=jax.ShapeDtypeStruct((count, width), jnp.bfloat16),
        in_specs=[vm] * 4,
        out_specs=vm,
        compiler_params=pltpu.CompilerParams(vmem_limit_bytes=VMEM_LIMIT),
    )(query, wide_kv, tag_q.reshape(count, 1), tag_k.reshape(1, -1))


def attn_bwd(query, wide_kv, tag_q, tag_k, grad_out):
    count, width = query.shape
    vm = pl.BlockSpec(memory_space=pltpu.VMEM)
    return pl.pallas_call(
        attn_bwd_kernel,
        out_shape=(
            jax.ShapeDtypeStruct((count, width), jnp.float32),
            jax.ShapeDtypeStruct(wide_kv.shape, jnp.float32),
        ),
        in_specs=[vm] * 5,
        out_specs=(vm, vm),
        compiler_params=pltpu.CompilerParams(vmem_limit_bytes=VMEM_LIMIT),
    )(query, wide_kv, tag_q.reshape(count, 1), tag_k.reshape(1, -1), grad_out)


def gain_rows(gain, width, rows=8):
    line = jnp.pad(gain, (0, width - gain.shape[0]))
    return jnp.concatenate([line[None], jnp.zeros((rows - 1, width), gain.dtype)], 0)


def gather_rows(payload, n_dp, n_seq):
    every = lax.all_gather(payload, ("dp", "seq"), axis=0, tiled=True)
    return every.reshape(n_dp, n_seq, payload.shape[0], payload.shape[1])


def gain_blocks(grad_gain, n_dp, n_seq, width, height=8):
    part = jnp.pad(grad_gain.reshape(n_seq, -1), ((0, 0), (0, width - grad_gain.shape[0] // n_seq)))
    rows = jnp.concatenate([part[:, None], jnp.zeros((n_seq, height - 1, width), part.dtype)], 1)
    return jnp.broadcast_to(rows[None], (n_dp, n_seq, height, width))


def front(value, n_dp):
    return value.reshape(value.shape[0], n_dp, -1)


def apply_t(left, weight_t, n_dp):
    return jnp.einsum("tdr,dnr->tn", front(left, n_dp), weight_t, preferred_element_type=jnp.float32)


def apply_back(grad, weight_t):
    out = jnp.einsum("tn,dnr->tdr", grad, weight_t, preferred_element_type=jnp.float32)
    return out.reshape(out.shape[0], -1)


def grad_t(grad, left, n_dp):
    return jnp.einsum("tn,tdr->dnr", grad, front(left, n_dp), preferred_element_type=jnp.float32)


def on_device(order, tokens, doc_start, real, w_qkv, w_out, w_in, w_down, gain_attn, gain_mlp, cotangent):
    count = tokens.shape[0]
    n_dp, n_seq = lax.axis_size("dp"), lax.axis_size("seq")
    rows, qkv_cols = w_qkv.shape
    out_cols, in_cols = w_out.shape[1], w_in.shape[1]
    down_rows, down_cols = w_down.shape
    down_lines = down_rows * down_cols // rows
    first = gather_rows(jnp.concatenate([w_qkv.T, gain_rows(gain_attn, rows)], 0), n_dp, n_seq)
    second = gather_rows(
        jnp.concatenate(
            [w_out.T, w_in.T, w_down.T.reshape(down_lines, rows), gain_rows(gain_mlp, rows)], 0
        ),
        n_dp,
        n_seq,
    )
    full_qkv = first[:, :, :qkv_cols].reshape(n_dp, n_seq * qkv_cols, rows)
    gain_one = first[0, :, qkv_cols, : gain_attn.shape[0]].reshape(-1).astype(jnp.float32)
    stream = tokens.astype(jnp.float32)
    normed_a, factor_a = layer_norm(stream)
    h_attn = (normed_a * gain_one).astype(jnp.bfloat16)
    qkv = apply_t(h_attn, full_qkv, n_dp)
    offset_base = lax.axis_index(("dp", "seq")) * count
    place = (offset_base + jnp.arange(count, dtype=jnp.int32) - doc_start).astype(jnp.float32)
    cosine, sine = rotary_tables(place)
    query = (qkv[:, :D] * cosine + rotate(qkv[:, :D]) * sine).astype(jnp.bfloat16)
    key_rows = (qkv[:, D : 2 * D] * cosine + rotate(qkv[:, D : 2 * D]) * sine).astype(jnp.bfloat16)
    value_rows = qkv[:, 2 * D :].astype(jnp.bfloat16)
    tag_query = doc_start + 1
    tag_key = jnp.where(real == 1, tag_query, 0)
    key_value = jnp.concatenate([key_rows, value_rows], 1)
    wide_kv, wide_tag = (
        padded(key_value, ((("dp", "seq"), 0),), HALF),
        padded(tag_key, ((("dp", "seq"), 0),), HALF),
    )
    attn_out = attn_fwd(query, wide_kv, tag_query, wide_tag)
    attn_out, second = lax.optimization_barrier((attn_out, second))
    at = 0
    full_out = second[:, :, at : at + out_cols].reshape(n_dp, n_seq * out_cols, rows)
    at += out_cols
    full_in = second[:, :, at : at + in_cols].reshape(n_dp, n_seq * in_cols, rows)
    at += in_cols
    full_down = (
        second[:, :, at : at + down_lines]
        .reshape(n_dp, n_seq, down_cols, down_rows)
        .reshape(n_dp, n_seq * down_cols, down_rows)
    )
    at += down_lines
    gain_two = second[0, :, at, : gain_mlp.shape[0]].reshape(-1).astype(jnp.float32)
    mid = stream + apply_t(attn_out, full_out, n_dp)
    normed_m, factor_m = layer_norm(mid)
    h_mlp = (normed_m * gain_two).astype(jnp.bfloat16)
    gate_up = apply_t(h_mlp, full_in, n_dp)
    hidden_out, glu_pull = jax.vjp(glu_piece, gate_up)
    hidden = hidden_out.astype(jnp.bfloat16)
    result = mid + apply_t(hidden, full_down, n_dp)
    output = result.astype(jnp.bfloat16)
    grad_down = grad_t(cotangent, hidden, n_dp)
    grad_hidden = apply_back(cotangent, full_down)
    grad_gate_up = glu_pull(grad_hidden)[0].astype(jnp.bfloat16)
    grad_inw = grad_t(grad_gate_up, h_mlp, n_dp)
    grad_hmlp = apply_back(grad_gate_up, full_in)
    grad_gain_two = jnp.sum(grad_hmlp * normed_m, axis=0)
    grad_mid = cotangent.astype(jnp.float32) + norm_back(grad_hmlp * gain_two, normed_m, factor_m)
    grad_branch = grad_mid.astype(jnp.bfloat16)
    grad_outw = grad_t(grad_branch, attn_out, n_dp)
    grad_attn = apply_back(grad_branch, full_out).astype(jnp.bfloat16)
    grad_query, grad_wide = attn_bwd(query, wide_kv, tag_query, wide_tag, grad_attn)
    from_above = shifted(grad_wide[:HALF].astype(jnp.bfloat16), ("dp", "seq"), -1).astype(
        jnp.float32
    )
    from_below = shifted(grad_wide[count + HALF :].astype(jnp.bfloat16), ("dp", "seq"), 1).astype(
        jnp.float32
    )
    grad_kv = grad_wide[HALF : HALF + count]
    grad_kv = grad_kv.at[:HALF].add(from_below)
    grad_kv = grad_kv.at[count - HALF :].add(from_above)
    grad_keys = grad_kv[:, :D]
    grad_qkv = jnp.concatenate(
        [
            grad_query * cosine - rotate(grad_query) * sine,
            grad_keys * cosine - rotate(grad_keys) * sine,
            grad_kv[:, D:],
        ],
        1,
    ).astype(jnp.bfloat16)
    grad_qkvw = grad_t(grad_qkv, h_attn, n_dp)
    grad_hattn = apply_back(grad_qkv, full_qkv)
    grad_gain_one = jnp.sum(grad_hattn * normed_a, axis=0)
    grad_tokens = grad_mid + norm_back(grad_hattn * gain_one, normed_a, factor_a)
    height = out_cols + in_cols + down_lines + qkv_cols + 16
    tail = 8 + (-height) % (2 * RING_WAYS * 16)
    blocks = jnp.concatenate(
        [
            grad_outw.reshape(n_dp, n_seq, out_cols, rows),
            grad_inw.reshape(n_dp, n_seq, in_cols, rows),
            grad_down.reshape(n_dp, n_seq, down_cols, down_rows).reshape(
                n_dp, n_seq, down_lines, rows
            ),
            gain_blocks(grad_gain_two, n_dp, n_seq, rows),
            grad_qkvw.reshape(n_dp, n_seq, qkv_cols, rows),
            gain_blocks(grad_gain_one, n_dp, n_seq, rows, tail),
        ],
        2,
    )
    depth = blocks.shape[2]
    half = lax.psum_scatter(
        blocks.reshape(n_dp, n_seq * depth, rows), "dp", scatter_dimension=0, tiled=True
    )
    late = ring_reduce(half.reshape(n_seq, depth, rows), order, RING_WAYS)
    last = late[out_cols + in_cols + down_lines + 8 :]
    at = 0
    late_out = late[at : at + out_cols].T
    at += out_cols
    late_in = late[at : at + in_cols].T
    at += in_cols
    late_down = late[at : at + down_lines].reshape(down_cols, down_rows).T
    at += down_lines
    late_gain_two = late[at, : gain_mlp.shape[0]]
    return (
        output,
        grad_tokens,
        last[:qkv_cols].T,
        late_out,
        late_in,
        late_down,
        last[qkv_cols, : gain_attn.shape[0]],
        late_gain_two,
    )


def solution(mesh):
    placed = (
        P(("dp", "seq"), None),
        P(("dp", "seq")),
        P(("dp", "seq")),
        P("dp", "seq"),
        P("dp", "seq"),
        P("dp", "seq"),
        P("dp", "seq"),
        P("seq"),
        P("seq"),
        P(("dp", "seq"), None),
    )
    return jax.shard_map(
        functools.partial(on_device, ring_order(mesh)),
        mesh=mesh,
        in_specs=placed,
        out_specs=(
            P(("dp", "seq"), None),
            P(("dp", "seq"), None),
            P("dp", "seq"),
            P("dp", "seq"),
            P("dp", "seq"),
            P("dp", "seq"),
            P("seq"),
            P("seq"),
        ),
        check_vma=False,
    )
```

```python
import functools
import math

import jax
import jax.numpy as jnp
from jax import lax
from jax.experimental import pallas as pl
from jax.experimental.pallas import tpu as pltpu
from jax.sharding import PartitionSpec as P

D = 768
HEADS = 12
HEAD = 64
FF = 1152
HALF = 64


def padded(value, sides, width):
    for axis, dim in sides:
        size, length = (lax.axis_size(axis), value.shape[dim])
        up = [(i, (i + 1) % size) for i in range(size - 1)]
        down = [(j, i) for i, j in up]
        last = lax.slice_in_dim(value, length - width, length, axis=dim)
        initial = lax.slice_in_dim(value, 0, width, axis=dim)
        before = lax.ppermute(last, axis, up)
        after = lax.ppermute(initial, axis, down)
        value = jnp.concatenate([before, value, after], axis=dim)
    return value


def shifted(value, axis, by):
    length = lax.axis_size(axis)
    pairs = [(i, i + by) for i in range(length) if 0 <= i + by < length]
    return lax.ppermute(value, axis, pairs)


def layer_norm(value):
    centre = value - jnp.mean(value, axis=-1, keepdims=True)
    factor = lax.rsqrt(jnp.mean(centre * centre, axis=-1, keepdims=True) + 1e-05)
    return (centre * factor, factor)


def norm_back(grad, normed, factor):
    return factor * (
        grad
        - jnp.mean(grad, axis=-1, keepdims=True)
        - normed * jnp.mean(grad * normed, axis=-1, keepdims=True)
    )


def rotary_tables(place):
    freq = jnp.exp(jnp.arange(HEAD // 2, dtype=jnp.float32) * (-2.0 * math.log(10000.0) / HEAD))
    angle = place[:, None] * freq[None, :]
    cosine = jnp.tile(jnp.concatenate([jnp.cos(angle), jnp.cos(angle)], 1), (1, HEADS))
    sine = jnp.tile(jnp.concatenate([jnp.sin(angle), jnp.sin(angle)], 1), (1, HEADS))
    return (cosine, sine)


def rotate(value):
    count = value.shape[0]
    shaped = value.reshape(count, HEADS, HEAD)
    first = shaped[..., : HEAD // 2]
    second = shaped[..., HEAD // 2 :]
    return jnp.concatenate([-second, first], -1).reshape(count, HEADS * HEAD)


def left_dot(left, right):
    return lax.dot_general(
        left, right, (((0,), (0,)), ((), ())), preferred_element_type=jnp.float32
    )


def right_dot(left, right):
    return lax.dot_general(
        left, right, (((1,), (1,)), ((), ())), preferred_element_type=jnp.float32
    )


def glu_piece(gate_up):
    return jax.nn.gelu(gate_up[:, :FF], approximate=False) * gate_up[:, FF:]


MESH = pl.DeviceIdType.MESH


def ring_order(mesh):
    n = mesh.shape["seq"]
    try:
        coords = [tuple(mesh.devices[0, s].coords) for s in range(n)]
    except Exception:
        return list(range(n))
    near = [
        [t for t in range(n) if sum(abs(a - b) for a, b in zip(coords[s], coords[t])) == 1]
        for s in range(n)
    ]
    path, seen = [0], {0}

    def grow(budget=[200000]):
        budget[0] -= 1
        if budget[0] < 0:
            return False
        if len(path) == n:
            return 0 in near[path[-1]]
        options = sorted(
            (t for t in near[path[-1]] if t not in seen),
            key=lambda t: sum(1 for u in near[t] if u not in seen),
        )
        for t in options:
            path.append(t)
            seen.add(t)
            if grow():
                return True
            path.pop()
            seen.discard(t)
        return False

    return list(path) if n > 2 and grow() else list(range(n))


def lookup(index, table):
    n = len(table)
    square = n * n
    total = jnp.int32(0)
    for k, value in enumerate(table):
        if value:
            gap = index - k
            differs = lax.div(gap * gap + (square - 1), jnp.int32(square))
            total = total + value * (1 - differs)
    return total


def ring_kernel(order, per_way, h_ref, out_ref, recv, send, ssem, rsem, free):
    n = len(order)
    where = [0] * n
    for p, s in enumerate(order):
        where[s] = p
    d = lax.axis_index("dp")
    me = lax.axis_index("seq")
    pos = lookup(me, where)
    nxt = lookup(lax.rem(pos + 1, n), order)
    prv = lookup(lax.rem(pos + n - 1, n), order)
    piece = out_ref.shape[0] // (2 * per_way)

    barrier = pltpu.get_barrier_semaphore()
    pl.semaphore_signal(barrier, 1, device_id=(d, nxt), device_id_type=MESH)
    pl.semaphore_signal(barrier, 1, device_id=(d, prv), device_id_type=MESH)
    pl.semaphore_wait(barrier, 2)

    lanes = []
    for li in range(2 * per_way):
        forward = li % 2 == 0
        lanes.append((recv.at[li], send.at[li], ssem.at[li], rsem.at[li], free.at[li],
                      nxt if forward else prv, prv if forward else nxt,
                      slice(li * piece, (li + 1) * piece), -1 if forward else 1))
    copies = {}
    for step in range(n - 1):
        slot = step % 2
        for li, (recv, send, ssem, rsem, free, to, frm, rows, sign) in enumerate(lanes):
            q = lookup(lax.rem(pos + sign * (1 + step) + n * (step + 2), n), order)
            own = h_ref[q, rows, :]
            if step == 0:
                part = own
            else:
                copies[(li, step - 1)].wait_recv()
                part = recv[1 - slot].astype(jnp.float32) + own
                if step <= n - 3:
                    pl.semaphore_signal(free, 1, device_id=(d, frm), device_id_type=MESH)
            if step >= 2:
                copies[(li, step - 2)].wait_send()
                pl.semaphore_wait(free, 1)
            send[slot] = part.astype(send.dtype)
            c = pltpu.make_async_remote_copy(
                src_ref=send.at[slot], dst_ref=recv.at[slot],
                send_sem=ssem.at[slot], recv_sem=rsem.at[slot],
                device_id=(d, to), device_id_type=MESH)
            c.start()
            copies[(li, step)] = c
    last = n - 2
    for li, (recv, send, ssem, rsem, free, to, frm, rows, sign) in enumerate(lanes):
        copies[(li, last)].wait_recv()
        out_ref[rows, :] = recv[last % 2].astype(jnp.float32) + h_ref[me, rows, :]
        if last >= 1:
            copies[(li, last - 1)].wait_send()
        copies[(li, last)].wait_send()


RING_WAYS = 2


def ring_reduce(h, order, per_way, link_dtype=jnp.bfloat16):
    n, rows, width = h.shape
    lanes = 2 * per_way
    piece = rows // lanes
    return pl.pallas_call(
        functools.partial(ring_kernel, tuple(order), per_way),
        out_shape=jax.ShapeDtypeStruct((rows, width), jnp.float32),
        in_specs=[pl.BlockSpec(memory_space=pltpu.VMEM)],
        out_specs=pl.BlockSpec(memory_space=pltpu.VMEM),
        scratch_shapes=[
            pltpu.VMEM((lanes, 2, piece, width), link_dtype),
            pltpu.VMEM((lanes, 2, piece, width), link_dtype),
            pltpu.SemaphoreType.DMA((lanes, 2)),
            pltpu.SemaphoreType.DMA((lanes, 2)),
            pltpu.SemaphoreType.REGULAR((lanes,)),
        ],
        compiler_params=pltpu.CompilerParams(collective_id=1, has_side_effects=True,
                                             vmem_limit_bytes=48 * 1024 * 1024),
    )(h)


QB = 128


def window_allow(tq_ref, tk_ref, a0, w0):
    rows = lax.broadcasted_iota(jnp.int32, (QB, QB + 2 * HALF), 0)
    cols = lax.broadcasted_iota(jnp.int32, (QB, QB + 2 * HALF), 1)
    offset = cols - rows - HALF
    near = jnp.abs(offset) <= HALF
    same = tk_ref[:, pl.ds(w0, QB + 2 * HALF)] == tq_ref[pl.ds(a0, QB), :]
    return near & (same | (offset == 0))


def nt(a, b):
    return lax.dot_general(a, b, (((1,), (1,)), ((), ())), preferred_element_type=jnp.float32)


def tn(a, b):
    return lax.dot_general(a, b, (((0,), (0,)), ((), ())), preferred_element_type=jnp.float32)


def probs_of(q_ref, kv_ref, allow, a0, w0, h):
    q_h = q_ref[pl.ds(a0, QB), pl.ds(h * HEAD, HEAD)]
    k_h = kv_ref[pl.ds(w0, QB + 2 * HALF), pl.ds(h * HEAD, HEAD)]
    scores = jnp.where(allow, nt(q_h, k_h) * 0.125, -1e30)
    largest = jnp.max(scores, axis=-1, keepdims=True)
    raised = jnp.exp(scores - largest)
    return raised / jnp.sum(raised, axis=-1, keepdims=True), q_h, k_h


def attn_fwd_kernel(q_ref, kv_ref, tq_ref, tk_ref, o_ref):
    width = q_ref.shape[1]

    def block(b, carry):
        a0 = pl.multiple_of(b * QB, QB)
        allow = window_allow(tq_ref, tk_ref, a0, a0)
        for h in range(HEADS):
            probs, _, _ = probs_of(q_ref, kv_ref, allow, a0, a0, h)
            v_h = kv_ref[pl.ds(a0, QB + 2 * HALF), pl.ds(width + h * HEAD, HEAD)]
            mixed = jnp.dot(probs.astype(jnp.bfloat16), v_h, preferred_element_type=jnp.float32)
            o_ref[pl.ds(a0, QB), pl.ds(h * HEAD, HEAD)] = mixed.astype(o_ref.dtype)
        return carry

    lax.fori_loop(0, q_ref.shape[0] // QB, block, 0)


def attn_bwd_kernel(q_ref, kv_ref, tq_ref, tk_ref, do_ref, dq_ref, dkv_ref):
    width = q_ref.shape[1]
    dkv_ref[...] = jnp.zeros(dkv_ref.shape, dkv_ref.dtype)

    def block(b, carry):
        a0 = pl.multiple_of(b * QB, QB)
        allow = window_allow(tq_ref, tk_ref, a0, a0)
        for h in range(HEADS):
            probs, q_h, k_h = probs_of(q_ref, kv_ref, allow, a0, a0, h)
            v_h = kv_ref[pl.ds(a0, QB + 2 * HALF), pl.ds(width + h * HEAD, HEAD)]
            do_h = do_ref[pl.ds(a0, QB), pl.ds(h * HEAD, HEAD)]
            grad_probs = nt(do_h, v_h)
            inner = jnp.sum(probs * grad_probs, axis=-1, keepdims=True)
            grad_scores = (probs * (grad_probs - inner)).astype(jnp.bfloat16)
            dq_ref[pl.ds(a0, QB), pl.ds(h * HEAD, HEAD)] = (
                jnp.dot(grad_scores, k_h, preferred_element_type=jnp.float32) * 0.125
            )
            rows = pl.ds(a0, QB + 2 * HALF)
            dkv_ref[rows, pl.ds(h * HEAD, HEAD)] += tn(grad_scores, q_h) * 0.125
            dkv_ref[rows, pl.ds(width + h * HEAD, HEAD)] += tn(probs.astype(jnp.bfloat16), do_h)
        return carry

    lax.fori_loop(0, q_ref.shape[0] // QB, block, 0)


VMEM_LIMIT = 48 * 1024 * 1024


def attn_fwd(query, wide_kv, tag_q, tag_k):
    count, width = query.shape
    vm = pl.BlockSpec(memory_space=pltpu.VMEM)
    return pl.pallas_call(
        attn_fwd_kernel,
        out_shape=jax.ShapeDtypeStruct((count, width), jnp.bfloat16),
        in_specs=[vm] * 4,
        out_specs=vm,
        compiler_params=pltpu.CompilerParams(vmem_limit_bytes=VMEM_LIMIT),
    )(query, wide_kv, tag_q.reshape(count, 1), tag_k.reshape(1, -1))


def attn_bwd(query, wide_kv, tag_q, tag_k, grad_out):
    count, width = query.shape
    vm = pl.BlockSpec(memory_space=pltpu.VMEM)
    return pl.pallas_call(
        attn_bwd_kernel,
        out_shape=(
            jax.ShapeDtypeStruct((count, width), jnp.float32),
            jax.ShapeDtypeStruct(wide_kv.shape, jnp.float32),
        ),
        in_specs=[vm] * 5,
        out_specs=(vm, vm),
        compiler_params=pltpu.CompilerParams(vmem_limit_bytes=VMEM_LIMIT),
    )(query, wide_kv, tag_q.reshape(count, 1), tag_k.reshape(1, -1), grad_out)


def gain_rows(gain, width, rows=8):
    line = jnp.pad(gain, (0, width - gain.shape[0]))
    return jnp.concatenate([line[None], jnp.zeros((rows - 1, width), gain.dtype)], 0)


def gather_rows(payload, n_dp, n_seq):
    every = lax.all_gather(payload, ("dp", "seq"), axis=0, tiled=True)
    return every.reshape(n_dp, n_seq, payload.shape[0], payload.shape[1])


def gain_blocks(grad_gain, n_dp, n_seq, width, height=8):
    part = jnp.pad(grad_gain.reshape(n_seq, -1), ((0, 0), (0, width - grad_gain.shape[0] // n_seq)))
    rows = jnp.concatenate([part[:, None], jnp.zeros((n_seq, height - 1, width), part.dtype)], 1)
    return jnp.broadcast_to(rows[None], (n_dp, n_seq, height, width))


def front(value, n_dp):
    return value.reshape(value.shape[0], n_dp, -1)


def apply_t(left, weight_t, n_dp):
    return jnp.einsum("tdr,dnr->tn", front(left, n_dp), weight_t, preferred_element_type=jnp.float32)


def apply_back(grad, weight_t):
    out = jnp.einsum("tn,dnr->tdr", grad, weight_t, preferred_element_type=jnp.float32)
    return out.reshape(out.shape[0], -1)


def grad_t(grad, left, n_dp):
    width = left.shape[1] // n_dp
    return [
        lax.dot_general(
            grad,
            left[:, d * width : (d + 1) * width],
            (((0,), (0,)), ((), ())),
            preferred_element_type=jnp.float32,
        )
        for d in range(n_dp)
    ]


def on_device(order, tokens, doc_start, real, w_qkv, w_out, w_in, w_down, gain_attn, gain_mlp, cotangent):
    count = tokens.shape[0]
    n_dp, n_seq = lax.axis_size("dp"), lax.axis_size("seq")
    rows, qkv_cols = w_qkv.shape
    out_cols, in_cols = w_out.shape[1], w_in.shape[1]
    down_rows, down_cols = w_down.shape
    down_lines = down_rows * down_cols // rows
    first = gather_rows(jnp.concatenate([w_qkv.T, gain_rows(gain_attn, rows)], 0), n_dp, n_seq)
    second = gather_rows(
        jnp.concatenate(
            [w_out.T, w_in.T, w_down.T.reshape(down_lines, rows), gain_rows(gain_mlp, rows)], 0
        ),
        n_dp,
        n_seq,
    )
    full_qkv = first[:, :, :qkv_cols].reshape(n_dp, n_seq * qkv_cols, rows)
    gain_one = first[0, :, qkv_cols, : gain_attn.shape[0]].reshape(-1).astype(jnp.float32)
    stream = tokens.astype(jnp.float32)
    normed_a, factor_a = layer_norm(stream)
    h_attn = (normed_a * gain_one).astype(jnp.bfloat16)
    qkv = apply_t(h_attn, full_qkv, n_dp)
    offset_base = lax.axis_index(("dp", "seq")) * count
    place = (offset_base + jnp.arange(count, dtype=jnp.int32) - doc_start).astype(jnp.float32)
    cosine, sine = rotary_tables(place)
    query = (qkv[:, :D] * cosine + rotate(qkv[:, :D]) * sine).astype(jnp.bfloat16)
    key_rows = (qkv[:, D : 2 * D] * cosine + rotate(qkv[:, D : 2 * D]) * sine).astype(jnp.bfloat16)
    value_rows = qkv[:, 2 * D :].astype(jnp.bfloat16)
    tag_query = doc_start + 1
    tag_key = jnp.where(real == 1, tag_query, 0)
    key_value = jnp.concatenate([key_rows, value_rows], 1)
    wide_kv, wide_tag = (
        padded(key_value, ((("dp", "seq"), 0),), HALF),
        padded(tag_key, ((("dp", "seq"), 0),), HALF),
    )
    attn_out = attn_fwd(query, wide_kv, tag_query, wide_tag)
    attn_out, second = lax.optimization_barrier((attn_out, second))
    at = 0
    full_out = second[:, :, at : at + out_cols].reshape(n_dp, n_seq * out_cols, rows)
    at += out_cols
    full_in = second[:, :, at : at + in_cols].reshape(n_dp, n_seq * in_cols, rows)
    at += in_cols
    full_down = (
        second[:, :, at : at + down_lines]
        .reshape(n_dp, n_seq, down_cols, down_rows)
        .reshape(n_dp, n_seq * down_cols, down_rows)
    )
    at += down_lines
    gain_two = second[0, :, at, : gain_mlp.shape[0]].reshape(-1).astype(jnp.float32)
    mid = stream + apply_t(attn_out, full_out, n_dp)
    normed_m, factor_m = layer_norm(mid)
    h_mlp = (normed_m * gain_two).astype(jnp.bfloat16)
    gate_up = apply_t(h_mlp, full_in, n_dp)
    hidden_out, glu_pull = jax.vjp(glu_piece, gate_up)
    hidden = hidden_out.astype(jnp.bfloat16)
    result = mid + apply_t(hidden, full_down, n_dp)
    output = result.astype(jnp.bfloat16)
    grad_down = grad_t(cotangent, hidden, n_dp)
    grad_hidden = apply_back(cotangent, full_down)
    grad_gate_up = glu_pull(grad_hidden)[0].astype(jnp.bfloat16)
    grad_inw = grad_t(grad_gate_up, h_mlp, n_dp)
    grad_hmlp = apply_back(grad_gate_up, full_in)
    grad_gain_two = jnp.sum(grad_hmlp * normed_m, axis=0)
    grad_mid = cotangent.astype(jnp.float32) + norm_back(grad_hmlp * gain_two, normed_m, factor_m)
    grad_branch = grad_mid.astype(jnp.bfloat16)
    grad_outw = grad_t(grad_branch, attn_out, n_dp)
    grad_attn = apply_back(grad_branch, full_out).astype(jnp.bfloat16)
    grad_query, grad_wide = attn_bwd(query, wide_kv, tag_query, wide_tag, grad_attn)
    from_above = shifted(grad_wide[:HALF].astype(jnp.bfloat16), ("dp", "seq"), -1).astype(
        jnp.float32
    )
    from_below = shifted(grad_wide[count + HALF :].astype(jnp.bfloat16), ("dp", "seq"), 1).astype(
        jnp.float32
    )
    grad_kv = grad_wide[HALF : HALF + count]
    grad_kv = grad_kv.at[:HALF].add(from_below)
    grad_kv = grad_kv.at[count - HALF :].add(from_above)
    grad_keys = grad_kv[:, :D]
    grad_qkv = jnp.concatenate(
        [
            grad_query * cosine - rotate(grad_query) * sine,
            grad_keys * cosine - rotate(grad_keys) * sine,
            grad_kv[:, D:],
        ],
        1,
    ).astype(jnp.bfloat16)
    grad_qkvw = grad_t(grad_qkv, h_attn, n_dp)
    grad_hattn = apply_back(grad_qkv, full_qkv)
    grad_gain_one = jnp.sum(grad_hattn * normed_a, axis=0)
    grad_tokens = grad_mid + norm_back(grad_hattn * gain_one, normed_a, factor_a)
    height = out_cols + in_cols + down_lines + qkv_cols + 16
    tail = 8 + (-height) % (2 * RING_WAYS * 16)
    gain_two_rows = gain_blocks(grad_gain_two, 1, n_seq, rows)[0]
    gain_one_rows = gain_blocks(grad_gain_one, 1, n_seq, rows, tail)[0]
    blocks = jnp.stack(
        [
            jnp.concatenate(
                [
                    grad_outw[d].reshape(n_seq, out_cols, rows),
                    grad_inw[d].reshape(n_seq, in_cols, rows),
                    grad_down[d].reshape(n_seq, down_cols, down_rows).reshape(n_seq, down_lines, rows),
                    gain_two_rows,
                    grad_qkvw[d].reshape(n_seq, qkv_cols, rows),
                    gain_one_rows,
                ],
                1,
            )
            for d in range(n_dp)
        ]
    )
    depth = blocks.shape[2]
    half = lax.psum_scatter(
        blocks.reshape(n_dp, n_seq * depth, rows), "dp", scatter_dimension=0, tiled=True
    )
    late = ring_reduce(half.reshape(n_seq, depth, rows), order, RING_WAYS)
    last = late[out_cols + in_cols + down_lines + 8 :]
    at = 0
    late_out = late[at : at + out_cols].T
    at += out_cols
    late_in = late[at : at + in_cols].T
    at += in_cols
    late_down = late[at : at + down_lines].reshape(down_cols, down_rows).T
    at += down_lines
    late_gain_two = late[at, : gain_mlp.shape[0]]
    return (
        output,
        grad_tokens,
        last[:qkv_cols].T,
        late_out,
        late_in,
        late_down,
        last[qkv_cols, : gain_attn.shape[0]],
        late_gain_two,
    )


def solution(mesh):
    placed = (
        P(("dp", "seq"), None),
        P(("dp", "seq")),
        P(("dp", "seq")),
        P("dp", "seq"),
        P("dp", "seq"),
        P("dp", "seq"),
        P("dp", "seq"),
        P("seq"),
        P("seq"),
        P(("dp", "seq"), None),
    )
    return jax.shard_map(
        functools.partial(on_device, ring_order(mesh)),
        mesh=mesh,
        in_specs=placed,
        out_specs=(
            P(("dp", "seq"), None),
            P(("dp", "seq"), None),
            P("dp", "seq"),
            P("dp", "seq"),
            P("dp", "seq"),
            P("dp", "seq"),
            P("seq"),
            P("seq"),
        ),
        check_vma=False,
    )
```

```python
import functools
import math

import jax
import jax.numpy as jnp
from jax import lax
from jax.experimental import pallas as pl
from jax.experimental.pallas import tpu as pltpu
from jax.sharding import PartitionSpec as P

D = 768
HEADS = 12
HEAD = 64
FF = 1152
HALF = 64


def padded(value, sides, width):
    for axis, dim in sides:
        size, length = (lax.axis_size(axis), value.shape[dim])
        up = [(i, (i + 1) % size) for i in range(size - 1)]
        down = [(j, i) for i, j in up]
        last = lax.slice_in_dim(value, length - width, length, axis=dim)
        initial = lax.slice_in_dim(value, 0, width, axis=dim)
        before = lax.ppermute(last, axis, up)
        after = lax.ppermute(initial, axis, down)
        value = jnp.concatenate([before, value, after], axis=dim)
    return value


def shifted(value, axis, by):
    length = lax.axis_size(axis)
    pairs = [(i, i + by) for i in range(length) if 0 <= i + by < length]
    return lax.ppermute(value, axis, pairs)


def layer_norm(value):
    centre = value - jnp.mean(value, axis=-1, keepdims=True)
    factor = lax.rsqrt(jnp.mean(centre * centre, axis=-1, keepdims=True) + 1e-05)
    return (centre * factor, factor)


def norm_back(grad, normed, factor):
    return factor * (
        grad
        - jnp.mean(grad, axis=-1, keepdims=True)
        - normed * jnp.mean(grad * normed, axis=-1, keepdims=True)
    )


def rotary_tables(place):
    freq = jnp.exp(jnp.arange(HEAD // 2, dtype=jnp.float32) * (-2.0 * math.log(10000.0) / HEAD))
    angle = place[:, None] * freq[None, :]
    cosine = jnp.tile(jnp.concatenate([jnp.cos(angle), jnp.cos(angle)], 1), (1, HEADS))
    sine = jnp.tile(jnp.concatenate([jnp.sin(angle), jnp.sin(angle)], 1), (1, HEADS))
    return (cosine, sine)


def rotate(value):
    count = value.shape[0]
    shaped = value.reshape(count, HEADS, HEAD)
    first = shaped[..., : HEAD // 2]
    second = shaped[..., HEAD // 2 :]
    return jnp.concatenate([-second, first], -1).reshape(count, HEADS * HEAD)


def left_dot(left, right):
    return lax.dot_general(
        left, right, (((0,), (0,)), ((), ())), preferred_element_type=jnp.float32
    )


def right_dot(left, right):
    return lax.dot_general(
        left, right, (((1,), (1,)), ((), ())), preferred_element_type=jnp.float32
    )


def glu_piece(gate_up):
    return jax.nn.gelu(gate_up[:, :FF], approximate=False) * gate_up[:, FF:]


MESH = pl.DeviceIdType.MESH


def ring_order(mesh):
    n = mesh.shape["seq"]
    try:
        coords = [tuple(mesh.devices[0, s].coords) for s in range(n)]
    except Exception:
        return list(range(n))
    near = [
        [t for t in range(n) if sum(abs(a - b) for a, b in zip(coords[s], coords[t])) == 1]
        for s in range(n)
    ]
    path, seen = [0], {0}

    def grow(budget=[200000]):
        budget[0] -= 1
        if budget[0] < 0:
            return False
        if len(path) == n:
            return 0 in near[path[-1]]
        options = sorted(
            (t for t in near[path[-1]] if t not in seen),
            key=lambda t: sum(1 for u in near[t] if u not in seen),
        )
        for t in options:
            path.append(t)
            seen.add(t)
            if grow():
                return True
            path.pop()
            seen.discard(t)
        return False

    return list(path) if n > 2 and grow() else list(range(n))


def lookup(index, table):
    n = len(table)
    square = n * n
    total = jnp.int32(0)
    for k, value in enumerate(table):
        if value:
            gap = index - k
            differs = lax.div(gap * gap + (square - 1), jnp.int32(square))
            total = total + value * (1 - differs)
    return total


def ring_kernel(order, per_way, h_ref, out_ref, recv, send, ssem, rsem, free):
    n = len(order)
    where = [0] * n
    for p, s in enumerate(order):
        where[s] = p
    d = lax.axis_index("dp")
    me = lax.axis_index("seq")
    pos = lookup(me, where)
    nxt = lookup(lax.rem(pos + 1, n), order)
    prv = lookup(lax.rem(pos + n - 1, n), order)
    piece = out_ref.shape[0] // (2 * per_way)

    barrier = pltpu.get_barrier_semaphore()
    pl.semaphore_signal(barrier, 1, device_id=(d, nxt), device_id_type=MESH)
    pl.semaphore_signal(barrier, 1, device_id=(d, prv), device_id_type=MESH)
    pl.semaphore_wait(barrier, 2)

    lanes = []
    for li in range(2 * per_way):
        forward = li % 2 == 0
        lanes.append((recv.at[li], send.at[li], ssem.at[li], rsem.at[li], free.at[li],
                      nxt if forward else prv, prv if forward else nxt,
                      slice(li * piece, (li + 1) * piece), -1 if forward else 1))
    copies = {}
    for step in range(n - 1):
        slot = step % 2
        for li, (recv, send, ssem, rsem, free, to, frm, rows, sign) in enumerate(lanes):
            q = lookup(lax.rem(pos + sign * (1 + step) + n * (step + 2), n), order)
            own = h_ref[q, rows, :]
            if step == 0:
                part = own
            else:
                copies[(li, step - 1)].wait_recv()
                part = recv[1 - slot].astype(jnp.float32) + own
                if step <= n - 3:
                    pl.semaphore_signal(free, 1, device_id=(d, frm), device_id_type=MESH)
            if step >= 2:
                copies[(li, step - 2)].wait_send()
                pl.semaphore_wait(free, 1)
            send[slot] = part.astype(send.dtype)
            c = pltpu.make_async_remote_copy(
                src_ref=send.at[slot], dst_ref=recv.at[slot],
                send_sem=ssem.at[slot], recv_sem=rsem.at[slot],
                device_id=(d, to), device_id_type=MESH)
            c.start()
            copies[(li, step)] = c
    last = n - 2
    for li, (recv, send, ssem, rsem, free, to, frm, rows, sign) in enumerate(lanes):
        copies[(li, last)].wait_recv()
        out_ref[rows, :] = recv[last % 2].astype(jnp.float32) + h_ref[me, rows, :]
        if last >= 1:
            copies[(li, last - 1)].wait_send()
        copies[(li, last)].wait_send()


RING_WAYS = 2


def ring_reduce(h, order, per_way, link_dtype=jnp.bfloat16):
    n, rows, width = h.shape
    lanes = 2 * per_way
    piece = rows // lanes
    return pl.pallas_call(
        functools.partial(ring_kernel, tuple(order), per_way),
        out_shape=jax.ShapeDtypeStruct((rows, width), jnp.float32),
        in_specs=[pl.BlockSpec(memory_space=pltpu.VMEM)],
        out_specs=pl.BlockSpec(memory_space=pltpu.VMEM),
        scratch_shapes=[
            pltpu.VMEM((lanes, 2, piece, width), link_dtype),
            pltpu.VMEM((lanes, 2, piece, width), link_dtype),
            pltpu.SemaphoreType.DMA((lanes, 2)),
            pltpu.SemaphoreType.DMA((lanes, 2)),
            pltpu.SemaphoreType.REGULAR((lanes,)),
        ],
        compiler_params=pltpu.CompilerParams(collective_id=1, has_side_effects=True,
                                             vmem_limit_bytes=48 * 1024 * 1024),
    )(h)


QB = 128


def window_allow(tq_ref, tk_ref, a0, w0):
    rows = lax.broadcasted_iota(jnp.int32, (QB, QB + 2 * HALF), 0)
    cols = lax.broadcasted_iota(jnp.int32, (QB, QB + 2 * HALF), 1)
    offset = cols - rows - HALF
    near = jnp.abs(offset) <= HALF
    same = tk_ref[:, pl.ds(w0, QB + 2 * HALF)] == tq_ref[pl.ds(a0, QB), :]
    return near & (same | (offset == 0))


def nt(a, b):
    return lax.dot_general(a, b, (((1,), (1,)), ((), ())), preferred_element_type=jnp.float32)


def tn(a, b):
    return lax.dot_general(a, b, (((0,), (0,)), ((), ())), preferred_element_type=jnp.float32)


def probs_of(q_ref, kv_ref, allow, a0, w0, h):
    q_h = q_ref[pl.ds(a0, QB), pl.ds(h * HEAD, HEAD)]
    k_h = kv_ref[pl.ds(w0, QB + 2 * HALF), pl.ds(h * HEAD, HEAD)]
    scores = jnp.where(allow, nt(q_h, k_h) * 0.125, -1e30)
    largest = jnp.max(scores, axis=-1, keepdims=True)
    raised = jnp.exp(scores - largest)
    return raised / jnp.sum(raised, axis=-1, keepdims=True), q_h, k_h


def attn_fwd_kernel(q_ref, kv_ref, tq_ref, tk_ref, o_ref):
    width = q_ref.shape[1]

    def block(b, carry):
        a0 = pl.multiple_of(b * QB, QB)
        allow = window_allow(tq_ref, tk_ref, a0, a0)
        for h in range(HEADS):
            probs, _, _ = probs_of(q_ref, kv_ref, allow, a0, a0, h)
            v_h = kv_ref[pl.ds(a0, QB + 2 * HALF), pl.ds(width + h * HEAD, HEAD)]
            mixed = jnp.dot(probs.astype(jnp.bfloat16), v_h, preferred_element_type=jnp.float32)
            o_ref[pl.ds(a0, QB), pl.ds(h * HEAD, HEAD)] = mixed.astype(o_ref.dtype)
        return carry

    lax.fori_loop(0, q_ref.shape[0] // QB, block, 0)


def attn_bwd_kernel(q_ref, kv_ref, tq_ref, tk_ref, do_ref, dq_ref, dkv_ref):
    width = q_ref.shape[1]
    dkv_ref[...] = jnp.zeros(dkv_ref.shape, dkv_ref.dtype)

    def block(b, carry):
        a0 = pl.multiple_of(b * QB, QB)
        allow = window_allow(tq_ref, tk_ref, a0, a0)
        for h in range(HEADS):
            probs, q_h, k_h = probs_of(q_ref, kv_ref, allow, a0, a0, h)
            v_h = kv_ref[pl.ds(a0, QB + 2 * HALF), pl.ds(width + h * HEAD, HEAD)]
            do_h = do_ref[pl.ds(a0, QB), pl.ds(h * HEAD, HEAD)]
            grad_probs = nt(do_h, v_h)
            inner = jnp.sum(probs * grad_probs, axis=-1, keepdims=True)
            grad_scores = (probs * (grad_probs - inner)).astype(jnp.bfloat16)
            dq_ref[pl.ds(a0, QB), pl.ds(h * HEAD, HEAD)] = (
                jnp.dot(grad_scores, k_h, preferred_element_type=jnp.float32) * 0.125
            )
            rows = pl.ds(a0, QB + 2 * HALF)
            dkv_ref[rows, pl.ds(h * HEAD, HEAD)] += tn(grad_scores, q_h) * 0.125
            dkv_ref[rows, pl.ds(width + h * HEAD, HEAD)] += tn(probs.astype(jnp.bfloat16), do_h)
        return carry

    lax.fori_loop(0, q_ref.shape[0] // QB, block, 0)


VMEM_LIMIT = 48 * 1024 * 1024


def attn_fwd(query, wide_kv, tag_q, tag_k):
    count, width = query.shape
    vm = pl.BlockSpec(memory_space=pltpu.VMEM)
    return pl.pallas_call(
        attn_fwd_kernel,
        out_shape=jax.ShapeDtypeStruct((count, width), jnp.bfloat16),
        in_specs=[vm] * 4,
        out_specs=vm,
        compiler_params=pltpu.CompilerParams(vmem_limit_bytes=VMEM_LIMIT),
    )(query, wide_kv, tag_q.reshape(count, 1), tag_k.reshape(1, -1))


def attn_bwd(query, wide_kv, tag_q, tag_k, grad_out):
    count, width = query.shape
    vm = pl.BlockSpec(memory_space=pltpu.VMEM)
    return pl.pallas_call(
        attn_bwd_kernel,
        out_shape=(
            jax.ShapeDtypeStruct((count, width), jnp.float32),
            jax.ShapeDtypeStruct(wide_kv.shape, jnp.float32),
        ),
        in_specs=[vm] * 5,
        out_specs=(vm, vm),
        compiler_params=pltpu.CompilerParams(vmem_limit_bytes=VMEM_LIMIT),
    )(query, wide_kv, tag_q.reshape(count, 1), tag_k.reshape(1, -1), grad_out)


def gain_rows(gain, width, rows=8):
    line = jnp.pad(gain, (0, width - gain.shape[0]))
    return jnp.concatenate([line[None], jnp.zeros((rows - 1, width), gain.dtype)], 0)


def gather_rows(payload, n_dp, n_seq):
    every = lax.all_gather(payload, ("dp", "seq"), axis=0, tiled=True)
    return every.reshape(n_dp, n_seq, payload.shape[0], payload.shape[1])


def gain_blocks(grad_gain, n_dp, n_seq, width, height=8):
    part = jnp.pad(grad_gain.reshape(n_seq, -1), ((0, 0), (0, width - grad_gain.shape[0] // n_seq)))
    rows = jnp.concatenate([part[:, None], jnp.zeros((n_seq, height - 1, width), part.dtype)], 1)
    return jnp.broadcast_to(rows[None], (n_dp, n_seq, height, width))


def front(value, n_dp):
    return value.reshape(value.shape[0], n_dp, -1)


def apply_t(left, weight_t, n_dp):
    return jnp.einsum("tdr,dnr->tn", front(left, n_dp), weight_t, preferred_element_type=jnp.float32)


def apply_back(grad, weight_t):
    out = jnp.einsum("tn,dnr->tdr", grad, weight_t, preferred_element_type=jnp.float32)
    return out.reshape(out.shape[0], -1)


def grad_t(grad, left, n_dp):
    width = left.shape[1] // n_dp
    return [
        lax.dot_general(
            grad,
            left[:, d * width : (d + 1) * width],
            (((0,), (0,)), ((), ())),
            preferred_element_type=jnp.float32,
        )
        for d in range(n_dp)
    ]


def on_device(order, tokens, doc_start, real, w_qkv, w_out, w_in, w_down, gain_attn, gain_mlp, cotangent):
    count = tokens.shape[0]
    n_dp, n_seq = lax.axis_size("dp"), lax.axis_size("seq")
    rows, qkv_cols = w_qkv.shape
    out_cols, in_cols = w_out.shape[1], w_in.shape[1]
    down_rows, down_cols = w_down.shape
    down_lines = down_rows * down_cols // rows
    first = gather_rows(jnp.concatenate([w_qkv.T, gain_rows(gain_attn, rows)], 0), n_dp, n_seq)
    second = gather_rows(
        jnp.concatenate(
            [w_out.T, w_in.T, w_down.T.reshape(down_lines, rows), gain_rows(gain_mlp, rows)], 0
        ),
        n_dp,
        n_seq,
    )
    full_qkv = first[:, :, :qkv_cols].reshape(n_dp, n_seq * qkv_cols, rows)
    gain_one = first[0, :, qkv_cols, : gain_attn.shape[0]].reshape(-1).astype(jnp.float32)
    stream = tokens.astype(jnp.float32)
    normed_a, factor_a = layer_norm(stream)
    h_attn = (normed_a * gain_one).astype(jnp.bfloat16)
    qkv = apply_t(h_attn, full_qkv, n_dp)
    offset_base = lax.axis_index(("dp", "seq")) * count
    place = (offset_base + jnp.arange(count, dtype=jnp.int32) - doc_start).astype(jnp.float32)
    cosine, sine = rotary_tables(place)
    query = (qkv[:, :D] * cosine + rotate(qkv[:, :D]) * sine).astype(jnp.bfloat16)
    key_rows = (qkv[:, D : 2 * D] * cosine + rotate(qkv[:, D : 2 * D]) * sine).astype(jnp.bfloat16)
    value_rows = qkv[:, 2 * D :].astype(jnp.bfloat16)
    tag_query = doc_start + 1
    tag_key = jnp.where(real == 1, tag_query, 0)
    key_value = jnp.concatenate([key_rows, value_rows], 1)
    wide_kv, wide_tag = (
        padded(key_value, ((("dp", "seq"), 0),), HALF),
        padded(tag_key, ((("dp", "seq"), 0),), HALF),
    )
    attn_out = attn_fwd(query, wide_kv, tag_query, wide_tag)
    attn_out, second = lax.optimization_barrier((attn_out, second))
    at = 0
    full_out = second[:, :, at : at + out_cols].reshape(n_dp, n_seq * out_cols, rows)
    at += out_cols
    full_in = second[:, :, at : at + in_cols].reshape(n_dp, n_seq * in_cols, rows)
    at += in_cols
    full_down = (
        second[:, :, at : at + down_lines]
        .reshape(n_dp, n_seq, down_cols, down_rows)
        .reshape(n_dp, n_seq * down_cols, down_rows)
    )
    at += down_lines
    gain_two = second[0, :, at, : gain_mlp.shape[0]].reshape(-1).astype(jnp.float32)
    mid = stream + apply_t(attn_out, full_out, n_dp)
    normed_m, factor_m = layer_norm(mid)
    h_mlp = (normed_m * gain_two).astype(jnp.bfloat16)
    gate_up = apply_t(h_mlp, full_in, n_dp)
    hidden_out, glu_pull = jax.vjp(glu_piece, gate_up)
    hidden = hidden_out.astype(jnp.bfloat16)
    result = mid + apply_t(hidden, full_down, n_dp)
    output = result.astype(jnp.bfloat16)
    grad_down = grad_t(cotangent, hidden, n_dp)
    grad_hidden = apply_back(cotangent, full_down)
    grad_gate_up = glu_pull(grad_hidden)[0].astype(jnp.bfloat16)
    grad_inw = grad_t(grad_gate_up, h_mlp, n_dp)
    grad_hmlp = apply_back(grad_gate_up, full_in)
    grad_gain_two = jnp.sum(grad_hmlp * normed_m, axis=0)
    grad_mid = cotangent.astype(jnp.float32) + norm_back(grad_hmlp * gain_two, normed_m, factor_m)
    grad_branch = grad_mid.astype(jnp.bfloat16)
    grad_outw = grad_t(grad_branch, attn_out, n_dp)
    grad_attn = apply_back(grad_branch, full_out).astype(jnp.bfloat16)
    grad_query, grad_wide = attn_bwd(query, wide_kv, tag_query, wide_tag, grad_attn)
    from_above = shifted(grad_wide[:HALF].astype(jnp.bfloat16), ("dp", "seq"), -1).astype(
        jnp.float32
    )
    from_below = shifted(grad_wide[count + HALF :].astype(jnp.bfloat16), ("dp", "seq"), 1).astype(
        jnp.float32
    )
    grad_kv = grad_wide[HALF : HALF + count]
    grad_kv = grad_kv.at[:HALF].add(from_below)
    grad_kv = grad_kv.at[count - HALF :].add(from_above)
    grad_keys = grad_kv[:, :D]
    grad_qkv = jnp.concatenate(
        [
            grad_query * cosine - rotate(grad_query) * sine,
            grad_keys * cosine - rotate(grad_keys) * sine,
            grad_kv[:, D:],
        ],
        1,
    ).astype(jnp.bfloat16)
    grad_qkvw = grad_t(grad_qkv, h_attn, n_dp)
    grad_hattn = apply_back(grad_qkv, full_qkv)
    grad_gain_one = jnp.sum(grad_hattn * normed_a, axis=0)
    grad_tokens = grad_mid + norm_back(grad_hattn * gain_one, normed_a, factor_a)
    height = out_cols + in_cols + down_lines + qkv_cols + 16
    tail = 8 + (-height) % (2 * RING_WAYS * 16)
    gain_two_rows = gain_blocks(grad_gain_two, 1, n_seq, rows)[0]
    gain_one_rows = gain_blocks(grad_gain_one, 1, n_seq, rows, tail)[0]
    blocks = jnp.stack(
        [
            jnp.concatenate(
                [
                    *lax.optimization_barrier(
                        (
                            grad_outw[d].reshape(n_seq, out_cols, rows),
                            grad_inw[d].reshape(n_seq, in_cols, rows),
                            grad_down[d]
                            .reshape(n_seq, down_cols, down_rows)
                            .reshape(n_seq, down_lines, rows),
                            gain_two_rows,
                            grad_qkvw[d].reshape(n_seq, qkv_cols, rows),
                            gain_one_rows,
                        )
                    ),
                ],
                1,
            )
            for d in range(n_dp)
        ]
    )
    depth = blocks.shape[2]
    half = lax.psum_scatter(
        blocks.reshape(n_dp, n_seq * depth, rows), "dp", scatter_dimension=0, tiled=True
    )
    late = ring_reduce(half.reshape(n_seq, depth, rows), order, RING_WAYS)
    last = late[out_cols + in_cols + down_lines + 8 :]
    at = 0
    late_out = late[at : at + out_cols].T
    at += out_cols
    late_in = late[at : at + in_cols].T
    at += in_cols
    late_down = late[at : at + down_lines].reshape(down_cols, down_rows).T
    at += down_lines
    late_gain_two = late[at, : gain_mlp.shape[0]]
    return (
        output,
        grad_tokens,
        last[:qkv_cols].T,
        late_out,
        late_in,
        late_down,
        last[qkv_cols, : gain_attn.shape[0]],
        late_gain_two,
    )


def solution(mesh):
    placed = (
        P(("dp", "seq"), None),
        P(("dp", "seq")),
        P(("dp", "seq")),
        P("dp", "seq"),
        P("dp", "seq"),
        P("dp", "seq"),
        P("dp", "seq"),
        P("seq"),
        P("seq"),
        P(("dp", "seq"), None),
    )
    return jax.shard_map(
        functools.partial(on_device, ring_order(mesh)),
        mesh=mesh,
        in_specs=placed,
        out_specs=(
            P(("dp", "seq"), None),
            P(("dp", "seq"), None),
            P("dp", "seq"),
            P("dp", "seq"),
            P("dp", "seq"),
            P("dp", "seq"),
            P("seq"),
            P("seq"),
        ),
        check_vma=False,
    )
```

```python
import functools
import math

import jax
import jax.numpy as jnp
from jax import lax
from jax.experimental import pallas as pl
from jax.experimental.pallas import tpu as pltpu
from jax.sharding import PartitionSpec as P

D = 768
HEADS = 12
HEAD = 64
FF = 1152
HALF = 64


def padded(value, sides, width):
    for axis, dim in sides:
        size, length = (lax.axis_size(axis), value.shape[dim])
        up = [(i, (i + 1) % size) for i in range(size - 1)]
        down = [(j, i) for i, j in up]
        last = lax.slice_in_dim(value, length - width, length, axis=dim)
        initial = lax.slice_in_dim(value, 0, width, axis=dim)
        before = lax.ppermute(last, axis, up)
        after = lax.ppermute(initial, axis, down)
        value = jnp.concatenate([before, value, after], axis=dim)
    return value


def shifted(value, axis, by):
    length = lax.axis_size(axis)
    pairs = [(i, i + by) for i in range(length) if 0 <= i + by < length]
    return lax.ppermute(value, axis, pairs)


def layer_norm(value):
    centre = value - jnp.mean(value, axis=-1, keepdims=True)
    factor = lax.rsqrt(jnp.mean(centre * centre, axis=-1, keepdims=True) + 1e-05)
    return (centre * factor, factor)


def norm_back(grad, normed, factor):
    return factor * (
        grad
        - jnp.mean(grad, axis=-1, keepdims=True)
        - normed * jnp.mean(grad * normed, axis=-1, keepdims=True)
    )


def rotary_tables(place):
    freq = jnp.exp(jnp.arange(HEAD // 2, dtype=jnp.float32) * (-2.0 * math.log(10000.0) / HEAD))
    angle = place[:, None] * freq[None, :]
    cosine = jnp.tile(jnp.concatenate([jnp.cos(angle), jnp.cos(angle)], 1), (1, HEADS))
    sine = jnp.tile(jnp.concatenate([jnp.sin(angle), jnp.sin(angle)], 1), (1, HEADS))
    return (cosine, sine)


def rotate(value):
    count = value.shape[0]
    shaped = value.reshape(count, HEADS, HEAD)
    first = shaped[..., : HEAD // 2]
    second = shaped[..., HEAD // 2 :]
    return jnp.concatenate([-second, first], -1).reshape(count, HEADS * HEAD)


def left_dot(left, right):
    return lax.dot_general(
        left, right, (((0,), (0,)), ((), ())), preferred_element_type=jnp.float32
    )


def right_dot(left, right):
    return lax.dot_general(
        left, right, (((1,), (1,)), ((), ())), preferred_element_type=jnp.float32
    )


def glu_piece(gate_up):
    return jax.nn.gelu(gate_up[:, :FF], approximate=False) * gate_up[:, FF:]


MESH = pl.DeviceIdType.MESH


def ring_order(mesh):
    n = mesh.shape["seq"]
    try:
        coords = [tuple(mesh.devices[0, s].coords) for s in range(n)]
    except Exception:
        return list(range(n))
    near = [
        [t for t in range(n) if sum(abs(a - b) for a, b in zip(coords[s], coords[t])) == 1]
        for s in range(n)
    ]
    path, seen = [0], {0}

    def grow(budget=[200000]):
        budget[0] -= 1
        if budget[0] < 0:
            return False
        if len(path) == n:
            return 0 in near[path[-1]]
        options = sorted(
            (t for t in near[path[-1]] if t not in seen),
            key=lambda t: sum(1 for u in near[t] if u not in seen),
        )
        for t in options:
            path.append(t)
            seen.add(t)
            if grow():
                return True
            path.pop()
            seen.discard(t)
        return False

    return list(path) if n > 2 and grow() else list(range(n))


def lookup(index, table):
    n = len(table)
    square = n * n
    total = jnp.int32(0)
    for k, value in enumerate(table):
        if value:
            gap = index - k
            differs = lax.div(gap * gap + (square - 1), jnp.int32(square))
            total = total + value * (1 - differs)
    return total


def ring_kernel(order, per_way, h_ref, out_ref, recv, send, ssem, rsem, free):
    n = len(order)
    where = [0] * n
    for p, s in enumerate(order):
        where[s] = p
    d = lax.axis_index("dp")
    me = lax.axis_index("seq")
    pos = lookup(me, where)
    nxt = lookup(lax.rem(pos + 1, n), order)
    prv = lookup(lax.rem(pos + n - 1, n), order)
    piece = out_ref.shape[0] // per_way
    ahead = (n - 1) // 2
    behind = n - 1 - ahead

    barrier = pltpu.get_barrier_semaphore()
    pl.semaphore_signal(barrier, 1, device_id=(d, nxt), device_id_type=MESH)
    pl.semaphore_signal(barrier, 1, device_id=(d, prv), device_id_type=MESH)
    pl.semaphore_wait(barrier, 2)

    lanes = []
    for forward in (True, False):
        for chunk in range(per_way):
            li = len(lanes)
            lanes.append((recv.at[li], send.at[li], ssem.at[li], rsem.at[li], free.at[li],
                          nxt if forward else prv, prv if forward else nxt,
                          slice(chunk * piece, (chunk + 1) * piece),
                          ahead if forward else behind, forward))
    copies = {}
    for step in range(max(ahead, behind)):
        slot = step % 2
        for li, (recv, send, ssem, rsem, free, to, frm, rows, sends, forward) in enumerate(lanes):
            if step >= sends:
                continue
            if forward:
                target = pos + sends - step
            else:
                target = pos + n - sends + step
            q = lookup(lax.rem(target, n), order)
            own = h_ref[q, rows, :]
            if step == 0:
                part = own
            else:
                copies[(li, step - 1)].wait_recv()
                part = recv[1 - slot].astype(jnp.float32) + own
                if step <= sends - 2:
                    pl.semaphore_signal(free, 1, device_id=(d, frm), device_id_type=MESH)
            if step >= 2:
                copies[(li, step - 2)].wait_send()
                pl.semaphore_wait(free, 1)
            send[slot] = part.astype(send.dtype)
            c = pltpu.make_async_remote_copy(
                src_ref=send.at[slot], dst_ref=recv.at[slot],
                send_sem=ssem.at[slot], recv_sem=rsem.at[slot],
                device_id=(d, to), device_id_type=MESH)
            c.start()
            copies[(li, step)] = c
    for chunk in range(per_way):
        rows = lanes[chunk][7]
        total = h_ref[me, rows, :]
        for li in (chunk, per_way + chunk):
            recv, sends = lanes[li][0], lanes[li][8]
            copies[(li, sends - 1)].wait_recv()
            total = total + recv[(sends - 1) % 2].astype(jnp.float32)
        out_ref[rows, :] = total
    for li, lane in enumerate(lanes):
        sends = lane[8]
        if sends >= 2:
            copies[(li, sends - 2)].wait_send()
        copies[(li, sends - 1)].wait_send()


RING_WAYS = 2


def ring_reduce(h, order, per_way, link_dtype=jnp.bfloat16):
    n, rows, width = h.shape
    lanes = 2 * per_way
    piece = rows // per_way
    return pl.pallas_call(
        functools.partial(ring_kernel, tuple(order), per_way),
        out_shape=jax.ShapeDtypeStruct((rows, width), jnp.float32),
        in_specs=[pl.BlockSpec(memory_space=pltpu.VMEM)],
        out_specs=pl.BlockSpec(memory_space=pltpu.VMEM),
        scratch_shapes=[
            pltpu.VMEM((lanes, 2, piece, width), link_dtype),
            pltpu.VMEM((lanes, 2, piece, width), link_dtype),
            pltpu.SemaphoreType.DMA((lanes, 2)),
            pltpu.SemaphoreType.DMA((lanes, 2)),
            pltpu.SemaphoreType.REGULAR((lanes,)),
        ],
        compiler_params=pltpu.CompilerParams(collective_id=1, has_side_effects=True,
                                             vmem_limit_bytes=48 * 1024 * 1024),
    )(h)


QB = 128


def window_allow(tq_ref, tk_ref, a0, w0):
    rows = lax.broadcasted_iota(jnp.int32, (QB, QB + 2 * HALF), 0)
    cols = lax.broadcasted_iota(jnp.int32, (QB, QB + 2 * HALF), 1)
    offset = cols - rows - HALF
    near = jnp.abs(offset) <= HALF
    same = tk_ref[:, pl.ds(w0, QB + 2 * HALF)] == tq_ref[pl.ds(a0, QB), :]
    return near & (same | (offset == 0))


def nt(a, b):
    return lax.dot_general(a, b, (((1,), (1,)), ((), ())), preferred_element_type=jnp.float32)


def tn(a, b):
    return lax.dot_general(a, b, (((0,), (0,)), ((), ())), preferred_element_type=jnp.float32)


def probs_of(q_ref, kv_ref, allow, a0, w0, h):
    q_h = q_ref[pl.ds(a0, QB), pl.ds(h * HEAD, HEAD)]
    k_h = kv_ref[pl.ds(w0, QB + 2 * HALF), pl.ds(h * HEAD, HEAD)]
    scores = jnp.where(allow, nt(q_h, k_h) * 0.125, -1e30)
    largest = jnp.max(scores, axis=-1, keepdims=True)
    raised = jnp.exp(scores - largest)
    return raised / jnp.sum(raised, axis=-1, keepdims=True), q_h, k_h


def attn_fwd_kernel(q_ref, kv_ref, tq_ref, tk_ref, o_ref):
    width = q_ref.shape[1]

    def block(b, carry):
        a0 = pl.multiple_of(b * QB, QB)
        allow = window_allow(tq_ref, tk_ref, a0, a0)
        for h in range(HEADS):
            probs, _, _ = probs_of(q_ref, kv_ref, allow, a0, a0, h)
            v_h = kv_ref[pl.ds(a0, QB + 2 * HALF), pl.ds(width + h * HEAD, HEAD)]
            mixed = jnp.dot(probs.astype(jnp.bfloat16), v_h, preferred_element_type=jnp.float32)
            o_ref[pl.ds(a0, QB), pl.ds(h * HEAD, HEAD)] = mixed.astype(o_ref.dtype)
        return carry

    lax.fori_loop(0, q_ref.shape[0] // QB, block, 0)


def attn_bwd_kernel(q_ref, kv_ref, tq_ref, tk_ref, do_ref, dq_ref, dkv_ref):
    width = q_ref.shape[1]
    dkv_ref[...] = jnp.zeros(dkv_ref.shape, dkv_ref.dtype)

    def block(b, carry):
        a0 = pl.multiple_of(b * QB, QB)
        allow = window_allow(tq_ref, tk_ref, a0, a0)
        for h in range(HEADS):
            probs, q_h, k_h = probs_of(q_ref, kv_ref, allow, a0, a0, h)
            v_h = kv_ref[pl.ds(a0, QB + 2 * HALF), pl.ds(width + h * HEAD, HEAD)]
            do_h = do_ref[pl.ds(a0, QB), pl.ds(h * HEAD, HEAD)]
            grad_probs = nt(do_h, v_h)
            inner = jnp.sum(probs * grad_probs, axis=-1, keepdims=True)
            grad_scores = (probs * (grad_probs - inner)).astype(jnp.bfloat16)
            dq_ref[pl.ds(a0, QB), pl.ds(h * HEAD, HEAD)] = (
                jnp.dot(grad_scores, k_h, preferred_element_type=jnp.float32) * 0.125
            )
            rows = pl.ds(a0, QB + 2 * HALF)
            dkv_ref[rows, pl.ds(h * HEAD, HEAD)] += tn(grad_scores, q_h) * 0.125
            dkv_ref[rows, pl.ds(width + h * HEAD, HEAD)] += tn(probs.astype(jnp.bfloat16), do_h)
        return carry

    lax.fori_loop(0, q_ref.shape[0] // QB, block, 0)


VMEM_LIMIT = 48 * 1024 * 1024


def attn_fwd(query, wide_kv, tag_q, tag_k):
    count, width = query.shape
    vm = pl.BlockSpec(memory_space=pltpu.VMEM)
    return pl.pallas_call(
        attn_fwd_kernel,
        out_shape=jax.ShapeDtypeStruct((count, width), jnp.bfloat16),
        in_specs=[vm] * 4,
        out_specs=vm,
        compiler_params=pltpu.CompilerParams(vmem_limit_bytes=VMEM_LIMIT),
    )(query, wide_kv, tag_q.reshape(count, 1), tag_k.reshape(1, -1))


def attn_bwd(query, wide_kv, tag_q, tag_k, grad_out):
    count, width = query.shape
    vm = pl.BlockSpec(memory_space=pltpu.VMEM)
    return pl.pallas_call(
        attn_bwd_kernel,
        out_shape=(
            jax.ShapeDtypeStruct((count, width), jnp.float32),
            jax.ShapeDtypeStruct(wide_kv.shape, jnp.float32),
        ),
        in_specs=[vm] * 5,
        out_specs=(vm, vm),
        compiler_params=pltpu.CompilerParams(vmem_limit_bytes=VMEM_LIMIT),
    )(query, wide_kv, tag_q.reshape(count, 1), tag_k.reshape(1, -1), grad_out)


def gain_rows(gain, width, rows=8):
    line = jnp.pad(gain, (0, width - gain.shape[0]))
    return jnp.concatenate([line[None], jnp.zeros((rows - 1, width), gain.dtype)], 0)


def gather_rows(payload, n_dp, n_seq):
    every = lax.all_gather(payload, ("dp", "seq"), axis=0, tiled=True)
    return every.reshape(n_dp, n_seq, payload.shape[0], payload.shape[1])


def gain_blocks(grad_gain, n_dp, n_seq, width, height=8):
    part = jnp.pad(grad_gain.reshape(n_seq, -1), ((0, 0), (0, width - grad_gain.shape[0] // n_seq)))
    rows = jnp.concatenate([part[:, None], jnp.zeros((n_seq, height - 1, width), part.dtype)], 1)
    return jnp.broadcast_to(rows[None], (n_dp, n_seq, height, width))


def front(value, n_dp):
    return value.reshape(value.shape[0], n_dp, -1)


def apply_t(left, weight_t, n_dp):
    return jnp.einsum("tdr,dnr->tn", front(left, n_dp), weight_t, preferred_element_type=jnp.float32)


def apply_back(grad, weight_t):
    out = jnp.einsum("tn,dnr->tdr", grad, weight_t, preferred_element_type=jnp.float32)
    return out.reshape(out.shape[0], -1)


def grad_t(grad, left, n_dp):
    width = left.shape[1] // n_dp
    return [
        lax.dot_general(
            grad,
            left[:, d * width : (d + 1) * width],
            (((0,), (0,)), ((), ())),
            preferred_element_type=jnp.float32,
        )
        for d in range(n_dp)
    ]


def on_device(order, tokens, doc_start, real, w_qkv, w_out, w_in, w_down, gain_attn, gain_mlp, cotangent):
    count = tokens.shape[0]
    n_dp, n_seq = lax.axis_size("dp"), lax.axis_size("seq")
    rows, qkv_cols = w_qkv.shape
    out_cols, in_cols = w_out.shape[1], w_in.shape[1]
    down_rows, down_cols = w_down.shape
    down_lines = down_rows * down_cols // rows
    first = gather_rows(jnp.concatenate([w_qkv.T, gain_rows(gain_attn, rows)], 0), n_dp, n_seq)
    second = gather_rows(
        jnp.concatenate(
            [w_out.T, w_in.T, w_down.T.reshape(down_lines, rows), gain_rows(gain_mlp, rows)], 0
        ),
        n_dp,
        n_seq,
    )
    full_qkv = first[:, :, :qkv_cols].reshape(n_dp, n_seq * qkv_cols, rows)
    gain_one = first[0, :, qkv_cols, : gain_attn.shape[0]].reshape(-1).astype(jnp.float32)
    stream = tokens.astype(jnp.float32)
    normed_a, factor_a = layer_norm(stream)
    h_attn = (normed_a * gain_one).astype(jnp.bfloat16)
    qkv = apply_t(h_attn, full_qkv, n_dp)
    offset_base = lax.axis_index(("dp", "seq")) * count
    place = (offset_base + jnp.arange(count, dtype=jnp.int32) - doc_start).astype(jnp.float32)
    cosine, sine = rotary_tables(place)
    query = (qkv[:, :D] * cosine + rotate(qkv[:, :D]) * sine).astype(jnp.bfloat16)
    key_rows = (qkv[:, D : 2 * D] * cosine + rotate(qkv[:, D : 2 * D]) * sine).astype(jnp.bfloat16)
    value_rows = qkv[:, 2 * D :].astype(jnp.bfloat16)
    tag_query = doc_start + 1
    tag_key = jnp.where(real == 1, tag_query, 0)
    key_value = jnp.concatenate([key_rows, value_rows], 1)
    wide_kv, wide_tag = (
        padded(key_value, ((("dp", "seq"), 0),), HALF),
        padded(tag_key, ((("dp", "seq"), 0),), HALF),
    )
    attn_out = attn_fwd(query, wide_kv, tag_query, wide_tag)
    attn_out, second = lax.optimization_barrier((attn_out, second))
    at = 0
    full_out = second[:, :, at : at + out_cols].reshape(n_dp, n_seq * out_cols, rows)
    at += out_cols
    full_in = second[:, :, at : at + in_cols].reshape(n_dp, n_seq * in_cols, rows)
    at += in_cols
    full_down = (
        second[:, :, at : at + down_lines]
        .reshape(n_dp, n_seq, down_cols, down_rows)
        .reshape(n_dp, n_seq * down_cols, down_rows)
    )
    at += down_lines
    gain_two = second[0, :, at, : gain_mlp.shape[0]].reshape(-1).astype(jnp.float32)
    mid = stream + apply_t(attn_out, full_out, n_dp)
    normed_m, factor_m = layer_norm(mid)
    h_mlp = (normed_m * gain_two).astype(jnp.bfloat16)
    gate_up = apply_t(h_mlp, full_in, n_dp)
    hidden_out, glu_pull = jax.vjp(glu_piece, gate_up)
    hidden = hidden_out.astype(jnp.bfloat16)
    result = mid + apply_t(hidden, full_down, n_dp)
    output = result.astype(jnp.bfloat16)
    grad_down = grad_t(cotangent, hidden, n_dp)
    grad_hidden = apply_back(cotangent, full_down)
    grad_gate_up = glu_pull(grad_hidden)[0].astype(jnp.bfloat16)
    grad_inw = grad_t(grad_gate_up, h_mlp, n_dp)
    grad_hmlp = apply_back(grad_gate_up, full_in)
    grad_gain_two = jnp.sum(grad_hmlp * normed_m, axis=0)
    grad_mid = cotangent.astype(jnp.float32) + norm_back(grad_hmlp * gain_two, normed_m, factor_m)
    grad_branch = grad_mid.astype(jnp.bfloat16)
    grad_outw = grad_t(grad_branch, attn_out, n_dp)
    grad_attn = apply_back(grad_branch, full_out).astype(jnp.bfloat16)
    grad_query, grad_wide = attn_bwd(query, wide_kv, tag_query, wide_tag, grad_attn)
    from_above = shifted(grad_wide[:HALF].astype(jnp.bfloat16), ("dp", "seq"), -1).astype(
        jnp.float32
    )
    from_below = shifted(grad_wide[count + HALF :].astype(jnp.bfloat16), ("dp", "seq"), 1).astype(
        jnp.float32
    )
    grad_kv = grad_wide[HALF : HALF + count]
    grad_kv = grad_kv.at[:HALF].add(from_below)
    grad_kv = grad_kv.at[count - HALF :].add(from_above)
    grad_keys = grad_kv[:, :D]
    grad_qkv = jnp.concatenate(
        [
            grad_query * cosine - rotate(grad_query) * sine,
            grad_keys * cosine - rotate(grad_keys) * sine,
            grad_kv[:, D:],
        ],
        1,
    ).astype(jnp.bfloat16)
    grad_qkvw = grad_t(grad_qkv, h_attn, n_dp)
    grad_hattn = apply_back(grad_qkv, full_qkv)
    grad_gain_one = jnp.sum(grad_hattn * normed_a, axis=0)
    grad_tokens = grad_mid + norm_back(grad_hattn * gain_one, normed_a, factor_a)
    height = out_cols + in_cols + down_lines + qkv_cols + 8
    tail = 8 + (-height) % (RING_WAYS * 16)
    gain_both = jnp.concatenate(
        [
            gain_blocks(grad_gain_two, 1, n_seq, rows, 1)[0],
            gain_blocks(grad_gain_one, 1, n_seq, rows, tail - 1)[0],
        ],
        1,
    )
    blocks = jnp.stack(
        [
            jnp.concatenate(
                [
                    *lax.optimization_barrier(
                        (
                            grad_outw[d].reshape(n_seq, out_cols, rows),
                            grad_inw[d].reshape(n_seq, in_cols, rows),
                            grad_down[d]
                            .reshape(n_seq, down_cols, down_rows)
                            .reshape(n_seq, down_lines, rows),
                            grad_qkvw[d].reshape(n_seq, qkv_cols, rows),
                            gain_both,
                        )
                    ),
                ],
                1,
            )
            for d in range(n_dp)
        ]
    )
    depth = blocks.shape[2]
    half = lax.psum_scatter(
        blocks.reshape(n_dp, n_seq * depth, rows), "dp", scatter_dimension=0, tiled=True
    )
    late = ring_reduce(half.reshape(n_seq, depth, rows), order, RING_WAYS)
    at = 0
    late_out = late[at : at + out_cols].T
    at += out_cols
    late_in = late[at : at + in_cols].T
    at += in_cols
    late_down = late[at : at + down_lines].reshape(down_cols, down_rows).T
    at += down_lines
    late_qkv = late[at : at + qkv_cols].T
    at += qkv_cols
    late_gain_two = late[at, : gain_mlp.shape[0]]
    late_gain_one = late[at + 1, : gain_attn.shape[0]]
    return (
        output,
        grad_tokens,
        late_qkv,
        late_out,
        late_in,
        late_down,
        late_gain_one,
        late_gain_two,
    )


def solution(mesh):
    placed = (
        P(("dp", "seq"), None),
        P(("dp", "seq")),
        P(("dp", "seq")),
        P("dp", "seq"),
        P("dp", "seq"),
        P("dp", "seq"),
        P("dp", "seq"),
        P("seq"),
        P("seq"),
        P(("dp", "seq"), None),
    )
    return jax.shard_map(
        functools.partial(on_device, ring_order(mesh)),
        mesh=mesh,
        in_specs=placed,
        out_specs=(
            P(("dp", "seq"), None),
            P(("dp", "seq"), None),
            P("dp", "seq"),
            P("dp", "seq"),
            P("dp", "seq"),
            P("dp", "seq"),
            P("seq"),
            P("seq"),
        ),
        check_vma=False,
    )
```

```python
import functools
import math

import jax
import jax.numpy as jnp
from jax import lax
from jax.experimental import pallas as pl
from jax.experimental.pallas import tpu as pltpu
from jax.sharding import PartitionSpec as P

D = 768
HEADS = 12
HEAD = 64
FF = 1152
HALF = 64


def padded(value, sides, width):
    for axis, dim in sides:
        size, length = (lax.axis_size(axis), value.shape[dim])
        up = [(i, (i + 1) % size) for i in range(size - 1)]
        down = [(j, i) for i, j in up]
        last = lax.slice_in_dim(value, length - width, length, axis=dim)
        initial = lax.slice_in_dim(value, 0, width, axis=dim)
        before = lax.ppermute(last, axis, up)
        after = lax.ppermute(initial, axis, down)
        value = jnp.concatenate([before, value, after], axis=dim)
    return value


def shifted(value, axis, by):
    length = lax.axis_size(axis)
    pairs = [(i, i + by) for i in range(length) if 0 <= i + by < length]
    return lax.ppermute(value, axis, pairs)


def layer_norm(value):
    centre = value - jnp.mean(value, axis=-1, keepdims=True)
    factor = lax.rsqrt(jnp.mean(centre * centre, axis=-1, keepdims=True) + 1e-05)
    return (centre * factor, factor)


def norm_back(grad, normed, factor):
    return factor * (
        grad
        - jnp.mean(grad, axis=-1, keepdims=True)
        - normed * jnp.mean(grad * normed, axis=-1, keepdims=True)
    )


def rotary_tables(place):
    freq = jnp.exp(jnp.arange(HEAD // 2, dtype=jnp.float32) * (-2.0 * math.log(10000.0) / HEAD))
    angle = place[:, None] * freq[None, :]
    cosine = jnp.tile(jnp.concatenate([jnp.cos(angle), jnp.cos(angle)], 1), (1, HEADS))
    sine = jnp.tile(jnp.concatenate([jnp.sin(angle), jnp.sin(angle)], 1), (1, HEADS))
    return (cosine, sine)


def rotate(value):
    count = value.shape[0]
    shaped = value.reshape(count, HEADS, HEAD)
    first = shaped[..., : HEAD // 2]
    second = shaped[..., HEAD // 2 :]
    return jnp.concatenate([-second, first], -1).reshape(count, HEADS * HEAD)


def left_dot(left, right):
    return lax.dot_general(
        left, right, (((0,), (0,)), ((), ())), preferred_element_type=jnp.float32
    )


def right_dot(left, right):
    return lax.dot_general(
        left, right, (((1,), (1,)), ((), ())), preferred_element_type=jnp.float32
    )


def glu_piece(gate_up):
    return jax.nn.gelu(gate_up[:, :FF], approximate=False) * gate_up[:, FF:]


MESH = pl.DeviceIdType.MESH


def ring_order(mesh):
    n = mesh.shape["seq"]
    try:
        coords = [tuple(mesh.devices[0, s].coords) for s in range(n)]
    except Exception:
        return list(range(n))
    near = [
        [t for t in range(n) if sum(abs(a - b) for a, b in zip(coords[s], coords[t])) == 1]
        for s in range(n)
    ]
    path, seen = [0], {0}

    def grow(budget=[200000]):
        budget[0] -= 1
        if budget[0] < 0:
            return False
        if len(path) == n:
            return 0 in near[path[-1]]
        options = sorted(
            (t for t in near[path[-1]] if t not in seen),
            key=lambda t: sum(1 for u in near[t] if u not in seen),
        )
        for t in options:
            path.append(t)
            seen.add(t)
            if grow():
                return True
            path.pop()
            seen.discard(t)
        return False

    return list(path) if n > 2 and grow() else list(range(n))


def lookup(index, table):
    n = len(table)
    square = n * n
    total = jnp.int32(0)
    for k, value in enumerate(table):
        if value:
            gap = index - k
            differs = lax.div(gap * gap + (square - 1), jnp.int32(square))
            total = total + value * (1 - differs)
    return total


def ring_kernel(order, per_way, h_ref, out_ref, recv, send, ssem, rsem, free):
    n = len(order)
    where = [0] * n
    for p, s in enumerate(order):
        where[s] = p
    d = lax.axis_index("dp")
    me = lax.axis_index("seq")
    pos = lookup(me, where)
    nxt = lookup(lax.rem(pos + 1, n), order)
    prv = lookup(lax.rem(pos + n - 1, n), order)
    piece = out_ref.shape[0] // per_way
    ahead = (n - 1) // 2
    behind = n - 1 - ahead

    barrier = pltpu.get_barrier_semaphore()
    pl.semaphore_signal(barrier, 1, device_id=(d, nxt), device_id_type=MESH)
    pl.semaphore_signal(barrier, 1, device_id=(d, prv), device_id_type=MESH)
    pl.semaphore_wait(barrier, 2)

    lanes = []
    for forward in (True, False):
        for chunk in range(per_way):
            li = len(lanes)
            lanes.append((recv.at[li], send.at[li], ssem.at[li], rsem.at[li], free.at[li],
                          nxt if forward else prv, prv if forward else nxt,
                          slice(chunk * piece, (chunk + 1) * piece),
                          ahead if forward else behind, forward))
    copies = {}
    for step in range(max(ahead, behind)):
        slot = step % 2
        for li, (recv, send, ssem, rsem, free, to, frm, rows, sends, forward) in enumerate(lanes):
            if step >= sends:
                continue
            if forward:
                target = pos + sends - step
            else:
                target = pos + n - sends + step
            q = lookup(lax.rem(target, n), order)
            own = h_ref[q, rows, :]
            if step == 0:
                part = own
            else:
                copies[(li, step - 1)].wait_recv()
                part = recv[1 - slot].astype(jnp.float32) + own
                if step <= sends - 2:
                    pl.semaphore_signal(free, 1, device_id=(d, frm), device_id_type=MESH)
            if step >= 2:
                copies[(li, step - 2)].wait_send()
                pl.semaphore_wait(free, 1)
            send[slot] = part.astype(send.dtype)
            c = pltpu.make_async_remote_copy(
                src_ref=send.at[slot], dst_ref=recv.at[slot],
                send_sem=ssem.at[slot], recv_sem=rsem.at[slot],
                device_id=(d, to), device_id_type=MESH)
            c.start()
            copies[(li, step)] = c
    for chunk in range(per_way):
        rows = lanes[chunk][7]
        total = h_ref[me, rows, :]
        for li in (chunk, per_way + chunk):
            recv, sends = lanes[li][0], lanes[li][8]
            copies[(li, sends - 1)].wait_recv()
            total = total + recv[(sends - 1) % 2].astype(jnp.float32)
        out_ref[rows, :] = total
    for li, lane in enumerate(lanes):
        sends = lane[8]
        if sends >= 2:
            copies[(li, sends - 2)].wait_send()
        copies[(li, sends - 1)].wait_send()


RING_WAYS = 2


def ring_reduce(h, order, per_way, link_dtype=jnp.bfloat16):
    n, rows, width = h.shape
    lanes = 2 * per_way
    piece = rows // per_way
    return pl.pallas_call(
        functools.partial(ring_kernel, tuple(order), per_way),
        out_shape=jax.ShapeDtypeStruct((rows, width), jnp.float32),
        in_specs=[pl.BlockSpec(memory_space=pltpu.VMEM)],
        out_specs=pl.BlockSpec(memory_space=pltpu.VMEM),
        scratch_shapes=[
            pltpu.VMEM((lanes, 2, piece, width), link_dtype),
            pltpu.VMEM((lanes, 2, piece, width), link_dtype),
            pltpu.SemaphoreType.DMA((lanes, 2)),
            pltpu.SemaphoreType.DMA((lanes, 2)),
            pltpu.SemaphoreType.REGULAR((lanes,)),
        ],
        compiler_params=pltpu.CompilerParams(collective_id=1, has_side_effects=True,
                                             vmem_limit_bytes=48 * 1024 * 1024),
    )(h)


QB = 128


def window_allow(tq_ref, tk_ref, a0, w0):
    rows = lax.broadcasted_iota(jnp.int32, (QB, QB + 2 * HALF), 0)
    cols = lax.broadcasted_iota(jnp.int32, (QB, QB + 2 * HALF), 1)
    offset = cols - rows - HALF
    near = jnp.abs(offset) <= HALF
    same = tk_ref[:, pl.ds(w0, QB + 2 * HALF)] == tq_ref[pl.ds(a0, QB), :]
    return near & (same | (offset == 0))


def nt(a, b):
    return lax.dot_general(a, b, (((1,), (1,)), ((), ())), preferred_element_type=jnp.float32)


def tn(a, b):
    return lax.dot_general(a, b, (((0,), (0,)), ((), ())), preferred_element_type=jnp.float32)


def probs_of(q_ref, kv_ref, allow, a0, w0, h):
    q_h = q_ref[pl.ds(a0, QB), pl.ds(h * HEAD, HEAD)]
    k_h = kv_ref[pl.ds(w0, QB + 2 * HALF), pl.ds(h * HEAD, HEAD)]
    scores = jnp.where(allow, nt(q_h, k_h) * 0.125, -1e30)
    largest = jnp.max(scores, axis=-1, keepdims=True)
    raised = jnp.exp(scores - largest)
    return raised / jnp.sum(raised, axis=-1, keepdims=True), q_h, k_h


def neighbours():
    n_seq = lax.axis_size("seq")
    total = lax.axis_size("dp") * n_seq
    me = lax.axis_index("dp") * n_seq + lax.axis_index("seq")
    before = lax.rem(me + total - 1, total)
    after = lax.rem(me + 1, total)
    return (
        (lax.div(before, n_seq), lax.rem(before, n_seq)),
        (lax.div(after, n_seq), lax.rem(after, n_seq)),
    )


def greet(before, after):
    barrier = pltpu.get_barrier_semaphore()
    pl.semaphore_signal(barrier, 1, device_id=before, device_id_type=MESH)
    pl.semaphore_signal(barrier, 1, device_id=after, device_id_type=MESH)
    pl.semaphore_wait(barrier, 2)


def start_of(b):
    return b * QB if isinstance(b, int) else pl.multiple_of(b * QB, QB)


def attn_fwd_kernel(q_ref, kv_ref, tq_ref, tk_ref, o_ref, lo_ref, hi_ref, wide, send_sem, recv_sem):
    width = q_ref.shape[1]
    count = q_ref.shape[0]
    blocks = count // QB
    before, after = neighbours()
    greet(before, after)
    to_before = pltpu.make_async_remote_copy(
        src_ref=kv_ref.at[pl.ds(0, HALF)], dst_ref=hi_ref,
        send_sem=send_sem.at[0], recv_sem=recv_sem.at[0],
        device_id=before, device_id_type=MESH)
    to_after = pltpu.make_async_remote_copy(
        src_ref=kv_ref.at[pl.ds(count - HALF, HALF)], dst_ref=lo_ref,
        send_sem=send_sem.at[1], recv_sem=recv_sem.at[1],
        device_id=after, device_id_type=MESH)
    to_before.start()
    to_after.start()
    wide[pl.ds(HALF, count), :] = kv_ref[...]

    def block(b, carry):
        a0 = start_of(b)
        allow = window_allow(tq_ref, tk_ref, a0, a0)
        for h in range(HEADS):
            probs, _, _ = probs_of(q_ref, wide, allow, a0, a0, h)
            v_h = wide[pl.ds(a0, QB + 2 * HALF), pl.ds(width + h * HEAD, HEAD)]
            mixed = jnp.dot(probs.astype(jnp.bfloat16), v_h, preferred_element_type=jnp.float32)
            o_ref[pl.ds(a0, QB), pl.ds(h * HEAD, HEAD)] = mixed.astype(o_ref.dtype)
        return carry

    lax.fori_loop(1, blocks - 1, block, 0)
    to_before.wait_recv()
    to_after.wait_recv()
    wide[pl.ds(0, HALF), :] = lo_ref[...]
    wide[pl.ds(count + HALF, HALF), :] = hi_ref[...]
    block(0, 0)
    block(blocks - 1, 0)
    to_before.wait_send()
    to_after.wait_send()


def attn_bwd_kernel(q_ref, kv_ref, lo_ref, hi_ref, tq_ref, tk_ref, do_ref, dq_ref, dkv_ref,
                    wide, dwide, send_lo, send_hi, recv_lo, recv_hi, send_sem, recv_sem):
    width = q_ref.shape[1]
    count = q_ref.shape[0]
    blocks = count // QB
    before, after = neighbours()
    greet(before, after)
    wide[pl.ds(0, HALF), :] = lo_ref[...]
    wide[pl.ds(HALF, count), :] = kv_ref[...]
    wide[pl.ds(count + HALF, HALF), :] = hi_ref[...]
    dwide[...] = jnp.zeros(dwide.shape, dwide.dtype)

    def block(b, carry):
        a0 = start_of(b)
        allow = window_allow(tq_ref, tk_ref, a0, a0)
        for h in range(HEADS):
            probs, q_h, k_h = probs_of(q_ref, wide, allow, a0, a0, h)
            v_h = wide[pl.ds(a0, QB + 2 * HALF), pl.ds(width + h * HEAD, HEAD)]
            do_h = do_ref[pl.ds(a0, QB), pl.ds(h * HEAD, HEAD)]
            grad_probs = nt(do_h, v_h)
            inner = jnp.sum(probs * grad_probs, axis=-1, keepdims=True)
            grad_scores = (probs * (grad_probs - inner)).astype(jnp.bfloat16)
            dq_ref[pl.ds(a0, QB), pl.ds(h * HEAD, HEAD)] = (
                jnp.dot(grad_scores, k_h, preferred_element_type=jnp.float32) * 0.125
            )
            rows = pl.ds(a0, QB + 2 * HALF)
            dwide[rows, pl.ds(h * HEAD, HEAD)] += tn(grad_scores, q_h) * 0.125
            dwide[rows, pl.ds(width + h * HEAD, HEAD)] += tn(probs.astype(jnp.bfloat16), do_h)
        return carry

    block(0, 0)
    block(blocks - 1, 0)
    send_lo[...] = dwide[pl.ds(0, HALF), :].astype(send_lo.dtype)
    send_hi[...] = dwide[pl.ds(count + HALF, HALF), :].astype(send_hi.dtype)
    to_before = pltpu.make_async_remote_copy(
        src_ref=send_lo, dst_ref=recv_hi,
        send_sem=send_sem.at[0], recv_sem=recv_sem.at[0],
        device_id=before, device_id_type=MESH)
    to_after = pltpu.make_async_remote_copy(
        src_ref=send_hi, dst_ref=recv_lo,
        send_sem=send_sem.at[1], recv_sem=recv_sem.at[1],
        device_id=after, device_id_type=MESH)
    to_before.start()
    to_after.start()
    lax.fori_loop(1, blocks - 1, block, 0)
    dkv_ref[...] = dwide[pl.ds(HALF, count), :]
    to_before.wait_recv()
    to_after.wait_recv()
    dkv_ref[pl.ds(0, HALF), :] += recv_lo[...].astype(jnp.float32)
    dkv_ref[pl.ds(count - HALF, HALF), :] += recv_hi[...].astype(jnp.float32)
    to_before.wait_send()
    to_after.wait_send()


VMEM_LIMIT = 48 * 1024 * 1024


def attn_fwd(query, kv, tag_q, tag_k):
    count, width = query.shape
    vm = pl.BlockSpec(memory_space=pltpu.VMEM)
    halo = jax.ShapeDtypeStruct((HALF, kv.shape[1]), kv.dtype)
    return pl.pallas_call(
        attn_fwd_kernel,
        out_shape=(jax.ShapeDtypeStruct((count, width), jnp.bfloat16), halo, halo),
        in_specs=[vm] * 4,
        out_specs=(vm, vm, vm),
        scratch_shapes=[
            pltpu.VMEM((count + 2 * HALF, kv.shape[1]), kv.dtype),
            pltpu.SemaphoreType.DMA((2,)),
            pltpu.SemaphoreType.DMA((2,)),
        ],
        compiler_params=pltpu.CompilerParams(
            collective_id=2, has_side_effects=True, vmem_limit_bytes=VMEM_LIMIT
        ),
    )(query, kv, tag_q.reshape(count, 1), tag_k.reshape(1, -1))


def attn_bwd(query, kv, lo, hi, tag_q, tag_k, grad_out):
    count, width = query.shape
    vm = pl.BlockSpec(memory_space=pltpu.VMEM)
    return pl.pallas_call(
        attn_bwd_kernel,
        out_shape=(
            jax.ShapeDtypeStruct((count, width), jnp.float32),
            jax.ShapeDtypeStruct(kv.shape, jnp.float32),
        ),
        in_specs=[vm] * 7,
        out_specs=(vm, vm),
        scratch_shapes=[
            pltpu.VMEM((count + 2 * HALF, kv.shape[1]), kv.dtype),
            pltpu.VMEM((count + 2 * HALF, kv.shape[1]), jnp.float32),
            pltpu.VMEM((HALF, kv.shape[1]), jnp.bfloat16),
            pltpu.VMEM((HALF, kv.shape[1]), jnp.bfloat16),
            pltpu.VMEM((HALF, kv.shape[1]), jnp.bfloat16),
            pltpu.VMEM((HALF, kv.shape[1]), jnp.bfloat16),
            pltpu.SemaphoreType.DMA((2,)),
            pltpu.SemaphoreType.DMA((2,)),
        ],
        compiler_params=pltpu.CompilerParams(
            collective_id=3, has_side_effects=True, vmem_limit_bytes=VMEM_LIMIT
        ),
    )(query, kv, lo, hi, tag_q.reshape(count, 1), tag_k.reshape(1, -1), grad_out)


def gain_rows(gain, width, rows=8):
    line = jnp.pad(gain, (0, width - gain.shape[0]))
    return jnp.concatenate([line[None], jnp.zeros((rows - 1, width), gain.dtype)], 0)


def gather_rows(payload, n_dp, n_seq):
    every = lax.all_gather(payload, ("dp", "seq"), axis=0, tiled=True)
    return every.reshape(n_dp, n_seq, payload.shape[0], payload.shape[1])


def gain_blocks(grad_gain, n_dp, n_seq, width, height=8):
    part = jnp.pad(grad_gain.reshape(n_seq, -1), ((0, 0), (0, width - grad_gain.shape[0] // n_seq)))
    rows = jnp.concatenate([part[:, None], jnp.zeros((n_seq, height - 1, width), part.dtype)], 1)
    return jnp.broadcast_to(rows[None], (n_dp, n_seq, height, width))


def front(value, n_dp):
    return value.reshape(value.shape[0], n_dp, -1)


def apply_t(left, weight_t, n_dp):
    return jnp.einsum("tdr,dnr->tn", front(left, n_dp), weight_t, preferred_element_type=jnp.float32)


def apply_back(grad, weight_t):
    out = jnp.einsum("tn,dnr->tdr", grad, weight_t, preferred_element_type=jnp.float32)
    return out.reshape(out.shape[0], -1)


def grad_t(grad, left, n_dp):
    width = left.shape[1] // n_dp
    return [
        lax.dot_general(
            grad,
            left[:, d * width : (d + 1) * width],
            (((0,), (0,)), ((), ())),
            preferred_element_type=jnp.float32,
        )
        for d in range(n_dp)
    ]


def on_device(order, tokens, doc_start, real, w_qkv, w_out, w_in, w_down, gain_attn, gain_mlp, cotangent):
    count = tokens.shape[0]
    n_dp, n_seq = lax.axis_size("dp"), lax.axis_size("seq")
    rows, qkv_cols = w_qkv.shape
    out_cols, in_cols = w_out.shape[1], w_in.shape[1]
    down_rows, down_cols = w_down.shape
    down_lines = down_rows * down_cols // rows
    first = gather_rows(jnp.concatenate([w_qkv.T, gain_rows(gain_attn, rows)], 0), n_dp, n_seq)
    second = gather_rows(
        jnp.concatenate(
            [w_out.T, w_in.T, w_down.T.reshape(down_lines, rows), gain_rows(gain_mlp, rows)], 0
        ),
        n_dp,
        n_seq,
    )
    full_qkv = first[:, :, :qkv_cols].reshape(n_dp, n_seq * qkv_cols, rows)
    gain_one = first[0, :, qkv_cols, : gain_attn.shape[0]].reshape(-1).astype(jnp.float32)
    stream = tokens.astype(jnp.float32)
    normed_a, factor_a = layer_norm(stream)
    h_attn = (normed_a * gain_one).astype(jnp.bfloat16)
    qkv = apply_t(h_attn, full_qkv, n_dp)
    offset_base = lax.axis_index(("dp", "seq")) * count
    place = (offset_base + jnp.arange(count, dtype=jnp.int32) - doc_start).astype(jnp.float32)
    cosine, sine = rotary_tables(place)
    query = (qkv[:, :D] * cosine + rotate(qkv[:, :D]) * sine).astype(jnp.bfloat16)
    key_rows = (qkv[:, D : 2 * D] * cosine + rotate(qkv[:, D : 2 * D]) * sine).astype(jnp.bfloat16)
    value_rows = qkv[:, 2 * D :].astype(jnp.bfloat16)
    tag_query = doc_start + 1
    tag_key = jnp.where(real == 1, tag_query, 0)
    key_value = jnp.concatenate([key_rows, value_rows], 1)
    wide_tag = padded(tag_key, ((("dp", "seq"), 0),), HALF)
    attn_out, halo_lo, halo_hi = attn_fwd(query, key_value, tag_query, wide_tag)
    attn_out, second = lax.optimization_barrier((attn_out, second))
    at = 0
    full_out = second[:, :, at : at + out_cols].reshape(n_dp, n_seq * out_cols, rows)
    at += out_cols
    full_in = second[:, :, at : at + in_cols].reshape(n_dp, n_seq * in_cols, rows)
    at += in_cols
    full_down = (
        second[:, :, at : at + down_lines]
        .reshape(n_dp, n_seq, down_cols, down_rows)
        .reshape(n_dp, n_seq * down_cols, down_rows)
    )
    at += down_lines
    gain_two = second[0, :, at, : gain_mlp.shape[0]].reshape(-1).astype(jnp.float32)
    mid = stream + apply_t(attn_out, full_out, n_dp)
    normed_m, factor_m = layer_norm(mid)
    h_mlp = (normed_m * gain_two).astype(jnp.bfloat16)
    gate_up = apply_t(h_mlp, full_in, n_dp)
    hidden_out, glu_pull = jax.vjp(glu_piece, gate_up)
    hidden = hidden_out.astype(jnp.bfloat16)
    result = mid + apply_t(hidden, full_down, n_dp)
    output = result.astype(jnp.bfloat16)
    grad_down = grad_t(cotangent, hidden, n_dp)
    grad_hidden = apply_back(cotangent, full_down)
    grad_gate_up = glu_pull(grad_hidden)[0].astype(jnp.bfloat16)
    grad_inw = grad_t(grad_gate_up, h_mlp, n_dp)
    grad_hmlp = apply_back(grad_gate_up, full_in)
    grad_gain_two = jnp.sum(grad_hmlp * normed_m, axis=0)
    grad_mid = cotangent.astype(jnp.float32) + norm_back(grad_hmlp * gain_two, normed_m, factor_m)
    grad_branch = grad_mid.astype(jnp.bfloat16)
    grad_outw = grad_t(grad_branch, attn_out, n_dp)
    grad_attn = apply_back(grad_branch, full_out).astype(jnp.bfloat16)
    grad_query, grad_kv = attn_bwd(query, key_value, halo_lo, halo_hi, tag_query, wide_tag, grad_attn)
    grad_keys = grad_kv[:, :D]
    grad_qkv = jnp.concatenate(
        [
            grad_query * cosine - rotate(grad_query) * sine,
            grad_keys * cosine - rotate(grad_keys) * sine,
            grad_kv[:, D:],
        ],
        1,
    ).astype(jnp.bfloat16)
    grad_qkvw = grad_t(grad_qkv, h_attn, n_dp)
    grad_hattn = apply_back(grad_qkv, full_qkv)
    grad_gain_one = jnp.sum(grad_hattn * normed_a, axis=0)
    grad_tokens = grad_mid + norm_back(grad_hattn * gain_one, normed_a, factor_a)
    height = out_cols + in_cols + down_lines + qkv_cols + 8
    tail = 8 + (-height) % (RING_WAYS * 16)
    gain_both = jnp.concatenate(
        [
            gain_blocks(grad_gain_two, 1, n_seq, rows, 1)[0],
            gain_blocks(grad_gain_one, 1, n_seq, rows, tail - 1)[0],
        ],
        1,
    )
    blocks = jnp.stack(
        [
            jnp.concatenate(
                [
                    *lax.optimization_barrier(
                        (
                            grad_outw[d].reshape(n_seq, out_cols, rows),
                            grad_inw[d].reshape(n_seq, in_cols, rows),
                            grad_down[d]
                            .reshape(n_seq, down_cols, down_rows)
                            .reshape(n_seq, down_lines, rows),
                            grad_qkvw[d].reshape(n_seq, qkv_cols, rows),
                            gain_both,
                        )
                    ),
                ],
                1,
            )
            for d in range(n_dp)
        ]
    )
    depth = blocks.shape[2]
    half = lax.psum_scatter(
        blocks.reshape(n_dp, n_seq * depth, rows), "dp", scatter_dimension=0, tiled=True
    )
    late = ring_reduce(half.reshape(n_seq, depth, rows), order, RING_WAYS)
    at = 0
    late_out = late[at : at + out_cols].T
    at += out_cols
    late_in = late[at : at + in_cols].T
    at += in_cols
    late_down = late[at : at + down_lines].reshape(down_cols, down_rows).T
    at += down_lines
    late_qkv = late[at : at + qkv_cols].T
    at += qkv_cols
    late_gain_two = late[at, : gain_mlp.shape[0]]
    late_gain_one = late[at + 1, : gain_attn.shape[0]]
    return (
        output,
        grad_tokens,
        late_qkv,
        late_out,
        late_in,
        late_down,
        late_gain_one,
        late_gain_two,
    )


def solution(mesh):
    placed = (
        P(("dp", "seq"), None),
        P(("dp", "seq")),
        P(("dp", "seq")),
        P("dp", "seq"),
        P("dp", "seq"),
        P("dp", "seq"),
        P("dp", "seq"),
        P("seq"),
        P("seq"),
        P(("dp", "seq"), None),
    )
    return jax.shard_map(
        functools.partial(on_device, ring_order(mesh)),
        mesh=mesh,
        in_specs=placed,
        out_specs=(
            P(("dp", "seq"), None),
            P(("dp", "seq"), None),
            P("dp", "seq"),
            P("dp", "seq"),
            P("dp", "seq"),
            P("dp", "seq"),
            P("seq"),
            P("seq"),
        ),
        check_vma=False,
    )
```

```python
import functools
import math

import jax
import jax.numpy as jnp
from jax import lax
from jax.experimental import pallas as pl
from jax.experimental.pallas import tpu as pltpu
from jax.sharding import PartitionSpec as P

D = 768
HEADS = 12
HEAD = 64
FF = 1152
HALF = 64


def padded(value, sides, width):
    for axis, dim in sides:
        size, length = (lax.axis_size(axis), value.shape[dim])
        up = [(i, (i + 1) % size) for i in range(size - 1)]
        down = [(j, i) for i, j in up]
        last = lax.slice_in_dim(value, length - width, length, axis=dim)
        initial = lax.slice_in_dim(value, 0, width, axis=dim)
        before = lax.ppermute(last, axis, up)
        after = lax.ppermute(initial, axis, down)
        value = jnp.concatenate([before, value, after], axis=dim)
    return value


def shifted(value, axis, by):
    length = lax.axis_size(axis)
    pairs = [(i, i + by) for i in range(length) if 0 <= i + by < length]
    return lax.ppermute(value, axis, pairs)


def layer_norm(value):
    centre = value - jnp.mean(value, axis=-1, keepdims=True)
    factor = lax.rsqrt(jnp.mean(centre * centre, axis=-1, keepdims=True) + 1e-05)
    return (centre * factor, factor)


def norm_back(grad, normed, factor):
    return factor * (
        grad
        - jnp.mean(grad, axis=-1, keepdims=True)
        - normed * jnp.mean(grad * normed, axis=-1, keepdims=True)
    )


def rotary_tables(place):
    freq = jnp.exp(jnp.arange(HEAD // 2, dtype=jnp.float32) * (-2.0 * math.log(10000.0) / HEAD))
    angle = place[:, None] * freq[None, :]
    cosine = jnp.tile(jnp.concatenate([jnp.cos(angle), jnp.cos(angle)], 1), (1, HEADS))
    sine = jnp.tile(jnp.concatenate([jnp.sin(angle), jnp.sin(angle)], 1), (1, HEADS))
    return (cosine, sine)


def rotate(value):
    count = value.shape[0]
    shaped = value.reshape(count, HEADS, HEAD)
    first = shaped[..., : HEAD // 2]
    second = shaped[..., HEAD // 2 :]
    return jnp.concatenate([-second, first], -1).reshape(count, HEADS * HEAD)


def left_dot(left, right):
    return lax.dot_general(
        left, right, (((0,), (0,)), ((), ())), preferred_element_type=jnp.float32
    )


def right_dot(left, right):
    return lax.dot_general(
        left, right, (((1,), (1,)), ((), ())), preferred_element_type=jnp.float32
    )


def glu_piece(gate_up):
    return jax.nn.gelu(gate_up[:, :FF], approximate=False) * gate_up[:, FF:]


MESH = pl.DeviceIdType.MESH


def ring_order(mesh):
    n = mesh.shape["seq"]
    try:
        coords = [tuple(mesh.devices[0, s].coords) for s in range(n)]
    except Exception:
        return list(range(n))
    near = [
        [t for t in range(n) if sum(abs(a - b) for a, b in zip(coords[s], coords[t])) == 1]
        for s in range(n)
    ]
    path, seen = [0], {0}

    def grow(budget=[200000]):
        budget[0] -= 1
        if budget[0] < 0:
            return False
        if len(path) == n:
            return 0 in near[path[-1]]
        options = sorted(
            (t for t in near[path[-1]] if t not in seen),
            key=lambda t: sum(1 for u in near[t] if u not in seen),
        )
        for t in options:
            path.append(t)
            seen.add(t)
            if grow():
                return True
            path.pop()
            seen.discard(t)
        return False

    return list(path) if n > 2 and grow() else list(range(n))


def lookup(index, table):
    n = len(table)
    square = n * n
    total = jnp.int32(0)
    for k, value in enumerate(table):
        if value:
            gap = index - k
            differs = lax.div(gap * gap + (square - 1), jnp.int32(square))
            total = total + value * (1 - differs)
    return total


def ring_kernel(order, per_way, h_ref, out_ref, recv, send, ssem, rsem, free):
    n = len(order)
    where = [0] * n
    for p, s in enumerate(order):
        where[s] = p
    d = lax.axis_index("dp")
    me = lax.axis_index("seq")
    pos = lookup(me, where)
    nxt = lookup(lax.rem(pos + 1, n), order)
    prv = lookup(lax.rem(pos + n - 1, n), order)
    piece = out_ref.shape[0] // per_way
    ahead = (n - 1) // 2
    behind = n - 1 - ahead

    barrier = pltpu.get_barrier_semaphore()
    pl.semaphore_signal(barrier, 1, device_id=(d, nxt), device_id_type=MESH)
    pl.semaphore_signal(barrier, 1, device_id=(d, prv), device_id_type=MESH)
    pl.semaphore_wait(barrier, 2)

    lanes = []
    for forward in (True, False):
        for chunk in range(per_way):
            li = len(lanes)
            lanes.append((recv.at[li], send.at[li], ssem.at[li], rsem.at[li], free.at[li],
                          nxt if forward else prv, prv if forward else nxt,
                          slice(chunk * piece, (chunk + 1) * piece),
                          ahead if forward else behind, forward))
    copies = {}
    for step in range(max(ahead, behind)):
        slot = step % 2
        for li, (recv, send, ssem, rsem, free, to, frm, rows, sends, forward) in enumerate(lanes):
            if step >= sends:
                continue
            if forward:
                target = pos + sends - step
            else:
                target = pos + n - sends + step
            q = lookup(lax.rem(target, n), order)
            own = h_ref[q, rows, :]
            if step == 0:
                part = own
            else:
                copies[(li, step - 1)].wait_recv()
                part = recv[1 - slot].astype(jnp.float32) + own
                if step <= sends - 2:
                    pl.semaphore_signal(free, 1, device_id=(d, frm), device_id_type=MESH)
            if step >= 2:
                copies[(li, step - 2)].wait_send()
                pl.semaphore_wait(free, 1)
            send[slot] = part.astype(send.dtype)
            c = pltpu.make_async_remote_copy(
                src_ref=send.at[slot], dst_ref=recv.at[slot],
                send_sem=ssem.at[slot], recv_sem=rsem.at[slot],
                device_id=(d, to), device_id_type=MESH)
            c.start()
            copies[(li, step)] = c
    for chunk in range(per_way):
        rows = lanes[chunk][7]
        total = h_ref[me, rows, :]
        for li in (chunk, per_way + chunk):
            recv, sends = lanes[li][0], lanes[li][8]
            copies[(li, sends - 1)].wait_recv()
            total = total + recv[(sends - 1) % 2].astype(jnp.float32)
        out_ref[rows, :] = total
    for li, lane in enumerate(lanes):
        sends = lane[8]
        if sends >= 2:
            copies[(li, sends - 2)].wait_send()
        copies[(li, sends - 1)].wait_send()


RING_WAYS = 2


def ring_reduce(h, order, per_way, link_dtype=jnp.bfloat16):
    n, rows, width = h.shape
    lanes = 2 * per_way
    piece = rows // per_way
    return pl.pallas_call(
        functools.partial(ring_kernel, tuple(order), per_way),
        out_shape=jax.ShapeDtypeStruct((rows, width), jnp.float32),
        in_specs=[pl.BlockSpec(memory_space=pltpu.VMEM)],
        out_specs=pl.BlockSpec(memory_space=pltpu.VMEM),
        scratch_shapes=[
            pltpu.VMEM((lanes, 2, piece, width), link_dtype),
            pltpu.VMEM((lanes, 2, piece, width), link_dtype),
            pltpu.SemaphoreType.DMA((lanes, 2)),
            pltpu.SemaphoreType.DMA((lanes, 2)),
            pltpu.SemaphoreType.REGULAR((lanes,)),
        ],
        compiler_params=pltpu.CompilerParams(collective_id=1, has_side_effects=True,
                                             vmem_limit_bytes=48 * 1024 * 1024),
    )(h)


QB = 128


def window_allow(tq_ref, tk_ref, a0, w0):
    rows = lax.broadcasted_iota(jnp.int32, (QB, QB + 2 * HALF), 0)
    cols = lax.broadcasted_iota(jnp.int32, (QB, QB + 2 * HALF), 1)
    offset = cols - rows - HALF
    near = jnp.abs(offset) <= HALF
    same = tk_ref[:, pl.ds(w0, QB + 2 * HALF)] == tq_ref[pl.ds(a0, QB), :]
    return near & (same | (offset == 0))


def nt(a, b):
    return lax.dot_general(a, b, (((1,), (1,)), ((), ())), preferred_element_type=jnp.float32)


def tn(a, b):
    return lax.dot_general(a, b, (((0,), (0,)), ((), ())), preferred_element_type=jnp.float32)


def probs_of(q_ref, kv_ref, allow, a0, w0, h):
    q_h = q_ref[pl.ds(a0, QB), pl.ds(h * HEAD, HEAD)]
    k_h = kv_ref[pl.ds(w0, QB + 2 * HALF), pl.ds(h * HEAD, HEAD)]
    scores = jnp.where(allow, nt(q_h, k_h) * 0.125, -1e30)
    largest = jnp.max(scores, axis=-1, keepdims=True)
    raised = jnp.exp(scores - largest)
    return raised / jnp.sum(raised, axis=-1, keepdims=True), q_h, k_h


def neighbours():
    n_seq = lax.axis_size("seq")
    total = lax.axis_size("dp") * n_seq
    me = lax.axis_index("dp") * n_seq + lax.axis_index("seq")
    before = lax.rem(me + total - 1, total)
    after = lax.rem(me + 1, total)
    return (
        (lax.div(before, n_seq), lax.rem(before, n_seq)),
        (lax.div(after, n_seq), lax.rem(after, n_seq)),
    )


def greet(before, after):
    barrier = pltpu.get_barrier_semaphore()
    pl.semaphore_signal(barrier, 1, device_id=before, device_id_type=MESH)
    pl.semaphore_signal(barrier, 1, device_id=after, device_id_type=MESH)
    pl.semaphore_wait(barrier, 2)


def start_of(b):
    return b * QB if isinstance(b, int) else pl.multiple_of(b * QB, QB)


def attn_fwd_kernel(q_ref, kv_ref, tq_ref, tk_ref, o_ref, lo_ref, hi_ref, wide, send_sem, recv_sem):
    width = q_ref.shape[1]
    count = q_ref.shape[0]
    blocks = count // QB
    before, after = neighbours()
    greet(before, after)
    to_before = pltpu.make_async_remote_copy(
        src_ref=kv_ref.at[pl.ds(0, HALF)], dst_ref=hi_ref,
        send_sem=send_sem.at[0], recv_sem=recv_sem.at[0],
        device_id=before, device_id_type=MESH)
    to_after = pltpu.make_async_remote_copy(
        src_ref=kv_ref.at[pl.ds(count - HALF, HALF)], dst_ref=lo_ref,
        send_sem=send_sem.at[1], recv_sem=recv_sem.at[1],
        device_id=after, device_id_type=MESH)
    to_before.start()
    to_after.start()
    wide[pl.ds(HALF, count), :] = kv_ref[...]

    def block(b, carry):
        a0 = start_of(b)
        allow = window_allow(tq_ref, tk_ref, a0, a0)
        for h in range(HEADS):
            probs, _, _ = probs_of(q_ref, wide, allow, a0, a0, h)
            v_h = wide[pl.ds(a0, QB + 2 * HALF), pl.ds(width + h * HEAD, HEAD)]
            mixed = jnp.dot(probs.astype(jnp.bfloat16), v_h, preferred_element_type=jnp.float32)
            o_ref[pl.ds(a0, QB), pl.ds(h * HEAD, HEAD)] = mixed.astype(o_ref.dtype)
        return carry

    lax.fori_loop(1, blocks - 1, block, 0)
    to_before.wait_recv()
    to_after.wait_recv()
    wide[pl.ds(0, HALF), :] = lo_ref[...]
    wide[pl.ds(count + HALF, HALF), :] = hi_ref[...]
    block(0, 0)
    block(blocks - 1, 0)
    to_before.wait_send()
    to_after.wait_send()


def attn_bwd_kernel(q_ref, kv_ref, lo_ref, hi_ref, tq_ref, tk_ref, do_ref, dq_ref, dkv_ref,
                    wide, dwide, send_lo, send_hi, recv_lo, recv_hi, send_sem, recv_sem):
    width = q_ref.shape[1]
    count = q_ref.shape[0]
    blocks = count // QB
    before, after = neighbours()
    greet(before, after)
    wide[pl.ds(0, HALF), :] = lo_ref[...]
    wide[pl.ds(HALF, count), :] = kv_ref[...]
    wide[pl.ds(count + HALF, HALF), :] = hi_ref[...]
    dwide[...] = jnp.zeros(dwide.shape, dwide.dtype)

    def block(b, carry):
        a0 = start_of(b)
        allow = window_allow(tq_ref, tk_ref, a0, a0)
        for h in range(HEADS):
            probs, q_h, k_h = probs_of(q_ref, wide, allow, a0, a0, h)
            v_h = wide[pl.ds(a0, QB + 2 * HALF), pl.ds(width + h * HEAD, HEAD)]
            do_h = do_ref[pl.ds(a0, QB), pl.ds(h * HEAD, HEAD)]
            grad_probs = nt(do_h, v_h)
            inner = jnp.sum(probs * grad_probs, axis=-1, keepdims=True)
            grad_scores = (probs * (grad_probs - inner)).astype(jnp.bfloat16)
            dq_ref[pl.ds(a0, QB), pl.ds(h * HEAD, HEAD)] = (
                jnp.dot(grad_scores, k_h, preferred_element_type=jnp.float32) * 0.125
            )
            rows = pl.ds(a0, QB + 2 * HALF)
            dwide[rows, pl.ds(h * HEAD, HEAD)] += tn(grad_scores, q_h) * 0.125
            dwide[rows, pl.ds(width + h * HEAD, HEAD)] += tn(probs.astype(jnp.bfloat16), do_h)
        return carry

    block(0, 0)
    block(blocks - 1, 0)
    send_lo[...] = dwide[pl.ds(0, HALF), :].astype(send_lo.dtype)
    send_hi[...] = dwide[pl.ds(count + HALF, HALF), :].astype(send_hi.dtype)
    to_before = pltpu.make_async_remote_copy(
        src_ref=send_lo, dst_ref=recv_hi,
        send_sem=send_sem.at[0], recv_sem=recv_sem.at[0],
        device_id=before, device_id_type=MESH)
    to_after = pltpu.make_async_remote_copy(
        src_ref=send_hi, dst_ref=recv_lo,
        send_sem=send_sem.at[1], recv_sem=recv_sem.at[1],
        device_id=after, device_id_type=MESH)
    to_before.start()
    to_after.start()
    lax.fori_loop(1, blocks - 1, block, 0)
    dkv_ref[...] = dwide[pl.ds(HALF, count), :]
    to_before.wait_recv()
    to_after.wait_recv()
    dkv_ref[pl.ds(0, HALF), :] += recv_lo[...].astype(jnp.float32)
    dkv_ref[pl.ds(count - HALF, HALF), :] += recv_hi[...].astype(jnp.float32)
    to_before.wait_send()
    to_after.wait_send()


VMEM_LIMIT = 48 * 1024 * 1024


def attn_fwd(query, kv, tag_q, tag_k):
    count, width = query.shape
    vm = pl.BlockSpec(memory_space=pltpu.VMEM)
    halo = jax.ShapeDtypeStruct((HALF, kv.shape[1]), kv.dtype)
    return pl.pallas_call(
        attn_fwd_kernel,
        out_shape=(jax.ShapeDtypeStruct((count, width), jnp.bfloat16), halo, halo),
        in_specs=[vm] * 4,
        out_specs=(vm, vm, vm),
        scratch_shapes=[
            pltpu.VMEM((count + 2 * HALF, kv.shape[1]), kv.dtype),
            pltpu.SemaphoreType.DMA((2,)),
            pltpu.SemaphoreType.DMA((2,)),
        ],
        compiler_params=pltpu.CompilerParams(
            collective_id=2, has_side_effects=True, vmem_limit_bytes=VMEM_LIMIT
        ),
    )(query, kv, tag_q.reshape(count, 1), tag_k.reshape(1, -1))


def attn_bwd(query, kv, lo, hi, tag_q, tag_k, grad_out):
    count, width = query.shape
    vm = pl.BlockSpec(memory_space=pltpu.VMEM)
    return pl.pallas_call(
        attn_bwd_kernel,
        out_shape=(
            jax.ShapeDtypeStruct((count, width), jnp.float32),
            jax.ShapeDtypeStruct(kv.shape, jnp.float32),
        ),
        in_specs=[vm] * 7,
        out_specs=(vm, vm),
        scratch_shapes=[
            pltpu.VMEM((count + 2 * HALF, kv.shape[1]), kv.dtype),
            pltpu.VMEM((count + 2 * HALF, kv.shape[1]), jnp.float32),
            pltpu.VMEM((HALF, kv.shape[1]), jnp.bfloat16),
            pltpu.VMEM((HALF, kv.shape[1]), jnp.bfloat16),
            pltpu.VMEM((HALF, kv.shape[1]), jnp.bfloat16),
            pltpu.VMEM((HALF, kv.shape[1]), jnp.bfloat16),
            pltpu.SemaphoreType.DMA((2,)),
            pltpu.SemaphoreType.DMA((2,)),
        ],
        compiler_params=pltpu.CompilerParams(
            collective_id=3, has_side_effects=True, vmem_limit_bytes=VMEM_LIMIT
        ),
    )(query, kv, lo, hi, tag_q.reshape(count, 1), tag_k.reshape(1, -1), grad_out)


ROPE_ROWS = 256


def head_rotate(x):
    width = x.shape[-1]
    lane = lax.broadcasted_iota(jnp.int32, x.shape, x.ndim - 1)
    ahead = pltpu.roll(x, width - HEAD // 2, x.ndim - 1)
    behind = pltpu.roll(x, HEAD // 2, x.ndim - 1)
    return jnp.where(lane % HEAD < HEAD // 2, -ahead, behind)


def rope_fwd_kernel(qkv_ref, cos_ref, sin_ref, q_ref, kv_ref):
    width = q_ref.shape[1]
    c = cos_ref[...]
    s = sin_ref[...]
    q = qkv_ref[:, pl.ds(0, width)]
    k = qkv_ref[:, pl.ds(width, width)]
    q_ref[...] = (q * c + head_rotate(q) * s).astype(q_ref.dtype)
    kv_ref[:, pl.ds(0, width)] = (k * c + head_rotate(k) * s).astype(kv_ref.dtype)
    kv_ref[:, pl.ds(width, width)] = qkv_ref[:, pl.ds(2 * width, width)].astype(kv_ref.dtype)


def rope_bwd_kernel(dq_ref, dkv_ref, cos_ref, sin_ref, out_ref):
    width = dq_ref.shape[1]
    c = cos_ref[...]
    s = sin_ref[...]
    dq = dq_ref[...]
    dk = dkv_ref[:, pl.ds(0, width)]
    out_ref[:, pl.ds(0, width)] = (dq * c - head_rotate(dq) * s).astype(out_ref.dtype)
    out_ref[:, pl.ds(width, width)] = (dk * c - head_rotate(dk) * s).astype(out_ref.dtype)
    out_ref[:, pl.ds(2 * width, width)] = dkv_ref[:, pl.ds(width, width)].astype(out_ref.dtype)


def rows_spec(cols):
    return pl.BlockSpec((ROPE_ROWS, cols), lambda i: (i, 0))


def rope_fwd(qkv, cosine, sine):
    count, width = cosine.shape
    return pl.pallas_call(
        rope_fwd_kernel,
        grid=(count // ROPE_ROWS,),
        out_shape=(
            jax.ShapeDtypeStruct((count, width), jnp.bfloat16),
            jax.ShapeDtypeStruct((count, 2 * width), jnp.bfloat16),
        ),
        in_specs=[rows_spec(3 * width), rows_spec(width), rows_spec(width)],
        out_specs=(rows_spec(width), rows_spec(2 * width)),
    )(qkv, cosine, sine)


def rope_bwd(dq, dkv, cosine, sine):
    count, width = cosine.shape
    return pl.pallas_call(
        rope_bwd_kernel,
        grid=(count // ROPE_ROWS,),
        out_shape=jax.ShapeDtypeStruct((count, 3 * width), jnp.bfloat16),
        in_specs=[rows_spec(width), rows_spec(2 * width), rows_spec(width), rows_spec(width)],
        out_specs=rows_spec(3 * width),
    )(dq, dkv, cosine, sine)


def gain_rows(gain, width, rows=8):
    line = jnp.pad(gain, (0, width - gain.shape[0]))
    return jnp.concatenate([line[None], jnp.zeros((rows - 1, width), gain.dtype)], 0)


def gather_rows(payload, n_dp, n_seq):
    every = lax.all_gather(payload, ("dp", "seq"), axis=0, tiled=True)
    return every.reshape(n_dp, n_seq, payload.shape[0], payload.shape[1])


def gain_blocks(grad_gain, n_dp, n_seq, width, height=8):
    part = jnp.pad(grad_gain.reshape(n_seq, -1), ((0, 0), (0, width - grad_gain.shape[0] // n_seq)))
    rows = jnp.concatenate([part[:, None], jnp.zeros((n_seq, height - 1, width), part.dtype)], 1)
    return jnp.broadcast_to(rows[None], (n_dp, n_seq, height, width))


def front(value, n_dp):
    return value.reshape(value.shape[0], n_dp, -1)


def apply_t(left, weight_t, n_dp):
    return jnp.einsum("tdr,dnr->tn", front(left, n_dp), weight_t, preferred_element_type=jnp.float32)


def apply_back(grad, weight_t):
    out = jnp.einsum("tn,dnr->tdr", grad, weight_t, preferred_element_type=jnp.float32)
    return out.reshape(out.shape[0], -1)


def grad_t(grad, left, n_dp):
    width = left.shape[1] // n_dp
    return [
        lax.dot_general(
            grad,
            left[:, d * width : (d + 1) * width],
            (((0,), (0,)), ((), ())),
            preferred_element_type=jnp.float32,
        )
        for d in range(n_dp)
    ]


def on_device(order, tokens, doc_start, real, w_qkv, w_out, w_in, w_down, gain_attn, gain_mlp, cotangent):
    count = tokens.shape[0]
    n_dp, n_seq = lax.axis_size("dp"), lax.axis_size("seq")
    rows, qkv_cols = w_qkv.shape
    out_cols, in_cols = w_out.shape[1], w_in.shape[1]
    down_rows, down_cols = w_down.shape
    down_lines = down_rows * down_cols // rows
    first = gather_rows(jnp.concatenate([w_qkv.T, gain_rows(gain_attn, rows)], 0), n_dp, n_seq)
    second = gather_rows(
        jnp.concatenate(
            [w_out.T, w_in.T, w_down.T.reshape(down_lines, rows), gain_rows(gain_mlp, rows)], 0
        ),
        n_dp,
        n_seq,
    )
    full_qkv = first[:, :, :qkv_cols].reshape(n_dp, n_seq * qkv_cols, rows)
    gain_one = first[0, :, qkv_cols, : gain_attn.shape[0]].reshape(-1).astype(jnp.float32)
    stream = tokens.astype(jnp.float32)
    normed_a, factor_a = layer_norm(stream)
    h_attn = (normed_a * gain_one).astype(jnp.bfloat16)
    qkv = apply_t(h_attn, full_qkv, n_dp)
    offset_base = lax.axis_index(("dp", "seq")) * count
    place = (offset_base + jnp.arange(count, dtype=jnp.int32) - doc_start).astype(jnp.float32)
    cosine, sine = rotary_tables(place)
    query, key_value = rope_fwd(qkv, cosine, sine)
    tag_query = doc_start + 1
    tag_key = jnp.where(real == 1, tag_query, 0)
    wide_tag = padded(tag_key, ((("dp", "seq"), 0),), HALF)
    attn_out, halo_lo, halo_hi = attn_fwd(query, key_value, tag_query, wide_tag)
    attn_out, second = lax.optimization_barrier((attn_out, second))
    at = 0
    full_out = second[:, :, at : at + out_cols].reshape(n_dp, n_seq * out_cols, rows)
    at += out_cols
    full_in = second[:, :, at : at + in_cols].reshape(n_dp, n_seq * in_cols, rows)
    at += in_cols
    full_down = (
        second[:, :, at : at + down_lines]
        .reshape(n_dp, n_seq, down_cols, down_rows)
        .reshape(n_dp, n_seq * down_cols, down_rows)
    )
    at += down_lines
    gain_two = second[0, :, at, : gain_mlp.shape[0]].reshape(-1).astype(jnp.float32)
    mid = stream + apply_t(attn_out, full_out, n_dp)
    normed_m, factor_m = layer_norm(mid)
    h_mlp = (normed_m * gain_two).astype(jnp.bfloat16)
    gate_up = apply_t(h_mlp, full_in, n_dp)
    hidden_out, glu_pull = jax.vjp(glu_piece, gate_up)
    hidden = hidden_out.astype(jnp.bfloat16)
    result = mid + apply_t(hidden, full_down, n_dp)
    output = result.astype(jnp.bfloat16)
    grad_down = grad_t(cotangent, hidden, n_dp)
    grad_hidden = apply_back(cotangent, full_down)
    grad_gate_up = glu_pull(grad_hidden)[0].astype(jnp.bfloat16)
    grad_inw = grad_t(grad_gate_up, h_mlp, n_dp)
    grad_hmlp = apply_back(grad_gate_up, full_in)
    grad_gain_two = jnp.sum(grad_hmlp * normed_m, axis=0)
    grad_mid = cotangent.astype(jnp.float32) + norm_back(grad_hmlp * gain_two, normed_m, factor_m)
    grad_branch = grad_mid.astype(jnp.bfloat16)
    grad_outw = grad_t(grad_branch, attn_out, n_dp)
    grad_attn = apply_back(grad_branch, full_out).astype(jnp.bfloat16)
    grad_query, grad_kv = attn_bwd(query, key_value, halo_lo, halo_hi, tag_query, wide_tag, grad_attn)
    grad_qkv = rope_bwd(grad_query, grad_kv, cosine, sine)
    grad_qkvw = grad_t(grad_qkv, h_attn, n_dp)
    grad_hattn = apply_back(grad_qkv, full_qkv)
    grad_gain_one = jnp.sum(grad_hattn * normed_a, axis=0)
    grad_tokens = grad_mid + norm_back(grad_hattn * gain_one, normed_a, factor_a)
    height = out_cols + in_cols + down_lines + qkv_cols + 8
    tail = 8 + (-height) % (RING_WAYS * 16)
    gain_both = jnp.concatenate(
        [
            gain_blocks(grad_gain_two, 1, n_seq, rows, 1)[0],
            gain_blocks(grad_gain_one, 1, n_seq, rows, tail - 1)[0],
        ],
        1,
    )
    blocks = jnp.stack(
        [
            jnp.concatenate(
                [
                    *lax.optimization_barrier(
                        (
                            grad_outw[d].reshape(n_seq, out_cols, rows),
                            grad_inw[d].reshape(n_seq, in_cols, rows),
                            grad_down[d]
                            .reshape(n_seq, down_cols, down_rows)
                            .reshape(n_seq, down_lines, rows),
                            grad_qkvw[d].reshape(n_seq, qkv_cols, rows),
                            gain_both,
                        )
                    ),
                ],
                1,
            )
            for d in range(n_dp)
        ]
    )
    depth = blocks.shape[2]
    half = lax.psum_scatter(
        blocks.reshape(n_dp, n_seq * depth, rows), "dp", scatter_dimension=0, tiled=True
    )
    late = ring_reduce(half.reshape(n_seq, depth, rows), order, RING_WAYS)
    at = 0
    late_out = late[at : at + out_cols].T
    at += out_cols
    late_in = late[at : at + in_cols].T
    at += in_cols
    late_down = late[at : at + down_lines].reshape(down_cols, down_rows).T
    at += down_lines
    late_qkv = late[at : at + qkv_cols].T
    at += qkv_cols
    late_gain_two = late[at, : gain_mlp.shape[0]]
    late_gain_one = late[at + 1, : gain_attn.shape[0]]
    return (
        output,
        grad_tokens,
        late_qkv,
        late_out,
        late_in,
        late_down,
        late_gain_one,
        late_gain_two,
    )


def solution(mesh):
    placed = (
        P(("dp", "seq"), None),
        P(("dp", "seq")),
        P(("dp", "seq")),
        P("dp", "seq"),
        P("dp", "seq"),
        P("dp", "seq"),
        P("dp", "seq"),
        P("seq"),
        P("seq"),
        P(("dp", "seq"), None),
    )
    return jax.shard_map(
        functools.partial(on_device, ring_order(mesh)),
        mesh=mesh,
        in_specs=placed,
        out_specs=(
            P(("dp", "seq"), None),
            P(("dp", "seq"), None),
            P("dp", "seq"),
            P("dp", "seq"),
            P("dp", "seq"),
            P("dp", "seq"),
            P("seq"),
            P("seq"),
        ),
        check_vma=False,
    )
```

```python
import functools
import math

import jax
import jax.numpy as jnp
from jax import lax
from jax.experimental import pallas as pl
from jax.experimental.pallas import tpu as pltpu
from jax.sharding import PartitionSpec as P

D = 768
HEADS = 12
HEAD = 64
FF = 1152
HALF = 64


def padded(value, sides, width):
    for axis, dim in sides:
        size, length = (lax.axis_size(axis), value.shape[dim])
        up = [(i, (i + 1) % size) for i in range(size - 1)]
        down = [(j, i) for i, j in up]
        last = lax.slice_in_dim(value, length - width, length, axis=dim)
        initial = lax.slice_in_dim(value, 0, width, axis=dim)
        before = lax.ppermute(last, axis, up)
        after = lax.ppermute(initial, axis, down)
        value = jnp.concatenate([before, value, after], axis=dim)
    return value


def shifted(value, axis, by):
    length = lax.axis_size(axis)
    pairs = [(i, i + by) for i in range(length) if 0 <= i + by < length]
    return lax.ppermute(value, axis, pairs)


def layer_norm(value):
    centre = value - jnp.mean(value, axis=-1, keepdims=True)
    factor = lax.rsqrt(jnp.mean(centre * centre, axis=-1, keepdims=True) + 1e-05)
    return (centre * factor, factor)


def norm_back(grad, normed, factor):
    return factor * (
        grad
        - jnp.mean(grad, axis=-1, keepdims=True)
        - normed * jnp.mean(grad * normed, axis=-1, keepdims=True)
    )


def rotary_tables(place):
    freq = jnp.exp(jnp.arange(HEAD // 2, dtype=jnp.float32) * (-2.0 * math.log(10000.0) / HEAD))
    angle = place[:, None] * freq[None, :]
    cosine = jnp.tile(jnp.concatenate([jnp.cos(angle), jnp.cos(angle)], 1), (1, HEADS))
    sine = jnp.tile(jnp.concatenate([jnp.sin(angle), jnp.sin(angle)], 1), (1, HEADS))
    return (cosine, sine)


def rotate(value):
    count = value.shape[0]
    shaped = value.reshape(count, HEADS, HEAD)
    first = shaped[..., : HEAD // 2]
    second = shaped[..., HEAD // 2 :]
    return jnp.concatenate([-second, first], -1).reshape(count, HEADS * HEAD)


def left_dot(left, right):
    return lax.dot_general(
        left, right, (((0,), (0,)), ((), ())), preferred_element_type=jnp.float32
    )


def right_dot(left, right):
    return lax.dot_general(
        left, right, (((1,), (1,)), ((), ())), preferred_element_type=jnp.float32
    )


def glu_piece(gate_up):
    return jax.nn.gelu(gate_up[:, :FF], approximate=False) * gate_up[:, FF:]


MESH = pl.DeviceIdType.MESH


def ring_order(mesh):
    n = mesh.shape["seq"]
    try:
        coords = [tuple(mesh.devices[0, s].coords) for s in range(n)]
    except Exception:
        return list(range(n))
    near = [
        [t for t in range(n) if sum(abs(a - b) for a, b in zip(coords[s], coords[t])) == 1]
        for s in range(n)
    ]
    path, seen = [0], {0}

    def grow(budget=[200000]):
        budget[0] -= 1
        if budget[0] < 0:
            return False
        if len(path) == n:
            return 0 in near[path[-1]]
        options = sorted(
            (t for t in near[path[-1]] if t not in seen),
            key=lambda t: sum(1 for u in near[t] if u not in seen),
        )
        for t in options:
            path.append(t)
            seen.add(t)
            if grow():
                return True
            path.pop()
            seen.discard(t)
        return False

    return list(path) if n > 2 and grow() else list(range(n))


def lookup(index, table):
    n = len(table)
    square = n * n
    total = jnp.int32(0)
    for k, value in enumerate(table):
        if value:
            gap = index - k
            differs = lax.div(gap * gap + (square - 1), jnp.int32(square))
            total = total + value * (1 - differs)
    return total


def ring_kernel(order, per_way, h_ref, out_ref, recv, send, ssem, rsem, free):
    n = len(order)
    where = [0] * n
    for p, s in enumerate(order):
        where[s] = p
    d = lax.axis_index("dp")
    me = lax.axis_index("seq")
    pos = lookup(me, where)
    nxt = lookup(lax.rem(pos + 1, n), order)
    prv = lookup(lax.rem(pos + n - 1, n), order)
    piece = out_ref.shape[0] // per_way
    ahead = (n - 1) // 2
    behind = n - 1 - ahead

    barrier = pltpu.get_barrier_semaphore()
    pl.semaphore_signal(barrier, 1, device_id=(d, nxt), device_id_type=MESH)
    pl.semaphore_signal(barrier, 1, device_id=(d, prv), device_id_type=MESH)
    pl.semaphore_wait(barrier, 2)

    lanes = []
    for forward in (True, False):
        for chunk in range(per_way):
            li = len(lanes)
            lanes.append((recv.at[li], send.at[li], ssem.at[li], rsem.at[li], free.at[li],
                          nxt if forward else prv, prv if forward else nxt,
                          slice(chunk * piece, (chunk + 1) * piece),
                          ahead if forward else behind, forward))
    copies = {}
    for step in range(max(ahead, behind)):
        slot = step % 2
        for li, (recv, send, ssem, rsem, free, to, frm, rows, sends, forward) in enumerate(lanes):
            if step >= sends:
                continue
            if forward:
                target = pos + sends - step
            else:
                target = pos + n - sends + step
            q = lookup(lax.rem(target, n), order)
            own = h_ref[q, rows, :]
            if step == 0:
                part = own
            else:
                copies[(li, step - 1)].wait_recv()
                part = recv[1 - slot].astype(jnp.float32) + own
                if step <= sends - 2:
                    pl.semaphore_signal(free, 1, device_id=(d, frm), device_id_type=MESH)
            if step >= 2:
                copies[(li, step - 2)].wait_send()
                pl.semaphore_wait(free, 1)
            send[slot] = part.astype(send.dtype)
            c = pltpu.make_async_remote_copy(
                src_ref=send.at[slot], dst_ref=recv.at[slot],
                send_sem=ssem.at[slot], recv_sem=rsem.at[slot],
                device_id=(d, to), device_id_type=MESH)
            c.start()
            copies[(li, step)] = c
    for chunk in range(per_way):
        rows = lanes[chunk][7]
        total = h_ref[me, rows, :]
        for li in (chunk, per_way + chunk):
            recv, sends = lanes[li][0], lanes[li][8]
            copies[(li, sends - 1)].wait_recv()
            total = total + recv[(sends - 1) % 2].astype(jnp.float32)
        out_ref[rows, :] = total
    for li, lane in enumerate(lanes):
        sends = lane[8]
        if sends >= 2:
            copies[(li, sends - 2)].wait_send()
        copies[(li, sends - 1)].wait_send()


RING_WAYS = 2


def ring_reduce(h, order, per_way, link_dtype=jnp.bfloat16):
    n, rows, width = h.shape
    lanes = 2 * per_way
    piece = rows // per_way
    return pl.pallas_call(
        functools.partial(ring_kernel, tuple(order), per_way),
        out_shape=jax.ShapeDtypeStruct((rows, width), jnp.float32),
        in_specs=[pl.BlockSpec(memory_space=pltpu.VMEM)],
        out_specs=pl.BlockSpec(memory_space=pltpu.VMEM),
        scratch_shapes=[
            pltpu.VMEM((lanes, 2, piece, width), link_dtype),
            pltpu.VMEM((lanes, 2, piece, width), link_dtype),
            pltpu.SemaphoreType.DMA((lanes, 2)),
            pltpu.SemaphoreType.DMA((lanes, 2)),
            pltpu.SemaphoreType.REGULAR((lanes,)),
        ],
        compiler_params=pltpu.CompilerParams(collective_id=1, has_side_effects=True,
                                             vmem_limit_bytes=48 * 1024 * 1024),
    )(h)


QB = 128


def window_allow(tq_ref, tk_ref, a0, w0):
    rows = lax.broadcasted_iota(jnp.int32, (QB, QB + 2 * HALF), 0)
    cols = lax.broadcasted_iota(jnp.int32, (QB, QB + 2 * HALF), 1)
    offset = cols - rows - HALF
    near = jnp.abs(offset) <= HALF
    same = tk_ref[:, pl.ds(w0, QB + 2 * HALF)] == tq_ref[pl.ds(a0, QB), :]
    return near & (same | (offset == 0))


def nt(a, b):
    return lax.dot_general(a, b, (((1,), (1,)), ((), ())), preferred_element_type=jnp.float32)


def tn(a, b):
    return lax.dot_general(a, b, (((0,), (0,)), ((), ())), preferred_element_type=jnp.float32)


def probs_of(q_ref, kv_ref, allow, a0, w0, h):
    q_h = q_ref[pl.ds(a0, QB), pl.ds(h * HEAD, HEAD)]
    k_h = kv_ref[pl.ds(w0, QB + 2 * HALF), pl.ds(h * HEAD, HEAD)]
    scores = jnp.where(allow, nt(q_h, k_h) * 0.125, -1e30)
    largest = jnp.max(scores, axis=-1, keepdims=True)
    raised = jnp.exp(scores - largest)
    return raised / jnp.sum(raised, axis=-1, keepdims=True), q_h, k_h


def neighbours():
    n_seq = lax.axis_size("seq")
    total = lax.axis_size("dp") * n_seq
    me = lax.axis_index("dp") * n_seq + lax.axis_index("seq")
    before = lax.rem(me + total - 1, total)
    after = lax.rem(me + 1, total)
    return (
        (lax.div(before, n_seq), lax.rem(before, n_seq)),
        (lax.div(after, n_seq), lax.rem(after, n_seq)),
    )


def greet(before, after):
    barrier = pltpu.get_barrier_semaphore()
    pl.semaphore_signal(barrier, 1, device_id=before, device_id_type=MESH)
    pl.semaphore_signal(barrier, 1, device_id=after, device_id_type=MESH)
    pl.semaphore_wait(barrier, 2)


def start_of(b):
    return b * QB if isinstance(b, int) else pl.multiple_of(b * QB, QB)


def attn_fwd_kernel(q_ref, kv_ref, tq_ref, tk_ref, o_ref, lo_ref, hi_ref, wide, send_sem, recv_sem):
    width = q_ref.shape[1]
    count = q_ref.shape[0]
    blocks = count // QB
    before, after = neighbours()
    greet(before, after)
    to_before = pltpu.make_async_remote_copy(
        src_ref=kv_ref.at[pl.ds(0, HALF)], dst_ref=hi_ref,
        send_sem=send_sem.at[0], recv_sem=recv_sem.at[0],
        device_id=before, device_id_type=MESH)
    to_after = pltpu.make_async_remote_copy(
        src_ref=kv_ref.at[pl.ds(count - HALF, HALF)], dst_ref=lo_ref,
        send_sem=send_sem.at[1], recv_sem=recv_sem.at[1],
        device_id=after, device_id_type=MESH)
    to_before.start()
    to_after.start()
    wide[pl.ds(HALF, count), :] = kv_ref[...]

    def block(b, carry):
        a0 = start_of(b)
        allow = window_allow(tq_ref, tk_ref, a0, a0)
        for h in range(HEADS):
            probs, _, _ = probs_of(q_ref, wide, allow, a0, a0, h)
            v_h = wide[pl.ds(a0, QB + 2 * HALF), pl.ds(width + h * HEAD, HEAD)]
            mixed = jnp.dot(probs.astype(jnp.bfloat16), v_h, preferred_element_type=jnp.float32)
            o_ref[pl.ds(a0, QB), pl.ds(h * HEAD, HEAD)] = mixed.astype(o_ref.dtype)
        return carry

    lax.fori_loop(1, blocks - 1, block, 0)
    to_before.wait_recv()
    to_after.wait_recv()
    wide[pl.ds(0, HALF), :] = lo_ref[...]
    wide[pl.ds(count + HALF, HALF), :] = hi_ref[...]
    block(0, 0)
    block(blocks - 1, 0)
    to_before.wait_send()
    to_after.wait_send()


def attn_bwd_kernel(q_ref, kv_ref, lo_ref, hi_ref, tq_ref, tk_ref, do_ref, dq_ref, dkv_ref,
                    wide, dwide, send_lo, send_hi, recv_lo, recv_hi, send_sem, recv_sem):
    width = q_ref.shape[1]
    count = q_ref.shape[0]
    blocks = count // QB
    before, after = neighbours()
    greet(before, after)
    wide[pl.ds(0, HALF), :] = lo_ref[...]
    wide[pl.ds(HALF, count), :] = kv_ref[...]
    wide[pl.ds(count + HALF, HALF), :] = hi_ref[...]
    dwide[...] = jnp.zeros(dwide.shape, dwide.dtype)

    def block(b, carry):
        a0 = start_of(b)
        allow = window_allow(tq_ref, tk_ref, a0, a0)
        for h in range(HEADS):
            probs, q_h, k_h = probs_of(q_ref, wide, allow, a0, a0, h)
            v_h = wide[pl.ds(a0, QB + 2 * HALF), pl.ds(width + h * HEAD, HEAD)]
            do_h = do_ref[pl.ds(a0, QB), pl.ds(h * HEAD, HEAD)]
            grad_probs = nt(do_h, v_h)
            inner = jnp.sum(probs * grad_probs, axis=-1, keepdims=True)
            grad_scores = (probs * (grad_probs - inner)).astype(jnp.bfloat16)
            dq_ref[pl.ds(a0, QB), pl.ds(h * HEAD, HEAD)] = (
                jnp.dot(grad_scores, k_h, preferred_element_type=jnp.float32) * 0.125
            )
            rows = pl.ds(a0, QB + 2 * HALF)
            dwide[rows, pl.ds(h * HEAD, HEAD)] += tn(grad_scores, q_h) * 0.125
            dwide[rows, pl.ds(width + h * HEAD, HEAD)] += tn(probs.astype(jnp.bfloat16), do_h)
        return carry

    block(0, 0)
    block(blocks - 1, 0)
    send_lo[...] = dwide[pl.ds(0, HALF), :].astype(send_lo.dtype)
    send_hi[...] = dwide[pl.ds(count + HALF, HALF), :].astype(send_hi.dtype)
    to_before = pltpu.make_async_remote_copy(
        src_ref=send_lo, dst_ref=recv_hi,
        send_sem=send_sem.at[0], recv_sem=recv_sem.at[0],
        device_id=before, device_id_type=MESH)
    to_after = pltpu.make_async_remote_copy(
        src_ref=send_hi, dst_ref=recv_lo,
        send_sem=send_sem.at[1], recv_sem=recv_sem.at[1],
        device_id=after, device_id_type=MESH)
    to_before.start()
    to_after.start()
    lax.fori_loop(1, blocks - 1, block, 0)
    dkv_ref[...] = dwide[pl.ds(HALF, count), :]
    to_before.wait_recv()
    to_after.wait_recv()
    dkv_ref[pl.ds(0, HALF), :] += recv_lo[...].astype(jnp.float32)
    dkv_ref[pl.ds(count - HALF, HALF), :] += recv_hi[...].astype(jnp.float32)
    to_before.wait_send()
    to_after.wait_send()


VMEM_LIMIT = 48 * 1024 * 1024


def attn_fwd(query, kv, tag_q, tag_k):
    count, width = query.shape
    vm = pl.BlockSpec(memory_space=pltpu.VMEM)
    halo = jax.ShapeDtypeStruct((HALF, kv.shape[1]), kv.dtype)
    return pl.pallas_call(
        attn_fwd_kernel,
        out_shape=(jax.ShapeDtypeStruct((count, width), jnp.bfloat16), halo, halo),
        in_specs=[vm] * 4,
        out_specs=(vm, vm, vm),
        scratch_shapes=[
            pltpu.VMEM((count + 2 * HALF, kv.shape[1]), kv.dtype),
            pltpu.SemaphoreType.DMA((2,)),
            pltpu.SemaphoreType.DMA((2,)),
        ],
        compiler_params=pltpu.CompilerParams(
            collective_id=2, has_side_effects=True, vmem_limit_bytes=VMEM_LIMIT
        ),
    )(query, kv, tag_q.reshape(count, 1), tag_k.reshape(1, -1))


def attn_bwd(query, kv, lo, hi, tag_q, tag_k, grad_out):
    count, width = query.shape
    vm = pl.BlockSpec(memory_space=pltpu.VMEM)
    return pl.pallas_call(
        attn_bwd_kernel,
        out_shape=(
            jax.ShapeDtypeStruct((count, width), jnp.float32),
            jax.ShapeDtypeStruct(kv.shape, jnp.float32),
        ),
        in_specs=[vm] * 7,
        out_specs=(vm, vm),
        scratch_shapes=[
            pltpu.VMEM((count + 2 * HALF, kv.shape[1]), kv.dtype),
            pltpu.VMEM((count + 2 * HALF, kv.shape[1]), jnp.float32),
            pltpu.VMEM((HALF, kv.shape[1]), jnp.bfloat16),
            pltpu.VMEM((HALF, kv.shape[1]), jnp.bfloat16),
            pltpu.VMEM((HALF, kv.shape[1]), jnp.bfloat16),
            pltpu.VMEM((HALF, kv.shape[1]), jnp.bfloat16),
            pltpu.SemaphoreType.DMA((2,)),
            pltpu.SemaphoreType.DMA((2,)),
        ],
        compiler_params=pltpu.CompilerParams(
            collective_id=3, has_side_effects=True, vmem_limit_bytes=VMEM_LIMIT
        ),
    )(query, kv, lo, hi, tag_q.reshape(count, 1), tag_k.reshape(1, -1), grad_out)


ROPE_ROWS = 256


def head_rotate(x):
    width = x.shape[-1]
    lane = lax.broadcasted_iota(jnp.int32, x.shape, x.ndim - 1)
    ahead = pltpu.roll(x, width - HEAD // 2, x.ndim - 1)
    behind = pltpu.roll(x, HEAD // 2, x.ndim - 1)
    return jnp.where(lane % HEAD < HEAD // 2, -ahead, behind)


def rope_fwd_kernel(qkv_ref, cos_ref, sin_ref, q_ref, kv_ref):
    width = q_ref.shape[1]
    c = cos_ref[...]
    s = sin_ref[...]
    q = qkv_ref[:, pl.ds(0, width)]
    k = qkv_ref[:, pl.ds(width, width)]
    q_ref[...] = (q * c + head_rotate(q) * s).astype(q_ref.dtype)
    kv_ref[:, pl.ds(0, width)] = (k * c + head_rotate(k) * s).astype(kv_ref.dtype)
    kv_ref[:, pl.ds(width, width)] = qkv_ref[:, pl.ds(2 * width, width)].astype(kv_ref.dtype)


def rope_bwd_kernel(dq_ref, dkv_ref, cos_ref, sin_ref, out_ref):
    width = dq_ref.shape[1]
    c = cos_ref[...]
    s = sin_ref[...]
    dq = dq_ref[...]
    dk = dkv_ref[:, pl.ds(0, width)]
    out_ref[:, pl.ds(0, width)] = (dq * c - head_rotate(dq) * s).astype(out_ref.dtype)
    out_ref[:, pl.ds(width, width)] = (dk * c - head_rotate(dk) * s).astype(out_ref.dtype)
    out_ref[:, pl.ds(2 * width, width)] = dkv_ref[:, pl.ds(width, width)].astype(out_ref.dtype)


def rows_spec(cols):
    return pl.BlockSpec((ROPE_ROWS, cols), lambda i: (i, 0))


def rope_fwd(qkv, cosine, sine):
    count, width = cosine.shape
    return pl.pallas_call(
        rope_fwd_kernel,
        grid=(count // ROPE_ROWS,),
        out_shape=(
            jax.ShapeDtypeStruct((count, width), jnp.bfloat16),
            jax.ShapeDtypeStruct((count, 2 * width), jnp.bfloat16),
        ),
        in_specs=[rows_spec(3 * width), rows_spec(width), rows_spec(width)],
        out_specs=(rows_spec(width), rows_spec(2 * width)),
    )(qkv, cosine, sine)


def rope_bwd(dq, dkv, cosine, sine):
    count, width = cosine.shape
    return pl.pallas_call(
        rope_bwd_kernel,
        grid=(count // ROPE_ROWS,),
        out_shape=jax.ShapeDtypeStruct((count, 3 * width), jnp.bfloat16),
        in_specs=[rows_spec(width), rows_spec(2 * width), rows_spec(width), rows_spec(width)],
        out_specs=rows_spec(3 * width),
    )(dq, dkv, cosine, sine)


def gain_rows(gain, width, rows=8):
    line = jnp.pad(gain, (0, width - gain.shape[0]))
    return jnp.concatenate([line[None], jnp.zeros((rows - 1, width), gain.dtype)], 0)


def gather_rows(payload, n_dp, n_seq):
    every = lax.all_gather(payload, ("dp", "seq"), axis=0, tiled=True)
    return every.reshape(n_dp, n_seq, payload.shape[0], payload.shape[1])


def gain_blocks(grad_gain, n_dp, n_seq, width, height=8):
    part = jnp.pad(grad_gain.reshape(n_seq, -1), ((0, 0), (0, width - grad_gain.shape[0] // n_seq)))
    rows = jnp.concatenate([part[:, None], jnp.zeros((n_seq, height - 1, width), part.dtype)], 1)
    return jnp.broadcast_to(rows[None], (n_dp, n_seq, height, width))


def front(value, n_dp):
    return value.reshape(value.shape[0], n_dp, -1)


def apply_t(left, weight_t, n_dp):
    return jnp.einsum("tdr,dnr->tn", front(left, n_dp), weight_t, preferred_element_type=jnp.float32)


def apply_back(grad, weight_t):
    out = jnp.einsum("tn,dnr->tdr", grad, weight_t, preferred_element_type=jnp.float32)
    return out.reshape(out.shape[0], -1)


def grad_t(grad, left, n_dp):
    width = left.shape[1] // n_dp
    return [
        lax.dot_general(
            grad,
            left[:, d * width : (d + 1) * width],
            (((0,), (0,)), ((), ())),
            preferred_element_type=jnp.float32,
        )
        for d in range(n_dp)
    ]


def on_device(order, tokens, doc_start, real, w_qkv, w_out, w_in, w_down, gain_attn, gain_mlp, cotangent):
    count = tokens.shape[0]
    n_dp, n_seq = lax.axis_size("dp"), lax.axis_size("seq")
    rows, qkv_cols = w_qkv.shape
    out_cols, in_cols = w_out.shape[1], w_in.shape[1]
    down_rows, down_cols = w_down.shape
    down_lines = down_rows * down_cols // rows
    first = gather_rows(
        jnp.concatenate([w_qkv.T, w_out.T, gain_rows(gain_attn, rows)], 0), n_dp, n_seq
    )
    second = gather_rows(
        jnp.concatenate([w_in.T, w_down.T.reshape(down_lines, rows), gain_rows(gain_mlp, rows)], 0),
        n_dp,
        n_seq,
    )
    full_qkv = first[:, :, :qkv_cols].reshape(n_dp, n_seq * qkv_cols, rows)
    full_out = first[:, :, qkv_cols : qkv_cols + out_cols].reshape(n_dp, n_seq * out_cols, rows)
    gain_one = (
        first[0, :, qkv_cols + out_cols, : gain_attn.shape[0]].reshape(-1).astype(jnp.float32)
    )
    stream = tokens.astype(jnp.float32)
    normed_a, factor_a = layer_norm(stream)
    h_attn = (normed_a * gain_one).astype(jnp.bfloat16)
    qkv = apply_t(h_attn, full_qkv, n_dp)
    offset_base = lax.axis_index(("dp", "seq")) * count
    place = (offset_base + jnp.arange(count, dtype=jnp.int32) - doc_start).astype(jnp.float32)
    cosine, sine = rotary_tables(place)
    query, key_value = rope_fwd(qkv, cosine, sine)
    tag_query = doc_start + 1
    tag_key = jnp.where(real == 1, tag_query, 0)
    wide_tag = padded(tag_key, ((("dp", "seq"), 0),), HALF)
    attn_out, halo_lo, halo_hi = attn_fwd(query, key_value, tag_query, wide_tag)
    mid = stream + apply_t(attn_out, full_out, n_dp)
    mid, second = lax.optimization_barrier((mid, second))
    at = 0
    full_in = second[:, :, at : at + in_cols].reshape(n_dp, n_seq * in_cols, rows)
    at += in_cols
    full_down = (
        second[:, :, at : at + down_lines]
        .reshape(n_dp, n_seq, down_cols, down_rows)
        .reshape(n_dp, n_seq * down_cols, down_rows)
    )
    at += down_lines
    gain_two = second[0, :, at, : gain_mlp.shape[0]].reshape(-1).astype(jnp.float32)
    normed_m, factor_m = layer_norm(mid)
    h_mlp = (normed_m * gain_two).astype(jnp.bfloat16)
    gate_up = apply_t(h_mlp, full_in, n_dp)
    hidden_out, glu_pull = jax.vjp(glu_piece, gate_up)
    hidden = hidden_out.astype(jnp.bfloat16)
    result = mid + apply_t(hidden, full_down, n_dp)
    output = result.astype(jnp.bfloat16)
    grad_down = grad_t(cotangent, hidden, n_dp)
    grad_hidden = apply_back(cotangent, full_down)
    grad_gate_up = glu_pull(grad_hidden)[0].astype(jnp.bfloat16)
    grad_inw = grad_t(grad_gate_up, h_mlp, n_dp)
    grad_hmlp = apply_back(grad_gate_up, full_in)
    grad_gain_two = jnp.sum(grad_hmlp * normed_m, axis=0)
    grad_mid = cotangent.astype(jnp.float32) + norm_back(grad_hmlp * gain_two, normed_m, factor_m)
    grad_branch = grad_mid.astype(jnp.bfloat16)
    grad_outw = grad_t(grad_branch, attn_out, n_dp)
    grad_attn = apply_back(grad_branch, full_out).astype(jnp.bfloat16)
    grad_query, grad_kv = attn_bwd(query, key_value, halo_lo, halo_hi, tag_query, wide_tag, grad_attn)
    grad_qkv = rope_bwd(grad_query, grad_kv, cosine, sine)
    grad_qkvw = grad_t(grad_qkv, h_attn, n_dp)
    grad_hattn = apply_back(grad_qkv, full_qkv)
    grad_gain_one = jnp.sum(grad_hattn * normed_a, axis=0)
    grad_tokens = grad_mid + norm_back(grad_hattn * gain_one, normed_a, factor_a)
    height = out_cols + in_cols + down_lines + qkv_cols + 8
    tail = 8 + (-height) % (RING_WAYS * 16)
    gain_both = jnp.concatenate(
        [
            gain_blocks(grad_gain_two, 1, n_seq, rows, 1)[0],
            gain_blocks(grad_gain_one, 1, n_seq, rows, tail - 1)[0],
        ],
        1,
    )
    blocks = jnp.stack(
        [
            jnp.concatenate(
                [
                    *lax.optimization_barrier(
                        (
                            grad_outw[d].reshape(n_seq, out_cols, rows),
                            grad_inw[d].reshape(n_seq, in_cols, rows),
                            grad_down[d]
                            .reshape(n_seq, down_cols, down_rows)
                            .reshape(n_seq, down_lines, rows),
                            grad_qkvw[d].reshape(n_seq, qkv_cols, rows),
                            gain_both,
                        )
                    ),
                ],
                1,
            )
            for d in range(n_dp)
        ]
    )
    depth = blocks.shape[2]
    half = lax.psum_scatter(
        blocks.reshape(n_dp, n_seq * depth, rows), "dp", scatter_dimension=0, tiled=True
    )
    late = ring_reduce(half.reshape(n_seq, depth, rows), order, RING_WAYS)
    at = 0
    late_out = late[at : at + out_cols].T
    at += out_cols
    late_in = late[at : at + in_cols].T
    at += in_cols
    late_down = late[at : at + down_lines].reshape(down_cols, down_rows).T
    at += down_lines
    late_qkv = late[at : at + qkv_cols].T
    at += qkv_cols
    late_gain_two = late[at, : gain_mlp.shape[0]]
    late_gain_one = late[at + 1, : gain_attn.shape[0]]
    return (
        output,
        grad_tokens,
        late_qkv,
        late_out,
        late_in,
        late_down,
        late_gain_one,
        late_gain_two,
    )


def solution(mesh):
    placed = (
        P(("dp", "seq"), None),
        P(("dp", "seq")),
        P(("dp", "seq")),
        P("dp", "seq"),
        P("dp", "seq"),
        P("dp", "seq"),
        P("dp", "seq"),
        P("seq"),
        P("seq"),
        P(("dp", "seq"), None),
    )
    return jax.shard_map(
        functools.partial(on_device, ring_order(mesh)),
        mesh=mesh,
        in_specs=placed,
        out_specs=(
            P(("dp", "seq"), None),
            P(("dp", "seq"), None),
            P("dp", "seq"),
            P("dp", "seq"),
            P("dp", "seq"),
            P("dp", "seq"),
            P("seq"),
            P("seq"),
        ),
        check_vma=False,
    )
```

```python
import functools
import math

import jax
import jax.numpy as jnp
from jax import lax
from jax.experimental import pallas as pl
from jax.experimental.pallas import tpu as pltpu
from jax.sharding import PartitionSpec as P

D = 768
HEADS = 12
HEAD = 64
FF = 1152
HALF = 64


def padded(value, sides, width):
    for axis, dim in sides:
        size, length = (lax.axis_size(axis), value.shape[dim])
        up = [(i, (i + 1) % size) for i in range(size - 1)]
        down = [(j, i) for i, j in up]
        last = lax.slice_in_dim(value, length - width, length, axis=dim)
        initial = lax.slice_in_dim(value, 0, width, axis=dim)
        before = lax.ppermute(last, axis, up)
        after = lax.ppermute(initial, axis, down)
        value = jnp.concatenate([before, value, after], axis=dim)
    return value


def shifted(value, axis, by):
    length = lax.axis_size(axis)
    pairs = [(i, i + by) for i in range(length) if 0 <= i + by < length]
    return lax.ppermute(value, axis, pairs)


def layer_norm(value):
    centre = value - jnp.mean(value, axis=-1, keepdims=True)
    factor = lax.rsqrt(jnp.mean(centre * centre, axis=-1, keepdims=True) + 1e-05)
    return (centre * factor, factor)


def norm_back(grad, normed, factor):
    return factor * (
        grad
        - jnp.mean(grad, axis=-1, keepdims=True)
        - normed * jnp.mean(grad * normed, axis=-1, keepdims=True)
    )


def rotary_tables(place):
    freq = jnp.exp(jnp.arange(HEAD // 2, dtype=jnp.float32) * (-2.0 * math.log(10000.0) / HEAD))
    angle = place[:, None] * freq[None, :]
    cosine = jnp.tile(jnp.concatenate([jnp.cos(angle), jnp.cos(angle)], 1), (1, HEADS))
    sine = jnp.tile(jnp.concatenate([jnp.sin(angle), jnp.sin(angle)], 1), (1, HEADS))
    return (cosine, sine)


def rotate(value):
    count = value.shape[0]
    shaped = value.reshape(count, HEADS, HEAD)
    first = shaped[..., : HEAD // 2]
    second = shaped[..., HEAD // 2 :]
    return jnp.concatenate([-second, first], -1).reshape(count, HEADS * HEAD)


def left_dot(left, right):
    return lax.dot_general(
        left, right, (((0,), (0,)), ((), ())), preferred_element_type=jnp.float32
    )


def right_dot(left, right):
    return lax.dot_general(
        left, right, (((1,), (1,)), ((), ())), preferred_element_type=jnp.float32
    )


def glu_piece(gate_up):
    return jax.nn.gelu(gate_up[:, :FF], approximate=False) * gate_up[:, FF:]


MESH = pl.DeviceIdType.MESH


def ring_order(mesh):
    n = mesh.shape["seq"]
    try:
        coords = [tuple(mesh.devices[0, s].coords) for s in range(n)]
    except Exception:
        return list(range(n))
    near = [
        [t for t in range(n) if sum(abs(a - b) for a, b in zip(coords[s], coords[t])) == 1]
        for s in range(n)
    ]
    path, seen = [0], {0}

    def grow(budget=[200000]):
        budget[0] -= 1
        if budget[0] < 0:
            return False
        if len(path) == n:
            return 0 in near[path[-1]]
        options = sorted(
            (t for t in near[path[-1]] if t not in seen),
            key=lambda t: sum(1 for u in near[t] if u not in seen),
        )
        for t in options:
            path.append(t)
            seen.add(t)
            if grow():
                return True
            path.pop()
            seen.discard(t)
        return False

    return list(path) if n > 2 and grow() else list(range(n))


def lookup(index, table):
    n = len(table)
    square = n * n
    total = jnp.int32(0)
    for k, value in enumerate(table):
        if value:
            gap = index - k
            differs = lax.div(gap * gap + (square - 1), jnp.int32(square))
            total = total + value * (1 - differs)
    return total


def ring_kernel(order, per_way, h_ref, out_ref, recv, send, ssem, rsem, free):
    n = len(order)
    where = [0] * n
    for p, s in enumerate(order):
        where[s] = p
    d = lax.axis_index("dp")
    me = lax.axis_index("seq")
    pos = lookup(me, where)
    nxt = lookup(lax.rem(pos + 1, n), order)
    prv = lookup(lax.rem(pos + n - 1, n), order)
    piece = out_ref.shape[0] // per_way
    ahead = (n - 1) // 2
    behind = n - 1 - ahead

    barrier = pltpu.get_barrier_semaphore()
    pl.semaphore_signal(barrier, 1, device_id=(d, nxt), device_id_type=MESH)
    pl.semaphore_signal(barrier, 1, device_id=(d, prv), device_id_type=MESH)
    pl.semaphore_wait(barrier, 2)

    lanes = []
    for forward in (True, False):
        for chunk in range(per_way):
            li = len(lanes)
            lanes.append((recv.at[li], send.at[li], ssem.at[li], rsem.at[li], free.at[li],
                          nxt if forward else prv, prv if forward else nxt,
                          slice(chunk * piece, (chunk + 1) * piece),
                          ahead if forward else behind, forward))
    copies = {}
    for step in range(max(ahead, behind)):
        slot = step % 2
        for li, (recv, send, ssem, rsem, free, to, frm, rows, sends, forward) in enumerate(lanes):
            if step >= sends:
                continue
            if forward:
                target = pos + sends - step
            else:
                target = pos + n - sends + step
            q = lookup(lax.rem(target, n), order)
            own = h_ref[q, rows, :].astype(jnp.float32)
            if step == 0:
                part = own
            else:
                copies[(li, step - 1)].wait_recv()
                part = recv[1 - slot].astype(jnp.float32) + own
                if step <= sends - 2:
                    pl.semaphore_signal(free, 1, device_id=(d, frm), device_id_type=MESH)
            if step >= 2:
                copies[(li, step - 2)].wait_send()
                pl.semaphore_wait(free, 1)
            send[slot] = part.astype(send.dtype)
            c = pltpu.make_async_remote_copy(
                src_ref=send.at[slot], dst_ref=recv.at[slot],
                send_sem=ssem.at[slot], recv_sem=rsem.at[slot],
                device_id=(d, to), device_id_type=MESH)
            c.start()
            copies[(li, step)] = c
    for chunk in range(per_way):
        rows = lanes[chunk][7]
        total = h_ref[me, rows, :].astype(jnp.float32)
        for li in (chunk, per_way + chunk):
            recv, sends = lanes[li][0], lanes[li][8]
            copies[(li, sends - 1)].wait_recv()
            total = total + recv[(sends - 1) % 2].astype(jnp.float32)
        out_ref[rows, :] = total
    for li, lane in enumerate(lanes):
        sends = lane[8]
        if sends >= 2:
            copies[(li, sends - 2)].wait_send()
        copies[(li, sends - 1)].wait_send()


RING_WAYS = 2


def ring_reduce(h, order, per_way, link_dtype=jnp.bfloat16):
    n, rows, width = h.shape
    lanes = 2 * per_way
    piece = rows // per_way
    return pl.pallas_call(
        functools.partial(ring_kernel, tuple(order), per_way),
        out_shape=jax.ShapeDtypeStruct((rows, width), jnp.float32),
        in_specs=[pl.BlockSpec(memory_space=pltpu.VMEM)],
        out_specs=pl.BlockSpec(memory_space=pltpu.VMEM),
        scratch_shapes=[
            pltpu.VMEM((lanes, 2, piece, width), link_dtype),
            pltpu.VMEM((lanes, 2, piece, width), link_dtype),
            pltpu.SemaphoreType.DMA((lanes, 2)),
            pltpu.SemaphoreType.DMA((lanes, 2)),
            pltpu.SemaphoreType.REGULAR((lanes,)),
        ],
        compiler_params=pltpu.CompilerParams(collective_id=1, has_side_effects=True,
                                             vmem_limit_bytes=48 * 1024 * 1024),
    )(h)


QB = 256


def window_allow(tq_ref, tk_ref, a0, w0):
    rows = lax.broadcasted_iota(jnp.int32, (QB, QB + 2 * HALF), 0)
    cols = lax.broadcasted_iota(jnp.int32, (QB, QB + 2 * HALF), 1)
    offset = cols - rows - HALF
    near = jnp.abs(offset) <= HALF
    same = tk_ref[:, pl.ds(w0, QB + 2 * HALF)] == tq_ref[pl.ds(a0, QB), :]
    return near & (same | (offset == 0))


def nt(a, b):
    return lax.dot_general(a, b, (((1,), (1,)), ((), ())), preferred_element_type=jnp.float32)


def tn(a, b):
    return lax.dot_general(a, b, (((0,), (0,)), ((), ())), preferred_element_type=jnp.float32)


def probs_of(q_ref, kv_ref, allow, a0, w0, h):
    q_h = q_ref[pl.ds(a0, QB), pl.ds(h * HEAD, HEAD)]
    k_h = kv_ref[pl.ds(w0, QB + 2 * HALF), pl.ds(h * HEAD, HEAD)]
    scores = jnp.where(allow, nt(q_h, k_h) * 0.125, -1e30)
    largest = jnp.max(scores, axis=-1, keepdims=True)
    raised = jnp.exp(scores - largest)
    return raised / jnp.sum(raised, axis=-1, keepdims=True), q_h, k_h


def neighbours():
    n_seq = lax.axis_size("seq")
    total = lax.axis_size("dp") * n_seq
    me = lax.axis_index("dp") * n_seq + lax.axis_index("seq")
    before = lax.rem(me + total - 1, total)
    after = lax.rem(me + 1, total)
    return (
        (lax.div(before, n_seq), lax.rem(before, n_seq)),
        (lax.div(after, n_seq), lax.rem(after, n_seq)),
    )


def greet(before, after):
    barrier = pltpu.get_barrier_semaphore()
    pl.semaphore_signal(barrier, 1, device_id=before, device_id_type=MESH)
    pl.semaphore_signal(barrier, 1, device_id=after, device_id_type=MESH)
    pl.semaphore_wait(barrier, 2)


def start_of(b):
    return b * QB if isinstance(b, int) else pl.multiple_of(b * QB, QB)


def attn_fwd_kernel(q_ref, kv_ref, tq_ref, tk_ref, o_ref, lo_ref, hi_ref, wide, send_sem, recv_sem):
    width = q_ref.shape[1]
    count = q_ref.shape[0]
    blocks = count // QB
    before, after = neighbours()
    greet(before, after)
    to_before = pltpu.make_async_remote_copy(
        src_ref=kv_ref.at[pl.ds(0, HALF)], dst_ref=hi_ref,
        send_sem=send_sem.at[0], recv_sem=recv_sem.at[0],
        device_id=before, device_id_type=MESH)
    to_after = pltpu.make_async_remote_copy(
        src_ref=kv_ref.at[pl.ds(count - HALF, HALF)], dst_ref=lo_ref,
        send_sem=send_sem.at[1], recv_sem=recv_sem.at[1],
        device_id=after, device_id_type=MESH)
    to_before.start()
    to_after.start()
    wide[pl.ds(HALF, count), :] = kv_ref[...]

    def block(b, carry):
        a0 = start_of(b)
        allow = window_allow(tq_ref, tk_ref, a0, a0)
        for h in range(HEADS):
            probs, _, _ = probs_of(q_ref, wide, allow, a0, a0, h)
            v_h = wide[pl.ds(a0, QB + 2 * HALF), pl.ds(width + h * HEAD, HEAD)]
            mixed = jnp.dot(probs.astype(jnp.bfloat16), v_h, preferred_element_type=jnp.float32)
            o_ref[pl.ds(a0, QB), pl.ds(h * HEAD, HEAD)] = mixed.astype(o_ref.dtype)
        return carry

    lax.fori_loop(1, blocks - 1, block, 0)
    to_before.wait_recv()
    to_after.wait_recv()
    wide[pl.ds(0, HALF), :] = lo_ref[...]
    wide[pl.ds(count + HALF, HALF), :] = hi_ref[...]
    block(0, 0)
    block(blocks - 1, 0)
    to_before.wait_send()
    to_after.wait_send()


def attn_bwd_kernel(q_ref, kv_ref, lo_ref, hi_ref, tq_ref, tk_ref, do_ref, dq_ref, dkv_ref,
                    wide, dwide, send_lo, send_hi, recv_lo, recv_hi, send_sem, recv_sem):
    width = q_ref.shape[1]
    count = q_ref.shape[0]
    blocks = count // QB
    before, after = neighbours()
    greet(before, after)
    wide[pl.ds(0, HALF), :] = lo_ref[...]
    wide[pl.ds(HALF, count), :] = kv_ref[...]
    wide[pl.ds(count + HALF, HALF), :] = hi_ref[...]
    dwide[...] = jnp.zeros(dwide.shape, dwide.dtype)

    def block(b, carry):
        a0 = start_of(b)
        allow = window_allow(tq_ref, tk_ref, a0, a0)
        for h in range(HEADS):
            probs, q_h, k_h = probs_of(q_ref, wide, allow, a0, a0, h)
            v_h = wide[pl.ds(a0, QB + 2 * HALF), pl.ds(width + h * HEAD, HEAD)]
            do_h = do_ref[pl.ds(a0, QB), pl.ds(h * HEAD, HEAD)]
            grad_probs = nt(do_h, v_h)
            inner = jnp.sum(probs * grad_probs, axis=-1, keepdims=True)
            grad_scores = (probs * (grad_probs - inner)).astype(jnp.bfloat16)
            dq_ref[pl.ds(a0, QB), pl.ds(h * HEAD, HEAD)] = (
                jnp.dot(grad_scores, k_h, preferred_element_type=jnp.float32) * 0.125
            )
            rows = pl.ds(a0, QB + 2 * HALF)
            dwide[rows, pl.ds(h * HEAD, HEAD)] += tn(grad_scores, q_h) * 0.125
            dwide[rows, pl.ds(width + h * HEAD, HEAD)] += tn(probs.astype(jnp.bfloat16), do_h)
        return carry

    block(0, 0)
    block(blocks - 1, 0)
    send_lo[...] = dwide[pl.ds(0, HALF), :].astype(send_lo.dtype)
    send_hi[...] = dwide[pl.ds(count + HALF, HALF), :].astype(send_hi.dtype)
    to_before = pltpu.make_async_remote_copy(
        src_ref=send_lo, dst_ref=recv_hi,
        send_sem=send_sem.at[0], recv_sem=recv_sem.at[0],
        device_id=before, device_id_type=MESH)
    to_after = pltpu.make_async_remote_copy(
        src_ref=send_hi, dst_ref=recv_lo,
        send_sem=send_sem.at[1], recv_sem=recv_sem.at[1],
        device_id=after, device_id_type=MESH)
    to_before.start()
    to_after.start()
    lax.fori_loop(1, blocks - 1, block, 0)
    dkv_ref[...] = dwide[pl.ds(HALF, count), :]
    to_before.wait_recv()
    to_after.wait_recv()
    dkv_ref[pl.ds(0, HALF), :] += recv_lo[...].astype(jnp.float32)
    dkv_ref[pl.ds(count - HALF, HALF), :] += recv_hi[...].astype(jnp.float32)
    to_before.wait_send()
    to_after.wait_send()


VMEM_LIMIT = 48 * 1024 * 1024


def attn_fwd(query, kv, tag_q, tag_k):
    count, width = query.shape
    vm = pl.BlockSpec(memory_space=pltpu.VMEM)
    halo = jax.ShapeDtypeStruct((HALF, kv.shape[1]), kv.dtype)
    return pl.pallas_call(
        attn_fwd_kernel,
        out_shape=(jax.ShapeDtypeStruct((count, width), jnp.bfloat16), halo, halo),
        in_specs=[vm] * 4,
        out_specs=(vm, vm, vm),
        scratch_shapes=[
            pltpu.VMEM((count + 2 * HALF, kv.shape[1]), kv.dtype),
            pltpu.SemaphoreType.DMA((2,)),
            pltpu.SemaphoreType.DMA((2,)),
        ],
        compiler_params=pltpu.CompilerParams(
            collective_id=2, has_side_effects=True, vmem_limit_bytes=VMEM_LIMIT
        ),
    )(query, kv, tag_q.reshape(count, 1), tag_k.reshape(1, -1))


def attn_bwd(query, kv, lo, hi, tag_q, tag_k, grad_out):
    count, width = query.shape
    vm = pl.BlockSpec(memory_space=pltpu.VMEM)
    return pl.pallas_call(
        attn_bwd_kernel,
        out_shape=(
            jax.ShapeDtypeStruct((count, width), jnp.float32),
            jax.ShapeDtypeStruct(kv.shape, jnp.float32),
        ),
        in_specs=[vm] * 7,
        out_specs=(vm, vm),
        scratch_shapes=[
            pltpu.VMEM((count + 2 * HALF, kv.shape[1]), kv.dtype),
            pltpu.VMEM((count + 2 * HALF, kv.shape[1]), jnp.float32),
            pltpu.VMEM((HALF, kv.shape[1]), jnp.bfloat16),
            pltpu.VMEM((HALF, kv.shape[1]), jnp.bfloat16),
            pltpu.VMEM((HALF, kv.shape[1]), jnp.bfloat16),
            pltpu.VMEM((HALF, kv.shape[1]), jnp.bfloat16),
            pltpu.SemaphoreType.DMA((2,)),
            pltpu.SemaphoreType.DMA((2,)),
        ],
        compiler_params=pltpu.CompilerParams(
            collective_id=3, has_side_effects=True, vmem_limit_bytes=VMEM_LIMIT
        ),
    )(query, kv, lo, hi, tag_q.reshape(count, 1), tag_k.reshape(1, -1), grad_out)


ROPE_ROWS = 256


def head_rotate(x):
    width = x.shape[-1]
    lane = lax.broadcasted_iota(jnp.int32, x.shape, x.ndim - 1)
    ahead = pltpu.roll(x, width - HEAD // 2, x.ndim - 1)
    behind = pltpu.roll(x, HEAD // 2, x.ndim - 1)
    return jnp.where(lane % HEAD < HEAD // 2, -ahead, behind)


def rope_fwd_kernel(qkv_ref, cos_ref, sin_ref, q_ref, kv_ref):
    width = q_ref.shape[1]
    c = cos_ref[...]
    s = sin_ref[...]
    q = qkv_ref[:, pl.ds(0, width)]
    k = qkv_ref[:, pl.ds(width, width)]
    q_ref[...] = (q * c + head_rotate(q) * s).astype(q_ref.dtype)
    kv_ref[:, pl.ds(0, width)] = (k * c + head_rotate(k) * s).astype(kv_ref.dtype)
    kv_ref[:, pl.ds(width, width)] = qkv_ref[:, pl.ds(2 * width, width)].astype(kv_ref.dtype)


def rope_bwd_kernel(dq_ref, dkv_ref, cos_ref, sin_ref, out_ref):
    width = dq_ref.shape[1]
    c = cos_ref[...]
    s = sin_ref[...]
    dq = dq_ref[...]
    dk = dkv_ref[:, pl.ds(0, width)]
    out_ref[:, pl.ds(0, width)] = (dq * c - head_rotate(dq) * s).astype(out_ref.dtype)
    out_ref[:, pl.ds(width, width)] = (dk * c - head_rotate(dk) * s).astype(out_ref.dtype)
    out_ref[:, pl.ds(2 * width, width)] = dkv_ref[:, pl.ds(width, width)].astype(out_ref.dtype)


def rows_spec(cols):
    return pl.BlockSpec((ROPE_ROWS, cols), lambda i: (i, 0))


def rope_fwd(qkv, cosine, sine):
    count, width = cosine.shape
    return pl.pallas_call(
        rope_fwd_kernel,
        grid=(count // ROPE_ROWS,),
        out_shape=(
            jax.ShapeDtypeStruct((count, width), jnp.bfloat16),
            jax.ShapeDtypeStruct((count, 2 * width), jnp.bfloat16),
        ),
        in_specs=[rows_spec(3 * width), rows_spec(width), rows_spec(width)],
        out_specs=(rows_spec(width), rows_spec(2 * width)),
    )(qkv, cosine, sine)


def rope_bwd(dq, dkv, cosine, sine):
    count, width = cosine.shape
    return pl.pallas_call(
        rope_bwd_kernel,
        grid=(count // ROPE_ROWS,),
        out_shape=jax.ShapeDtypeStruct((count, 3 * width), jnp.bfloat16),
        in_specs=[rows_spec(width), rows_spec(2 * width), rows_spec(width), rows_spec(width)],
        out_specs=rows_spec(3 * width),
    )(dq, dkv, cosine, sine)


def gain_rows(gain, width, rows=8):
    line = jnp.pad(gain, (0, width - gain.shape[0]))
    return jnp.concatenate([line[None], jnp.zeros((rows - 1, width), gain.dtype)], 0)


def gather_rows(payload, n_dp, n_seq):
    every = lax.all_gather(payload, ("dp", "seq"), axis=0, tiled=True)
    return every.reshape(n_dp, n_seq, payload.shape[0], payload.shape[1])


def gain_blocks(grad_gain, n_dp, n_seq, width, height=8):
    part = jnp.pad(grad_gain.reshape(n_seq, -1), ((0, 0), (0, width - grad_gain.shape[0] // n_seq)))
    rows = jnp.concatenate([part[:, None], jnp.zeros((n_seq, height - 1, width), part.dtype)], 1)
    return jnp.broadcast_to(rows[None], (n_dp, n_seq, height, width))


def front(value, n_dp):
    return value.reshape(value.shape[0], n_dp, -1)


def apply_t(left, weight_t, n_dp):
    return jnp.einsum("tdr,dnr->tn", front(left, n_dp), weight_t, preferred_element_type=jnp.float32)


def apply_back(grad, weight_t):
    out = jnp.einsum("tn,dnr->tdr", grad, weight_t, preferred_element_type=jnp.float32)
    return out.reshape(out.shape[0], -1)


def grad_t(grad, left, n_dp):
    width = left.shape[1] // n_dp
    return [
        lax.dot_general(
            grad,
            left[:, d * width : (d + 1) * width],
            (((0,), (0,)), ((), ())),
            preferred_element_type=jnp.float32,
        )
        for d in range(n_dp)
    ]


def on_device(order, tokens, doc_start, real, w_qkv, w_out, w_in, w_down, gain_attn, gain_mlp, cotangent):
    count = tokens.shape[0]
    n_dp, n_seq = lax.axis_size("dp"), lax.axis_size("seq")
    rows, qkv_cols = w_qkv.shape
    out_cols, in_cols = w_out.shape[1], w_in.shape[1]
    down_rows, down_cols = w_down.shape
    down_lines = down_rows * down_cols // rows
    first = gather_rows(
        jnp.concatenate([w_qkv.T, w_out.T, gain_rows(gain_attn, rows)], 0), n_dp, n_seq
    )
    second = gather_rows(
        jnp.concatenate([w_in.T, w_down.T.reshape(down_lines, rows), gain_rows(gain_mlp, rows)], 0),
        n_dp,
        n_seq,
    )
    full_qkv = first[:, :, :qkv_cols].reshape(n_dp, n_seq * qkv_cols, rows)
    full_out = first[:, :, qkv_cols : qkv_cols + out_cols].reshape(n_dp, n_seq * out_cols, rows)
    gain_one = (
        first[0, :, qkv_cols + out_cols, : gain_attn.shape[0]].reshape(-1).astype(jnp.float32)
    )
    stream = tokens.astype(jnp.float32)
    normed_a, factor_a = layer_norm(stream)
    h_attn = (normed_a * gain_one).astype(jnp.bfloat16)
    qkv = apply_t(h_attn, full_qkv, n_dp)
    offset_base = lax.axis_index(("dp", "seq")) * count
    place = (offset_base + jnp.arange(count, dtype=jnp.int32) - doc_start).astype(jnp.float32)
    cosine, sine = rotary_tables(place)
    query, key_value = rope_fwd(qkv, cosine, sine)
    tag_query = doc_start + 1
    tag_key = jnp.where(real == 1, tag_query, 0)
    wide_tag = padded(tag_key, ((("dp", "seq"), 0),), HALF)
    attn_out, halo_lo, halo_hi = attn_fwd(query, key_value, tag_query, wide_tag)
    mid = stream + apply_t(attn_out, full_out, n_dp)
    mid, second = lax.optimization_barrier((mid, second))
    at = 0
    full_in = second[:, :, at : at + in_cols].reshape(n_dp, n_seq * in_cols, rows)
    at += in_cols
    full_down = (
        second[:, :, at : at + down_lines]
        .reshape(n_dp, n_seq, down_cols, down_rows)
        .reshape(n_dp, n_seq * down_cols, down_rows)
    )
    at += down_lines
    gain_two = second[0, :, at, : gain_mlp.shape[0]].reshape(-1).astype(jnp.float32)
    normed_m, factor_m = layer_norm(mid)
    h_mlp = (normed_m * gain_two).astype(jnp.bfloat16)
    gate_up = apply_t(h_mlp, full_in, n_dp)
    hidden_out, glu_pull = jax.vjp(glu_piece, gate_up)
    hidden = hidden_out.astype(jnp.bfloat16)
    result = mid + apply_t(hidden, full_down, n_dp)
    output = result.astype(jnp.bfloat16)
    grad_down = grad_t(cotangent, hidden, n_dp)
    grad_hidden = apply_back(cotangent, full_down)
    grad_gate_up = glu_pull(grad_hidden)[0].astype(jnp.bfloat16)
    grad_inw = grad_t(grad_gate_up, h_mlp, n_dp)
    grad_hmlp = apply_back(grad_gate_up, full_in)
    grad_gain_two = jnp.sum(grad_hmlp * normed_m, axis=0)
    grad_mid = cotangent.astype(jnp.float32) + norm_back(grad_hmlp * gain_two, normed_m, factor_m)
    grad_branch = grad_mid.astype(jnp.bfloat16)
    grad_outw = grad_t(grad_branch, attn_out, n_dp)
    grad_attn = apply_back(grad_branch, full_out).astype(jnp.bfloat16)
    grad_query, grad_kv = attn_bwd(query, key_value, halo_lo, halo_hi, tag_query, wide_tag, grad_attn)
    grad_qkv = rope_bwd(grad_query, grad_kv, cosine, sine)
    grad_qkvw = grad_t(grad_qkv, h_attn, n_dp)
    grad_hattn = apply_back(grad_qkv, full_qkv)
    grad_gain_one = jnp.sum(grad_hattn * normed_a, axis=0)
    grad_tokens = grad_mid + norm_back(grad_hattn * gain_one, normed_a, factor_a)
    height = out_cols + in_cols + down_lines + qkv_cols + 8
    tail = 8 + (-height) % (RING_WAYS * 16)
    gain_both = jnp.concatenate(
        [
            gain_blocks(grad_gain_two, 1, n_seq, rows, 1)[0],
            gain_blocks(grad_gain_one, 1, n_seq, rows, tail - 1)[0],
        ],
        1,
    )
    blocks = jnp.stack(
        [
            jnp.concatenate(
                [
                    *lax.optimization_barrier(
                        (
                            grad_outw[d].reshape(n_seq, out_cols, rows),
                            grad_inw[d].reshape(n_seq, in_cols, rows),
                            grad_down[d]
                            .reshape(n_seq, down_cols, down_rows)
                            .reshape(n_seq, down_lines, rows),
                            grad_qkvw[d].reshape(n_seq, qkv_cols, rows),
                            gain_both,
                        )
                    ),
                ],
                1,
            )
            for d in range(n_dp)
        ]
    )
    depth = blocks.shape[2]
    half = lax.psum_scatter(
        blocks.reshape(n_dp, n_seq * depth, rows).astype(jnp.bfloat16),
        "dp",
        scatter_dimension=0,
        tiled=True,
    )
    late = ring_reduce(half.reshape(n_seq, depth, rows), order, RING_WAYS)
    at = 0
    late_out = late[at : at + out_cols].T
    at += out_cols
    late_in = late[at : at + in_cols].T
    at += in_cols
    late_down = late[at : at + down_lines].reshape(down_cols, down_rows).T
    at += down_lines
    late_qkv = late[at : at + qkv_cols].T
    at += qkv_cols
    late_gain_two = late[at, : gain_mlp.shape[0]]
    late_gain_one = late[at + 1, : gain_attn.shape[0]]
    return (
        output,
        grad_tokens,
        late_qkv,
        late_out,
        late_in,
        late_down,
        late_gain_one,
        late_gain_two,
    )


def solution(mesh):
    placed = (
        P(("dp", "seq"), None),
        P(("dp", "seq")),
        P(("dp", "seq")),
        P("dp", "seq"),
        P("dp", "seq"),
        P("dp", "seq"),
        P("dp", "seq"),
        P("seq"),
        P("seq"),
        P(("dp", "seq"), None),
    )
    return jax.shard_map(
        functools.partial(on_device, ring_order(mesh)),
        mesh=mesh,
        in_specs=placed,
        out_specs=(
            P(("dp", "seq"), None),
            P(("dp", "seq"), None),
            P("dp", "seq"),
            P("dp", "seq"),
            P("dp", "seq"),
            P("dp", "seq"),
            P("seq"),
            P("seq"),
        ),
        check_vma=False,
    )
```

```python
import functools
import math

import jax
import jax.numpy as jnp
from jax import lax
from jax.experimental import pallas as pl
from jax.experimental.pallas import tpu as pltpu
from jax.sharding import PartitionSpec as P

D = 768
HEADS = 12
HEAD = 64
FF = 1152
HALF = 64


def padded(value, sides, width):
    for axis, dim in sides:
        size, length = (lax.axis_size(axis), value.shape[dim])
        up = [(i, (i + 1) % size) for i in range(size - 1)]
        down = [(j, i) for i, j in up]
        last = lax.slice_in_dim(value, length - width, length, axis=dim)
        initial = lax.slice_in_dim(value, 0, width, axis=dim)
        before = lax.ppermute(last, axis, up)
        after = lax.ppermute(initial, axis, down)
        value = jnp.concatenate([before, value, after], axis=dim)
    return value


def shifted(value, axis, by):
    length = lax.axis_size(axis)
    pairs = [(i, i + by) for i in range(length) if 0 <= i + by < length]
    return lax.ppermute(value, axis, pairs)


def layer_norm(value):
    centre = value - jnp.mean(value, axis=-1, keepdims=True)
    factor = lax.rsqrt(jnp.mean(centre * centre, axis=-1, keepdims=True) + 1e-05)
    return (centre * factor, factor)


def norm_back(grad, normed, factor):
    return factor * (
        grad
        - jnp.mean(grad, axis=-1, keepdims=True)
        - normed * jnp.mean(grad * normed, axis=-1, keepdims=True)
    )


def rotary_tables(place):
    freq = jnp.exp(jnp.arange(HEAD // 2, dtype=jnp.float32) * (-2.0 * math.log(10000.0) / HEAD))
    angle = place[:, None] * freq[None, :]
    cosine = jnp.tile(jnp.concatenate([jnp.cos(angle), jnp.cos(angle)], 1), (1, HEADS))
    sine = jnp.tile(jnp.concatenate([jnp.sin(angle), jnp.sin(angle)], 1), (1, HEADS))
    return (cosine, sine)


def rotate(value):
    count = value.shape[0]
    shaped = value.reshape(count, HEADS, HEAD)
    first = shaped[..., : HEAD // 2]
    second = shaped[..., HEAD // 2 :]
    return jnp.concatenate([-second, first], -1).reshape(count, HEADS * HEAD)


def left_dot(left, right):
    return lax.dot_general(
        left, right, (((0,), (0,)), ((), ())), preferred_element_type=jnp.float32
    )


def right_dot(left, right):
    return lax.dot_general(
        left, right, (((1,), (1,)), ((), ())), preferred_element_type=jnp.float32
    )


def glu_piece(gate_up):
    return jax.nn.gelu(gate_up[:, :FF], approximate=False) * gate_up[:, FF:]


MESH = pl.DeviceIdType.MESH


def ring_order(mesh):
    n = mesh.shape["seq"]
    try:
        coords = [tuple(mesh.devices[0, s].coords) for s in range(n)]
    except Exception:
        return list(range(n))
    near = [
        [t for t in range(n) if sum(abs(a - b) for a, b in zip(coords[s], coords[t])) == 1]
        for s in range(n)
    ]
    path, seen = [0], {0}

    def grow(budget=[200000]):
        budget[0] -= 1
        if budget[0] < 0:
            return False
        if len(path) == n:
            return 0 in near[path[-1]]
        options = sorted(
            (t for t in near[path[-1]] if t not in seen),
            key=lambda t: sum(1 for u in near[t] if u not in seen),
        )
        for t in options:
            path.append(t)
            seen.add(t)
            if grow():
                return True
            path.pop()
            seen.discard(t)
        return False

    return list(path) if n > 2 and grow() else list(range(n))


def lookup(index, table):
    n = len(table)
    square = n * n
    total = jnp.int32(0)
    for k, value in enumerate(table):
        if value:
            gap = index - k
            differs = lax.div(gap * gap + (square - 1), jnp.int32(square))
            total = total + value * (1 - differs)
    return total


def ring_kernel(order, per_way, h_ref, out_ref, recv, send, ssem, rsem, free):
    n = len(order)
    where = [0] * n
    for p, s in enumerate(order):
        where[s] = p
    d = lax.axis_index("dp")
    me = lax.axis_index("seq")
    pos = lookup(me, where)
    nxt = lookup(lax.rem(pos + 1, n), order)
    prv = lookup(lax.rem(pos + n - 1, n), order)
    piece = out_ref.shape[0] // per_way
    ahead = (n - 1) // 2
    behind = n - 1 - ahead

    barrier = pltpu.get_barrier_semaphore()
    pl.semaphore_signal(barrier, 1, device_id=(d, nxt), device_id_type=MESH)
    pl.semaphore_signal(barrier, 1, device_id=(d, prv), device_id_type=MESH)
    pl.semaphore_wait(barrier, 2)

    lanes = []
    for forward in (True, False):
        for chunk in range(per_way):
            li = len(lanes)
            lanes.append((recv.at[li], send.at[li], ssem.at[li], rsem.at[li], free.at[li],
                          nxt if forward else prv, prv if forward else nxt,
                          slice(chunk * piece, (chunk + 1) * piece),
                          ahead if forward else behind, forward))
    copies = {}
    for step in range(max(ahead, behind)):
        slot = step % 2
        for li, (recv, send, ssem, rsem, free, to, frm, rows, sends, forward) in enumerate(lanes):
            if step >= sends:
                continue
            if forward:
                target = pos + sends - step
            else:
                target = pos + n - sends + step
            q = lookup(lax.rem(target, n), order)
            own = h_ref[q, rows, :].astype(jnp.float32)
            if step == 0:
                part = own
            else:
                copies[(li, step - 1)].wait_recv()
                part = recv[1 - slot].astype(jnp.float32) + own
                if step <= sends - 2:
                    pl.semaphore_signal(free, 1, device_id=(d, frm), device_id_type=MESH)
            if step >= 2:
                copies[(li, step - 2)].wait_send()
                pl.semaphore_wait(free, 1)
            send[slot] = part.astype(send.dtype)
            c = pltpu.make_async_remote_copy(
                src_ref=send.at[slot], dst_ref=recv.at[slot],
                send_sem=ssem.at[slot], recv_sem=rsem.at[slot],
                device_id=(d, to), device_id_type=MESH)
            c.start()
            copies[(li, step)] = c
    for chunk in range(per_way):
        rows = lanes[chunk][7]
        total = h_ref[me, rows, :].astype(jnp.float32)
        for li in (chunk, per_way + chunk):
            recv, sends = lanes[li][0], lanes[li][8]
            copies[(li, sends - 1)].wait_recv()
            total = total + recv[(sends - 1) % 2].astype(jnp.float32)
        out_ref[rows, :] = total
    for li, lane in enumerate(lanes):
        sends = lane[8]
        if sends >= 2:
            copies[(li, sends - 2)].wait_send()
        copies[(li, sends - 1)].wait_send()


RING_WAYS = 2


def ring_reduce(h, order, per_way, link_dtype=jnp.bfloat16):
    n, rows, width = h.shape
    lanes = 2 * per_way
    piece = rows // per_way
    return pl.pallas_call(
        functools.partial(ring_kernel, tuple(order), per_way),
        out_shape=jax.ShapeDtypeStruct((rows, width), jnp.float32),
        in_specs=[pl.BlockSpec(memory_space=pltpu.VMEM)],
        out_specs=pl.BlockSpec(memory_space=pltpu.VMEM),
        scratch_shapes=[
            pltpu.VMEM((lanes, 2, piece, width), link_dtype),
            pltpu.VMEM((lanes, 2, piece, width), link_dtype),
            pltpu.SemaphoreType.DMA((lanes, 2)),
            pltpu.SemaphoreType.DMA((lanes, 2)),
            pltpu.SemaphoreType.REGULAR((lanes,)),
        ],
        compiler_params=pltpu.CompilerParams(collective_id=1, has_side_effects=True,
                                             vmem_limit_bytes=48 * 1024 * 1024),
    )(h)


QB = 256


def window_allow(tq_ref, tk_ref, a0, w0):
    rows = lax.broadcasted_iota(jnp.int32, (QB, QB + 2 * HALF), 0)
    cols = lax.broadcasted_iota(jnp.int32, (QB, QB + 2 * HALF), 1)
    offset = cols - rows - HALF
    near = jnp.abs(offset) <= HALF
    same = tk_ref[:, pl.ds(w0, QB + 2 * HALF)] == tq_ref[pl.ds(a0, QB), :]
    return near & (same | (offset == 0))


def nt(a, b):
    return lax.dot_general(a, b, (((1,), (1,)), ((), ())), preferred_element_type=jnp.float32)


def tn(a, b):
    return lax.dot_general(a, b, (((0,), (0,)), ((), ())), preferred_element_type=jnp.float32)


def probs_of(q_ref, kv_ref, allow, a0, w0, h):
    q_h = q_ref[pl.ds(a0, QB), pl.ds(h * HEAD, HEAD)]
    k_h = kv_ref[pl.ds(w0, QB + 2 * HALF), pl.ds(h * HEAD, HEAD)]
    scores = jnp.where(allow, nt(q_h, k_h) * 0.125, -1e30)
    largest = jnp.max(scores, axis=-1, keepdims=True)
    raised = jnp.exp(scores - largest)
    return raised / jnp.sum(raised, axis=-1, keepdims=True), q_h, k_h


def neighbours():
    n_seq = lax.axis_size("seq")
    total = lax.axis_size("dp") * n_seq
    me = lax.axis_index("dp") * n_seq + lax.axis_index("seq")
    before = lax.rem(me + total - 1, total)
    after = lax.rem(me + 1, total)
    return (
        (lax.div(before, n_seq), lax.rem(before, n_seq)),
        (lax.div(after, n_seq), lax.rem(after, n_seq)),
    )


def greet(before, after):
    barrier = pltpu.get_barrier_semaphore()
    pl.semaphore_signal(barrier, 1, device_id=before, device_id_type=MESH)
    pl.semaphore_signal(barrier, 1, device_id=after, device_id_type=MESH)
    pl.semaphore_wait(barrier, 2)


def start_of(b):
    return b * QB if isinstance(b, int) else pl.multiple_of(b * QB, QB)


def attn_fwd_kernel(q_ref, kv_ref, tq_ref, tk_ref, o_ref, lo_ref, hi_ref, wide, send_sem, recv_sem):
    width = q_ref.shape[1]
    count = q_ref.shape[0]
    blocks = count // QB
    before, after = neighbours()
    greet(before, after)
    to_before = pltpu.make_async_remote_copy(
        src_ref=kv_ref.at[pl.ds(0, HALF)], dst_ref=hi_ref,
        send_sem=send_sem.at[0], recv_sem=recv_sem.at[0],
        device_id=before, device_id_type=MESH)
    to_after = pltpu.make_async_remote_copy(
        src_ref=kv_ref.at[pl.ds(count - HALF, HALF)], dst_ref=lo_ref,
        send_sem=send_sem.at[1], recv_sem=recv_sem.at[1],
        device_id=after, device_id_type=MESH)
    to_before.start()
    to_after.start()
    wide[pl.ds(HALF, count), :] = kv_ref[...]

    def block(b, carry):
        a0 = start_of(b)
        allow = window_allow(tq_ref, tk_ref, a0, a0)
        for h in range(HEADS):
            probs, _, _ = probs_of(q_ref, wide, allow, a0, a0, h)
            v_h = wide[pl.ds(a0, QB + 2 * HALF), pl.ds(width + h * HEAD, HEAD)]
            mixed = jnp.dot(probs.astype(jnp.bfloat16), v_h, preferred_element_type=jnp.float32)
            o_ref[pl.ds(a0, QB), pl.ds(h * HEAD, HEAD)] = mixed.astype(o_ref.dtype)
        return carry

    lax.fori_loop(1, blocks - 1, block, 0)
    to_before.wait_recv()
    to_after.wait_recv()
    wide[pl.ds(0, HALF), :] = lo_ref[...]
    wide[pl.ds(count + HALF, HALF), :] = hi_ref[...]
    block(0, 0)
    block(blocks - 1, 0)
    to_before.wait_send()
    to_after.wait_send()


def attn_bwd_kernel(q_ref, kv_ref, lo_ref, hi_ref, tq_ref, tk_ref, do_ref, dq_ref, dkv_ref,
                    wide, dwide, send_lo, send_hi, recv_lo, recv_hi, send_sem, recv_sem):
    width = q_ref.shape[1]
    count = q_ref.shape[0]
    blocks = count // QB
    before, after = neighbours()
    greet(before, after)
    wide[pl.ds(0, HALF), :] = lo_ref[...]
    wide[pl.ds(HALF, count), :] = kv_ref[...]
    wide[pl.ds(count + HALF, HALF), :] = hi_ref[...]
    dwide[...] = jnp.zeros(dwide.shape, dwide.dtype)

    def block(b, carry):
        a0 = start_of(b)
        allow = window_allow(tq_ref, tk_ref, a0, a0)
        for h in range(HEADS):
            probs, q_h, k_h = probs_of(q_ref, wide, allow, a0, a0, h)
            v_h = wide[pl.ds(a0, QB + 2 * HALF), pl.ds(width + h * HEAD, HEAD)]
            do_h = do_ref[pl.ds(a0, QB), pl.ds(h * HEAD, HEAD)]
            grad_probs = nt(do_h, v_h)
            inner = jnp.sum(probs * grad_probs, axis=-1, keepdims=True)
            grad_scores = (probs * (grad_probs - inner)).astype(jnp.bfloat16)
            dq_ref[pl.ds(a0, QB), pl.ds(h * HEAD, HEAD)] = (
                jnp.dot(grad_scores, k_h, preferred_element_type=jnp.float32) * 0.125
            )
            rows = pl.ds(a0, QB + 2 * HALF)
            dwide[rows, pl.ds(h * HEAD, HEAD)] += tn(grad_scores, q_h) * 0.125
            dwide[rows, pl.ds(width + h * HEAD, HEAD)] += tn(probs.astype(jnp.bfloat16), do_h)
        return carry

    block(0, 0)
    block(blocks - 1, 0)
    send_lo[...] = dwide[pl.ds(0, HALF), :].astype(send_lo.dtype)
    send_hi[...] = dwide[pl.ds(count + HALF, HALF), :].astype(send_hi.dtype)
    to_before = pltpu.make_async_remote_copy(
        src_ref=send_lo, dst_ref=recv_hi,
        send_sem=send_sem.at[0], recv_sem=recv_sem.at[0],
        device_id=before, device_id_type=MESH)
    to_after = pltpu.make_async_remote_copy(
        src_ref=send_hi, dst_ref=recv_lo,
        send_sem=send_sem.at[1], recv_sem=recv_sem.at[1],
        device_id=after, device_id_type=MESH)
    to_before.start()
    to_after.start()
    lax.fori_loop(1, blocks - 1, block, 0)
    dkv_ref[...] = dwide[pl.ds(HALF, count), :]
    to_before.wait_recv()
    to_after.wait_recv()
    dkv_ref[pl.ds(0, HALF), :] += recv_lo[...].astype(jnp.float32)
    dkv_ref[pl.ds(count - HALF, HALF), :] += recv_hi[...].astype(jnp.float32)
    to_before.wait_send()
    to_after.wait_send()


VMEM_LIMIT = 48 * 1024 * 1024


def attn_fwd(query, kv, tag_q, tag_k):
    count, width = query.shape
    vm = pl.BlockSpec(memory_space=pltpu.VMEM)
    halo = jax.ShapeDtypeStruct((HALF, kv.shape[1]), kv.dtype)
    return pl.pallas_call(
        attn_fwd_kernel,
        out_shape=(jax.ShapeDtypeStruct((count, width), jnp.bfloat16), halo, halo),
        in_specs=[vm] * 4,
        out_specs=(vm, vm, vm),
        scratch_shapes=[
            pltpu.VMEM((count + 2 * HALF, kv.shape[1]), kv.dtype),
            pltpu.SemaphoreType.DMA((2,)),
            pltpu.SemaphoreType.DMA((2,)),
        ],
        compiler_params=pltpu.CompilerParams(
            collective_id=2, has_side_effects=True, vmem_limit_bytes=VMEM_LIMIT
        ),
    )(query, kv, tag_q.reshape(count, 1), tag_k.reshape(1, -1))


def attn_bwd(query, kv, lo, hi, tag_q, tag_k, grad_out):
    count, width = query.shape
    vm = pl.BlockSpec(memory_space=pltpu.VMEM)
    return pl.pallas_call(
        attn_bwd_kernel,
        out_shape=(
            jax.ShapeDtypeStruct((count, width), jnp.float32),
            jax.ShapeDtypeStruct(kv.shape, jnp.float32),
        ),
        in_specs=[vm] * 7,
        out_specs=(vm, vm),
        scratch_shapes=[
            pltpu.VMEM((count + 2 * HALF, kv.shape[1]), kv.dtype),
            pltpu.VMEM((count + 2 * HALF, kv.shape[1]), jnp.float32),
            pltpu.VMEM((HALF, kv.shape[1]), jnp.bfloat16),
            pltpu.VMEM((HALF, kv.shape[1]), jnp.bfloat16),
            pltpu.VMEM((HALF, kv.shape[1]), jnp.bfloat16),
            pltpu.VMEM((HALF, kv.shape[1]), jnp.bfloat16),
            pltpu.SemaphoreType.DMA((2,)),
            pltpu.SemaphoreType.DMA((2,)),
        ],
        compiler_params=pltpu.CompilerParams(
            collective_id=3, has_side_effects=True, vmem_limit_bytes=VMEM_LIMIT
        ),
    )(query, kv, lo, hi, tag_q.reshape(count, 1), tag_k.reshape(1, -1), grad_out)


ROPE_ROWS = 256


def head_rotate(x):
    width = x.shape[-1]
    lane = lax.broadcasted_iota(jnp.int32, x.shape, x.ndim - 1)
    ahead = pltpu.roll(x, width - HEAD // 2, x.ndim - 1)
    behind = pltpu.roll(x, HEAD // 2, x.ndim - 1)
    return jnp.where(lane % HEAD < HEAD // 2, -ahead, behind)


def rope_fwd_kernel(qkv_ref, cos_ref, sin_ref, q_ref, kv_ref):
    width = q_ref.shape[1]
    c = cos_ref[...]
    s = sin_ref[...]
    q = qkv_ref[:, pl.ds(0, width)]
    k = qkv_ref[:, pl.ds(width, width)]
    q_ref[...] = (q * c + head_rotate(q) * s).astype(q_ref.dtype)
    kv_ref[:, pl.ds(0, width)] = (k * c + head_rotate(k) * s).astype(kv_ref.dtype)
    kv_ref[:, pl.ds(width, width)] = qkv_ref[:, pl.ds(2 * width, width)].astype(kv_ref.dtype)


def rope_bwd_kernel(dq_ref, dkv_ref, cos_ref, sin_ref, out_ref):
    width = dq_ref.shape[1]
    c = cos_ref[...]
    s = sin_ref[...]
    dq = dq_ref[...]
    dk = dkv_ref[:, pl.ds(0, width)]
    out_ref[:, pl.ds(0, width)] = (dq * c - head_rotate(dq) * s).astype(out_ref.dtype)
    out_ref[:, pl.ds(width, width)] = (dk * c - head_rotate(dk) * s).astype(out_ref.dtype)
    out_ref[:, pl.ds(2 * width, width)] = dkv_ref[:, pl.ds(width, width)].astype(out_ref.dtype)


def rows_spec(cols):
    return pl.BlockSpec((ROPE_ROWS, cols), lambda i: (i, 0))


def rope_fwd(qkv, cosine, sine):
    count, width = cosine.shape
    return pl.pallas_call(
        rope_fwd_kernel,
        grid=(count // ROPE_ROWS,),
        out_shape=(
            jax.ShapeDtypeStruct((count, width), jnp.bfloat16),
            jax.ShapeDtypeStruct((count, 2 * width), jnp.bfloat16),
        ),
        in_specs=[rows_spec(3 * width), rows_spec(width), rows_spec(width)],
        out_specs=(rows_spec(width), rows_spec(2 * width)),
    )(qkv, cosine, sine)


def rope_bwd(dq, dkv, cosine, sine):
    count, width = cosine.shape
    return pl.pallas_call(
        rope_bwd_kernel,
        grid=(count // ROPE_ROWS,),
        out_shape=jax.ShapeDtypeStruct((count, 3 * width), jnp.bfloat16),
        in_specs=[rows_spec(width), rows_spec(2 * width), rows_spec(width), rows_spec(width)],
        out_specs=rows_spec(3 * width),
    )(dq, dkv, cosine, sine)


def down_lines_of(block, width):
    cols, extra = block.shape[0] // 2, block.shape[1] - width
    return block[:, :width], jnp.concatenate([block[:cols, width:], block[cols:, width:]], 1)


def down_from_lines(lines, width):
    cols = lines.shape[2] * 2 // 3
    extra = width // 2
    head, tail = lines[:, :, :cols], lines[:, :, cols:]
    tail = jnp.concatenate([tail[..., :extra], tail[..., extra:]], 2)
    return jnp.concatenate([head, tail], 3)


def gain_rows(gain, width, rows=8):
    line = jnp.pad(gain, (0, width - gain.shape[0]))
    return jnp.concatenate([line[None], jnp.zeros((rows - 1, width), gain.dtype)], 0)


def gather_rows(payload, n_dp, n_seq):
    every = lax.all_gather(payload, ("dp", "seq"), axis=0, tiled=True)
    return every.reshape(n_dp, n_seq, payload.shape[0], payload.shape[1])


def gain_blocks(grad_gain, n_dp, n_seq, width, height=8):
    part = jnp.pad(grad_gain.reshape(n_seq, -1), ((0, 0), (0, width - grad_gain.shape[0] // n_seq)))
    rows = jnp.concatenate([part[:, None], jnp.zeros((n_seq, height - 1, width), part.dtype)], 1)
    return jnp.broadcast_to(rows[None], (n_dp, n_seq, height, width))


def front(value, n_dp):
    return value.reshape(value.shape[0], n_dp, -1)


def apply_t(left, weight_t, n_dp):
    return jnp.einsum("tdr,dnr->tn", front(left, n_dp), weight_t, preferred_element_type=jnp.float32)


def apply_back(grad, weight_t):
    out = jnp.einsum("tn,dnr->tdr", grad, weight_t, preferred_element_type=jnp.float32)
    return out.reshape(out.shape[0], -1)


def grad_t(grad, left, n_dp):
    width = left.shape[1] // n_dp
    return [
        lax.dot_general(
            grad,
            left[:, d * width : (d + 1) * width],
            (((0,), (0,)), ((), ())),
            preferred_element_type=jnp.float32,
        )
        for d in range(n_dp)
    ]


def on_device(order, tokens, doc_start, real, w_qkv, w_out, w_in, w_down, gain_attn, gain_mlp, cotangent):
    count = tokens.shape[0]
    n_dp, n_seq = lax.axis_size("dp"), lax.axis_size("seq")
    rows, qkv_cols = w_qkv.shape
    out_cols, in_cols = w_out.shape[1], w_in.shape[1]
    down_rows, down_cols = w_down.shape
    down_lines = down_rows * down_cols // rows
    first = gather_rows(
        jnp.concatenate([w_qkv.T, w_out.T, gain_rows(gain_attn, rows)], 0), n_dp, n_seq
    )
    second = gather_rows(
        jnp.concatenate([w_in.T, *down_lines_of(w_down.T, rows), gain_rows(gain_mlp, rows)], 0),
        n_dp,
        n_seq,
    )
    full_qkv = first[:, :, :qkv_cols].reshape(n_dp, n_seq * qkv_cols, rows)
    full_out = first[:, :, qkv_cols : qkv_cols + out_cols].reshape(n_dp, n_seq * out_cols, rows)
    gain_one = (
        first[0, :, qkv_cols + out_cols, : gain_attn.shape[0]].reshape(-1).astype(jnp.float32)
    )
    stream = tokens.astype(jnp.float32)
    normed_a, factor_a = layer_norm(stream)
    h_attn = (normed_a * gain_one).astype(jnp.bfloat16)
    qkv = apply_t(h_attn, full_qkv, n_dp)
    offset_base = lax.axis_index(("dp", "seq")) * count
    place = (offset_base + jnp.arange(count, dtype=jnp.int32) - doc_start).astype(jnp.float32)
    cosine, sine = rotary_tables(place)
    query, key_value = rope_fwd(qkv, cosine, sine)
    tag_query = doc_start + 1
    tag_key = jnp.where(real == 1, tag_query, 0)
    wide_tag = padded(tag_key, ((("dp", "seq"), 0),), HALF)
    attn_out, halo_lo, halo_hi = attn_fwd(query, key_value, tag_query, wide_tag)
    mid = stream + apply_t(attn_out, full_out, n_dp)
    mid, second = lax.optimization_barrier((mid, second))
    at = 0
    full_in = second[:, :, at : at + in_cols].reshape(n_dp, n_seq * in_cols, rows)
    at += in_cols
    full_down = down_from_lines(second[:, :, at : at + down_lines], rows).reshape(
        n_dp, n_seq * down_cols, down_rows
    )
    at += down_lines
    gain_two = second[0, :, at, : gain_mlp.shape[0]].reshape(-1).astype(jnp.float32)
    normed_m, factor_m = layer_norm(mid)
    h_mlp = (normed_m * gain_two).astype(jnp.bfloat16)
    gate_up = apply_t(h_mlp, full_in, n_dp)
    hidden_out, glu_pull = jax.vjp(glu_piece, gate_up)
    hidden = hidden_out.astype(jnp.bfloat16)
    result = mid + apply_t(hidden, full_down, n_dp)
    output = result.astype(jnp.bfloat16)
    grad_down = grad_t(cotangent, hidden, n_dp)
    grad_hidden = apply_back(cotangent, full_down)
    grad_gate_up = glu_pull(grad_hidden)[0].astype(jnp.bfloat16)
    grad_inw = grad_t(grad_gate_up, h_mlp, n_dp)
    grad_hmlp = apply_back(grad_gate_up, full_in)
    grad_gain_two = jnp.sum(grad_hmlp * normed_m, axis=0)
    grad_mid = cotangent.astype(jnp.float32) + norm_back(grad_hmlp * gain_two, normed_m, factor_m)
    grad_branch = grad_mid.astype(jnp.bfloat16)
    grad_outw = grad_t(grad_branch, attn_out, n_dp)
    grad_attn = apply_back(grad_branch, full_out).astype(jnp.bfloat16)
    grad_query, grad_kv = attn_bwd(query, key_value, halo_lo, halo_hi, tag_query, wide_tag, grad_attn)
    grad_qkv = rope_bwd(grad_query, grad_kv, cosine, sine)
    grad_qkvw = grad_t(grad_qkv, h_attn, n_dp)
    grad_hattn = apply_back(grad_qkv, full_qkv)
    grad_gain_one = jnp.sum(grad_hattn * normed_a, axis=0)
    grad_tokens = grad_mid + norm_back(grad_hattn * gain_one, normed_a, factor_a)
    height = out_cols + in_cols + down_lines + qkv_cols + 8
    tail = 8 + (-height) % (RING_WAYS * 16)
    gain_both = jnp.concatenate(
        [
            gain_blocks(grad_gain_two, 1, n_seq, rows, 1)[0],
            gain_blocks(grad_gain_one, 1, n_seq, rows, tail - 1)[0],
        ],
        1,
    )
    blocks = jnp.stack(
        [
            jnp.concatenate(
                [
                    *lax.optimization_barrier(
                        (
                            grad_outw[d].reshape(n_seq, out_cols, rows),
                            grad_inw[d].reshape(n_seq, in_cols, rows),
                            grad_down[d]
                            .reshape(n_seq, down_cols, down_rows)
                            .reshape(n_seq, down_lines, rows),
                            grad_qkvw[d].reshape(n_seq, qkv_cols, rows),
                            gain_both,
                        )
                    ),
                ],
                1,
            )
            for d in range(n_dp)
        ]
    )
    depth = blocks.shape[2]
    half = lax.psum_scatter(
        blocks.reshape(n_dp, n_seq * depth, rows).astype(jnp.bfloat16),
        "dp",
        scatter_dimension=0,
        tiled=True,
    )
    late = ring_reduce(half.reshape(n_seq, depth, rows), order, RING_WAYS)
    at = 0
    late_out = late[at : at + out_cols].T
    at += out_cols
    late_in = late[at : at + in_cols].T
    at += in_cols
    late_down = late[at : at + down_lines].reshape(down_cols, down_rows).T
    at += down_lines
    late_qkv = late[at : at + qkv_cols].T
    at += qkv_cols
    late_gain_two = late[at, : gain_mlp.shape[0]]
    late_gain_one = late[at + 1, : gain_attn.shape[0]]
    return (
        output,
        grad_tokens,
        late_qkv,
        late_out,
        late_in,
        late_down,
        late_gain_one,
        late_gain_two,
    )


def solution(mesh):
    placed = (
        P(("dp", "seq"), None),
        P(("dp", "seq")),
        P(("dp", "seq")),
        P("dp", "seq"),
        P("dp", "seq"),
        P("dp", "seq"),
        P("dp", "seq"),
        P("seq"),
        P("seq"),
        P(("dp", "seq"), None),
    )
    return jax.shard_map(
        functools.partial(on_device, ring_order(mesh)),
        mesh=mesh,
        in_specs=placed,
        out_specs=(
            P(("dp", "seq"), None),
            P(("dp", "seq"), None),
            P("dp", "seq"),
            P("dp", "seq"),
            P("dp", "seq"),
            P("dp", "seq"),
            P("seq"),
            P("seq"),
        ),
        check_vma=False,
    )
```

```python
import functools
import math

import jax
import jax.numpy as jnp
from jax import lax
from jax.experimental import pallas as pl
from jax.experimental.pallas import tpu as pltpu
from jax.sharding import PartitionSpec as P

D = 768
HEADS = 12
HEAD = 64
FF = 1152
HALF = 64


def padded(value, sides, width):
    for axis, dim in sides:
        size, length = (lax.axis_size(axis), value.shape[dim])
        up = [(i, (i + 1) % size) for i in range(size - 1)]
        down = [(j, i) for i, j in up]
        last = lax.slice_in_dim(value, length - width, length, axis=dim)
        initial = lax.slice_in_dim(value, 0, width, axis=dim)
        before = lax.ppermute(last, axis, up)
        after = lax.ppermute(initial, axis, down)
        value = jnp.concatenate([before, value, after], axis=dim)
    return value


def shifted(value, axis, by):
    length = lax.axis_size(axis)
    pairs = [(i, i + by) for i in range(length) if 0 <= i + by < length]
    return lax.ppermute(value, axis, pairs)


def layer_norm(value):
    centre = value - jnp.mean(value, axis=-1, keepdims=True)
    factor = lax.rsqrt(jnp.mean(centre * centre, axis=-1, keepdims=True) + 1e-05)
    return (centre * factor, factor)


def norm_back(grad, normed, factor):
    return factor * (
        grad
        - jnp.mean(grad, axis=-1, keepdims=True)
        - normed * jnp.mean(grad * normed, axis=-1, keepdims=True)
    )


def rotary_tables(place):
    freq = jnp.exp(jnp.arange(HEAD // 2, dtype=jnp.float32) * (-2.0 * math.log(10000.0) / HEAD))
    angle = place[:, None] * freq[None, :]
    cosine = jnp.tile(jnp.concatenate([jnp.cos(angle), jnp.cos(angle)], 1), (1, HEADS))
    sine = jnp.tile(jnp.concatenate([jnp.sin(angle), jnp.sin(angle)], 1), (1, HEADS))
    return (cosine, sine)


def rotate(value):
    count = value.shape[0]
    shaped = value.reshape(count, HEADS, HEAD)
    first = shaped[..., : HEAD // 2]
    second = shaped[..., HEAD // 2 :]
    return jnp.concatenate([-second, first], -1).reshape(count, HEADS * HEAD)


def left_dot(left, right):
    return lax.dot_general(
        left, right, (((0,), (0,)), ((), ())), preferred_element_type=jnp.float32
    )


def right_dot(left, right):
    return lax.dot_general(
        left, right, (((1,), (1,)), ((), ())), preferred_element_type=jnp.float32
    )


def glu_piece(gate_up):
    return jax.nn.gelu(gate_up[:, :FF], approximate=False) * gate_up[:, FF:]


MESH = pl.DeviceIdType.MESH


def ring_order(mesh):
    n = mesh.shape["seq"]
    try:
        coords = [tuple(mesh.devices[0, s].coords) for s in range(n)]
    except Exception:
        return list(range(n))
    near = [
        [t for t in range(n) if sum(abs(a - b) for a, b in zip(coords[s], coords[t])) == 1]
        for s in range(n)
    ]
    path, seen = [0], {0}

    def grow(budget=[200000]):
        budget[0] -= 1
        if budget[0] < 0:
            return False
        if len(path) == n:
            return 0 in near[path[-1]]
        options = sorted(
            (t for t in near[path[-1]] if t not in seen),
            key=lambda t: sum(1 for u in near[t] if u not in seen),
        )
        for t in options:
            path.append(t)
            seen.add(t)
            if grow():
                return True
            path.pop()
            seen.discard(t)
        return False

    return list(path) if n > 2 and grow() else list(range(n))


def lookup(index, table):
    n = len(table)
    square = n * n
    total = jnp.int32(0)
    for k, value in enumerate(table):
        if value:
            gap = index - k
            differs = lax.div(gap * gap + (square - 1), jnp.int32(square))
            total = total + value * (1 - differs)
    return total


def ring_kernel(order, per_way, h_ref, out_ref, recv, send, ssem, rsem, free):
    n = len(order)
    where = [0] * n
    for p, s in enumerate(order):
        where[s] = p
    d = lax.axis_index("dp")
    me = lax.axis_index("seq")
    pos = lookup(me, where)
    nxt = lookup(lax.rem(pos + 1, n), order)
    prv = lookup(lax.rem(pos + n - 1, n), order)
    piece = out_ref.shape[0] // per_way
    ahead = (n - 1) // 2
    behind = n - 1 - ahead

    barrier = pltpu.get_barrier_semaphore()
    pl.semaphore_signal(barrier, 1, device_id=(d, nxt), device_id_type=MESH)
    pl.semaphore_signal(barrier, 1, device_id=(d, prv), device_id_type=MESH)
    pl.semaphore_wait(barrier, 2)

    lanes = []
    for forward in (True, False):
        for chunk in range(per_way):
            li = len(lanes)
            lanes.append((recv.at[li], send.at[li], ssem.at[li], rsem.at[li], free.at[li],
                          nxt if forward else prv, prv if forward else nxt,
                          slice(chunk * piece, (chunk + 1) * piece),
                          ahead if forward else behind, forward))
    copies = {}
    for step in range(max(ahead, behind)):
        slot = step % 2
        for li, (recv, send, ssem, rsem, free, to, frm, rows, sends, forward) in enumerate(lanes):
            if step >= sends:
                continue
            if forward:
                target = pos + sends - step
            else:
                target = pos + n - sends + step
            q = lookup(lax.rem(target, n), order)
            own = h_ref[q, rows, :].astype(jnp.float32)
            if step == 0:
                part = own
            else:
                copies[(li, step - 1)].wait_recv()
                part = recv[1 - slot].astype(jnp.float32) + own
                if step <= sends - 2:
                    pl.semaphore_signal(free, 1, device_id=(d, frm), device_id_type=MESH)
            if step >= 2:
                copies[(li, step - 2)].wait_send()
                pl.semaphore_wait(free, 1)
            send[slot] = part.astype(send.dtype)
            c = pltpu.make_async_remote_copy(
                src_ref=send.at[slot], dst_ref=recv.at[slot],
                send_sem=ssem.at[slot], recv_sem=rsem.at[slot],
                device_id=(d, to), device_id_type=MESH)
            c.start()
            copies[(li, step)] = c
    for chunk in range(per_way):
        rows = lanes[chunk][7]
        total = h_ref[me, rows, :].astype(jnp.float32)
        for li in (chunk, per_way + chunk):
            recv, sends = lanes[li][0], lanes[li][8]
            copies[(li, sends - 1)].wait_recv()
            total = total + recv[(sends - 1) % 2].astype(jnp.float32)
        out_ref[rows, :] = total
    for li, lane in enumerate(lanes):
        sends = lane[8]
        if sends >= 2:
            copies[(li, sends - 2)].wait_send()
        copies[(li, sends - 1)].wait_send()


RING_WAYS = 2


def ring_reduce(h, order, per_way, link_dtype=jnp.bfloat16):
    n, rows, width = h.shape
    lanes = 2 * per_way
    piece = rows // per_way
    return pl.pallas_call(
        functools.partial(ring_kernel, tuple(order), per_way),
        out_shape=jax.ShapeDtypeStruct((rows, width), jnp.float32),
        in_specs=[pl.BlockSpec(memory_space=pltpu.VMEM)],
        out_specs=pl.BlockSpec(memory_space=pltpu.VMEM),
        scratch_shapes=[
            pltpu.VMEM((lanes, 2, piece, width), link_dtype),
            pltpu.VMEM((lanes, 2, piece, width), link_dtype),
            pltpu.SemaphoreType.DMA((lanes, 2)),
            pltpu.SemaphoreType.DMA((lanes, 2)),
            pltpu.SemaphoreType.REGULAR((lanes,)),
        ],
        compiler_params=pltpu.CompilerParams(collective_id=1, has_side_effects=True,
                                             vmem_limit_bytes=48 * 1024 * 1024),
    )(h)


QB = 256


def window_allow(tq_ref, tk_ref, a0, w0):
    rows = lax.broadcasted_iota(jnp.int32, (QB, QB + 2 * HALF), 0)
    cols = lax.broadcasted_iota(jnp.int32, (QB, QB + 2 * HALF), 1)
    offset = cols - rows - HALF
    near = jnp.abs(offset) <= HALF
    same = tk_ref[:, pl.ds(w0, QB + 2 * HALF)] == tq_ref[pl.ds(a0, QB), :]
    return near & (same | (offset == 0))


def nt(a, b):
    return lax.dot_general(a, b, (((1,), (1,)), ((), ())), preferred_element_type=jnp.float32)


def tn(a, b):
    return lax.dot_general(a, b, (((0,), (0,)), ((), ())), preferred_element_type=jnp.float32)


def probs_of(q_ref, kv_ref, allow, a0, w0, h):
    q_h = q_ref[pl.ds(a0, QB), pl.ds(h * HEAD, HEAD)]
    k_h = kv_ref[pl.ds(w0, QB + 2 * HALF), pl.ds(h * HEAD, HEAD)]
    scores = jnp.where(allow, nt(q_h, k_h) * 0.125, -1e30)
    largest = jnp.max(scores, axis=-1, keepdims=True)
    raised = jnp.exp(scores - largest)
    return raised / jnp.sum(raised, axis=-1, keepdims=True), q_h, k_h


def neighbours():
    n_seq = lax.axis_size("seq")
    total = lax.axis_size("dp") * n_seq
    me = lax.axis_index("dp") * n_seq + lax.axis_index("seq")
    before = lax.rem(me + total - 1, total)
    after = lax.rem(me + 1, total)
    return (
        (lax.div(before, n_seq), lax.rem(before, n_seq)),
        (lax.div(after, n_seq), lax.rem(after, n_seq)),
    )


def greet(before, after):
    barrier = pltpu.get_barrier_semaphore()
    pl.semaphore_signal(barrier, 1, device_id=before, device_id_type=MESH)
    pl.semaphore_signal(barrier, 1, device_id=after, device_id_type=MESH)
    return barrier


def start_of(b):
    return b * QB if isinstance(b, int) else pl.multiple_of(b * QB, QB)


def attn_fwd_kernel(q_ref, kv_ref, tq_ref, tk_ref, o_ref, lo_ref, hi_ref, wide, send_sem, recv_sem):
    width = q_ref.shape[1]
    count = q_ref.shape[0]
    blocks = count // QB
    before, after = neighbours()
    barrier = greet(before, after)
    to_before = pltpu.make_async_remote_copy(
        src_ref=kv_ref.at[pl.ds(0, HALF)], dst_ref=hi_ref,
        send_sem=send_sem.at[0], recv_sem=recv_sem.at[0],
        device_id=before, device_id_type=MESH)
    to_after = pltpu.make_async_remote_copy(
        src_ref=kv_ref.at[pl.ds(count - HALF, HALF)], dst_ref=lo_ref,
        send_sem=send_sem.at[1], recv_sem=recv_sem.at[1],
        device_id=after, device_id_type=MESH)
    wide[pl.ds(HALF, count), :] = kv_ref[...]

    def block(b, carry):
        a0 = start_of(b)
        allow = window_allow(tq_ref, tk_ref, a0, a0)
        for h in range(HEADS):
            probs, _, _ = probs_of(q_ref, wide, allow, a0, a0, h)
            v_h = wide[pl.ds(a0, QB + 2 * HALF), pl.ds(width + h * HEAD, HEAD)]
            mixed = jnp.dot(probs.astype(jnp.bfloat16), v_h, preferred_element_type=jnp.float32)
            o_ref[pl.ds(a0, QB), pl.ds(h * HEAD, HEAD)] = mixed.astype(o_ref.dtype)
        return carry

    block(1, 0)
    pl.semaphore_wait(barrier, 2)
    to_before.start()
    to_after.start()
    lax.fori_loop(2, blocks - 1, block, 0)
    to_before.wait_recv()
    to_after.wait_recv()
    wide[pl.ds(0, HALF), :] = lo_ref[...]
    wide[pl.ds(count + HALF, HALF), :] = hi_ref[...]
    block(0, 0)
    block(blocks - 1, 0)
    to_before.wait_send()
    to_after.wait_send()


def attn_bwd_kernel(q_ref, kv_ref, lo_ref, hi_ref, tq_ref, tk_ref, do_ref, dq_ref, dkv_ref,
                    wide, dwide, send_lo, send_hi, recv_lo, recv_hi, send_sem, recv_sem):
    width = q_ref.shape[1]
    count = q_ref.shape[0]
    blocks = count // QB
    before, after = neighbours()
    barrier = greet(before, after)
    wide[pl.ds(0, HALF), :] = lo_ref[...]
    wide[pl.ds(HALF, count), :] = kv_ref[...]
    wide[pl.ds(count + HALF, HALF), :] = hi_ref[...]
    dwide[...] = jnp.zeros(dwide.shape, dwide.dtype)

    def block(b, carry):
        a0 = start_of(b)
        allow = window_allow(tq_ref, tk_ref, a0, a0)
        for h in range(HEADS):
            probs, q_h, k_h = probs_of(q_ref, wide, allow, a0, a0, h)
            v_h = wide[pl.ds(a0, QB + 2 * HALF), pl.ds(width + h * HEAD, HEAD)]
            do_h = do_ref[pl.ds(a0, QB), pl.ds(h * HEAD, HEAD)]
            grad_probs = nt(do_h, v_h)
            inner = jnp.sum(probs * grad_probs, axis=-1, keepdims=True)
            grad_scores = (probs * (grad_probs - inner)).astype(jnp.bfloat16)
            dq_ref[pl.ds(a0, QB), pl.ds(h * HEAD, HEAD)] = (
                jnp.dot(grad_scores, k_h, preferred_element_type=jnp.float32) * 0.125
            )
            rows = pl.ds(a0, QB + 2 * HALF)
            dwide[rows, pl.ds(h * HEAD, HEAD)] += tn(grad_scores, q_h) * 0.125
            dwide[rows, pl.ds(width + h * HEAD, HEAD)] += tn(probs.astype(jnp.bfloat16), do_h)
        return carry

    block(0, 0)
    block(blocks - 1, 0)
    send_lo[...] = dwide[pl.ds(0, HALF), :].astype(send_lo.dtype)
    send_hi[...] = dwide[pl.ds(count + HALF, HALF), :].astype(send_hi.dtype)
    to_before = pltpu.make_async_remote_copy(
        src_ref=send_lo, dst_ref=recv_hi,
        send_sem=send_sem.at[0], recv_sem=recv_sem.at[0],
        device_id=before, device_id_type=MESH)
    to_after = pltpu.make_async_remote_copy(
        src_ref=send_hi, dst_ref=recv_lo,
        send_sem=send_sem.at[1], recv_sem=recv_sem.at[1],
        device_id=after, device_id_type=MESH)
    pl.semaphore_wait(barrier, 2)
    to_before.start()
    to_after.start()
    lax.fori_loop(1, blocks - 1, block, 0)
    dkv_ref[...] = dwide[pl.ds(HALF, count), :]
    to_before.wait_recv()
    to_after.wait_recv()
    dkv_ref[pl.ds(0, HALF), :] += recv_lo[...].astype(jnp.float32)
    dkv_ref[pl.ds(count - HALF, HALF), :] += recv_hi[...].astype(jnp.float32)
    to_before.wait_send()
    to_after.wait_send()


VMEM_LIMIT = 48 * 1024 * 1024


def attn_fwd(query, kv, tag_q, tag_k):
    count, width = query.shape
    vm = pl.BlockSpec(memory_space=pltpu.VMEM)
    halo = jax.ShapeDtypeStruct((HALF, kv.shape[1]), kv.dtype)
    return pl.pallas_call(
        attn_fwd_kernel,
        out_shape=(jax.ShapeDtypeStruct((count, width), jnp.bfloat16), halo, halo),
        in_specs=[vm] * 4,
        out_specs=(vm, vm, vm),
        scratch_shapes=[
            pltpu.VMEM((count + 2 * HALF, kv.shape[1]), kv.dtype),
            pltpu.SemaphoreType.DMA((2,)),
            pltpu.SemaphoreType.DMA((2,)),
        ],
        compiler_params=pltpu.CompilerParams(
            collective_id=2, has_side_effects=True, vmem_limit_bytes=VMEM_LIMIT
        ),
    )(query, kv, tag_q.reshape(count, 1), tag_k.reshape(1, -1))


def attn_bwd(query, kv, lo, hi, tag_q, tag_k, grad_out):
    count, width = query.shape
    vm = pl.BlockSpec(memory_space=pltpu.VMEM)
    return pl.pallas_call(
        attn_bwd_kernel,
        out_shape=(
            jax.ShapeDtypeStruct((count, width), jnp.float32),
            jax.ShapeDtypeStruct(kv.shape, jnp.float32),
        ),
        in_specs=[vm] * 7,
        out_specs=(vm, vm),
        scratch_shapes=[
            pltpu.VMEM((count + 2 * HALF, kv.shape[1]), kv.dtype),
            pltpu.VMEM((count + 2 * HALF, kv.shape[1]), jnp.float32),
            pltpu.VMEM((HALF, kv.shape[1]), jnp.bfloat16),
            pltpu.VMEM((HALF, kv.shape[1]), jnp.bfloat16),
            pltpu.VMEM((HALF, kv.shape[1]), jnp.bfloat16),
            pltpu.VMEM((HALF, kv.shape[1]), jnp.bfloat16),
            pltpu.SemaphoreType.DMA((2,)),
            pltpu.SemaphoreType.DMA((2,)),
        ],
        compiler_params=pltpu.CompilerParams(
            collective_id=3, has_side_effects=True, vmem_limit_bytes=VMEM_LIMIT
        ),
    )(query, kv, lo, hi, tag_q.reshape(count, 1), tag_k.reshape(1, -1), grad_out)


ROPE_ROWS = 256


def head_rotate(x):
    width = x.shape[-1]
    lane = lax.broadcasted_iota(jnp.int32, x.shape, x.ndim - 1)
    ahead = pltpu.roll(x, width - HEAD // 2, x.ndim - 1)
    behind = pltpu.roll(x, HEAD // 2, x.ndim - 1)
    return jnp.where(lane % HEAD < HEAD // 2, -ahead, behind)


def rope_fwd_kernel(qkv_ref, cos_ref, sin_ref, q_ref, kv_ref):
    width = q_ref.shape[1]
    c = cos_ref[...]
    s = sin_ref[...]
    q = qkv_ref[:, pl.ds(0, width)]
    k = qkv_ref[:, pl.ds(width, width)]
    q_ref[...] = (q * c + head_rotate(q) * s).astype(q_ref.dtype)
    kv_ref[:, pl.ds(0, width)] = (k * c + head_rotate(k) * s).astype(kv_ref.dtype)
    kv_ref[:, pl.ds(width, width)] = qkv_ref[:, pl.ds(2 * width, width)].astype(kv_ref.dtype)


def rope_bwd_kernel(dq_ref, dkv_ref, cos_ref, sin_ref, out_ref):
    width = dq_ref.shape[1]
    c = cos_ref[...]
    s = sin_ref[...]
    dq = dq_ref[...]
    dk = dkv_ref[:, pl.ds(0, width)]
    out_ref[:, pl.ds(0, width)] = (dq * c - head_rotate(dq) * s).astype(out_ref.dtype)
    out_ref[:, pl.ds(width, width)] = (dk * c - head_rotate(dk) * s).astype(out_ref.dtype)
    out_ref[:, pl.ds(2 * width, width)] = dkv_ref[:, pl.ds(width, width)].astype(out_ref.dtype)


def rows_spec(cols):
    return pl.BlockSpec((ROPE_ROWS, cols), lambda i: (i, 0))


def rope_fwd(qkv, cosine, sine):
    count, width = cosine.shape
    return pl.pallas_call(
        rope_fwd_kernel,
        grid=(count // ROPE_ROWS,),
        out_shape=(
            jax.ShapeDtypeStruct((count, width), jnp.bfloat16),
            jax.ShapeDtypeStruct((count, 2 * width), jnp.bfloat16),
        ),
        in_specs=[rows_spec(3 * width), rows_spec(width), rows_spec(width)],
        out_specs=(rows_spec(width), rows_spec(2 * width)),
    )(qkv, cosine, sine)


def rope_bwd(dq, dkv, cosine, sine):
    count, width = cosine.shape
    return pl.pallas_call(
        rope_bwd_kernel,
        grid=(count // ROPE_ROWS,),
        out_shape=jax.ShapeDtypeStruct((count, 3 * width), jnp.bfloat16),
        in_specs=[rows_spec(width), rows_spec(2 * width), rows_spec(width), rows_spec(width)],
        out_specs=rows_spec(3 * width),
    )(dq, dkv, cosine, sine)


def down_lines_of(block, width):
    cols, extra = block.shape[0] // 2, block.shape[1] - width
    return block[:, :width], jnp.concatenate([block[:cols, width:], block[cols:, width:]], 1)


def down_from_lines(lines, width):
    cols = lines.shape[2] * 2 // 3
    extra = width // 2
    head, tail = lines[:, :, :cols], lines[:, :, cols:]
    tail = jnp.concatenate([tail[..., :extra], tail[..., extra:]], 2)
    return jnp.concatenate([head, tail], 3)


def gain_rows(gain, width, rows=8):
    line = jnp.pad(gain, (0, width - gain.shape[0]))
    return jnp.concatenate([line[None], jnp.zeros((rows - 1, width), gain.dtype)], 0)


def gather_rows(payload, n_dp, n_seq):
    every = lax.all_gather(payload, ("dp", "seq"), axis=0, tiled=True)
    return every.reshape(n_dp, n_seq, payload.shape[0], payload.shape[1])


def gain_blocks(grad_gain, n_dp, n_seq, width, height=8):
    part = jnp.pad(grad_gain.reshape(n_seq, -1), ((0, 0), (0, width - grad_gain.shape[0] // n_seq)))
    rows = jnp.concatenate([part[:, None], jnp.zeros((n_seq, height - 1, width), part.dtype)], 1)
    return jnp.broadcast_to(rows[None], (n_dp, n_seq, height, width))


def front(value, n_dp):
    return value.reshape(value.shape[0], n_dp, -1)


def apply_t(left, weight_t, n_dp):
    return jnp.einsum("tdr,dnr->tn", front(left, n_dp), weight_t, preferred_element_type=jnp.float32)


def apply_back(grad, weight_t):
    out = jnp.einsum("tn,dnr->tdr", grad, weight_t, preferred_element_type=jnp.float32)
    return out.reshape(out.shape[0], -1)


def grad_t(grad, left, n_dp):
    width = left.shape[1] // n_dp
    return [
        lax.dot_general(
            grad,
            left[:, d * width : (d + 1) * width],
            (((0,), (0,)), ((), ())),
            preferred_element_type=jnp.float32,
        )
        for d in range(n_dp)
    ]


def on_device(order, tokens, doc_start, real, w_qkv, w_out, w_in, w_down, gain_attn, gain_mlp, cotangent):
    count = tokens.shape[0]
    n_dp, n_seq = lax.axis_size("dp"), lax.axis_size("seq")
    rows, qkv_cols = w_qkv.shape
    out_cols, in_cols = w_out.shape[1], w_in.shape[1]
    down_rows, down_cols = w_down.shape
    down_lines = down_rows * down_cols // rows
    first = gather_rows(
        jnp.concatenate([w_qkv.T, w_out.T, gain_rows(gain_attn, rows)], 0), n_dp, n_seq
    )
    second = gather_rows(
        jnp.concatenate([w_in.T, *down_lines_of(w_down.T, rows), gain_rows(gain_mlp, rows)], 0),
        n_dp,
        n_seq,
    )
    full_qkv = first[:, :, :qkv_cols].reshape(n_dp, n_seq * qkv_cols, rows)
    full_out = first[:, :, qkv_cols : qkv_cols + out_cols].reshape(n_dp, n_seq * out_cols, rows)
    gain_one = (
        first[0, :, qkv_cols + out_cols, : gain_attn.shape[0]].reshape(-1).astype(jnp.float32)
    )
    stream = tokens.astype(jnp.float32)
    normed_a, factor_a = layer_norm(stream)
    h_attn = (normed_a * gain_one).astype(jnp.bfloat16)
    qkv = apply_t(h_attn, full_qkv, n_dp)
    offset_base = lax.axis_index(("dp", "seq")) * count
    place = (offset_base + jnp.arange(count, dtype=jnp.int32) - doc_start).astype(jnp.float32)
    cosine, sine = rotary_tables(place)
    query, key_value = rope_fwd(qkv, cosine, sine)
    tag_query = doc_start + 1
    tag_key = jnp.where(real == 1, tag_query, 0)
    wide_tag = padded(tag_key, ((("dp", "seq"), 0),), HALF)
    attn_out, halo_lo, halo_hi = attn_fwd(query, key_value, tag_query, wide_tag)
    mid = stream + apply_t(attn_out, full_out, n_dp)
    mid, second = lax.optimization_barrier((mid, second))
    at = 0
    full_in = second[:, :, at : at + in_cols].reshape(n_dp, n_seq * in_cols, rows)
    at += in_cols
    full_down = down_from_lines(second[:, :, at : at + down_lines], rows).reshape(
        n_dp, n_seq * down_cols, down_rows
    )
    at += down_lines
    gain_two = second[0, :, at, : gain_mlp.shape[0]].reshape(-1).astype(jnp.float32)
    normed_m, factor_m = layer_norm(mid)
    h_mlp = (normed_m * gain_two).astype(jnp.bfloat16)
    gate_up = apply_t(h_mlp, full_in, n_dp)
    hidden_out, glu_pull = jax.vjp(glu_piece, gate_up)
    hidden = hidden_out.astype(jnp.bfloat16)
    result = mid + apply_t(hidden, full_down, n_dp)
    output = result.astype(jnp.bfloat16)
    grad_down = grad_t(cotangent, hidden, n_dp)
    grad_hidden = apply_back(cotangent, full_down)
    grad_gate_up = glu_pull(grad_hidden)[0].astype(jnp.bfloat16)
    grad_inw = grad_t(grad_gate_up, h_mlp, n_dp)
    grad_hmlp = apply_back(grad_gate_up, full_in)
    grad_gain_two = jnp.sum(grad_hmlp * normed_m, axis=0)
    grad_mid = cotangent.astype(jnp.float32) + norm_back(grad_hmlp * gain_two, normed_m, factor_m)
    grad_branch = grad_mid.astype(jnp.bfloat16)
    grad_outw = grad_t(grad_branch, attn_out, n_dp)
    grad_attn = apply_back(grad_branch, full_out).astype(jnp.bfloat16)
    grad_query, grad_kv = attn_bwd(query, key_value, halo_lo, halo_hi, tag_query, wide_tag, grad_attn)
    grad_qkv = rope_bwd(grad_query, grad_kv, cosine, sine)
    grad_qkvw = grad_t(grad_qkv, h_attn, n_dp)
    grad_hattn = apply_back(grad_qkv, full_qkv)
    grad_gain_one = jnp.sum(grad_hattn * normed_a, axis=0)
    grad_tokens = grad_mid + norm_back(grad_hattn * gain_one, normed_a, factor_a)
    height = out_cols + in_cols + down_lines + qkv_cols + 8
    tail = 8 + (-height) % (RING_WAYS * 16)
    gain_both = jnp.concatenate(
        [
            gain_blocks(grad_gain_two, 1, n_seq, rows, 1)[0],
            gain_blocks(grad_gain_one, 1, n_seq, rows, tail - 1)[0],
        ],
        1,
    )
    blocks = jnp.stack(
        [
            jnp.concatenate(
                [
                    *lax.optimization_barrier(
                        (
                            grad_outw[d].reshape(n_seq, out_cols, rows),
                            grad_inw[d].reshape(n_seq, in_cols, rows),
                            grad_down[d]
                            .reshape(n_seq, down_cols, down_rows)
                            .reshape(n_seq, down_lines, rows),
                            grad_qkvw[d].reshape(n_seq, qkv_cols, rows),
                            gain_both,
                        )
                    ),
                ],
                1,
            )
            for d in range(n_dp)
        ]
    )
    depth = blocks.shape[2]
    half = lax.psum_scatter(
        blocks.reshape(n_dp, n_seq * depth, rows).astype(jnp.bfloat16),
        "dp",
        scatter_dimension=0,
        tiled=True,
    )
    late = ring_reduce(half.reshape(n_seq, depth, rows), order, RING_WAYS)
    at = 0
    late_out = late[at : at + out_cols].T
    at += out_cols
    late_in = late[at : at + in_cols].T
    at += in_cols
    late_down = late[at : at + down_lines].reshape(down_cols, down_rows).T
    at += down_lines
    late_qkv = late[at : at + qkv_cols].T
    at += qkv_cols
    late_gain_two = late[at, : gain_mlp.shape[0]]
    late_gain_one = late[at + 1, : gain_attn.shape[0]]
    return (
        output,
        grad_tokens,
        late_qkv,
        late_out,
        late_in,
        late_down,
        late_gain_one,
        late_gain_two,
    )


def solution(mesh):
    placed = (
        P(("dp", "seq"), None),
        P(("dp", "seq")),
        P(("dp", "seq")),
        P("dp", "seq"),
        P("dp", "seq"),
        P("dp", "seq"),
        P("dp", "seq"),
        P("seq"),
        P("seq"),
        P(("dp", "seq"), None),
    )
    return jax.shard_map(
        functools.partial(on_device, ring_order(mesh)),
        mesh=mesh,
        in_specs=placed,
        out_specs=(
            P(("dp", "seq"), None),
            P(("dp", "seq"), None),
            P("dp", "seq"),
            P("dp", "seq"),
            P("dp", "seq"),
            P("dp", "seq"),
            P("seq"),
            P("seq"),
        ),
        check_vma=False,
    )
```

```python
import functools
import math

import jax
import jax.numpy as jnp
from jax import lax
from jax.experimental import pallas as pl
from jax.experimental.pallas import tpu as pltpu
from jax.sharding import PartitionSpec as P

D = 768
HEADS = 12
HEAD = 64
FF = 1152
HALF = 64


def padded(value, sides, width):
    for axis, dim in sides:
        size, length = (lax.axis_size(axis), value.shape[dim])
        up = [(i, (i + 1) % size) for i in range(size - 1)]
        down = [(j, i) for i, j in up]
        last = lax.slice_in_dim(value, length - width, length, axis=dim)
        initial = lax.slice_in_dim(value, 0, width, axis=dim)
        before = lax.ppermute(last, axis, up)
        after = lax.ppermute(initial, axis, down)
        value = jnp.concatenate([before, value, after], axis=dim)
    return value


def shifted(value, axis, by):
    length = lax.axis_size(axis)
    pairs = [(i, i + by) for i in range(length) if 0 <= i + by < length]
    return lax.ppermute(value, axis, pairs)


def layer_norm(value):
    centre = value - jnp.mean(value, axis=-1, keepdims=True)
    factor = lax.rsqrt(jnp.mean(centre * centre, axis=-1, keepdims=True) + 1e-05)
    return (centre * factor, factor)


def norm_back(grad, normed, factor):
    return factor * (
        grad
        - jnp.mean(grad, axis=-1, keepdims=True)
        - normed * jnp.mean(grad * normed, axis=-1, keepdims=True)
    )


def rotary_tables(place):
    freq = jnp.exp(jnp.arange(HEAD // 2, dtype=jnp.float32) * (-2.0 * math.log(10000.0) / HEAD))
    angle = place[:, None] * freq[None, :]
    cosine = jnp.tile(jnp.concatenate([jnp.cos(angle), jnp.cos(angle)], 1), (1, HEADS))
    sine = jnp.tile(jnp.concatenate([jnp.sin(angle), jnp.sin(angle)], 1), (1, HEADS))
    return (cosine, sine)


def rotate(value):
    count = value.shape[0]
    shaped = value.reshape(count, HEADS, HEAD)
    first = shaped[..., : HEAD // 2]
    second = shaped[..., HEAD // 2 :]
    return jnp.concatenate([-second, first], -1).reshape(count, HEADS * HEAD)


def left_dot(left, right):
    return lax.dot_general(
        left, right, (((0,), (0,)), ((), ())), preferred_element_type=jnp.float32
    )


def right_dot(left, right):
    return lax.dot_general(
        left, right, (((1,), (1,)), ((), ())), preferred_element_type=jnp.float32
    )


def glu_piece(gate_up):
    return jax.nn.gelu(gate_up[:, :FF], approximate=False) * gate_up[:, FF:]


MESH = pl.DeviceIdType.MESH


def ring_order(mesh):
    n = mesh.shape["seq"]
    try:
        coords = [tuple(mesh.devices[0, s].coords) for s in range(n)]
    except Exception:
        return list(range(n))
    near = [
        [t for t in range(n) if sum(abs(a - b) for a, b in zip(coords[s], coords[t])) == 1]
        for s in range(n)
    ]
    path, seen = [0], {0}

    def grow(budget=[200000]):
        budget[0] -= 1
        if budget[0] < 0:
            return False
        if len(path) == n:
            return 0 in near[path[-1]]
        options = sorted(
            (t for t in near[path[-1]] if t not in seen),
            key=lambda t: sum(1 for u in near[t] if u not in seen),
        )
        for t in options:
            path.append(t)
            seen.add(t)
            if grow():
                return True
            path.pop()
            seen.discard(t)
        return False

    return list(path) if n > 2 and grow() else list(range(n))


def lookup(index, table):
    n = len(table)
    square = n * n
    total = jnp.int32(0)
    for k, value in enumerate(table):
        if value:
            gap = index - k
            differs = lax.div(gap * gap + (square - 1), jnp.int32(square))
            total = total + value * (1 - differs)
    return total


def ring_kernel(order, per_way, h_ref, out_ref, recv, send, ssem, rsem, free):
    n = len(order)
    where = [0] * n
    for p, s in enumerate(order):
        where[s] = p
    d = lax.axis_index("dp")
    me = lax.axis_index("seq")
    pos = lookup(me, where)
    nxt = lookup(lax.rem(pos + 1, n), order)
    prv = lookup(lax.rem(pos + n - 1, n), order)
    piece = out_ref.shape[0] // per_way
    ahead = (n - 1) // 2
    behind = n - 1 - ahead

    barrier = pltpu.get_barrier_semaphore()
    pl.semaphore_signal(barrier, 1, device_id=(d, nxt), device_id_type=MESH)
    pl.semaphore_signal(barrier, 1, device_id=(d, prv), device_id_type=MESH)
    pl.semaphore_wait(barrier, 2)

    lanes = []
    for forward in (True, False):
        for chunk in range(per_way):
            li = len(lanes)
            lanes.append((recv.at[li], send.at[li], ssem.at[li], rsem.at[li], free.at[li],
                          nxt if forward else prv, prv if forward else nxt,
                          slice(chunk * piece, (chunk + 1) * piece),
                          ahead if forward else behind, forward))
    copies = {}
    for step in range(max(ahead, behind)):
        slot = step % 2
        for li, (recv, send, ssem, rsem, free, to, frm, rows, sends, forward) in enumerate(lanes):
            if step >= sends:
                continue
            if forward:
                target = pos + sends - step
            else:
                target = pos + n - sends + step
            q = lookup(lax.rem(target, n), order)
            own = h_ref[q, rows, :].astype(jnp.float32)
            if step == 0:
                part = own
            else:
                copies[(li, step - 1)].wait_recv()
                part = recv[1 - slot].astype(jnp.float32) + own
                if step <= sends - 2:
                    pl.semaphore_signal(free, 1, device_id=(d, frm), device_id_type=MESH)
            if step >= 2:
                copies[(li, step - 2)].wait_send()
                pl.semaphore_wait(free, 1)
            send[slot] = part.astype(send.dtype)
            c = pltpu.make_async_remote_copy(
                src_ref=send.at[slot], dst_ref=recv.at[slot],
                send_sem=ssem.at[slot], recv_sem=rsem.at[slot],
                device_id=(d, to), device_id_type=MESH)
            c.start()
            copies[(li, step)] = c
    for chunk in range(per_way):
        rows = lanes[chunk][7]
        total = h_ref[me, rows, :].astype(jnp.float32)
        for li in (chunk, per_way + chunk):
            recv, sends = lanes[li][0], lanes[li][8]
            copies[(li, sends - 1)].wait_recv()
            total = total + recv[(sends - 1) % 2].astype(jnp.float32)
        out_ref[rows, :] = total
    for li, lane in enumerate(lanes):
        sends = lane[8]
        if sends >= 2:
            copies[(li, sends - 2)].wait_send()
        copies[(li, sends - 1)].wait_send()


RING_WAYS = 2


def ring_reduce(h, order, per_way, link_dtype=jnp.bfloat16):
    n, rows, width = h.shape
    lanes = 2 * per_way
    piece = rows // per_way
    return pl.pallas_call(
        functools.partial(ring_kernel, tuple(order), per_way),
        out_shape=jax.ShapeDtypeStruct((rows, width), jnp.float32),
        in_specs=[pl.BlockSpec(memory_space=pltpu.VMEM)],
        out_specs=pl.BlockSpec(memory_space=pltpu.VMEM),
        scratch_shapes=[
            pltpu.VMEM((lanes, 2, piece, width), link_dtype),
            pltpu.VMEM((lanes, 2, piece, width), link_dtype),
            pltpu.SemaphoreType.DMA((lanes, 2)),
            pltpu.SemaphoreType.DMA((lanes, 2)),
            pltpu.SemaphoreType.REGULAR((lanes,)),
        ],
        compiler_params=pltpu.CompilerParams(collective_id=1, has_side_effects=True,
                                             vmem_limit_bytes=48 * 1024 * 1024),
    )(h)


QB = 256


def window_allow(tq_ref, tk_ref, a0, w0):
    rows = lax.broadcasted_iota(jnp.int32, (QB, QB + 2 * HALF), 0)
    cols = lax.broadcasted_iota(jnp.int32, (QB, QB + 2 * HALF), 1)
    offset = cols - rows - HALF
    near = jnp.abs(offset) <= HALF
    same = tk_ref[:, pl.ds(w0, QB + 2 * HALF)] == tq_ref[pl.ds(a0, QB), :]
    return near & (same | (offset == 0))


def nt(a, b):
    return lax.dot_general(a, b, (((1,), (1,)), ((), ())), preferred_element_type=jnp.float32)


def tn(a, b):
    return lax.dot_general(a, b, (((0,), (0,)), ((), ())), preferred_element_type=jnp.float32)


def probs_of(q_ref, kv_ref, allow, a0, w0, h):
    q_h = q_ref[pl.ds(a0, QB), pl.ds(h * HEAD, HEAD)]
    k_h = kv_ref[pl.ds(w0, QB + 2 * HALF), pl.ds(h * HEAD, HEAD)]
    scores = jnp.where(allow, nt(q_h, k_h) * 0.125, -1e30)
    largest = jnp.max(scores, axis=-1, keepdims=True)
    raised = jnp.exp(scores - largest)
    return raised / jnp.sum(raised, axis=-1, keepdims=True), q_h, k_h


def neighbours():
    n_seq = lax.axis_size("seq")
    total = lax.axis_size("dp") * n_seq
    me = lax.axis_index("dp") * n_seq + lax.axis_index("seq")
    before = lax.rem(me + total - 1, total)
    after = lax.rem(me + 1, total)
    return (
        (lax.div(before, n_seq), lax.rem(before, n_seq)),
        (lax.div(after, n_seq), lax.rem(after, n_seq)),
    )


def greet(before, after):
    barrier = pltpu.get_barrier_semaphore()
    pl.semaphore_signal(barrier, 1, device_id=before, device_id_type=MESH)
    pl.semaphore_signal(barrier, 1, device_id=after, device_id_type=MESH)
    return barrier


def start_of(b):
    return b * QB if isinstance(b, int) else pl.multiple_of(b * QB, QB)


def attn_fwd_kernel(q_ref, kv_ref, tq_ref, tk_ref, o_ref, lo_ref, hi_ref, wide, send_sem, recv_sem):
    width = q_ref.shape[1]
    count = q_ref.shape[0]
    blocks = count // QB
    before, after = neighbours()
    barrier = greet(before, after)
    to_before = pltpu.make_async_remote_copy(
        src_ref=kv_ref.at[pl.ds(0, HALF)], dst_ref=hi_ref,
        send_sem=send_sem.at[0], recv_sem=recv_sem.at[0],
        device_id=before, device_id_type=MESH)
    to_after = pltpu.make_async_remote_copy(
        src_ref=kv_ref.at[pl.ds(count - HALF, HALF)], dst_ref=lo_ref,
        send_sem=send_sem.at[1], recv_sem=recv_sem.at[1],
        device_id=after, device_id_type=MESH)
    wide[pl.ds(HALF, count), :] = kv_ref[...]

    def block(b, carry):
        a0 = start_of(b)
        allow = window_allow(tq_ref, tk_ref, a0, a0)
        for h in range(HEADS):
            probs, _, _ = probs_of(q_ref, wide, allow, a0, a0, h)
            v_h = wide[pl.ds(a0, QB + 2 * HALF), pl.ds(width + h * HEAD, HEAD)]
            mixed = jnp.dot(probs.astype(jnp.bfloat16), v_h, preferred_element_type=jnp.float32)
            o_ref[pl.ds(a0, QB), pl.ds(h * HEAD, HEAD)] = mixed.astype(o_ref.dtype)
        return carry

    block(1, 0)
    pl.semaphore_wait(barrier, 2)
    to_before.start()
    to_after.start()
    lax.fori_loop(2, blocks - 1, block, 0)
    to_before.wait_recv()
    to_after.wait_recv()
    wide[pl.ds(0, HALF), :] = lo_ref[...]
    wide[pl.ds(count + HALF, HALF), :] = hi_ref[...]
    block(0, 0)
    block(blocks - 1, 0)
    to_before.wait_send()
    to_after.wait_send()


def attn_bwd_kernel(q_ref, kv_ref, lo_ref, hi_ref, tq_ref, tk_ref, do_ref, cos_ref, sin_ref, g_ref,
                    dq_ref, wide, dwide, send_lo, send_hi, recv_lo, recv_hi, send_sem, recv_sem):
    width = q_ref.shape[1]
    count = q_ref.shape[0]
    blocks = count // QB
    before, after = neighbours()
    barrier = greet(before, after)
    wide[pl.ds(0, HALF), :] = lo_ref[...]
    wide[pl.ds(HALF, count), :] = kv_ref[...]
    wide[pl.ds(count + HALF, HALF), :] = hi_ref[...]
    dwide[...] = jnp.zeros(dwide.shape, dwide.dtype)

    def block(b, carry):
        a0 = start_of(b)
        allow = window_allow(tq_ref, tk_ref, a0, a0)
        for h in range(HEADS):
            probs, q_h, k_h = probs_of(q_ref, wide, allow, a0, a0, h)
            v_h = wide[pl.ds(a0, QB + 2 * HALF), pl.ds(width + h * HEAD, HEAD)]
            do_h = do_ref[pl.ds(a0, QB), pl.ds(h * HEAD, HEAD)]
            grad_probs = nt(do_h, v_h)
            inner = jnp.sum(probs * grad_probs, axis=-1, keepdims=True)
            grad_scores = (probs * (grad_probs - inner)).astype(jnp.bfloat16)
            dq_ref[pl.ds(a0, QB), pl.ds(h * HEAD, HEAD)] = (
                jnp.dot(grad_scores, k_h, preferred_element_type=jnp.float32) * 0.125
            )
            rows = pl.ds(a0, QB + 2 * HALF)
            dwide[rows, pl.ds(h * HEAD, HEAD)] += tn(grad_scores, q_h) * 0.125
            dwide[rows, pl.ds(width + h * HEAD, HEAD)] += tn(probs.astype(jnp.bfloat16), do_h)
        return carry

    block(0, 0)
    block(blocks - 1, 0)
    send_lo[...] = dwide[pl.ds(0, HALF), :].astype(send_lo.dtype)
    send_hi[...] = dwide[pl.ds(count + HALF, HALF), :].astype(send_hi.dtype)
    to_before = pltpu.make_async_remote_copy(
        src_ref=send_lo, dst_ref=recv_hi,
        send_sem=send_sem.at[0], recv_sem=recv_sem.at[0],
        device_id=before, device_id_type=MESH)
    to_after = pltpu.make_async_remote_copy(
        src_ref=send_hi, dst_ref=recv_lo,
        send_sem=send_sem.at[1], recv_sem=recv_sem.at[1],
        device_id=after, device_id_type=MESH)
    pl.semaphore_wait(barrier, 2)
    to_before.start()
    to_after.start()
    lax.fori_loop(1, blocks - 1, block, 0)
    to_before.wait_recv()
    to_after.wait_recv()
    dwide[pl.ds(HALF, HALF), :] += recv_lo[...].astype(jnp.float32)
    dwide[pl.ds(count, HALF), :] += recv_hi[...].astype(jnp.float32)
    for chunk in range(count // ROPE_ROWS):
        r0 = chunk * ROPE_ROWS
        c = cos_ref[pl.ds(r0, ROPE_ROWS), :]
        s = sin_ref[pl.ds(r0, ROPE_ROWS), :]
        dq = dq_ref[pl.ds(r0, ROPE_ROWS), :]
        dk = dwide[pl.ds(HALF + r0, ROPE_ROWS), pl.ds(0, width)]
        g_ref[pl.ds(r0, ROPE_ROWS), pl.ds(0, width)] = (dq * c - head_rotate(dq) * s).astype(g_ref.dtype)
        g_ref[pl.ds(r0, ROPE_ROWS), pl.ds(width, width)] = (dk * c - head_rotate(dk) * s).astype(g_ref.dtype)
        g_ref[pl.ds(r0, ROPE_ROWS), pl.ds(2 * width, width)] = dwide[
            pl.ds(HALF + r0, ROPE_ROWS), pl.ds(width, width)
        ].astype(g_ref.dtype)
    to_before.wait_send()
    to_after.wait_send()


VMEM_LIMIT = 48 * 1024 * 1024


def attn_fwd(query, kv, tag_q, tag_k):
    count, width = query.shape
    vm = pl.BlockSpec(memory_space=pltpu.VMEM)
    halo = jax.ShapeDtypeStruct((HALF, kv.shape[1]), kv.dtype)
    return pl.pallas_call(
        attn_fwd_kernel,
        out_shape=(jax.ShapeDtypeStruct((count, width), jnp.bfloat16), halo, halo),
        in_specs=[vm] * 4,
        out_specs=(vm, vm, vm),
        scratch_shapes=[
            pltpu.VMEM((count + 2 * HALF, kv.shape[1]), kv.dtype),
            pltpu.SemaphoreType.DMA((2,)),
            pltpu.SemaphoreType.DMA((2,)),
        ],
        compiler_params=pltpu.CompilerParams(
            collective_id=2, has_side_effects=True, vmem_limit_bytes=VMEM_LIMIT
        ),
    )(query, kv, tag_q.reshape(count, 1), tag_k.reshape(1, -1))


def attn_bwd(query, kv, lo, hi, tag_q, tag_k, grad_out, cosine, sine):
    count, width = query.shape
    vm = pl.BlockSpec(memory_space=pltpu.VMEM)
    return pl.pallas_call(
        attn_bwd_kernel,
        out_shape=jax.ShapeDtypeStruct((count, 3 * width), jnp.bfloat16),
        in_specs=[vm] * 9,
        out_specs=vm,
        scratch_shapes=[
            pltpu.VMEM((count, width), jnp.float32),
            pltpu.VMEM((count + 2 * HALF, kv.shape[1]), kv.dtype),
            pltpu.VMEM((count + 2 * HALF, kv.shape[1]), jnp.float32),
            pltpu.VMEM((HALF, kv.shape[1]), jnp.bfloat16),
            pltpu.VMEM((HALF, kv.shape[1]), jnp.bfloat16),
            pltpu.VMEM((HALF, kv.shape[1]), jnp.bfloat16),
            pltpu.VMEM((HALF, kv.shape[1]), jnp.bfloat16),
            pltpu.SemaphoreType.DMA((2,)),
            pltpu.SemaphoreType.DMA((2,)),
        ],
        compiler_params=pltpu.CompilerParams(
            collective_id=3, has_side_effects=True, vmem_limit_bytes=VMEM_LIMIT
        ),
    )(query, kv, lo, hi, tag_q.reshape(count, 1), tag_k.reshape(1, -1), grad_out, cosine, sine)


ROPE_ROWS = 256


def head_rotate(x):
    width = x.shape[-1]
    lane = lax.broadcasted_iota(jnp.int32, x.shape, x.ndim - 1)
    ahead = pltpu.roll(x, width - HEAD // 2, x.ndim - 1)
    behind = pltpu.roll(x, HEAD // 2, x.ndim - 1)
    return jnp.where(lane % HEAD < HEAD // 2, -ahead, behind)


def rope_fwd_kernel(qkv_ref, cos_ref, sin_ref, q_ref, kv_ref):
    width = q_ref.shape[1]
    c = cos_ref[...]
    s = sin_ref[...]
    q = qkv_ref[:, pl.ds(0, width)]
    k = qkv_ref[:, pl.ds(width, width)]
    q_ref[...] = (q * c + head_rotate(q) * s).astype(q_ref.dtype)
    kv_ref[:, pl.ds(0, width)] = (k * c + head_rotate(k) * s).astype(kv_ref.dtype)
    kv_ref[:, pl.ds(width, width)] = qkv_ref[:, pl.ds(2 * width, width)].astype(kv_ref.dtype)


def rope_bwd_kernel(dq_ref, dkv_ref, cos_ref, sin_ref, out_ref):
    width = dq_ref.shape[1]
    c = cos_ref[...]
    s = sin_ref[...]
    dq = dq_ref[...]
    dk = dkv_ref[:, pl.ds(0, width)]
    out_ref[:, pl.ds(0, width)] = (dq * c - head_rotate(dq) * s).astype(out_ref.dtype)
    out_ref[:, pl.ds(width, width)] = (dk * c - head_rotate(dk) * s).astype(out_ref.dtype)
    out_ref[:, pl.ds(2 * width, width)] = dkv_ref[:, pl.ds(width, width)].astype(out_ref.dtype)


def rows_spec(cols):
    return pl.BlockSpec((ROPE_ROWS, cols), lambda i: (i, 0))


def rope_fwd(qkv, cosine, sine):
    count, width = cosine.shape
    return pl.pallas_call(
        rope_fwd_kernel,
        grid=(count // ROPE_ROWS,),
        out_shape=(
            jax.ShapeDtypeStruct((count, width), jnp.bfloat16),
            jax.ShapeDtypeStruct((count, 2 * width), jnp.bfloat16),
        ),
        in_specs=[rows_spec(3 * width), rows_spec(width), rows_spec(width)],
        out_specs=(rows_spec(width), rows_spec(2 * width)),
    )(qkv, cosine, sine)


def rope_bwd(dq, dkv, cosine, sine):
    count, width = cosine.shape
    return pl.pallas_call(
        rope_bwd_kernel,
        grid=(count // ROPE_ROWS,),
        out_shape=jax.ShapeDtypeStruct((count, 3 * width), jnp.bfloat16),
        in_specs=[rows_spec(width), rows_spec(2 * width), rows_spec(width), rows_spec(width)],
        out_specs=rows_spec(3 * width),
    )(dq, dkv, cosine, sine)


def down_lines_of(block, width):
    cols, extra = block.shape[0] // 2, block.shape[1] - width
    return block[:, :width], jnp.concatenate([block[:cols, width:], block[cols:, width:]], 1)


def down_from_lines(lines, width):
    cols = lines.shape[2] * 2 // 3
    extra = width // 2
    head, tail = lines[:, :, :cols], lines[:, :, cols:]
    tail = jnp.concatenate([tail[..., :extra], tail[..., extra:]], 2)
    return jnp.concatenate([head, tail], 3)


def gain_rows(gain, width, rows=8):
    line = jnp.pad(gain, (0, width - gain.shape[0]))
    return jnp.concatenate([line[None], jnp.zeros((rows - 1, width), gain.dtype)], 0)


def gather_rows(payload, n_dp, n_seq):
    every = lax.all_gather(payload, ("dp", "seq"), axis=0, tiled=True)
    return every.reshape(n_dp, n_seq, payload.shape[0], payload.shape[1])


def gain_blocks(grad_gain, n_dp, n_seq, width, height=8):
    part = jnp.pad(grad_gain.reshape(n_seq, -1), ((0, 0), (0, width - grad_gain.shape[0] // n_seq)))
    rows = jnp.concatenate([part[:, None], jnp.zeros((n_seq, height - 1, width), part.dtype)], 1)
    return jnp.broadcast_to(rows[None], (n_dp, n_seq, height, width))


def front(value, n_dp):
    return value.reshape(value.shape[0], n_dp, -1)


def apply_t(left, weight_t, n_dp):
    return jnp.einsum("tdr,dnr->tn", front(left, n_dp), weight_t, preferred_element_type=jnp.float32)


def apply_back(grad, weight_t):
    out = jnp.einsum("tn,dnr->tdr", grad, weight_t, preferred_element_type=jnp.float32)
    return out.reshape(out.shape[0], -1)


def grad_t(grad, left, n_dp):
    width = left.shape[1] // n_dp
    return [
        lax.dot_general(
            grad,
            left[:, d * width : (d + 1) * width],
            (((0,), (0,)), ((), ())),
            preferred_element_type=jnp.float32,
        )
        for d in range(n_dp)
    ]


def on_device(order, tokens, doc_start, real, w_qkv, w_out, w_in, w_down, gain_attn, gain_mlp, cotangent):
    count = tokens.shape[0]
    n_dp, n_seq = lax.axis_size("dp"), lax.axis_size("seq")
    rows, qkv_cols = w_qkv.shape
    out_cols, in_cols = w_out.shape[1], w_in.shape[1]
    down_rows, down_cols = w_down.shape
    down_lines = down_rows * down_cols // rows
    first = gather_rows(
        jnp.concatenate([w_qkv.T, w_out.T, gain_rows(gain_attn, rows)], 0), n_dp, n_seq
    )
    second = gather_rows(
        jnp.concatenate([w_in.T, *down_lines_of(w_down.T, rows), gain_rows(gain_mlp, rows)], 0),
        n_dp,
        n_seq,
    )
    full_qkv = first[:, :, :qkv_cols].reshape(n_dp, n_seq * qkv_cols, rows)
    full_out = first[:, :, qkv_cols : qkv_cols + out_cols].reshape(n_dp, n_seq * out_cols, rows)
    gain_one = (
        first[0, :, qkv_cols + out_cols, : gain_attn.shape[0]].reshape(-1).astype(jnp.float32)
    )
    stream = tokens.astype(jnp.float32)
    normed_a, factor_a = layer_norm(stream)
    h_attn = (normed_a * gain_one).astype(jnp.bfloat16)
    qkv = apply_t(h_attn, full_qkv, n_dp)
    offset_base = lax.axis_index(("dp", "seq")) * count
    place = (offset_base + jnp.arange(count, dtype=jnp.int32) - doc_start).astype(jnp.float32)
    cosine, sine = rotary_tables(place)
    query, key_value = rope_fwd(qkv, cosine, sine)
    tag_query = doc_start + 1
    tag_key = jnp.where(real == 1, tag_query, 0)
    wide_tag = padded(tag_key, ((("dp", "seq"), 0),), HALF)
    attn_out, halo_lo, halo_hi = attn_fwd(query, key_value, tag_query, wide_tag)
    mid = stream + apply_t(attn_out, full_out, n_dp)
    mid, second = lax.optimization_barrier((mid, second))
    at = 0
    full_in = second[:, :, at : at + in_cols].reshape(n_dp, n_seq * in_cols, rows)
    at += in_cols
    full_down = down_from_lines(second[:, :, at : at + down_lines], rows).reshape(
        n_dp, n_seq * down_cols, down_rows
    )
    at += down_lines
    gain_two = second[0, :, at, : gain_mlp.shape[0]].reshape(-1).astype(jnp.float32)
    normed_m, factor_m = layer_norm(mid)
    h_mlp = (normed_m * gain_two).astype(jnp.bfloat16)
    gate_up = apply_t(h_mlp, full_in, n_dp)
    hidden_out, glu_pull = jax.vjp(glu_piece, gate_up)
    hidden = hidden_out.astype(jnp.bfloat16)
    result = mid + apply_t(hidden, full_down, n_dp)
    output = result.astype(jnp.bfloat16)
    grad_down = grad_t(cotangent, hidden, n_dp)
    grad_hidden = apply_back(cotangent, full_down)
    grad_gate_up = glu_pull(grad_hidden)[0].astype(jnp.bfloat16)
    grad_inw = grad_t(grad_gate_up, h_mlp, n_dp)
    grad_hmlp = apply_back(grad_gate_up, full_in)
    grad_gain_two = jnp.sum(grad_hmlp * normed_m, axis=0)
    grad_mid = cotangent.astype(jnp.float32) + norm_back(grad_hmlp * gain_two, normed_m, factor_m)
    grad_branch = grad_mid.astype(jnp.bfloat16)
    grad_outw = grad_t(grad_branch, attn_out, n_dp)
    grad_attn = apply_back(grad_branch, full_out).astype(jnp.bfloat16)
    grad_qkv = attn_bwd(
        query, key_value, halo_lo, halo_hi, tag_query, wide_tag, grad_attn, cosine, sine
    )
    grad_qkvw = grad_t(grad_qkv, h_attn, n_dp)
    grad_hattn = apply_back(grad_qkv, full_qkv)
    grad_gain_one = jnp.sum(grad_hattn * normed_a, axis=0)
    grad_tokens = grad_mid + norm_back(grad_hattn * gain_one, normed_a, factor_a)
    height = out_cols + in_cols + down_lines + qkv_cols + 8
    tail = 8 + (-height) % (RING_WAYS * 16)
    gain_both = jnp.concatenate(
        [
            gain_blocks(grad_gain_two, 1, n_seq, rows, 1)[0],
            gain_blocks(grad_gain_one, 1, n_seq, rows, tail - 1)[0],
        ],
        1,
    )
    blocks = jnp.stack(
        [
            jnp.concatenate(
                [
                    *lax.optimization_barrier(
                        (
                            grad_outw[d].reshape(n_seq, out_cols, rows),
                            grad_inw[d].reshape(n_seq, in_cols, rows),
                            grad_down[d]
                            .reshape(n_seq, down_cols, down_rows)
                            .reshape(n_seq, down_lines, rows),
                            grad_qkvw[d].reshape(n_seq, qkv_cols, rows),
                            gain_both,
                        )
                    ),
                ],
                1,
            )
            for d in range(n_dp)
        ]
    )
    depth = blocks.shape[2]
    half = lax.psum_scatter(
        blocks.reshape(n_dp, n_seq * depth, rows).astype(jnp.bfloat16),
        "dp",
        scatter_dimension=0,
        tiled=True,
    )
    late = ring_reduce(half.reshape(n_seq, depth, rows), order, RING_WAYS)
    at = 0
    late_out = late[at : at + out_cols].T
    at += out_cols
    late_in = late[at : at + in_cols].T
    at += in_cols
    late_down = late[at : at + down_lines].reshape(down_cols, down_rows).T
    at += down_lines
    late_qkv = late[at : at + qkv_cols].T
    at += qkv_cols
    late_gain_two = late[at, : gain_mlp.shape[0]]
    late_gain_one = late[at + 1, : gain_attn.shape[0]]
    return (
        output,
        grad_tokens,
        late_qkv,
        late_out,
        late_in,
        late_down,
        late_gain_one,
        late_gain_two,
    )


def solution(mesh):
    placed = (
        P(("dp", "seq"), None),
        P(("dp", "seq")),
        P(("dp", "seq")),
        P("dp", "seq"),
        P("dp", "seq"),
        P("dp", "seq"),
        P("dp", "seq"),
        P("seq"),
        P("seq"),
        P(("dp", "seq"), None),
    )
    return jax.shard_map(
        functools.partial(on_device, ring_order(mesh)),
        mesh=mesh,
        in_specs=placed,
        out_specs=(
            P(("dp", "seq"), None),
            P(("dp", "seq"), None),
            P("dp", "seq"),
            P("dp", "seq"),
            P("dp", "seq"),
            P("dp", "seq"),
            P("seq"),
            P("seq"),
        ),
        check_vma=False,
    )
```
